32 devices in a mesh: dp: 16 (over z, y, core), space: 2 (over x).
Axes of the slice: x: 2, y: 2, z: 4, core: 2. Of those that a mesh axis runs over, the one named last changes fastest.
Arguments:
- image_in: bfloat16 [96, 14, 14, 1024], P('dp', 'space'), may hold values from -6 to 6
- text_in: bfloat16 [96, 64, 768], P(('dp', 'space')), may hold values from -6 to 6
- prefix: int32 [96], P(('dp', 'space')), may hold values from 0 to 32
- text_len: int32 [96], P(('dp', 'space')), may hold values from 33 to 64
- cotangent: bfloat16 [96, 260, 768], P(('dp', 'space')), may hold values from -6 to 6
- conv_in_w: bfloat16 [1024, 256], replicated, may hold values from -0.1875 to 0.1875
- bn1_gain: float32 [256], replicated, may hold values from 0.5 to 1.5
- bn1_shift: float32 [256], replicated, may hold values from -1.5 to 1.5
- conv_mid_w: bfloat16 [3, 3, 256, 256], replicated, may hold values from -0.125 to 0.125
- bn2_gain: float32 [256], replicated, may hold values from 0.5 to 1.5
- bn2_shift: float32 [256], replicated, may hold values from -1.5 to 1.5
- conv_out_w: bfloat16 [256, 1024], replicated, may hold values from -0.375 to 0.375
- bn3_gain: float32 [1024], replicated, may hold values from 0.5 to 1.5
- bn3_shift: float32 [1024], replicated, may hold values from -1.5 to 1.5
- proj_w: bfloat16 [1024, 768], replicated, may hold values from -0.1875 to 0.1875
- proj_b: float32 [768], replicated, may hold values from -1.5 to 1.5
- ln1_gain: float32 [768], replicated, may hold values from 0.5 to 1.5
- ln1_shift: float32 [768], replicated, may hold values from -1.5 to 1.5
- qkv_w: bfloat16 [768, 2304], replicated, may hold values from -0.21875 to 0.21875
- query_bias: float32 [768], replicated, may hold values from -1.5 to 1.5
- value_bias: float32 [768], replicated, may hold values from -1.5 to 1.5
- out_w: bfloat16 [768, 768], replicated, may hold values from -0.875 to 0.875
- out_b: float32 [768], replicated, may hold values from -1.5 to 1.5
- ln2_gain: float32 [768], replicated, may hold values from 0.5 to 1.5
- ln2_shift: float32 [768], replicated, may hold values from -1.5 to 1.5
- up_w: bfloat16 [768, 3072], replicated, may hold values from -0.21875 to 0.21875
- up_b: float32 [3072], replicated, may hold values from -1.5 to 1.5
- down_w: bfloat16 [3072, 768], replicated, may hold values from -0.109375 to 0.109375
- down_b: float32 [768], replicated, may hold values from -1.5 to 1.5
Outputs:
- block_out: bfloat16 [96, 260, 768], P(('dp', 'space'))
- image_grad: bfloat16 [96, 14, 14, 1024], P('dp', 'space')
- text_grad: bfloat16 [96, 64, 768], P(('dp', 'space'))
- conv_in_grad: float32 [1024, 256], P('space', 'dp')
- bn1_gain_grad: float32 [256], replicated
- bn1_shift_grad: float32 [256], replicated
- conv_mid_grad: float32 [3, 3, 256, 256], P(None, None, 'space', 'dp')
- bn2_gain_grad: float32 [256], replicated
- bn2_shift_grad: float32 [256], replicated
- conv_out_grad: float32 [256, 1024], P('space', 'dp')
- bn3_gain_grad: float32 [1024], replicated
- bn3_shift_grad: float32 [1024], replicated
- proj_w_grad: float32 [1024, 768], P('space', 'dp')
- proj_b_grad: float32 [768], replicated
- ln1_gain_grad: float32 [768], replicated
- ln1_shift_grad: float32 [768], replicated
- qkv_w_grad: float32 [768, 2304], P('space', 'dp')
- query_bias_grad: float32 [768], replicated
- value_bias_grad: float32 [768], replicated
- out_w_grad: float32 [768, 768], P('space', 'dp')
- out_b_grad: float32 [768], replicated
- ln2_gain_grad: float32 [768], replicated
- ln2_shift_grad: float32 [768], replicated
- up_w_grad: float32 [768, 3072], P('space', 'dp')
- up_b_grad: float32 [3072], replicated
- down_w_grad: float32 [3072, 768], P('space', 'dp')
- down_b_grad: float32 [768], replicated
The draws below stay inside these ranges and needn't reach their ends.
Inputs may be any that keep to these rules, and one draw needn't show every extreme that they name: prefix never exceeds the example's text_len. Text rows from text_len on are padding that no position attends to.
All inputs are finite; a program needn't handle non-finite values.
Results may differ from the reference program's by a relative error of at most 0.02.
Values may be sent and summed in bfloat16 or wider, within the bound.
No kernel may reach another device: no remote copies, remote signals or barrier semaphores. Data moves between devices by JAX's collectives and lax.ppermute only.
A program may use at most 192 MiB of HBM per device.

```python
import jax
import jax.numpy as jnp
from jax import lax

C = 1024
M = 256
HD = 64
D = 768
FF = 3072
IMG_ROWS = 14
IMG_COLS = 14
TXT = 64
NIMG = 196
SEQ = 260
GROUP = 6
EXAMPLES = 96


def place_ends(drawn, key, low, high):
    spot = [jax.random.randint(jax.random.fold_in(key, axis), (), 0, length) for axis, length in enumerate(drawn.shape)]
    longest = drawn.shape.index(max(drawn.shape))
    beside = spot[:longest] + [(spot[longest] + 1) % drawn.shape[longest]] + spot[longest + 1:]
    return drawn.at[tuple(spot)].set(low).at[tuple(beside)].set(high)


def raised(drawn, own_key, source, target, parts, factor):
    def block_of(axis_at):
        return (jnp.arange(drawn.shape[axis_at]) // (drawn.shape[axis_at] // parts)).reshape((-1,) + (1,) * (drawn.ndim - 1 - axis_at))

    first = jax.random.permutation(own_key, parts)[block_of(target)]
    second = (block_of(target) + parts // 2) % parts
    return jnp.where((block_of(source) == first) | (block_of(source) == second), factor * drawn, drawn)


def level_of(key, dims, split, least, high):
    factor_of = 1.0
    for dim, blocks in split:
        heights = jax.random.uniform(jax.random.fold_in(jax.random.fold_in(key, 6), dim), (blocks,), jnp.float32, least / len(split), high / len(split))
        factor_of = factor_of * jnp.repeat(jnp.exp(heights), dims[dim] // blocks).reshape((-1,) + (1,) * (len(dims) - 1 - dim))
    return factor_of


def bell_draw(stream_key, dims, scale, most, pieces=(), kind=jnp.bfloat16):
    drawn = scale * jax.random.normal(stream_key, dims, jnp.float32)
    if pieces:
        drawn = drawn * level_of(stream_key, dims, pieces, -0.22, 0.18)
    return jnp.clip(drawn, -most, most).astype(kind)


def gaussian_with(own_key, dims, deviation, most, shards, heavy, kind=jnp.bfloat16):
    values = deviation * jax.random.normal(own_key, dims, jnp.float32)
    if shards:
        values = values * level_of(own_key, dims, shards, -0.22, 0.18)
    return jnp.clip(raised(values, jax.random.fold_in(own_key, 3), *heavy), -most, most).astype(kind)


def setup_inputs(seed: int = 0) -> dict:
    seeds = jax.random.split(jax.random.key(seed), 30)
    image_in = bell_draw(seeds[0], (EXAMPLES, IMG_ROWS, IMG_COLS, C), 1.0, 6.0, ((0, 16), (1, 2)))
    text_in = bell_draw(seeds[1], (EXAMPLES, TXT, D), 1.0, 6.0, ((0, 32),))
    prefix = place_ends(jax.random.randint(seeds[2], (EXAMPLES,), 0, TXT // 2 + 1), jax.random.fold_in(seeds[2], 1), 0, (TXT // 2 + 1) - 1).astype(jnp.int32)
    text_len = place_ends(jax.random.randint(seeds[3], (EXAMPLES,), TXT // 2 + 1, TXT + 1), jax.random.fold_in(seeds[3], 1), TXT // 2 + 1, TXT).astype(jnp.int32)
    cotangent = gaussian_with(seeds[4], (EXAMPLES, SEQ, D), 1.0, 6.0, ((0, 32),), (0, 2, 32, 2.75))
    conv_in_w = bell_draw(seeds[5], (C, M), C ** -0.5, 0.1875)
    bn1_gain = jnp.clip(1.0 + 0.1 * jax.random.normal(seeds[6], (M,), jnp.float32), 0.5, 1.5)
    bn1_shift = bell_draw(seeds[7], (M,), 0.3, 1.5, (), jnp.float32)
    conv_mid_w = bell_draw(seeds[8], (3, 3, M, M), (9 * M) ** -0.5, 0.125)
    bn2_gain = jnp.clip(1.0 + 0.1 * jax.random.normal(seeds[9], (M,), jnp.float32), 0.5, 1.5)
    bn2_shift = bell_draw(seeds[10], (M,), 0.3, 1.5, (), jnp.float32)
    conv_out_w = bell_draw(seeds[11], (M, C), M ** -0.5, 0.375)
    bn3_gain = jnp.clip(1.0 + 0.1 * jax.random.normal(seeds[12], (C,), jnp.float32), 0.5, 1.5)
    bn3_shift = bell_draw(seeds[13], (C,), 0.3, 1.5, (), jnp.float32)
    proj_w = bell_draw(seeds[14], (C, D), C ** -0.5, 0.1875)
    proj_b = bell_draw(seeds[15], (D,), 0.3, 1.5, (), jnp.float32)
    ln1_gain = jnp.clip(1.0 + 0.1 * jax.random.normal(seeds[16], (D,), jnp.float32), 0.5, 1.5)
    ln1_shift = bell_draw(seeds[17], (D,), 0.3, 1.5, (), jnp.float32)
    qkv_w = bell_draw(seeds[18], (D, 3 * D), D ** -0.5, 0.21875)
    query_bias = bell_draw(seeds[19], (D,), 0.3, 1.5, (), jnp.float32)
    value_bias = bell_draw(seeds[20], (D,), 0.3, 1.5, (), jnp.float32)
    out_w = bell_draw(seeds[21], (D, D), (D // 16) ** -0.5, 0.875)
    out_b = bell_draw(seeds[22], (D,), 0.3, 1.5, (), jnp.float32)
    ln2_gain = jnp.clip(1.0 + 0.1 * jax.random.normal(seeds[23], (D,), jnp.float32), 0.5, 1.5)
    ln2_shift = bell_draw(seeds[24], (D,), 0.3, 1.5, (), jnp.float32)
    up_w = bell_draw(seeds[25], (D, FF), D ** -0.5, 0.21875)
    up_b = bell_draw(seeds[26], (FF,), 0.3, 1.5, (), jnp.float32)
    down_w = bell_draw(seeds[27], (FF, D), FF ** -0.5, 0.109375)
    down_b = bell_draw(seeds[28], (D,), 0.3, 1.5, (), jnp.float32)
    return dict(image_in=image_in, text_in=text_in, prefix=prefix, text_len=text_len, cotangent=cotangent, conv_in_w=conv_in_w, bn1_gain=bn1_gain, bn1_shift=bn1_shift, conv_mid_w=conv_mid_w, bn2_gain=bn2_gain, bn2_shift=bn2_shift, conv_out_w=conv_out_w, bn3_gain=bn3_gain, bn3_shift=bn3_shift, proj_w=proj_w, proj_b=proj_b, ln1_gain=ln1_gain, ln1_shift=ln1_shift, qkv_w=qkv_w, query_bias=query_bias, value_bias=value_bias, out_w=out_w, out_b=out_b, ln2_gain=ln2_gain, ln2_shift=ln2_shift, up_w=up_w, up_b=up_b, down_w=down_w, down_b=down_b)


@jax.custom_vjp
def low(v):
    return lax.optimization_barrier(v.astype(jnp.bfloat16)).astype(jnp.float32)

@jax.custom_vjp
def low_back(v):
    return v

def low_keep(v):
    return (low(v), None)

def low_pass(kept, grad):
    return (grad,)

def back_keep(v):
    return (v, None)

def back_low(kept, grad):
    return (low(grad),)
low.defvjp(low_keep, low_pass)
low_back.defvjp(back_keep, back_low)
highest = lax.Precision.HIGHEST
eps_batch = 1e-05
eps_layer = 1e-06
masked_value = -1e+30
score_scale = 0.125

def matmul(left, right):
    return jnp.dot(left, right, precision=highest, preferred_element_type=jnp.float32)

def one_by_one(values, weight):
    dims_in = values.shape
    return matmul(values.reshape(-1, dims_in[-1]), weight).reshape(dims_in[:-1] + (weight.shape[1],))

def conv_three(values, weight):
    return lax.conv_general_dilated(values, weight, (1, 1), ((1, 1), (1, 1)), dimension_numbers=('NHWC', 'HWIO', 'NHWC'), precision=highest, preferred_element_type=jnp.float32)

def batch_norm(values, bn_gain, bn_shift):
    batch_mean = lax.optimization_barrier(jnp.mean(values, axis=(0, 1, 2)))
    spread = lax.optimization_barrier(jnp.mean(values * values, axis=(0, 1, 2))) - batch_mean * batch_mean
    return (values - batch_mean) * lax.rsqrt(spread + eps_batch) * bn_gain + bn_shift

def layer_norm(hidden, ln_gain, ln_shift):
    row_mean = lax.optimization_barrier(jnp.mean(hidden, axis=-1, keepdims=True))
    centered = hidden - row_mean
    spread = lax.optimization_barrier(jnp.mean(centered * centered, axis=-1, keepdims=True))
    return centered * lax.rsqrt(spread + eps_layer) * ln_gain + ln_shift

def block(hidden_in, prefix, text_len, params):
    ln1_gain, ln1_shift, qkv_w, query_bias, value_bias, out_w, out_b, ln2_gain, ln2_shift, up_w, up_b, down_w, down_b = params
    group_ex, seq_len, width = hidden_in.shape
    heads = width // HD
    z_one = low(layer_norm(hidden_in, ln1_gain, ln1_shift))
    qkv_all = jnp.einsum('gsd,de->gse', z_one, qkv_w, precision=highest)
    query_rows = low_back(low(qkv_all[..., :width] + query_bias)).reshape(group_ex, seq_len, heads, HD)
    key_rows = low_back(low(qkv_all[..., width:2 * width])).reshape(group_ex, seq_len, heads, HD)
    value_rows = low_back(low(qkv_all[..., 2 * width:] + value_bias)).reshape(group_ex, seq_len, heads, HD)
    positions = jnp.arange(seq_len, dtype=jnp.int32)
    open_end = (NIMG + prefix)[:, None, None]
    valid_end = (NIMG + text_len)[:, None, None]
    key_pos = positions[None, None, :]
    query_pos = positions[None, :, None]
    visible = (key_pos < valid_end) & ((key_pos < open_end) | (key_pos <= query_pos))
    scores = low_back(jnp.einsum('gqhe,gkhe->ghqk', query_rows, key_rows, precision=highest) * score_scale)
    scores = jnp.where(visible[:, None], scores, masked_value)
    row_max = lax.optimization_barrier(jnp.max(scores, axis=-1, keepdims=True))
    expo = jnp.exp(scores - row_max)
    probs = expo / lax.optimization_barrier(jnp.sum(expo, axis=-1, keepdims=True))
    attended = jnp.einsum('ghqk,gkhe->gqhe', low(probs), value_rows, precision=highest)
    attended = low_back(low(attended)).reshape(group_ex, seq_len, width)
    resid_one = hidden_in + low_back(jnp.einsum('gsd,de->gse', attended, out_w, precision=highest)) + out_b
    z_two = low(layer_norm(resid_one, ln2_gain, ln2_shift))
    pre_gelu = low_back(jnp.einsum('gsd,df->gsf', z_two, up_w, precision=highest) + up_b)
    gelu_out = low(jax.nn.gelu(pre_gelu))
    return resid_one + low_back(jnp.einsum('gsf,fd->gsd', gelu_out, down_w, precision=highest)) + down_b

def forward(image_f, text_f, weights, prefix, text_len):
    conv_in_w, bn1_gain, bn1_shift, conv_mid_w, bn2_gain, bn2_shift, conv_out_w, bn3_gain, bn3_shift, proj_w, proj_b, ln1_gain, ln1_shift, qkv_w, query_bias, value_bias, out_w, out_b, ln2_gain, ln2_shift, up_w, up_b, down_w, down_b = weights
    act_one = low_back(one_by_one(image_f, conv_in_w))
    relu_one = low(jax.nn.gelu(batch_norm(act_one, bn1_gain, bn1_shift)))
    act_two = low_back(conv_three(relu_one, conv_mid_w))
    relu_two = low(jax.nn.gelu(batch_norm(act_two, bn2_gain, bn2_shift)))
    act_three = low_back(one_by_one(relu_two, conv_out_w))
    stem_out = low(jax.nn.gelu(batch_norm(act_three, bn3_gain, bn3_shift) + image_f))
    tokens_img = low_back(low(one_by_one(stem_out, proj_w) + proj_b))
    hidden_in = jnp.concatenate([tokens_img.reshape(EXAMPLES, NIMG, D), text_f], axis=1)
    block_params = (ln1_gain, ln1_shift, qkv_w, query_bias, value_bias, out_w, out_b, ln2_gain, ln2_shift, up_w, up_b, down_w, down_b)
    grouped = hidden_in.reshape(EXAMPLES // GROUP, GROUP, SEQ, D)
    run_block = jax.checkpoint(lambda item: block(item[0], item[1], item[2], block_params))
    output = lax.map(run_block, (grouped, prefix.reshape(-1, GROUP), text_len.reshape(-1, GROUP)))
    return output.reshape(EXAMPLES, SEQ, D)

def reference(image_in, text_in, prefix, text_len, cotangent, conv_in_w, bn1_gain, bn1_shift, conv_mid_w, bn2_gain, bn2_shift, conv_out_w, bn3_gain, bn3_shift, proj_w, proj_b, ln1_gain, ln1_shift, qkv_w, query_bias, value_bias, out_w, out_b, ln2_gain, ln2_shift, up_w, up_b, down_w, down_b):
    params = (conv_in_w, bn1_gain, bn1_shift, conv_mid_w, bn2_gain, bn2_shift, conv_out_w, bn3_gain, bn3_shift, proj_w, proj_b, ln1_gain, ln1_shift, qkv_w, query_bias, value_bias, out_w, out_b, ln2_gain, ln2_shift, up_w, up_b, down_w, down_b)
    floats = tuple((weight.astype(jnp.float32) for weight in params))
    result, pullback = jax.vjp(lambda image_f, text_f, weights: forward(image_f, text_f, weights, prefix, text_len), image_in.astype(jnp.float32), text_in.astype(jnp.float32), floats)
    image_grad, text_grad, weight_grads = pullback(cotangent.astype(jnp.float32))
    g_conv_in, g_bn1_gain, g_bn1_shift, g_conv_mid, g_bn2_gain, g_bn2_shift, g_conv_out, g_bn3_gain, g_bn3_shift, g_proj_w, g_proj_b, g_ln1_gain, g_ln1_shift, g_qkv_w, g_query_bias, g_value_bias, g_out_w, g_out_b, g_ln2_gain, g_ln2_shift, g_up_w, g_up_b, g_down_w, g_down_b = weight_grads
    return (result.astype(jnp.bfloat16), image_grad.astype(jnp.bfloat16), text_grad.astype(jnp.bfloat16), g_conv_in, g_bn1_gain, g_bn1_shift, g_conv_mid, g_bn2_gain, g_bn2_shift, g_conv_out, g_bn3_gain, g_bn3_shift, g_proj_w, g_proj_b, g_ln1_gain, g_ln1_shift, g_qkv_w, g_query_bias, g_value_bias, g_out_w, g_out_b, g_ln2_gain, g_ln2_shift, g_up_w, g_up_b, g_down_w, g_down_b)
```

```python
import jax
import jax.numpy as jnp
from jax import lax
from jax.sharding import PartitionSpec as P

HD = 64


eps_batch = 1e-05
eps_layer = 1e-06
masked_value = -1e30
score_scale = 0.125


def padded_2(x, sides, width):
    for axis, dim in sides:
        size, length = (lax.axis_size(axis), x.shape[dim])
        up = [(i, (i + 1) % size) for i in range(size - 1)]
        down = [(j, i) for i, j in up]
        last = lax.slice_in_dim(x, length - width, length, axis=dim)
        initial = lax.slice_in_dim(x, 0, width, axis=dim)
        before = lax.ppermute(last, axis, up)
        after = lax.ppermute(initial, axis, down)
        x = jnp.concatenate([before, x, after], axis=dim)
    return x


def matmul(left, right):
    return jnp.dot(left, right, preferred_element_type=jnp.float32)


def by_transpose(left, right):
    return lax.dot_general(
        left, right, (((1,), (1,)), ((), ())), preferred_element_type=jnp.float32
    )


def weight_grad(left, right):
    return lax.dot_general(
        left, right, (((0,), (0,)), ((), ())), preferred_element_type=jnp.float32
    )


def layer_norm(hidden, ln_gain, ln_shift):
    row_mean = jnp.mean(hidden, axis=-1, keepdims=True)
    centered = hidden - row_mean
    spread = jnp.mean(centered * centered, axis=-1, keepdims=True)
    return centered * lax.rsqrt(spread + eps_layer) * ln_gain + ln_shift


EVERY = ("dp", "space")


def group_sum(part):
    count = lax.axis_size(EVERY)
    copies = jnp.broadcast_to(part[None], (count,) + part.shape)
    return jnp.sum(lax.all_to_all(copies, EVERY, split_axis=0, concat_axis=0, tiled=True), axis=0)


def vector_sums(vectors):
    count = lax.axis_size(EVERY)
    sizes = [v.shape[0] for v in vectors]
    flat = jnp.concatenate(vectors)
    chunk = -(-flat.shape[0] // (count * 128)) * 128
    flat = jnp.pad(flat, (0, chunk * count - flat.shape[0])).reshape(count, chunk)
    mine = jnp.sum(lax.all_to_all(flat, EVERY, split_axis=0, concat_axis=0, tiled=True), axis=0)
    copies = jnp.broadcast_to(mine[None], (count, chunk))
    whole = lax.all_to_all(copies, EVERY, split_axis=0, concat_axis=0, tiled=True).reshape(-1)
    out, at = [], 0
    for size in sizes:
        out.append(whole[at : at + size])
        at += size
    return out


def halve_axis(x, axis, bit):
    size = lax.axis_size("dp")
    mine = (lax.axis_index("dp") // bit) % 2
    keep = lax.dynamic_index_in_dim(x, mine, axis, keepdims=True)
    send = lax.dynamic_index_in_dim(x, 1 - mine, axis, keepdims=True)
    return keep + lax.ppermute(send, "dp", [(j, j ^ bit) for j in range(size)])


def halve_space(x, axis):
    mine = lax.axis_index("space")
    keep = lax.dynamic_index_in_dim(x, mine, axis, keepdims=True)
    send = lax.dynamic_index_in_dim(x, 1 - mine, axis, keepdims=True)
    return keep + lax.ppermute(send, "space", [(0, 1), (1, 0)])


def scattered(grad_t, order):
    size = lax.axis_size("dp")
    bits = size.bit_length() - 1
    cols, rows = grad_t.shape
    x = grad_t.astype(jnp.bfloat16).reshape((2,) * bits + (cols // size, 2, rows // 2))
    x = halve_axis(x, bits - 1, 1)
    rest = list(range(1, bits))
    rest = rest[order % len(rest):] + rest[: order % len(rest)] if order else rest
    stages = [("dp", b) for b in rest]
    stages.insert((0, 1, len(stages))[order % 3], ("space", 0))
    for kind, b in stages:
        x = halve_space(x, bits + 1) if kind == "space" else halve_axis(x, bits - 1 - b, 1 << b)
    return x.reshape(cols // size, rows // 2).astype(jnp.float32).T


def batch_stats(values, pixel_count):
    totals = group_sum(jnp.stack((jnp.sum(values, axis=0), jnp.sum(values * values, axis=0))))
    batch_mean = totals[0] / pixel_count
    spread = totals[1] / pixel_count - batch_mean * batch_mean
    return (batch_mean, lax.rsqrt(spread + eps_batch))


def batch_back(grad_out, normed, inv_std, bn_gain, pixel_count):
    totals = group_sum(
        jnp.stack((jnp.sum(grad_out, axis=0), jnp.sum(grad_out * normed, axis=0)))
    )
    grad_in = (
        bn_gain
        * inv_std
        * (grad_out - totals[0] / pixel_count - normed * (totals[1] / pixel_count))
    )
    return (grad_in, totals[1], totals[0])


def conv_taps(padded, band_rows, band_cols, flipped):
    tap_list = []
    for row_off in range(3):
        for col_off in range(3):
            start_row = 2 - row_off if flipped else row_off
            start_col = 2 - col_off if flipped else col_off
            tap_list.append(
                padded[:, start_row : start_row + band_rows, start_col : start_col + band_cols, :]
            )
    return jnp.concatenate(tap_list, axis=-1).reshape(-1, 9 * padded.shape[-1])


def band_halo_pad(values):
    return jnp.pad(values, ((0, 0), (0, 0), (1, 1), (0, 0)))


def shards(
    image_in,
    text_in,
    prefix,
    text_len,
    cotangent,
    conv_in_w,
    bn1_gain,
    bn1_shift,
    conv_mid_w,
    bn2_gain,
    bn2_shift,
    conv_out_w,
    bn3_gain,
    bn3_shift,
    proj_w,
    proj_b,
    ln1_gain,
    ln1_shift,
    qkv_w,
    query_bias,
    value_bias,
    out_w,
    out_b,
    ln2_gain,
    ln2_shift,
    up_w,
    up_b,
    down_w,
    down_b,
):
    band_ex, band_rows, band_cols, channels = image_in.shape
    middle = conv_in_w.shape[1]
    width = proj_w.shape[1]
    examples = text_in.shape[0]
    all_rows = band_rows * lax.axis_size("space")
    n_image = all_rows * band_cols
    seq_len = n_image + text_in.shape[1]
    rows_all = examples * seq_len
    heads = width // HD
    pixel_count = float(
        band_ex * band_rows * band_cols * lax.axis_size("dp") * lax.axis_size("space")
    )
    x_flat = image_in.reshape(-1, channels)
    act_one = matmul(x_flat, conv_in_w)
    mean_one, rstd_one = batch_stats(act_one, pixel_count)
    norm_one = (act_one - mean_one) * rstd_one
    pre_one = norm_one * bn1_gain + bn1_shift
    smooth_one, smooth_one_pull = jax.vjp(jax.nn.gelu, pre_one)
    relu_one = smooth_one.astype(jnp.bfloat16)
    halo_one = padded_2(relu_one.reshape(band_ex, band_rows, band_cols, middle), (("space", 1),), 1)
    patch_fwd = conv_taps(band_halo_pad(halo_one), band_rows, band_cols, False)
    act_two = matmul(patch_fwd, conv_mid_w.reshape(9 * middle, middle))
    mean_two, rstd_two = batch_stats(act_two, pixel_count)
    norm_two = (act_two - mean_two) * rstd_two
    pre_two = norm_two * bn2_gain + bn2_shift
    smooth_two, smooth_two_pull = jax.vjp(jax.nn.gelu, pre_two)
    relu_two = smooth_two.astype(jnp.bfloat16)
    act_three = matmul(relu_two, conv_out_w)
    mean_three, rstd_three = batch_stats(act_three, pixel_count)
    norm_three = (act_three - mean_three) * rstd_three
    pre_three = norm_three * bn3_gain + bn3_shift + x_flat.astype(jnp.float32)
    smooth_three, smooth_three_pull = jax.vjp(jax.nn.gelu, pre_three)
    stem_out = smooth_three.astype(jnp.bfloat16)
    tokens_img = (matmul(stem_out, proj_w) + proj_b).astype(jnp.bfloat16)
    moved = lax.all_to_all(
        tokens_img.reshape(band_ex, band_rows, band_cols, width),
        "space",
        split_axis=0,
        concat_axis=1,
        tiled=True,
    )
    hidden_in = jnp.concatenate(
        [moved.reshape(examples, n_image, width).astype(jnp.float32), text_in.astype(jnp.float32)],
        axis=1,
    )
    normed_one, ln_one_pull = jax.vjp(layer_norm, hidden_in, ln1_gain, ln1_shift)
    z_one = normed_one.astype(jnp.bfloat16).reshape(rows_all, width)
    qkv_all = matmul(z_one, qkv_w)
    query_rows = (
        (qkv_all[:, :width] + query_bias).astype(jnp.bfloat16).reshape(examples, seq_len, heads, HD)
    )
    key_rows = (
        qkv_all[:, width : 2 * width].astype(jnp.bfloat16).reshape(examples, seq_len, heads, HD)
    )
    value_rows = (
        (qkv_all[:, 2 * width :] + value_bias)
        .astype(jnp.bfloat16)
        .reshape(examples, seq_len, heads, HD)
    )
    positions = jnp.arange(seq_len, dtype=jnp.int32)
    open_end = (n_image + prefix)[:, None, None]
    valid_end = (n_image + text_len)[:, None, None]
    key_pos = positions[None, None, :]
    query_pos = positions[None, :, None]
    visible = (key_pos < valid_end) & ((key_pos < open_end) | (key_pos <= query_pos))

    def scores_of():
        raw_scores = (
            jnp.einsum("bqhe,bkhe->bhqk", query_rows, key_rows, preferred_element_type=jnp.float32)
            * score_scale
        )
        return jnp.where(visible[:, None], raw_scores, masked_value)

    scores = scores_of()
    row_max = jnp.max(scores, axis=-1, keepdims=True)
    expo = jnp.exp(scores - row_max)
    row_sum = jnp.sum(expo, axis=-1, keepdims=True)
    probs = expo / row_sum
    log_total = row_max + jnp.log(row_sum)
    attended = jnp.einsum(
        "bhqk,bkhe->bqhe",
        probs.astype(jnp.bfloat16),
        value_rows,
        preferred_element_type=jnp.float32,
    )
    attn_out = attended.astype(jnp.bfloat16).reshape(rows_all, width)
    resid_one = hidden_in.reshape(rows_all, width) + matmul(attn_out, out_w) + out_b
    normed_two, ln_two_pull = jax.vjp(layer_norm, resid_one, ln2_gain, ln2_shift)
    z_two = normed_two.astype(jnp.bfloat16)
    pre_gelu = matmul(z_two, up_w) + up_b
    gelu_out, gelu_pull = jax.vjp(jax.nn.gelu, pre_gelu)
    gelu_low = gelu_out.astype(jnp.bfloat16)
    block_out = (
        (resid_one + matmul(gelu_low, down_w) + down_b)
        .astype(jnp.bfloat16)
        .reshape(examples, seq_len, width)
    )
    grad_top = cotangent.astype(jnp.float32).reshape(rows_all, width)
    down_b_grad = jnp.sum(grad_top, axis=0)
    branch_low = grad_top.astype(jnp.bfloat16)
    down_w_grad = weight_grad(branch_low, gelu_low)
    gelu_grad = gelu_pull(by_transpose(branch_low, down_w))[0].astype(jnp.bfloat16)
    up_b_grad = jnp.sum(gelu_grad.astype(jnp.float32), axis=0)
    up_w_grad = weight_grad(gelu_grad, z_two)
    norm_grad_two, ln2_gain_grad, ln2_shift_grad = ln_two_pull(by_transpose(gelu_grad, up_w))
    resid_grad = grad_top + norm_grad_two
    out_b_grad = jnp.sum(resid_grad, axis=0)
    proj_low = resid_grad.astype(jnp.bfloat16)
    out_w_grad = weight_grad(proj_low, attn_out)
    attn_grad = (
        by_transpose(proj_low, out_w).astype(jnp.bfloat16).reshape(examples, seq_len, heads, HD)
    )
    probs_back = jnp.exp(scores_of() - log_total)
    value_grad = jnp.einsum(
        "bhqk,bqhe->bkhe",
        probs_back.astype(jnp.bfloat16),
        attn_grad,
        preferred_element_type=jnp.float32,
    ).astype(jnp.bfloat16)
    prob_grad = jnp.einsum(
        "bqhe,bkhe->bhqk", attn_grad, value_rows, preferred_element_type=jnp.float32
    )
    inner_sum = jnp.sum(probs_back * prob_grad, axis=-1, keepdims=True)
    score_grad = (probs_back * (prob_grad - inner_sum)).astype(jnp.bfloat16)
    query_grad = (
        jnp.einsum("bhqk,bkhe->bqhe", score_grad, key_rows, preferred_element_type=jnp.float32)
        * score_scale
    ).astype(jnp.bfloat16)
    key_grad = (
        jnp.einsum("bhqk,bqhe->bkhe", score_grad, query_rows, preferred_element_type=jnp.float32)
        * score_scale
    ).astype(jnp.bfloat16)
    qkv_grad = jnp.concatenate(
        [
            query_grad.reshape(rows_all, width),
            key_grad.reshape(rows_all, width),
            value_grad.reshape(rows_all, width),
        ],
        axis=1,
    )
    qkv_w_grad = weight_grad(qkv_grad, z_one)
    query_b_grad = jnp.sum(query_grad.astype(jnp.float32).reshape(rows_all, width), axis=0)
    value_b_grad = jnp.sum(value_grad.astype(jnp.float32).reshape(rows_all, width), axis=0)
    norm_grad_one, ln1_gain_grad, ln1_shift_grad = ln_one_pull(
        by_transpose(qkv_grad, qkv_w).reshape(examples, seq_len, width)
    )
    input_grad = resid_grad.reshape(examples, seq_len, width) + norm_grad_one
    text_grad = input_grad[:, n_image:].astype(jnp.bfloat16)
    image_tok_grad = (
        input_grad[:, :n_image].astype(jnp.bfloat16).reshape(examples, all_rows, band_cols, width)
    )
    back_bands = lax.all_to_all(
        image_tok_grad, "space", split_axis=1, concat_axis=0, tiled=True
    ).reshape(-1, width)
    proj_b_grad = jnp.sum(back_bands.astype(jnp.float32), axis=0)
    proj_w_grad = weight_grad(back_bands, stem_out)
    relu_grad_three = smooth_three_pull(by_transpose(back_bands, proj_w))[0]
    act_grad_three, bn3_gain_grad, bn3_shift_grad = batch_back(
        relu_grad_three, norm_three, rstd_three, bn3_gain, pixel_count
    )
    low_three = act_grad_three.astype(jnp.bfloat16)
    conv_out_grad = weight_grad(low_three, relu_two)
    relu_grad_two = smooth_two_pull(by_transpose(low_three, conv_out_w))[0]
    act_grad_two, bn2_gain_grad, bn2_shift_grad = batch_back(
        relu_grad_two, norm_two, rstd_two, bn2_gain, pixel_count
    )
    low_two = act_grad_two.astype(jnp.bfloat16)
    conv_mid_grad = weight_grad(low_two, patch_fwd)
    halo_two = padded_2(low_two.reshape(band_ex, band_rows, band_cols, middle), (("space", 1),), 1)
    patch_back = conv_taps(band_halo_pad(halo_two), band_rows, band_cols, True)
    flipped_w = jnp.transpose(conv_mid_w, (0, 1, 3, 2)).reshape(9 * middle, middle)
    relu_grad_one = smooth_one_pull(matmul(patch_back, flipped_w))[0]
    act_grad_one, bn1_gain_grad, bn1_shift_grad = batch_back(
        relu_grad_one, norm_one, rstd_one, bn1_gain, pixel_count
    )
    low_one = act_grad_one.astype(jnp.bfloat16)
    conv_in_grad = weight_grad(low_one, x_flat)
    image_grad = (
        (by_transpose(low_one, conv_in_w) + relu_grad_three)
        .astype(jnp.bfloat16)
        .reshape(image_in.shape)
    )
    small_sums = vector_sums(
        [
            proj_b_grad,
            ln1_gain_grad,
            ln1_shift_grad,
            query_b_grad,
            value_b_grad,
            out_b_grad,
            ln2_gain_grad,
            ln2_shift_grad,
            up_b_grad,
            down_b_grad,
        ]
    )
    mid_t = conv_mid_grad.reshape(middle, 9, 2, middle // 2).transpose(0, 2, 1, 3).reshape(middle, -1)
    mid_out = scattered(mid_t, 2)
    reduced = (
        scattered(conv_in_grad, 0),
        mid_out.reshape(3, 3, middle // 2, mid_out.shape[1]),
        scattered(conv_out_grad, 1),
        scattered(proj_w_grad, 2),
        scattered(qkv_w_grad, 2),
        scattered(out_w_grad, 1),
        scattered(up_w_grad, 2),
        scattered(down_w_grad, 1),
    )
    return (
        block_out,
        image_grad,
        text_grad,
        reduced[0],
        bn1_gain_grad,
        bn1_shift_grad,
        reduced[1],
        bn2_gain_grad,
        bn2_shift_grad,
        reduced[2],
        bn3_gain_grad,
        bn3_shift_grad,
        reduced[3],
        small_sums[0],
        small_sums[1],
        small_sums[2],
        reduced[4],
        small_sums[3],
        small_sums[4],
        reduced[5],
        small_sums[5],
        small_sums[6],
        small_sums[7],
        reduced[6],
        small_sums[8],
        reduced[7],
        small_sums[9],
    )


def solution(mesh):
    return jax.shard_map(
        shards,
        mesh=mesh,
        in_specs=(
            P("dp", "space", None, None),
            P(("dp", "space"), None, None),
            P(("dp", "space")),
            P(("dp", "space")),
            P(("dp", "space"), None, None),
            P(),
            P(),
            P(),
            P(),
            P(),
            P(),
            P(),
            P(),
            P(),
            P(),
            P(),
            P(),
            P(),
            P(),
            P(),
            P(),
            P(),
            P(),
            P(),
            P(),
            P(),
            P(),
            P(),
            P(),
        ),
        out_specs=(
            P(("dp", "space"), None, None),
            P("dp", "space", None, None),
            P(("dp", "space"), None, None),
            P("space", "dp"),
            P(),
            P(),
            P(None, None, "space", "dp"),
            P(),
            P(),
            P("space", "dp"),
            P(),
            P(),
            P("space", "dp"),
            P(),
            P(),
            P(),
            P("space", "dp"),
            P(),
            P(),
            P("space", "dp"),
            P(),
            P(),
            P(),
            P("space", "dp"),
            P(),
            P("space", "dp"),
            P(),
        ),
        check_vma=False,
    )
```

```python
import functools
import jax
import jax.numpy as jnp
from jax import lax
from jax.experimental import pallas as pl
from jax.experimental.pallas import tpu as pltpu
from jax.sharding import PartitionSpec as P

HD = 64
F32 = jnp.float32
BF16 = jnp.bfloat16
eps_batch = 1e-05
eps_layer = 1e-06
masked_value = -1e30
GELU_C = 0.7978845608028654
GELU_A = 0.044715


def nn(a, b):
    return lax.dot_general(a, b, (((1,), (0,)), ((), ())), preferred_element_type=F32)


def nt(a, b):
    return lax.dot_general(a, b, (((1,), (1,)), ((), ())), preferred_element_type=F32)


def tn(a, b):
    return lax.dot_general(a, b, (((0,), (0,)), ((), ())), preferred_element_type=F32)


def gelu_of(x):
    t = jnp.tanh(GELU_C * (x + GELU_A * x * x * x))
    return 0.5 * x * (1.0 + t)


def gelu_and_slope(x):
    x2 = x * x
    t = jnp.tanh(x * (GELU_C + (GELU_C * GELU_A) * x2))
    half = 0.5 + 0.5 * t
    slope = half + (0.5 * x) * (1.0 - t * t) * (GELU_C + (3.0 * GELU_C * GELU_A) * x2)
    return x * half, slope


def ln_parts(x):
    mean = jnp.mean(x, axis=-1, keepdims=True)
    c = x - mean
    var = jnp.mean(c * c, axis=-1, keepdims=True)
    r = lax.rsqrt(var + eps_layer)
    return c * r, r


def ln_back(dz, nrm, r, gain):
    u = dz * gain
    return r * (u - jnp.mean(u, axis=-1, keepdims=True) - nrm * jnp.mean(u * nrm, axis=-1, keepdims=True))


def mlp_kernel(ex, seq, pad, z2_ref, h1_ref, cot_ref, upw_ref, upb_ref, dnw_ref, dnb_ref, g_ref, s_ref,
               out_ref, dnwg_ref, upwg_ref, upbg_ref, g1_ref, vec_ref,
               g2_s, g2t_s, acc_o, acc_d):
    i = pl.program_id(0)
    last = pl.num_programs(0) - 1

    @pl.when(i == 0)
    def _():
        g2_s[...] = jnp.zeros_like(g2_s)
        for e in range(ex):
            g2_s[e * pad : e * pad + seq, :] = cot_ref[e]
        g2t_s[...] = g2_s[...].T
        acc_o[...] = jnp.zeros_like(acc_o)
        acc_d[...] = jnp.zeros_like(acc_d)

    z2 = z2_ref[...]
    g2 = g2_s[...]
    pre = nn(z2, upw_ref[...]) + upb_ref[...]
    act, slope = gelu_and_slope(pre)
    low = act.astype(BF16)
    dg32 = nt(g2, dnw_ref[...]) * slope
    dg = dg32.astype(BF16)
    acc_o[...] += nn(low, dnw_ref[...])
    dnwg_ref[...] = nn(g2t_s[...], low).astype(BF16)
    upwg_ref[...] = tn(dg, z2).astype(BF16)
    acc_d[...] += nt(dg, upw_ref[...])
    upbg_ref[...] = jnp.sum(dg.astype(F32), axis=0, keepdims=True)

    @pl.when(i == last)
    def _():
        h1 = h1_ref[...]
        out = (h1 + acc_o[...] + dnb_ref[...]).astype(BF16)
        for e in range(ex):
            out_ref[e] = out[e * pad : e * pad + seq, :]
        nrm, r = ln_parts(h1)
        dz = acc_d[...]
        gf = g2_s[...].astype(F32)
        g1 = gf + ln_back(dz, nrm, r, g_ref[...])
        g1_ref[...] = g1
        vec_ref[0:1, :] = jnp.sum(gf, axis=0, keepdims=True)
        vec_ref[1:2, :] = jnp.sum(dz * nrm, axis=0, keepdims=True)
        vec_ref[2:3, :] = jnp.sum(dz, axis=0, keepdims=True)
        vec_ref[3:4, :] = jnp.sum(g1, axis=0, keepdims=True)


def whole(shape):
    return pl.BlockSpec(shape, lambda *_: (0,) * len(shape))


def mlp(z2, h1, cot, up_w, up_b, down_w, down_b, gain, shift, pad, tile=256):
    ex, seq, width = cot.shape
    rows = z2.shape[0]
    ff = up_w.shape[1]
    steps = ff // tile
    return pl.pallas_call(
        functools.partial(mlp_kernel, ex, seq, pad),
        grid=(steps,),
        in_specs=[
            whole((rows, width)), whole((rows, width)), whole((ex, seq, width)),
            pl.BlockSpec((width, tile), lambda i: (0, i)),
            pl.BlockSpec((1, tile), lambda i: (0, i)),
            pl.BlockSpec((tile, width), lambda i: (i, 0)),
            whole((1, width)), whole((1, width)), whole((1, width)),
        ],
        out_specs=[
            whole((ex, seq, width)),
            pl.BlockSpec((width, tile), lambda i: (0, i)),
            pl.BlockSpec((tile, width), lambda i: (i, 0)),
            pl.BlockSpec((1, tile), lambda i: (0, i)),
            whole((rows, width)),
            whole((8, width)),
        ],
        out_shape=[
            jax.ShapeDtypeStruct((ex, seq, width), BF16),
            jax.ShapeDtypeStruct((width, ff), BF16),
            jax.ShapeDtypeStruct((ff, width), BF16),
            jax.ShapeDtypeStruct((1, ff), F32),
            jax.ShapeDtypeStruct((rows, width), F32),
            jax.ShapeDtypeStruct((8, width), F32),
        ],
        scratch_shapes=[
            pltpu.VMEM((rows, width), BF16),
            pltpu.VMEM((width, rows), BF16),
            pltpu.VMEM((rows, width), F32),
            pltpu.VMEM((rows, width), F32),
        ],
        compiler_params=pltpu.CompilerParams(dimension_semantics=("arbitrary",), vmem_limit_bytes=56 << 20),
        cost_estimate=pl.CostEstimate(flops=12 * rows * width * ff, bytes_accessed=40 << 20, transcendentals=rows * ff),
        name="mlp_both_ways",
    )(z2, h1, cot, up_w, up_b.reshape(1, -1), down_w, down_b.reshape(1, -1), gain.reshape(1, -1), shift.reshape(1, -1))


def head_mask(rows, second):
    lane = lax.broadcasted_iota(jnp.int32, (rows, 2 * HD), 1)
    return (lane >= HD) if second else (lane < HD)


def attn_fwd_kernel(ex, n_image, pad, pre_ref, len_ref, h0_ref, g_ref, s_ref, wq_ref, wk_ref, wv_ref, qb_ref, vb_ref,
                    ow_ref, ob_ref, g2_ref, s2_ref,
                    z1_ref, q_ref, k_ref, v_ref, p_ref, attn_ref, h1_ref, z2_ref, acc):
    i = pl.program_id(0)
    last = pl.num_programs(0) - 1
    wide = wq_ref.shape[1]

    @pl.when(i == 0)
    def _():
        nrm, _r = ln_parts(h0_ref[...].astype(F32))
        z1_ref[...] = (nrm * g_ref[...] + s_ref[...]).astype(BF16)
        acc[...] = jnp.zeros_like(acc)

    z1 = z1_ref[...]
    q_ref[...] = (nn(z1, wq_ref[...]) + qb_ref[...]).astype(BF16)
    k_ref[...] = nn(z1, wk_ref[...]).astype(BF16)
    v_ref[...] = (nn(z1, wv_ref[...]) + vb_ref[...]).astype(BF16)
    zero = jnp.zeros((pad, 2 * HD), BF16)
    first = head_mask(pad, False)

    def example(e, carry):
        row0 = pl.multiple_of(e * pad, 16)
        key = lax.broadcasted_iota(jnp.int32, (pad, pad), 1)
        qry = lax.broadcasted_iota(jnp.int32, (pad, pad), 0)
        limit = jnp.maximum(qry + 1, n_image + pre_ref[e])
        limit = jnp.minimum(limit, n_image + len_ref[e])
        vis = key < limit
        for pair in range(wide // (2 * HD)):
            cols = slice(pair * 2 * HD, (pair + 1) * 2 * HD)
            q2 = q_ref[pl.ds(row0, pad), cols] * jnp.asarray(0.125, BF16)
            k2 = k_ref[pl.ds(row0, pad), cols]
            v2 = v_ref[pl.ds(row0, pad), cols]
            out = None
            for h in range(2):
                sel = first if h == 0 else jnp.logical_not(first)
                sc = nt(jnp.where(sel, q2, zero), k2)
                sc = jnp.where(vis, sc, masked_value)
                top = jnp.max(sc, axis=-1, keepdims=True)
                ex_ = jnp.exp(sc - top)
                tot = jnp.sum(ex_, axis=-1, keepdims=True)
                p = (ex_ * (1.0 / tot)).astype(BF16)
                p_ref[e, pair * 2 + h] = p
                o = nn(p, jnp.where(sel, v2, zero))
                out = o if out is None else out + o
            attn_ref[pl.ds(row0, pad), cols] = out.astype(BF16)
        return carry

    lax.fori_loop(0, ex, example, 0)
    acc[...] += nn(attn_ref[...], ow_ref[...])

    @pl.when(i == last)
    def _():
        h1 = h0_ref[...].astype(F32) + acc[...] + ob_ref[...]
        h1_ref[...] = h1
        nrm, _r = ln_parts(h1)
        z2_ref[...] = (nrm * g2_ref[...] + s2_ref[...]).astype(BF16)


def attn_fwd(h0, prefix, text_len, ln1_gain, ln1_shift, qkv_w, qb, vb, out_w, out_b, ln2_gain, ln2_shift, ex, n_image, pad, wide=256):
    rows, width = h0.shape
    groups = width // wide
    heads = width // HD
    hg = wide // HD
    cols = lambda off: pl.BlockSpec((width, wide), lambda i, *_: (0, i + off * groups))
    vec = whole((1, width))
    part = pl.BlockSpec((rows, wide), lambda i, *_: (0, i))
    bias = pl.BlockSpec((1, wide), lambda i, *_: (0, i))
    row = lambda v: v.reshape(1, -1)
    return pl.pallas_call(
        functools.partial(attn_fwd_kernel, ex, n_image, pad),
        grid_spec=pltpu.PrefetchScalarGridSpec(
            num_scalar_prefetch=2,
            grid=(groups,),
            in_specs=[whole((rows, width)), vec, vec, cols(0), cols(1), cols(2), bias, bias,
                      pl.BlockSpec((wide, width), lambda i, *_: (i, 0)), vec, vec, vec],
            out_specs=[whole((rows, width)), part, part, part,
                       pl.BlockSpec((ex, hg, pad, pad), lambda i, *_: (0, i, 0, 0)),
                       part, whole((rows, width)), whole((rows, width))],
            scratch_shapes=[pltpu.VMEM((rows, width), F32)],
        ),
        out_shape=[jax.ShapeDtypeStruct((rows, width), BF16)] * 4 + [
            jax.ShapeDtypeStruct((ex, heads, pad, pad), BF16),
            jax.ShapeDtypeStruct((rows, width), BF16),
            jax.ShapeDtypeStruct((rows, width), F32),
            jax.ShapeDtypeStruct((rows, width), BF16)],
        compiler_params=pltpu.CompilerParams(dimension_semantics=("arbitrary",), vmem_limit_bytes=56 << 20),
        cost_estimate=pl.CostEstimate(flops=8 * rows * width * width + 4 * heads * rows * pad * 128, bytes_accessed=30 << 20, transcendentals=heads * rows * pad),
        name="attention_forward",
    )(prefix, text_len, h0, row(ln1_gain), row(ln1_shift), qkv_w, qkv_w, qkv_w, row(qb), row(vb), out_w, row(out_b), row(ln2_gain), row(ln2_shift))


def attn_bwd_kernel(ex, n_image, txt, cols_real, pad, g1_ref, ow_ref, attn_ref, q_ref, k_ref, v_ref, p_ref, z1_ref, h0_ref, wq_ref, wk_ref, wv_ref, g_ref,
                    owg_ref, qkvg_ref, bias_ref, text_ref, dtok_ref, vec_ref,
                    g1b_s, g1t_s, dat_s, dq_s, dk_s, dv_s, acc):
    i = pl.program_id(0)
    last = pl.num_programs(0) - 1
    wide = wq_ref.shape[1]

    @pl.when(i == 0)
    def _():
        g1b_s[...] = g1_ref[...].astype(BF16)
        g1t_s[...] = g1b_s[...].T
        acc[...] = jnp.zeros_like(acc)

    owg_ref[...] = nn(g1t_s[...], attn_ref[...]).astype(BF16)
    dat_s[...] = nt(g1b_s[...], ow_ref[...]).astype(BF16)
    zero = jnp.zeros((pad, 2 * HD), BF16)
    first = head_mask(pad, False)

    def example(e, carry):
        row0 = pl.multiple_of(e * pad, 16)
        for pair in range(wide // (2 * HD)):
            cols = slice(pair * 2 * HD, (pair + 1) * 2 * HD)
            q2 = q_ref[pl.ds(row0, pad), cols]
            k2 = k_ref[pl.ds(row0, pad), cols]
            v2 = v_ref[pl.ds(row0, pad), cols]
            da2 = dat_s[pl.ds(row0, pad), cols]
            dq = dk = dv = None
            for h in range(2):
                sel = first if h == 0 else jnp.logical_not(first)
                pb = p_ref[e, pair * 2 + h]
                p = pb.astype(F32)
                dah = jnp.where(sel, da2, zero)
                dp = nt(dah, v2)
                inner = jnp.sum(p * dp, axis=-1, keepdims=True)
                ds = (p * (dp - inner)).astype(BF16)
                dvh = tn(pb, dah)
                dqh = nn(ds, jnp.where(sel, k2, zero))
                dkh = tn(ds, jnp.where(sel, q2, zero))
                dq = dqh if dq is None else dq + dqh
                dk = dkh if dk is None else dk + dkh
                dv = dvh if dv is None else dv + dvh
            dq_s[pl.ds(row0, pad), cols] = (dq * 0.125).astype(BF16)
            dk_s[pl.ds(row0, pad), cols] = (dk * 0.125).astype(BF16)
            dv_s[pl.ds(row0, pad), cols] = dv.astype(BF16)
        return carry

    lax.fori_loop(0, ex, example, 0)
    z1 = z1_ref[...]
    dq, dk, dv = dq_s[...], dk_s[...], dv_s[...]
    qkvg_ref[0] = tn(dq, z1).astype(BF16)
    qkvg_ref[1] = tn(dk, z1).astype(BF16)
    qkvg_ref[2] = tn(dv, z1).astype(BF16)
    acc[...] += nt(dq, wq_ref[...]) + nt(dk, wk_ref[...]) + nt(dv, wv_ref[...])
    bias_ref[0:1, :] = jnp.sum(dq.astype(F32), axis=0, keepdims=True)
    bias_ref[1:2, :] = jnp.sum(dv.astype(F32), axis=0, keepdims=True)

    @pl.when(i == last)
    def _():
        nrm, r = ln_parts(h0_ref[...].astype(F32))
        dz = acc[...]
        g0 = g1_ref[...] + ln_back(dz, nrm, r, g_ref[...])
        vec_ref[0:1, :] = jnp.sum(dz * nrm, axis=0, keepdims=True)
        vec_ref[1:2, :] = jnp.sum(dz, axis=0, keepdims=True)
        gb = g0.astype(BF16)
        px = dtok_ref.shape[0] // ex
        pick_image = image_pick(px, pad, n_image, cols_real)
        tr = lax.broadcasted_iota(jnp.int32, (txt, pad), 0)
        tc = lax.broadcasted_iota(jnp.int32, (txt, pad), 1)
        pick_text = jnp.where(tc == tr + n_image, 1.0, 0.0).astype(BF16)
        tot = jnp.zeros((1, gb.shape[1]), F32)
        for e in range(ex):
            ge = gb[e * pad : (e + 1) * pad, :]
            text_ref[e] = nn(pick_text, ge).astype(BF16)
            dt = nn(pick_image, ge)
            dtok_ref[e * px : (e + 1) * px, :] = dt.astype(BF16)
            tot = tot + jnp.sum(dt, axis=0, keepdims=True)
        vec_ref[2:3, :] = tot


def image_pick(px, pad, n_image, cols_real):
    p = lax.broadcasted_iota(jnp.int32, (px, pad), 0)
    t = lax.broadcasted_iota(jnp.int32, (px, pad), 1)
    col = p & 15
    tok = (p >> 4) * cols_real + col
    return jnp.where((col < cols_real) & (tok == t) & (t < n_image), 1.0, 0.0).astype(BF16)


def attn_bwd(g1, out_w, attn, q, k, v, p, z1, h0, qkv_w, ln1_gain, ex, n_image, txt, img_rows, img_cols, pad, wide=256):
    rows, width = h0.shape
    groups = width // wide
    heads = width // HD
    hg = wide // HD
    px = img_rows * 16
    cols = lambda off: pl.BlockSpec((width, wide), lambda i: (0, i + off * groups))
    part = pl.BlockSpec((rows, wide), lambda i: (0, i))
    return pl.pallas_call(
        functools.partial(attn_bwd_kernel, ex, n_image, txt, img_cols, pad),
        grid=(groups,),
        in_specs=[whole((rows, width)), pl.BlockSpec((wide, width), lambda i: (i, 0)), part, part, part, part,
                  pl.BlockSpec((ex, hg, pad, pad), lambda i: (0, i, 0, 0)),
                  whole((rows, width)), whole((rows, width)), cols(0), cols(1), cols(2), whole((1, width))],
        out_specs=[pl.BlockSpec((width, wide), lambda i: (0, i)),
                   pl.BlockSpec((3, wide, width), lambda i: (0, i, 0)),
                   pl.BlockSpec((8, wide), lambda i: (0, i)),
                   whole((ex, txt, width)), whole((ex * px, width)), whole((8, width))],
        out_shape=[jax.ShapeDtypeStruct((width, width), BF16),
                   jax.ShapeDtypeStruct((3, width, width), BF16),
                   jax.ShapeDtypeStruct((8, width), F32),
                   jax.ShapeDtypeStruct((ex, txt, width), BF16),
                   jax.ShapeDtypeStruct((ex * px, width), BF16),
                   jax.ShapeDtypeStruct((8, width), F32)],
        scratch_shapes=[pltpu.VMEM((rows, width), BF16), pltpu.VMEM((width, rows), BF16)]
        + [pltpu.VMEM((rows, wide), BF16)] * 4 + [pltpu.VMEM((rows, width), F32)],
        compiler_params=pltpu.CompilerParams(dimension_semantics=("arbitrary",), vmem_limit_bytes=56 << 20),
        cost_estimate=pl.CostEstimate(flops=16 * rows * width * width + 10 * heads * rows * pad * 128, bytes_accessed=40 << 20, transcendentals=0),
        name="attention_backward",
    )(g1, out_w, attn, q, k, v, p, z1, h0, qkv_w, qkv_w, qkv_w, ln1_gain.reshape(1, -1))


def stat_rows(channels):
    return max(8, 2 * channels // 128)


def put_stats(ref, first, second):
    lanes = jnp.concatenate([first, second], axis=1)
    n = ref.shape[0]
    for r in range(lanes.shape[1] // 128):
        ref[:, r, :] = jnp.broadcast_to(lanes[:, r * 128 : (r + 1) * 128], (n, 128))


def get_stats(ref, channels):
    total = jnp.sum(ref[...], axis=0)
    rows = 2 * channels // 128
    half = rows // 2
    first = jnp.concatenate([total[r : r + 1, :] for r in range(half)], axis=1)
    second = jnp.concatenate([total[r : r + 1, :] for r in range(half, rows)], axis=1)
    return first, second


def mean_rstd(ref, channels, count):
    s1, s2 = get_stats(ref, channels)
    mean = s1 * (1.0 / count)
    return mean, lax.rsqrt(s2 * (1.0 / count) - mean * mean + eps_batch)


def real_columns(rows, cols):
    return (lax.broadcasted_iota(jnp.int32, (rows, 1), 0) & 15) < cols


def col_sum(x):
    return jnp.sum(x, axis=0, keepdims=True)


def stats_kernel(cols, x_ref, w_ref, parts_ref, xp):
    xp[...] = jnp.zeros_like(xp)
    shape = x_ref.shape
    xp[:, 0:cols, :] = x_ref[...].reshape(shape[0] * shape[1], cols, shape[3])
    a = nn(xp[...].reshape(shape[0] * shape[1] * 16, shape[3]), w_ref[...])
    put_stats(parts_ref, col_sum(a), col_sum(a * a))


def conv_fwd_kernel(count, ex, rows, cols, sp_ref, parts_ref, own_ref, got_ref, win_ref, g_ref, s_ref, wmid_ref,
                    xs_ref, act1_ref, wide_ref, act2_ref, parts2_ref):
    s = sp_ref[0]
    half = rows // 2
    px = rows * 16
    chan = xs_ref.shape[-1]
    xs_ref[...] = jnp.zeros_like(xs_ref)
    for e in range(ex):
        xs_ref[e, pl.ds(s * half, half), 0:cols, :] = own_ref[s * ex + e]
        xs_ref[e, pl.ds((1 - s) * half, half), 0:cols, :] = got_ref[e]
    a1 = nn(xs_ref[...].reshape(ex * px, chan), win_ref[...])
    act1_ref[...] = a1
    mid = a1.shape[1]
    mean, rstd = mean_rstd(parts_ref, mid, count)
    real = real_columns(ex * px, cols)
    act = gelu_of((a1 - mean) * rstd * g_ref[...] + s_ref[...])
    act = jnp.where(real, act, 0.0)
    for e in range(ex):
        part = act[e * px : (e + 1) * px]
        wide_ref[e, 0:16, :] = jnp.zeros((16, 3 * mid), BF16)
        wide_ref[e, px + 16 : px + 32, :] = jnp.zeros((16, 3 * mid), BF16)
        wide_ref[e, 16 : px + 16, 0:mid] = pltpu.roll(part, 1, 0).astype(BF16)
        wide_ref[e, 16 : px + 16, mid : 2 * mid] = part.astype(BF16)
        wide_ref[e, 16 : px + 16, 2 * mid : 3 * mid] = pltpu.roll(part, px - 1, 0).astype(BF16)
    one = real_columns(px, cols)
    t1 = jnp.zeros((1, mid), F32)
    t2 = jnp.zeros((1, mid), F32)
    for e in range(ex):
        a2 = nn(wide_ref[e, 0:px, :], wmid_ref[0])
        a2 = a2 + nn(wide_ref[e, 16 : px + 16, :], wmid_ref[1])
        a2 = a2 + nn(wide_ref[e, 32 : px + 32, :], wmid_ref[2])
        a2 = jnp.where(one, a2, 0.0)
        act2_ref[e * px : (e + 1) * px, :] = a2
        t1 = t1 + col_sum(a2)
        t2 = t2 + col_sum(a2 * a2)
    put_stats(parts2_ref, t1, t2)


def expand_kernel(count, cols, parts_ref, act2_ref, g_ref, s_ref, w_ref, relu2_ref, act3_ref, parts3_ref):
    a2 = act2_ref[...]
    mean, rstd = mean_rstd(parts_ref, a2.shape[1], count)
    act = gelu_of((a2 - mean) * rstd * g_ref[...] + s_ref[...])
    low = jnp.where(real_columns(a2.shape[0], cols), act, 0.0).astype(BF16)
    relu2_ref[...] = low
    a3 = nn(low, w_ref[...])
    act3_ref[...] = a3
    put_stats(parts3_ref, col_sum(a3), col_sum(a3 * a3))


def tokens_kernel(count, ex, cols, n_image, pad, parts_ref, act3_ref, xs_ref, g_ref, s_ref, w_ref, b_ref, text_ref,
                  stem_ref, h0_ref):
    a3 = act3_ref[...]
    mean, rstd = mean_rstd(parts_ref, a3.shape[1], count)
    pre = (a3 - mean) * rstd * g_ref[...] + s_ref[...] + xs_ref[...].reshape(a3.shape).astype(F32)
    stem = gelu_of(pre).astype(BF16)
    stem_ref[...] = stem
    tok = (nn(stem, w_ref[...]) + b_ref[...]).astype(BF16)
    px = a3.shape[0] // ex
    txt = text_ref.shape[1]
    t = lax.broadcasted_iota(jnp.int32, (pad, px), 0)
    p = lax.broadcasted_iota(jnp.int32, (pad, px), 1)
    col = p & 15
    pick = jnp.where((col < cols) & ((p >> 4) * cols + col == t), 1.0, 0.0).astype(BF16)
    tr = lax.broadcasted_iota(jnp.int32, (pad, txt), 0)
    tc = lax.broadcasted_iota(jnp.int32, (pad, txt), 1)
    pick_text = jnp.where(tr == tc + n_image, 1.0, 0.0).astype(BF16)
    for e in range(ex):
        both = nn(pick, tok[e * px : (e + 1) * px, :]) + nn(pick_text, text_ref[e])
        h0_ref[e * pad : (e + 1) * pad, :] = both.astype(BF16)


def dpre_kernel(count, ex, rows, sp_ref, parts_ref, act3_ref, xs_ref, g_ref, s_ref, dtok_ref, w_ref, dpre_ref, send_ref, parts4_ref):
    a3 = act3_ref[...]
    mean, rstd = mean_rstd(parts_ref, a3.shape[1], count)
    nrm = (a3 - mean) * rstd
    pre = nrm * g_ref[...] + s_ref[...] + xs_ref[...].reshape(a3.shape).astype(F32)
    _, slope = gelu_and_slope(pre)
    d = nt(dtok_ref[...], w_ref[...]) * slope
    dpre_ref[...] = d.reshape(dpre_ref.shape)
    put_stats(parts4_ref, col_sum(d), col_sum(d * nrm))
    half = rows // 2
    other = 1 - sp_ref[0]
    for e in range(ex):
        send_ref[e] = dpre_ref[e, pl.ds(other * half, half)].astype(BF16)


def back3_kernel(count, cols, parts4_ref, parts3_ref, parts2_ref, act3_ref, dpre_ref, g3_ref, w_ref, act2_ref, g2_ref, s2_ref,
                 low3_ref, t2_ref, parts5_ref, bn_ref):
    a3 = act3_ref[...]
    chan = a3.shape[1]
    mean, rstd = mean_rstd(parts3_ref, chan, count)
    s1, s2 = get_stats(parts4_ref, chan)
    bn_ref[0:1, :] = s2
    bn_ref[1:2, :] = s1
    nrm = (a3 - mean) * rstd
    d = (g3_ref[...] * rstd) * (dpre_ref[...].reshape(a3.shape) - s1 * (1.0 / count) - nrm * (s2 * (1.0 / count)))
    low = jnp.where(real_columns(a3.shape[0], cols), d, 0.0).astype(BF16)
    low3_ref[...] = low
    a2 = act2_ref[...]
    mean2, rstd2 = mean_rstd(parts2_ref, a2.shape[1], count)
    nrm2 = (a2 - mean2) * rstd2
    _, slope = gelu_and_slope(nrm2 * g2_ref[...] + s2_ref[...])
    t2 = nt(low, w_ref[...]) * slope
    t2_ref[...] = t2
    put_stats(parts5_ref, col_sum(t2), col_sum(t2 * nrm2))


def back2_kernel(count, ex, rows, cols, sp_ref, parts5_ref, parts2_ref, parts1_ref, act2_ref, t2_ref, g2_ref, wmid_ref, act1_ref, g1_ref, s1_ref,
                 low2_ref, t1_ref, send_ref, parts6_ref, bn_ref, wide):
    a2 = act2_ref[...]
    mid = a2.shape[1]
    px = rows * 16
    mean, rstd = mean_rstd(parts2_ref, mid, count)
    s1, s2 = get_stats(parts5_ref, mid)
    bn_ref[0:1, :] = s2
    bn_ref[1:2, :] = s1
    nrm = (a2 - mean) * rstd
    d = (g2_ref[...] * rstd) * (t2_ref[...] - s1 * (1.0 / count) - nrm * (s2 * (1.0 / count)))
    d = jnp.where(real_columns(ex * px, cols), d, 0.0)
    low2_ref[...] = d.astype(BF16)
    for e in range(ex):
        part = d[e * px : (e + 1) * px]
        wide[e, 0:16, :] = jnp.zeros((16, 3 * mid), BF16)
        wide[e, px + 16 : px + 32, :] = jnp.zeros((16, 3 * mid), BF16)
        wide[e, 16 : px + 16, 0:mid] = pltpu.roll(part, px - 1, 0).astype(BF16)
        wide[e, 16 : px + 16, mid : 2 * mid] = part.astype(BF16)
        wide[e, 16 : px + 16, 2 * mid : 3 * mid] = pltpu.roll(part, 1, 0).astype(BF16)
    mean1, rstd1 = mean_rstd(parts1_ref, mid, count)
    one = real_columns(px, cols)
    q1 = jnp.zeros((1, mid), F32)
    q2 = jnp.zeros((1, mid), F32)
    for e in range(ex):
        t = None
        for r in range(3):
            for c in range(3):
                term = nt(wide[e, (2 - r) * 16 : (2 - r) * 16 + px, c * mid : (c + 1) * mid], wmid_ref[r, c * mid : (c + 1) * mid, :])
                t = term if t is None else t + term
        nrm1 = (act1_ref[e * px : (e + 1) * px, :] - mean1) * rstd1
        _, slope = gelu_and_slope(nrm1 * g1_ref[...] + s1_ref[...])
        t = jnp.where(one, t * slope, 0.0)
        t1_ref[e] = t.reshape(rows, 16, mid)
        q1 = q1 + col_sum(t)
        q2 = q2 + col_sum(t * nrm1)
    put_stats(parts6_ref, q1, q2)
    half = rows // 2
    other = 1 - sp_ref[0]
    for e in range(ex):
        send_ref[e] = t1_ref[e, pl.ds(other * half, half)].astype(BF16)


def mid_grad_kernel(ex, px, low2_ref, wide_ref, out_ref):
    mid = low2_ref.shape[1]
    for r in range(3):
        tot = None
        for e in range(ex):
            term = tn(low2_ref[e * px : (e + 1) * px, :], wide_ref[e, r * 16 : r * 16 + px, :])
            tot = term if tot is None else tot + term
        for c in range(3):
            for h in range(2):
                at = (r * 3 + c) * (mid // 2)
                src = c * mid + h * (mid // 2)
                out_ref[h, :, at : at + mid // 2] = tot[:, src : src + mid // 2].astype(BF16)


def tn_kernel(a_ref, b_ref, out_ref):
    out_ref[...] = tn(a_ref[...], b_ref[...]).astype(BF16)


def image_kernel(count, ex, rows, cols, sp_ref, parts6_ref, parts1_ref, x_ref, win_ref, g_ref, t1_ref, gott_ref, dpre_ref, gotd_ref,
                 grad_ref, win_grad_ref, bn_ref, xp):
    s = sp_ref[0]
    half = rows // 2
    chan = x_ref.shape[-1]
    mid = win_ref.shape[1]
    mean, rstd = mean_rstd(parts1_ref, mid, count)
    s1, s2 = get_stats(parts6_ref, mid)
    bn_ref[0:1, :] = s2
    bn_ref[1:2, :] = s1
    real = real_columns(ex * half * 16, cols)
    size = ex * half * 16
    xp[...] = jnp.zeros_like(xp)
    wg = None
    for own in (True, False):
        at = (s if own else 1 - s) * ex
        xp[:, 0:cols, :] = x_ref[pl.ds(at, ex)].reshape(ex * half, cols, chan)
        x = xp[...].reshape(size, chan)
        nrm = (nn(x, win_ref[...]) - mean) * rstd
        if own:
            t = t1_ref[:, pl.ds(s * half, half)].reshape(size, mid)
            dp = dpre_ref[:, pl.ds(s * half, half)].reshape(size, chan)
        else:
            t = gott_ref[...].reshape(size, mid).astype(F32)
            dp = gotd_ref[...].reshape(size, chan).astype(F32)
        d = (g_ref[...] * rstd) * (t - s1 * (1.0 / count) - nrm * (s2 * (1.0 / count)))
        low = jnp.where(real, d, 0.0).astype(BF16)
        grad = (nt(low, win_ref[...]) + dp).astype(BF16).reshape(ex, half, 16, chan)
        grad_ref[pl.ds(at, ex)] = grad[:, :, 0:cols, :]
        term = tn(low, x)
        wg = term if wg is None else wg + term
    win_grad_ref[...] = wg.astype(BF16)


def call(kernel, outs, *args, scalars=(), scratch=(), name=None, flops=0):
    n_s = len(scalars)
    nbytes = sum(a.size * a.dtype.itemsize for a in args)
    params = dict(
        out_shape=[jax.ShapeDtypeStruct(s, d) for s, d in outs],
        compiler_params=pltpu.CompilerParams(vmem_limit_bytes=48 << 20),
        cost_estimate=pl.CostEstimate(flops=flops, bytes_accessed=nbytes, transcendentals=0),
        name=name,
    )
    spec = lambda s: pl.BlockSpec(s, lambda *_: (0,) * len(s))
    return pl.pallas_call(
        kernel,
        grid_spec=pltpu.PrefetchScalarGridSpec(
            num_scalar_prefetch=n_s, grid=(1,),
            in_specs=[spec(a.shape) for a in args],
            out_specs=[spec(s) for s, _ in outs],
            scratch_shapes=list(scratch),
        ),
        **params,
    )(*scalars, *args)


EVERY = ("dp", "space")


def spread(parts):
    return lax.all_to_all(parts, EVERY, split_axis=0, concat_axis=0, tiled=True)


def swap(x):
    return lax.ppermute(x, "space", [(0, 1), (1, 0)])


def vector_sums(vectors):
    count = lax.axis_size(EVERY)
    sizes = [v.shape[0] for v in vectors]
    flat = jnp.concatenate(vectors)
    chunk = -(-flat.shape[0] // (count * 128)) * 128
    flat = jnp.pad(flat, (0, chunk * count - flat.shape[0])).reshape(count, chunk)
    mine = jnp.sum(spread(flat), axis=0)
    whole_v = spread(jnp.broadcast_to(mine[None], (count, chunk))).reshape(-1)
    out, at = [], 0
    for size in sizes:
        out.append(whole_v[at : at + size])
        at += size
    return out


def halve_dp(x, axis, bit):
    size = lax.axis_size("dp")
    mine = (lax.axis_index("dp") // bit) % 2
    keep = lax.dynamic_index_in_dim(x, mine, axis, keepdims=True)
    send = lax.dynamic_index_in_dim(x, 1 - mine, axis, keepdims=True)
    return keep + lax.ppermute(send, "dp", [(j, j ^ bit) for j in range(size)])


def halve_columns(x):
    half = x.shape[-1] // 2
    mine = lax.axis_index("space")
    keep = lax.dynamic_slice_in_dim(x, mine * half, half, axis=x.ndim - 1)
    send = lax.dynamic_slice_in_dim(x, (1 - mine) * half, half, axis=x.ndim - 1)
    return keep + swap(send)


def scattered(grad_t, order):
    size = lax.axis_size("dp")
    bits = size.bit_length() - 1
    cols, rows = grad_t.shape
    x = grad_t.reshape((2,) * bits + (cols // size, rows))
    x = halve_dp(x, bits - 1, 1)
    stages = list(range(1, bits))
    if order == 0:
        stages = stages + ["space"]
    elif order == 1:
        stages = ["space"] + stages[1:] + stages[:1]
    else:
        stages = stages[:1] + stages[1:] + ["space"]
    for b in stages:
        x = halve_columns(x) if b == "space" else halve_dp(x, bits - 1 - b, 1 << b)
    return x.reshape(cols // size, rows // 2).astype(F32).T


def shards(
    image_in, text_in, prefix, text_len, cotangent,
    conv_in_w, bn1_gain, bn1_shift, conv_mid_w, bn2_gain, bn2_shift, conv_out_w, bn3_gain, bn3_shift,
    proj_w, proj_b, ln1_gain, ln1_shift, qkv_w, query_bias, value_bias, out_w, out_b,
    ln2_gain, ln2_shift, up_w, up_b, down_w, down_b,
):
    n_dev = lax.axis_size(EVERY)
    band_ex, band_rows, cols, chan = image_in.shape
    mid = conv_in_w.shape[1]
    width = proj_w.shape[1]
    ex, txt, _ = text_in.shape
    rows = band_rows * lax.axis_size("space")
    n_image = rows * cols
    seq = n_image + txt
    pad = -(-seq // 16) * 16
    px = rows * 16
    count = float(band_ex * band_rows * cols * n_dev)
    me = lax.axis_index("space").astype(jnp.int32)
    sp = me.reshape(1)
    row = lambda v: v.reshape(1, -1)
    small, large = (n_dev, stat_rows(mid), 128), (n_dev, stat_rows(chan), 128)
    wmid = conv_mid_w.reshape(3, 3 * mid, mid)

    got_x = swap(lax.dynamic_slice_in_dim(image_in, (1 - me) * ex, ex, axis=0))
    parts1, = call(functools.partial(stats_kernel, cols), [(small, F32)], image_in, conv_in_w,
                   scratch=[pltpu.VMEM((band_ex * band_rows, 16, chan), BF16)], name="stats_one")
    parts1 = spread(parts1)
    xs, act1, wide, act2, parts2 = call(
        functools.partial(conv_fwd_kernel, count, ex, rows, cols),
        [((ex, rows, 16, chan), BF16), ((ex * px, mid), F32), ((ex, px + 32, 3 * mid), BF16), ((ex * px, mid), F32), (small, F32)],
        parts1, image_in, got_x, conv_in_w, row(bn1_gain), row(bn1_shift), wmid, scalars=(sp,), name="conv_three")
    parts2 = spread(parts2)
    relu2, act3, parts3 = call(
        functools.partial(expand_kernel, count, cols),
        [((ex * px, mid), BF16), ((ex * px, chan), F32), (large, F32)],
        parts2, act2, row(bn2_gain), row(bn2_shift), conv_out_w, name="expand")
    parts3 = spread(parts3)
    stem, h0 = call(
        functools.partial(tokens_kernel, count, ex, cols, n_image, pad),
        [((ex * px, chan), BF16), ((ex * pad, width), BF16)],
        parts3, act3, xs, row(bn3_gain), row(bn3_shift), proj_w, row(proj_b), text_in, name="tokens")
    z1, q, k, v, p, attn, h1, z2 = attn_fwd(h0, prefix, text_len, ln1_gain, ln1_shift, qkv_w, query_bias, value_bias,
                                            out_w, out_b, ln2_gain, ln2_shift, ex, n_image, pad)
    block_out, down_g, up_g, up_bg, g1, vec2 = mlp(z2, h1, cotangent, up_w, up_b, down_w, down_b, ln2_gain, ln2_shift, pad)
    out_g, qkv_g, bias, text_grad, dtok, vec1 = attn_bwd(g1, out_w, attn, q, k, v, p, z1, h0, qkv_w, ln1_gain,
                                                         ex, n_image, txt, rows, cols, pad)
    dpre, dsend, parts4 = call(
        functools.partial(dpre_kernel, count, ex, rows),
        [((ex, rows, 16, chan), F32), ((ex, band_rows, 16, chan), BF16), (large, F32)],
        parts3, act3, xs, row(bn3_gain), row(bn3_shift), dtok, proj_w, scalars=(sp,), name="stem_back")
    got_d = swap(dsend)
    parts4 = spread(parts4)
    proj_g, = call(tn_kernel, [((width, chan), BF16)], dtok, stem, name="proj_grad", flops=2 * ex * px * width * chan)
    low3, t2, parts5, bn3 = call(
        functools.partial(back3_kernel, count, cols),
        [((ex * px, chan), BF16), ((ex * px, mid), F32), (small, F32), ((8, chan), F32)],
        parts4, parts3, parts2, act3, dpre, row(bn3_gain), conv_out_w, act2, row(bn2_gain), row(bn2_shift), name="back_three")
    parts5 = spread(parts5)
    conv_out_g, = call(tn_kernel, [((chan, mid), BF16)], low3, relu2, name="conv_out_grad", flops=2 * ex * px * mid * chan)
    low2, t1, tsend, parts6, bn2 = call(
        functools.partial(back2_kernel, count, ex, rows, cols),
        [((ex * px, mid), BF16), ((ex, rows, 16, mid), F32), ((ex, band_rows, 16, mid), BF16), (small, F32), ((8, mid), F32)],
        parts5, parts2, parts1, act2, t2, row(bn2_gain), wmid, act1, row(bn1_gain), row(bn1_shift),
        scalars=(sp,), scratch=[pltpu.VMEM((ex, px + 32, 3 * mid), BF16)], name="back_two")
    got_t = swap(tsend)
    parts6 = spread(parts6)
    mid_g, = call(functools.partial(mid_grad_kernel, ex, px), [((2, mid, 9 * mid // 2), BF16)], low2, wide, name="conv_mid_grad",
                  flops=18 * ex * px * mid * mid)
    image_grad, conv_in_g, bn1 = call(
        functools.partial(image_kernel, count, ex, rows, cols),
        [(image_in.shape, BF16), ((mid, chan), BF16), ((8, mid), F32)],
        parts6, parts1, image_in, conv_in_w, row(bn1_gain), t1, got_t, dpre, got_d,
        scalars=(sp,), scratch=[pltpu.VMEM((ex * band_rows, 16, chan), BF16)], name="image_back")
    small_sums = vector_sums([vec1[2], vec1[0], vec1[1], bias[0], bias[1], vec2[3], vec2[1], vec2[2], up_bg[0], vec2[0]])
    mid_out = scattered(mid_g.transpose(1, 0, 2).reshape(mid, 9 * mid), 0)
    return (
        block_out, image_grad, text_grad,
        scattered(conv_in_g, 0), bn1[0], bn1[1],
        mid_out.reshape(3, 3, mid // 2, mid_out.shape[1]), bn2[0], bn2[1],
        scattered(conv_out_g, 1), bn3[0], bn3[1],
        scattered(proj_g, 1), small_sums[0], small_sums[1], small_sums[2],
        scattered(qkv_g.reshape(3 * width, width), 0), small_sums[3], small_sums[4],
        scattered(out_g, 1), small_sums[5], small_sums[6], small_sums[7],
        scattered(up_g, 0), small_sums[8],
        scattered(down_g, 1), small_sums[9],
    )


def solution(mesh):
    return jax.shard_map(
        shards,
        mesh=mesh,
        in_specs=(
            P("dp", "space", None, None),
            P(("dp", "space"), None, None),
            P(("dp", "space")),
            P(("dp", "space")),
            P(("dp", "space"), None, None),
            P(),
            P(),
            P(),
            P(),
            P(),
            P(),
            P(),
            P(),
            P(),
            P(),
            P(),
            P(),
            P(),
            P(),
            P(),
            P(),
            P(),
            P(),
            P(),
            P(),
            P(),
            P(),
            P(),
            P(),
        ),
        out_specs=(
            P(("dp", "space"), None, None),
            P("dp", "space", None, None),
            P(("dp", "space"), None, None),
            P("space", "dp"),
            P(),
            P(),
            P(None, None, "space", "dp"),
            P(),
            P(),
            P("space", "dp"),
            P(),
            P(),
            P("space", "dp"),
            P(),
            P(),
            P(),
            P("space", "dp"),
            P(),
            P(),
            P("space", "dp"),
            P(),
            P(),
            P(),
            P("space", "dp"),
            P(),
            P("space", "dp"),
            P(),
        ),
        check_vma=False,
    )
```

```python
import functools
import jax
import jax.numpy as jnp
from jax import lax
from jax.experimental import pallas as pl
from jax.experimental.pallas import tpu as pltpu
from jax.sharding import Mesh, PartitionSpec as P

HD = 64
F32 = jnp.float32
BF16 = jnp.bfloat16
eps_batch = 1e-05
eps_layer = 1e-06
masked_value = -1e30
GELU_C = 0.7978845608028654
GELU_A = 0.044715


def nn(a, b):
    return lax.dot_general(a, b, (((1,), (0,)), ((), ())), preferred_element_type=F32)


def nt(a, b):
    return lax.dot_general(a, b, (((1,), (1,)), ((), ())), preferred_element_type=F32)


def tn(a, b):
    return lax.dot_general(a, b, (((0,), (0,)), ((), ())), preferred_element_type=F32)


def gelu_of(x):
    t = jnp.tanh(GELU_C * (x + GELU_A * x * x * x))
    return 0.5 * x * (1.0 + t)


def gelu_and_slope(x):
    x2 = x * x
    t = jnp.tanh(x * (GELU_C + (GELU_C * GELU_A) * x2))
    half = 0.5 + 0.5 * t
    slope = half + (0.5 * x) * (1.0 - t * t) * (GELU_C + (3.0 * GELU_C * GELU_A) * x2)
    return x * half, slope


def ln_parts(x):
    mean = jnp.mean(x, axis=-1, keepdims=True)
    c = x - mean
    var = jnp.mean(c * c, axis=-1, keepdims=True)
    r = lax.rsqrt(var + eps_layer)
    return c * r, r


def ln_back(dz, nrm, r, gain):
    u = dz * gain
    return r * (u - jnp.mean(u, axis=-1, keepdims=True) - nrm * jnp.mean(u * nrm, axis=-1, keepdims=True))


def whole(shape):
    return pl.BlockSpec(shape, lambda *_: (0,) * len(shape), pipeline_mode=pl.Buffered(1))


SMEM = pl.BlockSpec(memory_space=pltpu.SMEM)
VMEM = pl.BlockSpec(memory_space=pltpu.VMEM)


def row_of(ref):
    return ref[...].reshape(1, -1)


def put_rows(ref, at, vector):
    for r in range(vector.shape[1] // 128):
        ref[at + r : at + r + 1, :] = vector[:, r * 128 : (r + 1) * 128]


def take_rows(ref, at, size):
    return jnp.concatenate([ref[at + r : at + r + 1, :] for r in range(size // 128)], axis=1)


def part_shape(cols, rows, dp):
    return (2, dp // 2, cols // dp * (rows // 2) // 128, 128)


def part_it(natural, keep_ref, send_ref, core, at=0, lead=None):
    rows, cols = natural.shape[-2:]
    _, hi = keep_ref.shape[:2]
    r, blocks = rows // (2 * hi), cols // 256
    for h in range(hi):
        mine = pl.ds(pl.multiple_of((2 * h + core) * r, 16), r)
        other = pl.ds(pl.multiple_of((2 * h + 1 - core) * r, 16), r)
        for s in range(2):
            for b in range(blocks):
                lanes = slice((s * blocks + b) * 128, (s * blocks + b + 1) * 128)
                keep_ref[s, h, at + b * r : at + (b + 1) * r, :] = natural[mine, lanes]
                send_ref[s, h, at + b * r : at + (b + 1) * r, :] = natural[other, lanes]


def mlp_kernel(ex, seq, pad, parted, place_ref, z2_ref, h1_ref, cot_ref, upw_ref, upb_ref, dnw_ref, dnb_ref, g_ref, *refs):
    if parted:
        out_ref, dk_ref, ds_ref, uk_ref, us_ref, g1_ref, vec_ref, g2_s, g2t_s, acc_o, acc_d, ub_s, bg_s = refs
    else:
        out_ref, dn_ref, up_ref, g1_ref, vec_ref, g2_s, g2t_s, acc_o, acc_d, ub_s, bg_s = refs
    i = pl.program_id(0)
    last = pl.num_programs(0) - 1
    tile = upw_ref.shape[1]

    @pl.when(i == 0)
    def _():
        g2_s[...] = jnp.zeros_like(g2_s)
        for e in range(ex):
            g2_s[e * pad : e * pad + seq, :] = cot_ref[e]
        g2t_s[...] = g2_s[...].T
        acc_o[...] = jnp.zeros_like(acc_o)
        acc_d[...] = jnp.zeros_like(acc_d)
        ub = row_of(upb_ref)
        for j in range(ub_s.shape[0]):
            ub_s[j] = ub[:, j * tile : (j + 1) * tile]

    z2 = z2_ref[...]
    g2 = g2_s[...]
    pre = nn(z2, upw_ref[...]) + ub_s[i]
    act, slope = gelu_and_slope(pre)
    low = act.astype(BF16)
    dg = (nt(g2, dnw_ref[...]) * slope).astype(BF16)
    acc_o[...] += nn(low, dnw_ref[...])
    acc_d[...] += nt(dg, upw_ref[...])
    dn = nn(g2t_s[...], low).astype(BF16)
    up = tn(dg, z2).astype(BF16)
    bg_s[i] = jnp.sum(dg.astype(F32), axis=0, keepdims=True)
    if parted:
        core = place_ref[1]
        even = core == 0
        hi = dk_ref.shape[1]
        r = dn.shape[0] // (2 * hi)
        for j in range(tile // 128):
            d4 = dn[:, j * 128 : (j + 1) * 128].reshape(hi, 2, r, 128)
            dk_ref[0, :, j * r : (j + 1) * r, :] = jnp.where(even, d4[:, 0], d4[:, 1])
            ds_ref[0, :, j * r : (j + 1) * r, :] = jnp.where(even, d4[:, 1], d4[:, 0])
        r, blocks = up.shape[0] // 2, up.shape[1] // 256
        for s in range(2):
            for j in range(blocks):
                lanes = slice((s * blocks + j) * 128, (s * blocks + j + 1) * 128)
                first, second = up[0:r, lanes], up[r : 2 * r, lanes]
                uk_ref[s, 0, j * r : (j + 1) * r, :] = jnp.where(even, first, second)
                us_ref[s, 0, j * r : (j + 1) * r, :] = jnp.where(even, second, first)
    else:
        dn_ref[...] = dn
        up_ref[...] = up

    @pl.when(i == last)
    def _():
        h1 = h1_ref[...]
        out = (h1 + acc_o[...] + row_of(dnb_ref)).astype(BF16)
        for e in range(ex):
            out_ref[e] = out[e * pad : e * pad + seq, :]
        nrm, r = ln_parts(h1)
        dz = acc_d[...]
        gf = g2_s[...].astype(F32)
        g1 = gf + ln_back(dz, nrm, r, row_of(g_ref))
        g1_ref[...] = g1
        n = g1.shape[1] // 128
        for j, v in enumerate((col_sum(gf), col_sum(dz * nrm), col_sum(dz), col_sum(g1))):
            put_rows(vec_ref, j * n, v)
        for j in range(bg_s.shape[0]):
            put_rows(vec_ref, 4 * n + j * (tile // 128), bg_s[j])


def mlp(place, z2, h1, cot, up_w, up_b, down_w, down_b, gain, pad, dp, parted):
    ex, seq, width = cot.shape
    rows = z2.shape[0]
    ff = up_w.shape[1]
    tile = 2 * ff // dp if parted else 384
    steps = ff // tile
    vec_rows = 4 * width // 128 + ff // 128
    if parted:
        dn, up = part_shape(width, ff, dp), part_shape(ff, width, dp)
        per_half = steps // 2
        dn_spec = pl.BlockSpec((1, dn[1], dn[2] // per_half, 128), lambda i: (i // per_half, 0, i % per_half, 0))
        up_spec = pl.BlockSpec((2, 1, up[2], 128), lambda i: (0, i, 0, 0))
        grads = [(dn, dn_spec), (dn, dn_spec), (up, up_spec), (up, up_spec)]
    else:
        grads = [((width, ff), pl.BlockSpec((width, tile), lambda i: (0, i))),
                 ((ff, width), pl.BlockSpec((tile, width), lambda i: (i, 0)))]
    outs = [((ex, seq, width), whole((ex, seq, width)), BF16)] + [(s, b, BF16) for s, b in grads]
    outs += [((rows, width), whole((rows, width)), F32), ((vec_rows, 128), whole((vec_rows, 128)), F32)]
    return pl.pallas_call(
        functools.partial(mlp_kernel, ex, seq, pad, parted),
        grid=(steps,),
        in_specs=[
            SMEM, whole((rows, width)), whole((rows, width)), whole((ex, seq, width)),
            pl.BlockSpec((width, tile), lambda i: (0, i)), whole((ff,)),
            pl.BlockSpec((tile, width), lambda i: (i, 0)),
            whole((width,)), whole((width,)),
        ],
        out_specs=[b for _, b, _ in outs],
        out_shape=[jax.ShapeDtypeStruct(s, d) for s, _, d in outs],
        scratch_shapes=[
            pltpu.VMEM((rows, width), BF16), pltpu.VMEM((width, rows), BF16),
            pltpu.VMEM((rows, width), F32), pltpu.VMEM((rows, width), F32),
            pltpu.VMEM((steps, 1, tile), F32), pltpu.VMEM((steps, 1, tile), F32),
        ],
        compiler_params=pltpu.CompilerParams(dimension_semantics=("arbitrary",), vmem_limit_bytes=44 << 20),
        cost_estimate=pl.CostEstimate(flops=46 * 10**9, bytes_accessed=30 << 20, transcendentals=rows * ff),
        name="mlp_both_ways",
    )(place, z2, h1, cot, up_w, up_b, down_w, down_b, gain)


def stat_rows(channels):
    return max(8, 2 * channels // 128)


def put_stats(ref, first, second):
    lanes = jnp.concatenate([first, second], axis=1)
    n = ref.shape[0]
    for r in range(lanes.shape[1] // 128):
        ref[:, r, :] = jnp.broadcast_to(lanes[:, r * 128 : (r + 1) * 128], (n, 128))


def get_stats(ref, channels):
    total = jnp.sum(ref[...], axis=0)
    rows = 2 * channels // 128
    half = rows // 2
    first = jnp.concatenate([total[r : r + 1, :] for r in range(half)], axis=1)
    second = jnp.concatenate([total[r : r + 1, :] for r in range(half, rows)], axis=1)
    return first, second


def mean_rstd(ref, channels, count):
    s1, s2 = get_stats(ref, channels)
    mean = s1 * (1.0 / count)
    return mean, lax.rsqrt(s2 * (1.0 / count) - mean * mean + eps_batch)


def real_columns(rows, cols):
    return (lax.broadcasted_iota(jnp.int32, (rows, 1), 0) & 15) < cols


def col_sum(x):
    return jnp.sum(x, axis=0, keepdims=True)


def head_mask(rows, second):
    lane = lax.broadcasted_iota(jnp.int32, (rows, 2 * HD), 1)
    return (lane >= HD) if second else (lane < HD)


def attn_fwd_kernel(ex, n_image, pad, pre_ref, len_ref, h0_ref, g_ref, s_ref, wq_ref, wk_ref, wv_ref, qb_ref, vb_ref,
                    ow_ref, ob_ref, g2_ref, s2_ref,
                    z1_ref, q_ref, k_ref, v_ref, p_ref, attn_ref, h1_ref, z2_ref, acc, qb_s, vb_s):
    i = pl.program_id(0)
    last = pl.num_programs(0) - 1
    wide = wq_ref.shape[1]

    @pl.when(i == 0)
    def _():
        nrm, _r = ln_parts(h0_ref[...].astype(F32))
        z1_ref[...] = (nrm * row_of(g_ref) + row_of(s_ref)).astype(BF16)
        acc[...] = jnp.zeros_like(acc)
        qb, vb = row_of(qb_ref), row_of(vb_ref)
        for j in range(qb_s.shape[0]):
            qb_s[j] = qb[:, j * wide : (j + 1) * wide]
            vb_s[j] = vb[:, j * wide : (j + 1) * wide]

    z1 = z1_ref[...]
    q_ref[...] = (nn(z1, wq_ref[...]) + qb_s[i]).astype(BF16)
    k_ref[...] = nn(z1, wk_ref[...]).astype(BF16)
    v_ref[...] = (nn(z1, wv_ref[...]) + vb_s[i]).astype(BF16)
    zero = jnp.zeros((pad, 2 * HD), BF16)
    first = head_mask(pad, False)

    def example(e, carry):
        row0 = pl.multiple_of(e * pad, 16)
        key = lax.broadcasted_iota(jnp.int32, (pad, pad), 1)
        qry = lax.broadcasted_iota(jnp.int32, (pad, pad), 0)
        limit = jnp.maximum(qry + 1, n_image + pre_ref[e])
        limit = jnp.minimum(limit, n_image + len_ref[e])
        vis = key < limit
        for pair in range(wide // (2 * HD)):
            cols = slice(pair * 2 * HD, (pair + 1) * 2 * HD)
            q2 = q_ref[pl.ds(row0, pad), cols] * jnp.asarray(0.125, BF16)
            k2 = k_ref[pl.ds(row0, pad), cols]
            v2 = v_ref[pl.ds(row0, pad), cols]
            out = None
            for h in range(2):
                sel = first if h == 0 else jnp.logical_not(first)
                sc = nt(jnp.where(sel, q2, zero), k2)
                sc = jnp.where(vis, sc, masked_value)
                top = jnp.max(sc, axis=-1, keepdims=True)
                ex_ = jnp.exp(sc - top)
                tot = jnp.sum(ex_, axis=-1, keepdims=True)
                p = (ex_ * (1.0 / tot)).astype(BF16)
                p_ref[e, pair * 2 + h] = p
                o = nn(p, jnp.where(sel, v2, zero))
                out = o if out is None else out + o
            attn_ref[pl.ds(row0, pad), cols] = out.astype(BF16)
        return carry

    lax.fori_loop(0, ex, example, 0)
    acc[...] += nn(attn_ref[...], ow_ref[...])

    @pl.when(i == last)
    def _():
        h1 = h0_ref[...].astype(F32) + acc[...] + row_of(ob_ref)
        h1_ref[...] = h1
        nrm, _r = ln_parts(h1)
        z2_ref[...] = (nrm * row_of(g2_ref) + row_of(s2_ref)).astype(BF16)


def attn_fwd(h0, prefix, text_len, ln1_gain, ln1_shift, qkv_w, qb, vb, out_w, out_b, ln2_gain, ln2_shift, ex, n_image, pad, wide=256):
    rows, width = h0.shape
    groups = width // wide
    heads = width // HD
    hg = wide // HD
    cols = lambda off: pl.BlockSpec((width, wide), lambda i, *_: (0, i + off * groups))
    vec = whole((width,))
    part = pl.BlockSpec((rows, wide), lambda i, *_: (0, i))
    return pl.pallas_call(
        functools.partial(attn_fwd_kernel, ex, n_image, pad),
        grid_spec=pltpu.PrefetchScalarGridSpec(
            num_scalar_prefetch=2,
            grid=(groups,),
            in_specs=[whole((rows, width)), vec, vec, cols(0), cols(1), cols(2), vec, vec,
                      pl.BlockSpec((wide, width), lambda i, *_: (i, 0)), vec, vec, vec],
            out_specs=[whole((rows, width)), part, part, part,
                       pl.BlockSpec((ex, hg, pad, pad), lambda i, *_: (0, i, 0, 0)),
                       part, whole((rows, width)), whole((rows, width))],
            scratch_shapes=[pltpu.VMEM((rows, width), F32)] + [pltpu.VMEM((groups, 1, wide), F32)] * 2,
        ),
        out_shape=[jax.ShapeDtypeStruct((rows, width), BF16)] * 4 + [
            jax.ShapeDtypeStruct((ex, heads, pad, pad), BF16),
            jax.ShapeDtypeStruct((rows, width), BF16),
            jax.ShapeDtypeStruct((rows, width), F32),
            jax.ShapeDtypeStruct((rows, width), BF16)],
        compiler_params=pltpu.CompilerParams(dimension_semantics=("arbitrary",), vmem_limit_bytes=40 << 20),
        cost_estimate=pl.CostEstimate(flops=32 * 10**9, bytes_accessed=30 << 20, transcendentals=heads * rows * pad),
        name="attention_forward",
    )(prefix, text_len, h0, ln1_gain, ln1_shift, qkv_w, qkv_w, qkv_w, qb, vb, out_w, out_b, ln2_gain, ln2_shift)


def attn_bwd_kernel(ex, n_image, txt, cols_real, pad, parted, place_ref, g1_ref, ow_ref, attn_ref, q_ref, k_ref, v_ref, p_ref, z1_ref, h0_ref, wq_ref, wk_ref, wv_ref, g_ref, *refs):
    if parted:
        ak_ref, as_ref, text_ref, dtok_ref, vec_ref, ow_s, qkv_s = refs[:7]
    else:
        ow_s, qkv_s, text_ref, dtok_ref, vec_ref = refs[:5]
    g1b_s, g1t_s, dat_s, dq_s, dk_s, dv_s, acc, bias_s = refs[-8:]
    i = pl.program_id(0)
    last = pl.num_programs(0) - 1
    wide = wq_ref.shape[1]

    @pl.when(i == 0)
    def _():
        g1b_s[...] = g1_ref[...].astype(BF16)
        g1t_s[...] = g1b_s[...].T
        acc[...] = jnp.zeros_like(acc)

    ow_s[i] = nn(g1t_s[...], attn_ref[...]).astype(BF16)
    dat_s[...] = nt(g1b_s[...], ow_ref[...]).astype(BF16)
    zero = jnp.zeros((pad, 2 * HD), BF16)
    first = head_mask(pad, False)

    def example(e, carry):
        row0 = pl.multiple_of(e * pad, 16)
        for pair in range(wide // (2 * HD)):
            cols = slice(pair * 2 * HD, (pair + 1) * 2 * HD)
            q2 = q_ref[pl.ds(row0, pad), cols]
            k2 = k_ref[pl.ds(row0, pad), cols]
            v2 = v_ref[pl.ds(row0, pad), cols]
            da2 = dat_s[pl.ds(row0, pad), cols]
            dq = dk = dv = None
            for h in range(2):
                sel = first if h == 0 else jnp.logical_not(first)
                pb = p_ref[e, pair * 2 + h]
                p = pb.astype(F32)
                dah = jnp.where(sel, da2, zero)
                dp = nt(dah, v2)
                inner = jnp.sum(p * dp, axis=-1, keepdims=True)
                ds = (p * (dp - inner)).astype(BF16)
                dvh = tn(pb, dah)
                dqh = nn(ds, jnp.where(sel, k2, zero))
                dkh = tn(ds, jnp.where(sel, q2, zero))
                dq = dqh if dq is None else dq + dqh
                dk = dkh if dk is None else dk + dkh
                dv = dvh if dv is None else dv + dvh
            dq_s[pl.ds(row0, pad), cols] = (dq * 0.125).astype(BF16)
            dk_s[pl.ds(row0, pad), cols] = (dk * 0.125).astype(BF16)
            dv_s[pl.ds(row0, pad), cols] = dv.astype(BF16)
        return carry

    lax.fori_loop(0, ex, example, 0)
    z1 = z1_ref[...]
    dq, dk, dv = dq_s[...], dk_s[...], dv_s[...]
    width = z1.shape[1]
    for j, d in enumerate((dq, dk, dv)):
        qkv_s[pl.ds(pl.multiple_of(j * width + i * wide, wide), wide), :] = tn(d, z1).astype(BF16)
    acc[...] += nt(dq, wq_ref[...]) + nt(dk, wk_ref[...]) + nt(dv, wv_ref[...])
    bias_s[0, i] = col_sum(dq.astype(F32))
    bias_s[1, i] = col_sum(dv.astype(F32))

    @pl.when(i == last)
    def _():
        nrm, r = ln_parts(h0_ref[...].astype(F32))
        dz = acc[...]
        g0 = g1_ref[...] + ln_back(dz, nrm, r, row_of(g_ref))
        n = width // 128
        vec_ref[5 * n :, :] = jnp.zeros_like(vec_ref[5 * n :, :])
        put_rows(vec_ref, n, col_sum(dz * nrm))
        put_rows(vec_ref, 2 * n, col_sum(dz))
        for j in range(2):
            for t in range(bias_s.shape[1]):
                put_rows(vec_ref, (3 + j) * n + t * (wide // 128), bias_s[j, t])
        gb = g0.astype(BF16)
        px = dtok_ref.shape[0] // ex
        pick_image = image_pick(px, pad, n_image, cols_real)
        tr = lax.broadcasted_iota(jnp.int32, (txt, pad), 0)
        tc = lax.broadcasted_iota(jnp.int32, (txt, pad), 1)
        pick_text = jnp.where(tc == tr + n_image, 1.0, 0.0).astype(BF16)
        tot = jnp.zeros((1, gb.shape[1]), F32)
        for e in range(ex):
            ge = gb[e * pad : (e + 1) * pad, :]
            text_ref[e] = nn(pick_text, ge).astype(BF16)
            dt = nn(pick_image, ge)
            dtok_ref[e * px : (e + 1) * px, :] = dt.astype(BF16)
            tot = tot + jnp.sum(dt, axis=0, keepdims=True)
        put_rows(vec_ref, 0, tot)
        if parted:
            core = place_ref[1]
            part_it(qkv_s, ak_ref, as_ref, core)
            hi = ak_ref.shape[1]
            r = width // (2 * hi)
            at = qkv_s.shape[0] // (2 * hi) * (width // 256)
            for h in range(hi):
                mine = pl.ds(pl.multiple_of((2 * h + core) * r, 16), r)
                other = pl.ds(pl.multiple_of((2 * h + 1 - core) * r, 16), r)
                for blk in range(width // 128):
                    s, j = divmod(blk, width // 256)
                    t, lane = divmod(blk * 128, wide)
                    dst = slice(at + j * r, at + (j + 1) * r)
                    ak_ref[s, h, dst, :] = ow_s[t, mine, lane : lane + 128]
                    as_ref[s, h, dst, :] = ow_s[t, other, lane : lane + 128]


def image_pick(px, pad, n_image, cols_real):
    p = lax.broadcasted_iota(jnp.int32, (px, pad), 0)
    t = lax.broadcasted_iota(jnp.int32, (px, pad), 1)
    col = p & 15
    tok = (p >> 4) * cols_real + col
    return jnp.where((col < cols_real) & (tok == t) & (t < n_image), 1.0, 0.0).astype(BF16)


def attn_bwd(place, g1, out_w, attn, q, k, v, p, z1, h0, qkv_w, ln1_gain, ex, n_image, txt, img_rows, img_cols, pad, dp, parted, wide=256):
    rows, width = h0.shape
    groups = width // wide
    heads = width // HD
    hg = wide // HD
    px = img_rows * 16
    vec_rows = -(-5 * width // 128 // 8) * 8
    cols = lambda off: pl.BlockSpec((width, wide), lambda i: (0, i + off * groups))
    part = pl.BlockSpec((rows, wide), lambda i: (0, i))
    nat_o, nat_q = (groups, width, wide), (3 * width, width)
    sent = part_shape(4 * width, width, dp)
    outs = [(s, BF16) for s in ((sent, sent) if parted else (nat_o, nat_q))]
    outs += [((ex, txt, width), BF16), ((ex * px, width), BF16), ((vec_rows, 128), F32)]
    natural = [pltpu.VMEM(nat_o, BF16), pltpu.VMEM(nat_q, BF16)] if parted else []
    return pl.pallas_call(
        functools.partial(attn_bwd_kernel, ex, n_image, txt, img_cols, pad, parted),
        grid=(groups,),
        in_specs=[SMEM, whole((rows, width)), pl.BlockSpec((wide, width), lambda i: (i, 0)), part, part, part, part,
                  pl.BlockSpec((ex, hg, pad, pad), lambda i: (0, i, 0, 0)),
                  whole((rows, width)), whole((rows, width)), cols(0), cols(1), cols(2), whole((width,))],
        out_specs=[whole(s) for s, _ in outs],
        out_shape=[jax.ShapeDtypeStruct(s, d) for s, d in outs],
        scratch_shapes=natural + [pltpu.VMEM((rows, width), BF16), pltpu.VMEM((width, rows), BF16)]
        + [pltpu.VMEM((rows, wide), BF16)] * 4 + [pltpu.VMEM((rows, width), F32), pltpu.VMEM((2, groups, 1, wide), F32)],
        compiler_params=pltpu.CompilerParams(dimension_semantics=("arbitrary",), vmem_limit_bytes=48 << 20),
        cost_estimate=pl.CostEstimate(flops=42 * 10**9, bytes_accessed=40 << 20, transcendentals=0),
        name="attention_backward",
    )(place, g1, out_w, attn, q, k, v, p, z1, h0, qkv_w, qkv_w, qkv_w, ln1_gain)

def stats_kernel(cols, x_ref, w_ref, parts_ref, xp):
    xp[...] = jnp.zeros_like(xp)
    shape = x_ref.shape
    xp[:, 0:cols, :] = x_ref[...].reshape(shape[0] * shape[1], cols, shape[3])
    a = nn(xp[...].reshape(shape[0] * shape[1] * 16, shape[3]), w_ref[...])
    put_stats(parts_ref, col_sum(a), col_sum(a * a))


def conv_fwd_kernel(count, ex, rows, cols, place_ref, parts_ref, own_ref, got_ref, win_ref, g_ref, s_ref, wmid_ref,
                    xs_ref, act1_ref, wide_ref, act2_ref, parts2_ref):
    s = place_ref[0]
    half = rows // 2
    px = rows * 16
    chan = xs_ref.shape[-1]
    xs_ref[...] = jnp.zeros_like(xs_ref)
    for e in range(ex):
        xs_ref[e, pl.ds(s * half, half), 0:cols, :] = own_ref[s * ex + e]
        xs_ref[e, pl.ds((1 - s) * half, half), 0:cols, :] = got_ref[e]
    a1 = nn(xs_ref[...].reshape(ex * px, chan), win_ref[...])
    act1_ref[...] = a1
    mid = a1.shape[1]
    mean, rstd = mean_rstd(parts_ref, mid, count)
    real = real_columns(ex * px, cols)
    act = gelu_of((a1 - mean) * rstd * row_of(g_ref) + row_of(s_ref))
    act = jnp.where(real, act, 0.0)
    for e in range(ex):
        part = act[e * px : (e + 1) * px]
        wide_ref[e, 0:16, :] = jnp.zeros((16, 3 * mid), BF16)
        wide_ref[e, px + 16 : px + 32, :] = jnp.zeros((16, 3 * mid), BF16)
        wide_ref[e, 16 : px + 16, 0:mid] = pltpu.roll(part, 1, 0).astype(BF16)
        wide_ref[e, 16 : px + 16, mid : 2 * mid] = part.astype(BF16)
        wide_ref[e, 16 : px + 16, 2 * mid : 3 * mid] = pltpu.roll(part, px - 1, 0).astype(BF16)
    one = real_columns(px, cols)
    t1 = jnp.zeros((1, mid), F32)
    t2 = jnp.zeros((1, mid), F32)
    for e in range(ex):
        a2 = nn(wide_ref[e, 0:px, :], wmid_ref[0])
        a2 = a2 + nn(wide_ref[e, 16 : px + 16, :], wmid_ref[1])
        a2 = a2 + nn(wide_ref[e, 32 : px + 32, :], wmid_ref[2])
        a2 = jnp.where(one, a2, 0.0)
        act2_ref[e * px : (e + 1) * px, :] = a2
        t1 = t1 + col_sum(a2)
        t2 = t2 + col_sum(a2 * a2)
    put_stats(parts2_ref, t1, t2)


def expand_kernel(count, cols, parts_ref, act2_ref, g_ref, s_ref, w_ref, relu2_ref, act3_ref, parts3_ref):
    a2 = act2_ref[...]
    mean, rstd = mean_rstd(parts_ref, a2.shape[1], count)
    act = gelu_of((a2 - mean) * rstd * row_of(g_ref) + row_of(s_ref))
    low = jnp.where(real_columns(a2.shape[0], cols), act, 0.0).astype(BF16)
    relu2_ref[...] = low
    a3 = nn(low, w_ref[...])
    act3_ref[...] = a3
    put_stats(parts3_ref, col_sum(a3), col_sum(a3 * a3))


def tokens_kernel(count, ex, cols, n_image, pad, parts_ref, act3_ref, xs_ref, g_ref, s_ref, w_ref, b_ref, text_ref,
                  stem_ref, h0_ref):
    a3 = act3_ref[...]
    mean, rstd = mean_rstd(parts_ref, a3.shape[1], count)
    pre = (a3 - mean) * rstd * row_of(g_ref) + row_of(s_ref) + xs_ref[...].reshape(a3.shape).astype(F32)
    stem = gelu_of(pre).astype(BF16)
    stem_ref[...] = stem
    tok = (nn(stem, w_ref[...]) + row_of(b_ref)).astype(BF16)
    px = a3.shape[0] // ex
    txt = text_ref.shape[1]
    t = lax.broadcasted_iota(jnp.int32, (pad, px), 0)
    p = lax.broadcasted_iota(jnp.int32, (pad, px), 1)
    col = p & 15
    pick = jnp.where((col < cols) & ((p >> 4) * cols + col == t), 1.0, 0.0).astype(BF16)
    tr = lax.broadcasted_iota(jnp.int32, (pad, txt), 0)
    tc = lax.broadcasted_iota(jnp.int32, (pad, txt), 1)
    pick_text = jnp.where(tr == tc + n_image, 1.0, 0.0).astype(BF16)
    for e in range(ex):
        both = nn(pick, tok[e * px : (e + 1) * px, :]) + nn(pick_text, text_ref[e])
        h0_ref[e * pad : (e + 1) * pad, :] = both.astype(BF16)


def dpre_kernel(count, ex, rows, place_ref, parts_ref, act3_ref, xs_ref, g_ref, s_ref, dtok_ref, w_ref, dpre_ref, send_ref, parts4_ref):
    a3 = act3_ref[...]
    mean, rstd = mean_rstd(parts_ref, a3.shape[1], count)
    nrm = (a3 - mean) * rstd
    pre = nrm * row_of(g_ref) + row_of(s_ref) + xs_ref[...].reshape(a3.shape).astype(F32)
    _, slope = gelu_and_slope(pre)
    d = nt(dtok_ref[...], w_ref[...]) * slope
    dpre_ref[...] = d.reshape(dpre_ref.shape)
    put_stats(parts4_ref, col_sum(d), col_sum(d * nrm))
    half = rows // 2
    other = 1 - place_ref[0]
    for e in range(ex):
        send_ref[e] = dpre_ref[e, pl.ds(other * half, half)].astype(BF16)


def back3_kernel(count, cols, parts4_ref, parts3_ref, parts2_ref, act3_ref, dpre_ref, g3_ref, w_ref, act2_ref, g2_ref, s2_ref, veca_ref, vecb_ref,
                 low3_ref, t2_ref, parts5_ref, gain_ref, shift_ref, small_s):
    a3 = act3_ref[...]
    chan = a3.shape[1]
    mean, rstd = mean_rstd(parts3_ref, chan, count)
    s1, s2 = get_stats(parts4_ref, chan)
    gain_ref[...] = s2.reshape(-1)
    shift_ref[...] = s1.reshape(-1)
    nrm = (a3 - mean) * rstd
    d = (row_of(g3_ref) * rstd) * (dpre_ref[...].reshape(a3.shape) - s1 * (1.0 / count) - nrm * (s2 * (1.0 / count)))
    low = jnp.where(real_columns(a3.shape[0], cols), d, 0.0).astype(BF16)
    low3_ref[...] = low
    a2 = act2_ref[...]
    mean2, rstd2 = mean_rstd(parts2_ref, a2.shape[1], count)
    nrm2 = (a2 - mean2) * rstd2
    _, slope = gelu_and_slope(nrm2 * row_of(g2_ref) + row_of(s2_ref))
    t2 = nt(low, w_ref[...]) * slope
    t2_ref[...] = t2
    parts5_ref[...] = jnp.zeros_like(parts5_ref)
    put_stats(parts5_ref, col_sum(t2), col_sum(t2 * nrm2))
    used = veca_ref.shape[0] + vecb_ref.shape[0]
    n = parts5_ref.shape[0]
    each = -(-used // n)
    small_s[0 : veca_ref.shape[0], :] = veca_ref[...]
    small_s[veca_ref.shape[0] : used, :] = vecb_ref[...]
    if used < small_s.shape[0]:
        small_s[used:, :] = jnp.zeros_like(small_s[used:, :])
    for d in range(n):
        parts5_ref[d, 4 : 4 + each, :] = small_s[d * each : (d + 1) * each, :]


def back2_kernel(count, ex, rows, cols, place_ref, parts5_ref, parts2_ref, parts1_ref, act2_ref, t2_ref, g2_ref, wmid_ref, act1_ref, g1_ref, s1_ref,
                 low2_ref, t1_ref, send_ref, parts6_ref, gain_ref, shift_ref, wide):
    a2 = act2_ref[...]
    mid = a2.shape[1]
    px = rows * 16
    mean, rstd = mean_rstd(parts2_ref, mid, count)
    s1, s2 = get_stats(parts5_ref, mid)
    gain_ref[...] = s2.reshape(-1)
    shift_ref[...] = s1.reshape(-1)
    nrm = (a2 - mean) * rstd
    d = (row_of(g2_ref) * rstd) * (t2_ref[...] - s1 * (1.0 / count) - nrm * (s2 * (1.0 / count)))
    d = jnp.where(real_columns(ex * px, cols), d, 0.0)
    low2_ref[...] = d.astype(BF16)
    for e in range(ex):
        part = d[e * px : (e + 1) * px]
        wide[e, 0:16, :] = jnp.zeros((16, 3 * mid), BF16)
        wide[e, px + 16 : px + 32, :] = jnp.zeros((16, 3 * mid), BF16)
        wide[e, 16 : px + 16, 0:mid] = pltpu.roll(part, px - 1, 0).astype(BF16)
        wide[e, 16 : px + 16, mid : 2 * mid] = part.astype(BF16)
        wide[e, 16 : px + 16, 2 * mid : 3 * mid] = pltpu.roll(part, 1, 0).astype(BF16)
    mean1, rstd1 = mean_rstd(parts1_ref, mid, count)
    one = real_columns(px, cols)
    q1 = jnp.zeros((1, mid), F32)
    q2 = jnp.zeros((1, mid), F32)
    for e in range(ex):
        t = None
        for r in range(3):
            for c in range(3):
                term = nt(wide[e, (2 - r) * 16 : (2 - r) * 16 + px, c * mid : (c + 1) * mid], wmid_ref[r, c * mid : (c + 1) * mid, :])
                t = term if t is None else t + term
        nrm1 = (act1_ref[e * px : (e + 1) * px, :] - mean1) * rstd1
        _, slope = gelu_and_slope(nrm1 * row_of(g1_ref) + row_of(s1_ref))
        t = jnp.where(one, t * slope, 0.0)
        t1_ref[e] = t.reshape(rows, 16, mid)
        q1 = q1 + col_sum(t)
        q2 = q2 + col_sum(t * nrm1)
    put_stats(parts6_ref, q1, q2)
    chunk = jnp.sum(parts5_ref[:, 4:8, :], axis=0)
    parts6_ref[:, 4:8, :] = jnp.broadcast_to(chunk[None], (parts6_ref.shape[0], 4, 128))
    half = rows // 2
    other = 1 - place_ref[0]
    for e in range(ex):
        send_ref[e] = t1_ref[e, pl.ds(other * half, half)].astype(BF16)


def conv_grads_kernel(ex, px, parted, place_ref, low2_ref, wide_ref, low3_ref, relu2_ref, *refs):
    mid = low2_ref.shape[1]
    nat_m, nat_o = (refs[2], refs[3]) if parted else (refs[0], refs[1])
    nat_o[...] = tn(low3_ref[...], relu2_ref[...]).astype(BF16)
    for r in range(3):
        tot = None
        for e in range(ex):
            term = tn(low2_ref[e * px : (e + 1) * px, :], wide_ref[e, r * 16 : r * 16 + px, :])
            tot = term if tot is None else tot + term
        for c in range(3):
            for h in range(2):
                at = (h * 9 + r * 3 + c) * (mid // 2)
                src = c * mid + h * (mid // 2)
                nat_m[:, at : at + mid // 2] = tot[:, src : src + mid // 2].astype(BF16)
    if parted:
        part_it(nat_m, refs[0], refs[1], place_ref[1])
        part_it(nat_o, refs[0], refs[1], place_ref[1], at=nat_m.shape[0] // (2 * refs[0].shape[1]) * (nat_m.shape[1] // 256))


def tn_kernel(parted, place_ref, a_ref, b_ref, *refs):
    natural = refs[2] if parted else refs[0]
    natural[...] = tn(a_ref[...], b_ref[...]).astype(BF16)
    if parted:
        part_it(natural, refs[0], refs[1], place_ref[1])


def image_kernel(count, ex, rows, cols, parted, each, places, place_ref, parts6_ref, parts1_ref, x_ref, win_ref, g_ref, t1_ref, gott_ref, dpre_ref, gotd_ref,
                 grad_ref, *refs):
    if parted:
        keep_ref, send_ref, win_grad_ref = refs[0], refs[1], refs[-1]
        refs = refs[2:-1]
    else:
        win_grad_ref, refs = refs[0], refs[1:]
    gain_ref, shift_ref, vec_refs, xp, small_s = refs[0], refs[1], refs[2:-2], refs[-2], refs[-1]
    s = place_ref[0]
    half = rows // 2
    chan = x_ref.shape[-1]
    mid = win_ref.shape[1]
    mean, rstd = mean_rstd(parts1_ref, mid, count)
    s1, s2 = get_stats(parts6_ref, mid)
    gain_ref[...] = s2.reshape(-1)
    shift_ref[...] = s1.reshape(-1)
    real = real_columns(ex * half * 16, cols)
    size = ex * half * 16
    xp[...] = jnp.zeros_like(xp)
    wg = None
    for own in (True, False):
        at = (s if own else 1 - s) * ex
        xp[:, 0:cols, :] = x_ref[pl.ds(at, ex)].reshape(ex * half, cols, chan)
        x = xp[...].reshape(size, chan)
        nrm = (nn(x, win_ref[...]) - mean) * rstd
        if own:
            t = t1_ref[:, pl.ds(s * half, half)].reshape(size, mid)
            dp = dpre_ref[:, pl.ds(s * half, half)].reshape(size, chan)
        else:
            t = gott_ref[...].reshape(size, mid).astype(F32)
            dp = gotd_ref[...].reshape(size, chan).astype(F32)
        d = (row_of(g_ref) * rstd) * (t - s1 * (1.0 / count) - nrm * (s2 * (1.0 / count)))
        low = jnp.where(real, d, 0.0).astype(BF16)
        grad = (nt(low, win_ref[...]) + dp).astype(BF16).reshape(ex, half, 16, chan)
        grad_ref[pl.ds(at, ex)] = grad[:, :, 0:cols, :]
        term = tn(low, x)
        wg = term if wg is None else wg + term
    win_grad_ref[...] = wg.astype(BF16)
    if parted:
        part_it(win_grad_ref, keep_ref, send_ref, place_ref[1])
    for d in range(parts6_ref.shape[0]):
        small_s[d * each : (d + 1) * each, :] = parts6_ref[d, 4 : 4 + each, :]
    for ref, at in zip(vec_refs, places):
        ref[...] = take_rows(small_s, at, ref.shape[0]).reshape(-1)


def call(kernel, outs, *args, place=None, scratch=(), name=None, us=2, limit=24):
    nbytes = sum(a.size * a.dtype.itemsize for a in args)
    return pl.pallas_call(
        kernel,
        out_shape=[jax.ShapeDtypeStruct(s, d) for s, d in outs],
        in_specs=([SMEM] if place is not None else []) + [VMEM] * len(args),
        out_specs=[VMEM] * len(outs),
        scratch_shapes=list(scratch),
        compiler_params=pltpu.CompilerParams(vmem_limit_bytes=limit << 20),
        cost_estimate=pl.CostEstimate(flops=us * 10**9, bytes_accessed=nbytes, transcendentals=0),
        name=name,
    )(*([place] if place is not None else []), *args)


DP = ("far", "near", "core")
AXES = DP + ("space",)


def spread(parts):
    return lax.all_to_all(parts, AXES, split_axis=0, concat_axis=0, tiled=True)


def swap(x, axis="space"):
    return lax.ppermute(x, axis, [(0, 1), (1, 0)])


def tie(*values):
    return lax.optimization_barrier(values)


def combine_kernel(pairs, bits_ref, *refs):
    ins, outs = refs[: 4 * pairs], refs[4 * pairs :]
    for j in range(pairs):
        a, b, c, d = ins[4 * j : 4 * j + 4]
        outs[2 * j][...] = a[:, 0] + b[:, 0]
        outs[2 * j + 1][...] = c[:, 0] + d[:, 0]


def combine(items, tiles):
    bits = jnp.stack([bit for _, _, bit, _, _ in items]).astype(jnp.int32)
    args, in_specs, outs, out_specs = [], [], [], []
    for j, (keep, got, _, before, after) in enumerate(items):
        rows = keep.shape[-2]
        rt = rows // tiles
        view = (before, 2, after, rows, 128)
        block = (before, 1, after, rt, 128)
        mine = pl.BlockSpec(block, lambda t, bits_ref, j=j: (0, bits_ref[j], 0, t, 0))
        other = pl.BlockSpec(block, lambda t, bits_ref, j=j: (0, 1 - bits_ref[j], 0, t, 0))
        keep, got = keep.reshape(view), got.reshape(view)
        args += [keep, got, keep, got]
        in_specs += [mine, mine, other, other]
        outs += [jax.ShapeDtypeStruct((before, after, rows, 128), BF16)] * 2
        out_specs += [pl.BlockSpec((before, after, rt, 128), lambda t, bits_ref: (0, 0, t, 0))] * 2
    size = sum(a.size for a in args)
    res = pl.pallas_call(
        functools.partial(combine_kernel, len(items)),
        grid_spec=pltpu.PrefetchScalarGridSpec(num_scalar_prefetch=1, grid=(tiles,), in_specs=in_specs, out_specs=out_specs),
        out_shape=outs,
        compiler_params=pltpu.CompilerParams(dimension_semantics=("arbitrary",), vmem_limit_bytes=24 << 20),
        cost_estimate=pl.CostEstimate(flops=3 * 10**9, bytes_accessed=3 * size, transcendentals=0),
        name="combine",
    )(bits, *args)
    return [(res[2 * j], res[2 * j + 1]) for j in range(len(items))]


class Halving:
    def __init__(self, keep, send):
        self.left = ["space", "f1", "f0", "near"]
        self.keep, self.got = keep, self.exchange("core", send)

    def exchange(self, name, send):
        if name in ("f0", "f1"):
            flip = 1 if name == "f0" else 2
            return lax.ppermute(send, "far", [(j, j ^ flip) for j in range(4)])
        return lax.ppermute(send, name, [(0, 1), (1, 0)])

    def item(self, name):
        at = self.left.index(name)
        if name in ("f0", "f1"):
            bit = (lax.axis_index("far") // (1 if name == "f0" else 2)) % 2
        else:
            bit = lax.axis_index(name)
        return self.keep, self.got, bit, 2**at, 2 ** (len(self.left) - at - 1)

    def advance(self, name, keep, send):
        self.left.remove(name)
        self.keep, self.got = keep, self.exchange(name, send)

    def done(self):
        rows = self.keep.shape[-2]
        return self.keep.reshape(rows, 128).astype(F32) + self.got.reshape(rows, 128).astype(F32)


def step(moves, tiles, tied):
    res = combine([h.item(name) for h, name in moves], tiles)
    flat = tie(tied, *[x for pair in res for x in pair])
    for j, (h, name) in enumerate(moves):
        h.advance(name, flat[1 + 2 * j], flat[2 + 2 * j])
    return flat[0]


def final(x, r, at=0, blocks=None):
    blocks = x.shape[0] // r if blocks is None else blocks
    x = x[at : at + r * blocks].astype(F32).reshape(blocks, r, 128)
    return x.transpose(0, 2, 1).reshape(blocks * 128, r)


def halve_dp(x, axis, bit):
    size = lax.axis_size(DP)
    mine = (lax.axis_index(DP) // bit) % 2
    keep = lax.dynamic_index_in_dim(x, mine, axis, keepdims=True)
    send = lax.dynamic_index_in_dim(x, 1 - mine, axis, keepdims=True)
    return keep + lax.ppermute(send, DP, [(j, j ^ bit) for j in range(size)])


def scattered(grad_t):
    size = lax.axis_size(DP)
    bits = size.bit_length() - 1
    cols, rows = grad_t.shape
    x = grad_t.reshape((2,) * bits + (cols // size, rows))
    for b in range(bits):
        x = halve_dp(x, bits - 1 - b, 1 << b)
    half = rows // 2
    mine = lax.axis_index("space")
    keep = lax.dynamic_slice_in_dim(x, mine * half, half, axis=x.ndim - 1)
    send = lax.dynamic_slice_in_dim(x, (1 - mine) * half, half, axis=x.ndim - 1)
    return (keep + swap(send)).reshape(cols // size, half).astype(F32).T


def shards(
    image_in, text_in, prefix, text_len, cotangent,
    conv_in_w, bn1_gain, bn1_shift, conv_mid_w, bn2_gain, bn2_shift, conv_out_w, bn3_gain, bn3_shift,
    proj_w, proj_b, ln1_gain, ln1_shift, qkv_w, query_bias, value_bias, out_w, out_b,
    ln2_gain, ln2_shift, up_w, up_b, down_w, down_b,
):
    n_dev, dp = lax.axis_size(AXES), lax.axis_size(DP)
    band_ex, band_rows, cols, chan = image_in.shape
    mid = conv_in_w.shape[1]
    width = proj_w.shape[1]
    ff = up_w.shape[1]
    ex, txt, _ = text_in.shape
    rows = band_rows * lax.axis_size("space")
    n_image = rows * cols
    seq = n_image + txt
    pad = -(-seq // 16) * 16
    px = rows * 16
    count = float(band_ex * band_rows * cols * n_dev)
    me = lax.axis_index("space").astype(jnp.int32)
    place = jnp.stack([me, lax.axis_index("core").astype(jnp.int32)])
    small, large = (n_dev, stat_rows(mid), 128), (n_dev, stat_rows(chan), 128)
    wmid = conv_mid_w.reshape(3, 3 * mid, mid)
    weights = [(mid, chan), (mid, 9 * mid), (chan, mid), (width, chan), (3 * width, width), (width, width), (ff, width), (width, ff)]
    parted = dp == 16 and all(c % (16 * dp) == 0 and r % 256 == 0 for c, r in weights)
    hi = dp // 2

    def grad_outs(c, r):
        return [(part_shape(c, r, dp), BF16)] * 2 if parted else [((c, r), BF16)]

    def natural(c, r):
        return [pltpu.VMEM((c, r), BF16)] if parted else []

    got_x = swap(lax.dynamic_slice_in_dim(image_in, (1 - me) * ex, ex, axis=0))
    parts1, = call(functools.partial(stats_kernel, cols), [(small, F32)], image_in, conv_in_w,
                   scratch=[pltpu.VMEM((band_ex * band_rows, 16, chan), BF16)], name="stats_one")
    parts1 = spread(parts1)
    xs, act1, wide, act2, parts2 = call(
        functools.partial(conv_fwd_kernel, count, ex, rows, cols),
        [((ex, rows, 16, chan), BF16), ((ex * px, mid), F32), ((ex, px + 32, 3 * mid), BF16), ((ex * px, mid), F32), (small, F32)],
        parts1, image_in, got_x, conv_in_w, bn1_gain, bn1_shift, wmid, place=place, name="conv_three", us=4)
    parts2 = spread(parts2)
    relu2, act3, parts3 = call(
        functools.partial(expand_kernel, count, cols),
        [((ex * px, mid), BF16), ((ex * px, chan), F32), (large, F32)],
        parts2, act2, bn2_gain, bn2_shift, conv_out_w, name="expand")
    parts3 = spread(parts3)
    stem, h0 = call(
        functools.partial(tokens_kernel, count, ex, cols, n_image, pad),
        [((ex * px, chan), BF16), ((ex * pad, width), BF16)],
        parts3, act3, xs, bn3_gain, bn3_shift, proj_w, proj_b, text_in, name="tokens", us=5)
    z1, q, k, v, p, attn, h1, z2 = attn_fwd(h0, prefix, text_len, ln1_gain, ln1_shift, qkv_w, query_bias, value_bias,
                                            out_w, out_b, ln2_gain, ln2_shift, ex, n_image, pad)
    mlp_outs = mlp(place, z2, h1, cotangent, up_w, up_b, down_w, down_b, ln2_gain, pad, dp, parted)
    block_out, mlp_grads, (g1, veca) = mlp_outs[0], mlp_outs[1:-2], mlp_outs[-2:]
    if parted:
        down, up = Halving(*mlp_grads[:2]), Halving(*mlp_grads[2:])
    att_outs = attn_bwd(place, g1, out_w, attn, q, k, v, p, z1, h0, qkv_w, ln1_gain, ex, n_image, txt, rows, cols, pad, dp, parted)
    att_grads, (text_grad, dtok, vecb) = att_outs[:-3], att_outs[-3:]
    if parted:
        dtok = step([(down, "space"), (up, "f0")], 3, dtok)
        att = Halving(*att_grads)
    dpre, dsend, parts4 = call(
        functools.partial(dpre_kernel, count, ex, rows),
        [((ex, rows, 16, chan), F32), ((ex, band_rows, 16, chan), BF16), (large, F32)],
        parts3, act3, xs, bn3_gain, bn3_shift, dtok, proj_w, place=place, name="stem_back", us=7)
    got_d = swap(dsend)
    parts4 = spread(parts4)
    proj_g = call(functools.partial(tn_kernel, parted), grad_outs(width, chan), dtok, stem, place=place, scratch=natural(width, chan), name="proj_grad")
    if parted:
        proj = Halving(*proj_g)
        dpre = step([(att, "near")], 3, dpre)
    low3, t2, parts5, bn3_gg, bn3_sg = call(
        functools.partial(back3_kernel, count, cols),
        [((ex * px, chan), BF16), ((ex * px, mid), F32), (small, F32), ((chan,), F32), ((chan,), F32)],
        parts4, parts3, parts2, act3, dpre, bn3_gain, conv_out_w, act2, bn2_gain, bn2_shift, veca, vecb,
        scratch=[pltpu.VMEM((n_dev * -(-(veca.shape[0] + vecb.shape[0]) // n_dev), 128), F32)], name="back_three", us=4)
    parts5 = spread(parts5)
    if parted:
        t2 = step([(down, "near"), (up, "space"), (proj, "f0")], 3, t2)
    low2, t1, tsend, parts6, bn2_gg, bn2_sg = call(
        functools.partial(back2_kernel, count, ex, rows, cols),
        [((ex * px, mid), BF16), ((ex, rows, 16, mid), F32), ((ex, band_rows, 16, mid), BF16), (small, F32), ((mid,), F32), ((mid,), F32)],
        parts5, parts2, parts1, act2, t2, bn2_gain, wmid, act1, bn1_gain, bn1_shift,
        place=place, scratch=[pltpu.VMEM((ex, px + 32, 3 * mid), BF16)], name="back_two", us=4)
    got_t = swap(tsend)
    parts6 = spread(parts6)
    conv_g = call(
        functools.partial(conv_grads_kernel, ex, px, parted),
        [(part_shape(mid, 9 * mid, dp)[:2] + (part_shape(mid, 9 * mid, dp)[2] + part_shape(chan, mid, dp)[2], 128), BF16)] * 2
        if parted else [((mid, 9 * mid), BF16), ((chan, mid), BF16)],
        low2, wide, low3, relu2, place=place, scratch=natural(mid, 9 * mid) + natural(chan, mid), name="conv_grads")
    if parted:
        conv = Halving(*conv_g)
        t1 = step([(down, "f0"), (up, "near"), (att, "f0"), (proj, "near")], 3, t1)
        t1 = step([(conv, "space")], 1, t1)
    each = -(-(veca.shape[0] + vecb.shape[0]) // n_dev)
    n, off = width // 128, veca.shape[0]
    places = [off, off + n, off + 2 * n, off + 3 * n, off + 4 * n, 3 * n, n, 2 * n, 4 * n, 0]
    sizes = [width] * 8 + [ff, width]
    last = call(
        functools.partial(image_kernel, count, ex, rows, cols, parted, each, places),
        [(image_in.shape, BF16)] + grad_outs(mid, chan) + [((mid,), F32)] * 2 + [((s,), F32) for s in sizes],
        parts6, parts1, image_in, conv_in_w, bn1_gain, t1, got_t, dpre, got_d,
        place=place, scratch=[pltpu.VMEM((ex * band_rows, 16, chan), BF16), pltpu.VMEM((n_dev * each, 128), F32)] + natural(mid, chan),
        name="image_back", us=5)
    image_grad, sums = last[0], last[3 if parted else 2 :]
    bn1_gg, bn1_sg, vecs = sums[0], sums[1], sums[2:]
    if parted:
        in_x = (last[1] + swap(last[2], "core")).reshape((2 * hi,) + last[1].shape[2:])
        image_grad = step([(conv, "near")], 1, image_grad)
        image_grad = step([(down, "f1"), (up, "f1"), (att, "space"), (proj, "space")], 3, image_grad)
        in_x = jnp.sum(lax.all_to_all(in_x, ("space", "far", "near"), split_axis=0, concat_axis=0, tiled=True).astype(F32), axis=0)
        image_grad = step([(conv, "f0"), (proj, "f1")], 1, image_grad)
        image_grad = step([(att, "f1"), (conv, "f1")], 1, image_grad)
        conv_x, att_x = conv.done(), att.done()
        r_mid, r_out3, r_q, r_w = mid // dp, chan // dp, 3 * width // dp, width // dp
        g_in = final(in_x, r_mid)
        g_mid = final(conv_x, r_mid, 0, 9 * mid // 256)
        g_out3 = final(conv_x, r_out3, r_mid * (9 * mid // 256), mid // 256)
        g_proj = final(proj.done(), r_w)
        g_qkv = final(att_x, r_q, 0, width // 256)
        g_out = final(att_x, r_w, r_q * (width // 256), width // 256)
        g_up = final(up.done(), ff // dp)
        g_down = final(down.done(), r_w)
    else:
        out_n = att_outs[0].transpose(1, 0, 2).reshape(width, width)
        g_in, g_mid, g_out3, g_proj, g_qkv, g_out, g_up, g_down = [
            scattered(x) for x in (last[1], conv_g[0], conv_g[1], proj_g[0], att_outs[1], out_n, mlp_grads[1], mlp_grads[0])]
    return (
        block_out, image_grad, text_grad,
        g_in, bn1_gg, bn1_sg,
        g_mid.reshape(3, 3, mid // 2, g_mid.shape[1]), bn2_gg, bn2_sg,
        g_out3, bn3_gg, bn3_sg,
        g_proj, vecs[0], vecs[1], vecs[2],
        g_qkv, vecs[3], vecs[4],
        g_out, vecs[5], vecs[6], vecs[7],
        g_up, vecs[8],
        g_down, vecs[9],
    )


def solution(mesh):
    dp, space = mesh.devices.shape
    fine = Mesh(mesh.devices.reshape(dp // 4, 2, 2, space), AXES)
    return jax.shard_map(
        shards,
        mesh=fine,
        in_specs=(
            P(DP, "space", None, None),
            P(AXES, None, None),
            P(AXES),
            P(AXES),
            P(AXES, None, None),
            P(),
            P(),
            P(),
            P(),
            P(),
            P(),
            P(),
            P(),
            P(),
            P(),
            P(),
            P(),
            P(),
            P(),
            P(),
            P(),
            P(),
            P(),
            P(),
            P(),
            P(),
            P(),
            P(),
            P(),
        ),
        out_specs=(
            P(AXES, None, None),
            P(DP, "space", None, None),
            P(AXES, None, None),
            P("space", DP),
            P(),
            P(),
            P(None, None, "space", DP),
            P(),
            P(),
            P("space", DP),
            P(),
            P(),
            P("space", DP),
            P(),
            P(),
            P(),
            P("space", DP),
            P(),
            P(),
            P("space", DP),
            P(),
            P(),
            P(),
            P("space", DP),
            P(),
            P("space", DP),
            P(),
        ),
        check_vma=False,
    )
```

```python
import functools
import jax
import jax.numpy as jnp
from jax import lax
from jax.experimental import pallas as pl
from jax.experimental.pallas import tpu as pltpu
from jax.sharding import Mesh, PartitionSpec as P

HD = 64
F32 = jnp.float32
BF16 = jnp.bfloat16
eps_batch = 1e-05
eps_layer = 1e-06
masked_value = -1e30
GELU_C = 0.7978845608028654
GELU_A = 0.044715


def nn(a, b):
    return lax.dot_general(a, b, (((1,), (0,)), ((), ())), preferred_element_type=F32)


def nt(a, b):
    return lax.dot_general(a, b, (((1,), (1,)), ((), ())), preferred_element_type=F32)


def tn(a, b):
    return lax.dot_general(a, b, (((0,), (0,)), ((), ())), preferred_element_type=F32)


def gelu_of(x):
    t = jnp.tanh(GELU_C * (x + GELU_A * x * x * x))
    return 0.5 * x * (1.0 + t)


def gelu_and_slope(x):
    x2 = x * x
    t = jnp.tanh(x * (GELU_C + (GELU_C * GELU_A) * x2))
    half = 0.5 + 0.5 * t
    slope = half + (0.5 * x) * (1.0 - t * t) * (GELU_C + (3.0 * GELU_C * GELU_A) * x2)
    return x * half, slope


def ln_parts(x):
    mean = jnp.mean(x, axis=-1, keepdims=True)
    c = x - mean
    var = jnp.mean(c * c, axis=-1, keepdims=True)
    r = lax.rsqrt(var + eps_layer)
    return c * r, r


def ln_back(dz, nrm, r, gain):
    u = dz * gain
    return r * (u - jnp.mean(u, axis=-1, keepdims=True) - nrm * jnp.mean(u * nrm, axis=-1, keepdims=True))


def whole(shape):
    return pl.BlockSpec(shape, lambda *_: (0,) * len(shape), pipeline_mode=pl.Buffered(1))


SMEM = pl.BlockSpec(memory_space=pltpu.SMEM)
VMEM = pl.BlockSpec(memory_space=pltpu.VMEM)


def row_of(ref):
    return ref[...].reshape(1, -1)


def put_rows(ref, at, vector):
    for r in range(vector.shape[1] // 128):
        ref[at + r : at + r + 1, :] = vector[:, r * 128 : (r + 1) * 128]


def take_rows(ref, at, size):
    return jnp.concatenate([ref[at + r : at + r + 1, :] for r in range(size // 128)], axis=1)


def part_shape(cols, rows, dp):
    return (2, dp // 2, cols // dp * (rows // 2) // 128, 128)


def part_it(natural, keep_ref, send_ref, core, at=0, lead=None):
    rows, cols = natural.shape[-2:]
    _, hi = keep_ref.shape[:2]
    r, blocks = rows // (2 * hi), cols // 256
    for h in range(hi):
        mine = pl.ds(pl.multiple_of((2 * h + core) * r, 16), r)
        other = pl.ds(pl.multiple_of((2 * h + 1 - core) * r, 16), r)
        for s in range(2):
            for b in range(blocks):
                lanes = slice((s * blocks + b) * 128, (s * blocks + b + 1) * 128)
                keep_ref[s, h, at + b * r : at + (b + 1) * r, :] = natural[mine, lanes]
                send_ref[s, h, at + b * r : at + (b + 1) * r, :] = natural[other, lanes]


def mlp_kernel(ex, seq, pad, parted, place_ref, z2_ref, h1_ref, cot_ref, upw_ref, upb_ref, dnw_ref, dnb_ref, g_ref, *refs):
    if parted:
        out_ref, dk_ref, ds_ref, uk_ref, us_ref, g1_ref, vec_ref, g2_s, g2t_s, acc_o, acc_d, ub_s, bg_s = refs
    else:
        out_ref, dn_ref, up_ref, g1_ref, vec_ref, g2_s, g2t_s, acc_o, acc_d, ub_s, bg_s = refs
    i = pl.program_id(0)
    last = pl.num_programs(0) - 1
    tile = upw_ref.shape[1]

    @pl.when(i == 0)
    def _():
        g2_s[...] = jnp.zeros_like(g2_s)
        for e in range(ex):
            g2_s[e * pad : e * pad + seq, :] = cot_ref[e]
        g2t_s[...] = g2_s[...].T
        acc_o[...] = jnp.zeros_like(acc_o)
        acc_d[...] = jnp.zeros_like(acc_d)
        ub = row_of(upb_ref)
        for j in range(ub_s.shape[0]):
            ub_s[j] = ub[:, j * tile : (j + 1) * tile]

    z2 = z2_ref[...]
    g2 = g2_s[...]
    pre = nn(z2, upw_ref[...]) + ub_s[i]
    act, slope = gelu_and_slope(pre)
    low = act.astype(BF16)
    dg = (nt(g2, dnw_ref[...]) * slope).astype(BF16)
    acc_o[...] += nn(low, dnw_ref[...])
    acc_d[...] += nt(dg, upw_ref[...])
    dn = nn(g2t_s[...], low).astype(BF16)
    up = tn(dg, z2).astype(BF16)
    bg_s[i] = jnp.sum(dg.astype(F32), axis=0, keepdims=True)
    if parted:
        core = place_ref[1]
        even = core == 0
        hi = dk_ref.shape[1]
        r = dn.shape[0] // (2 * hi)
        for j in range(tile // 128):
            d4 = dn[:, j * 128 : (j + 1) * 128].reshape(hi, 2, r, 128)
            dk_ref[0, :, j * r : (j + 1) * r, :] = jnp.where(even, d4[:, 0], d4[:, 1])
            ds_ref[0, :, j * r : (j + 1) * r, :] = jnp.where(even, d4[:, 1], d4[:, 0])
        r, blocks = up.shape[0] // 4, up.shape[1] // 256
        for s in range(2):
            for j in range(blocks):
                lanes = slice((s * blocks + j) * 128, (s * blocks + j + 1) * 128)
                for t in range(2):
                    first, second = up[2 * t * r : (2 * t + 1) * r, lanes], up[(2 * t + 1) * r : (2 * t + 2) * r, lanes]
                    uk_ref[s, t, j * r : (j + 1) * r, :] = jnp.where(even, first, second)
                    us_ref[s, t, j * r : (j + 1) * r, :] = jnp.where(even, second, first)
    else:
        dn_ref[...] = dn
        up_ref[...] = up

    @pl.when(i == last)
    def _():
        h1 = h1_ref[...]
        out = (h1 + acc_o[...] + row_of(dnb_ref)).astype(BF16)
        for e in range(ex):
            out_ref[e] = out[e * pad : e * pad + seq, :]
        nrm, r = ln_parts(h1)
        dz = acc_d[...]
        gf = g2_s[...].astype(F32)
        g1 = gf + ln_back(dz, nrm, r, row_of(g_ref))
        g1_ref[...] = g1
        n = g1.shape[1] // 128
        for j, v in enumerate((col_sum(gf), col_sum(dz * nrm), col_sum(dz), col_sum(g1))):
            put_rows(vec_ref, j * n, v)
        for j in range(bg_s.shape[0]):
            put_rows(vec_ref, 4 * n + j * (tile // 128), bg_s[j])


def mlp(place, z2, h1, cot, up_w, up_b, down_w, down_b, gain, pad, dp, parted):
    ex, seq, width = cot.shape
    rows = z2.shape[0]
    ff = up_w.shape[1]
    tile = 4 * ff // dp if parted else 384
    steps = ff // tile
    vec_rows = 4 * width // 128 + ff // 128
    if parted:
        dn, up = part_shape(width, ff, dp), part_shape(ff, width, dp)
        per_half = steps // 2
        dn_spec = pl.BlockSpec((1, dn[1], dn[2] // per_half, 128), lambda i: (i // per_half, 0, i % per_half, 0))
        up_spec = pl.BlockSpec((2, 2, up[2], 128), lambda i: (0, i, 0, 0))
        grads = [(dn, dn_spec), (dn, dn_spec), (up, up_spec), (up, up_spec)]
    else:
        grads = [((width, ff), pl.BlockSpec((width, tile), lambda i: (0, i))),
                 ((ff, width), pl.BlockSpec((tile, width), lambda i: (i, 0)))]
    outs = [((ex, seq, width), whole((ex, seq, width)), BF16)] + [(s, b, BF16) for s, b in grads]
    outs += [((rows, width), whole((rows, width)), F32), ((vec_rows, 128), whole((vec_rows, 128)), F32)]
    return pl.pallas_call(
        functools.partial(mlp_kernel, ex, seq, pad, parted),
        grid=(steps,),
        in_specs=[
            SMEM, whole((rows, width)), whole((rows, width)), whole((ex, seq, width)),
            pl.BlockSpec((width, tile), lambda i: (0, i)), whole((ff,)),
            pl.BlockSpec((tile, width), lambda i: (i, 0)),
            whole((width,)), whole((width,)),
        ],
        out_specs=[b for _, b, _ in outs],
        out_shape=[pltpu.HBM(s, d) for s, _, d in outs],
        scratch_shapes=[
            pltpu.VMEM((rows, width), BF16), pltpu.VMEM((width, rows), BF16),
            pltpu.VMEM((rows, width), F32), pltpu.VMEM((rows, width), F32),
            pltpu.VMEM((steps, 1, tile), F32), pltpu.VMEM((steps, 1, tile), F32),
        ],
        compiler_params=pltpu.CompilerParams(dimension_semantics=("arbitrary",), vmem_limit_bytes=44 << 20),
        cost_estimate=pl.CostEstimate(flops=46 * 10**9, bytes_accessed=30 << 20, transcendentals=rows * ff),
        name="mlp_both_ways",
    )(place, *[in_hbm(x) for x in (z2, h1, cot, up_w, up_b, down_w, down_b, gain)])


def stat_rows(channels):
    return max(8, 2 * channels // 128)


def put_stats(ref, first, second):
    lanes = jnp.concatenate([first, second], axis=1)
    n = ref.shape[0]
    for r in range(lanes.shape[1] // 128):
        ref[:, r, :] = jnp.broadcast_to(lanes[:, r * 128 : (r + 1) * 128], (n, 128))


def get_stats(ref, channels):
    total = jnp.sum(ref[...], axis=0)
    rows = 2 * channels // 128
    half = rows // 2
    first = jnp.concatenate([total[r : r + 1, :] for r in range(half)], axis=1)
    second = jnp.concatenate([total[r : r + 1, :] for r in range(half, rows)], axis=1)
    return first, second


def mean_rstd(ref, channels, count):
    s1, s2 = get_stats(ref, channels)
    mean = s1 * (1.0 / count)
    return mean, lax.rsqrt(s2 * (1.0 / count) - mean * mean + eps_batch)


def real_columns(rows, cols):
    return (lax.broadcasted_iota(jnp.int32, (rows, 1), 0) & 15) < cols


def col_sum(x):
    return jnp.sum(x, axis=0, keepdims=True)


def head_mask(rows, second):
    lane = lax.broadcasted_iota(jnp.int32, (rows, 2 * HD), 1)
    return (lane >= HD) if second else (lane < HD)


def attn_fwd_kernel(ex, n_image, pad, pre_ref, len_ref, h0_ref, g_ref, s_ref, wq_ref, wk_ref, wv_ref, qb_ref, vb_ref,
                    ow_ref, ob_ref, g2_ref, s2_ref,
                    z1_ref, q_ref, k_ref, v_ref, p_ref, attn_ref, h1_ref, z2_ref, acc, qb_s, vb_s):
    i = pl.program_id(0)
    last = pl.num_programs(0) - 1
    wide = wq_ref.shape[1]

    @pl.when(i == 0)
    def _():
        nrm, _r = ln_parts(h0_ref[...].astype(F32))
        z1_ref[...] = (nrm * row_of(g_ref) + row_of(s_ref)).astype(BF16)
        acc[...] = jnp.zeros_like(acc)
        qb, vb = row_of(qb_ref), row_of(vb_ref)
        for j in range(qb_s.shape[0]):
            qb_s[j] = qb[:, j * wide : (j + 1) * wide]
            vb_s[j] = vb[:, j * wide : (j + 1) * wide]

    z1 = z1_ref[...]
    q_ref[...] = (nn(z1, wq_ref[...]) + qb_s[i]).astype(BF16)
    k_ref[...] = nn(z1, wk_ref[...]).astype(BF16)
    v_ref[...] = (nn(z1, wv_ref[...]) + vb_s[i]).astype(BF16)
    zero = jnp.zeros((pad, 2 * HD), BF16)
    first = head_mask(pad, False)

    def example(e, carry):
        row0 = pl.multiple_of(e * pad, 16)
        key = lax.broadcasted_iota(jnp.int32, (pad, pad), 1)
        qry = lax.broadcasted_iota(jnp.int32, (pad, pad), 0)
        limit = jnp.maximum(qry + 1, n_image + pre_ref[e])
        limit = jnp.minimum(limit, n_image + len_ref[e])
        vis = key < limit
        for pair in range(wide // (2 * HD)):
            cols = slice(pair * 2 * HD, (pair + 1) * 2 * HD)
            q2 = q_ref[pl.ds(row0, pad), cols] * jnp.asarray(0.125, BF16)
            k2 = k_ref[pl.ds(row0, pad), cols]
            v2 = v_ref[pl.ds(row0, pad), cols]
            out = None
            for h in range(2):
                sel = first if h == 0 else jnp.logical_not(first)
                sc = nt(jnp.where(sel, q2, zero), k2)
                sc = jnp.where(vis, sc, masked_value)
                top = jnp.max(sc, axis=-1, keepdims=True)
                ex_ = jnp.exp(sc - top)
                tot = jnp.sum(ex_, axis=-1, keepdims=True)
                p = (ex_ * (1.0 / tot)).astype(BF16)
                p_ref[e, pair * 2 + h] = p
                o = nn(p, jnp.where(sel, v2, zero))
                out = o if out is None else out + o
            attn_ref[pl.ds(row0, pad), cols] = out.astype(BF16)
        return carry

    lax.fori_loop(0, ex, example, 0)
    acc[...] += nn(attn_ref[...], ow_ref[...])

    @pl.when(i == last)
    def _():
        h1 = h0_ref[...].astype(F32) + acc[...] + row_of(ob_ref)
        h1_ref[...] = h1
        nrm, _r = ln_parts(h1)
        z2_ref[...] = (nrm * row_of(g2_ref) + row_of(s2_ref)).astype(BF16)


def attn_fwd(h0, prefix, text_len, ln1_gain, ln1_shift, qkv_w, qb, vb, out_w, out_b, ln2_gain, ln2_shift, ex, n_image, pad, wide=256):
    rows, width = h0.shape
    groups = width // wide
    heads = width // HD
    hg = wide // HD
    cols = lambda off: pl.BlockSpec((width, wide), lambda i, *_: (0, i + off * groups))
    vec = whole((width,))
    part = pl.BlockSpec((rows, wide), lambda i, *_: (0, i))
    return pl.pallas_call(
        functools.partial(attn_fwd_kernel, ex, n_image, pad),
        grid_spec=pltpu.PrefetchScalarGridSpec(
            num_scalar_prefetch=2,
            grid=(groups,),
            in_specs=[whole((rows, width)), vec, vec, cols(0), cols(1), cols(2), vec, vec,
                      pl.BlockSpec((wide, width), lambda i, *_: (i, 0)), vec, vec, vec],
            out_specs=[whole((rows, width)), part, part, part,
                       pl.BlockSpec((ex, hg, pad, pad), lambda i, *_: (0, i, 0, 0)),
                       part, whole((rows, width)), whole((rows, width))],
            scratch_shapes=[pltpu.VMEM((rows, width), F32)] + [pltpu.VMEM((groups, 1, wide), F32)] * 2,
        ),
        out_shape=[pltpu.HBM((rows, width), BF16)] * 4 + [
            pltpu.HBM((ex, heads, pad, pad), BF16),
            pltpu.HBM((rows, width), BF16),
            pltpu.HBM((rows, width), F32),
            pltpu.HBM((rows, width), BF16)],
        compiler_params=pltpu.CompilerParams(dimension_semantics=("arbitrary",), vmem_limit_bytes=40 << 20),
        cost_estimate=pl.CostEstimate(flops=32 * 10**9, bytes_accessed=30 << 20, transcendentals=heads * rows * pad),
        name="attention_forward",
    )(prefix, text_len, *[in_hbm(x) for x in (h0, ln1_gain, ln1_shift, qkv_w, qkv_w, qkv_w, qb, vb, out_w, out_b, ln2_gain, ln2_shift)])


def attn_bwd_kernel(ex, n_image, txt, cols_real, pad, parted, lo, final, place_ref, g1_ref, ow_ref, attn_ref, q_ref, k_ref, v_ref, p_ref, z1_ref, wq_ref, wk_ref, wv_ref, *refs):
    if lo:
        acc_c, ow_c, qkv_c, bias_c = refs[:4]
        refs = refs[4:]
    if not final:
        acc, ow_s, qkv_s, bias_s = refs[:4]
        g1b_s, g1t_s, dat_s, dq_s, dk_s, dv_s = refs[4:]
    else:
        h0_ref, g_ref, refs = refs[0], refs[1], refs[2:]
        if parted:
            stem_ref, ak_ref, as_ref, text_ref, dtok_ref, vec_ref, ow_s, qkv_s, proj_s = refs[:9]
        else:
            ow_s, qkv_s, text_ref, dtok_ref, vec_ref = refs[:5]
        g1b_s, g1t_s, dat_s, dq_s, dk_s, dv_s, acc, bias_s = refs[-8:]
    i = pl.program_id(0)
    last = pl.num_programs(0) - 1
    wide = wq_ref.shape[1]

    @pl.when(i == 0)
    def _():
        g1b_s[...] = g1_ref[...].astype(BF16)
        g1t_s[...] = g1b_s[...].T
        if lo:
            acc[...] = acc_c[...]
            ow_s[0:lo] = ow_c[...]
            bias_s[:, 0:lo] = bias_c[...]
            for j in range(3):
                qkv_s[j * z1_ref.shape[1] : j * z1_ref.shape[1] + lo * wide, :] = qkv_c[j]
        else:
            acc[...] = jnp.zeros_like(acc)

    gi = i + lo
    ow_s[gi] = nn(g1t_s[...], attn_ref[...]).astype(BF16)
    dat_s[...] = nt(g1b_s[...], ow_ref[...]).astype(BF16)
    zero = jnp.zeros((pad, 2 * HD), BF16)
    first = head_mask(pad, False)

    def example(e, carry):
        row0 = pl.multiple_of(e * pad, 16)
        for pair in range(wide // (2 * HD)):
            cols = slice(pair * 2 * HD, (pair + 1) * 2 * HD)
            q2 = q_ref[pl.ds(row0, pad), cols]
            k2 = k_ref[pl.ds(row0, pad), cols]
            v2 = v_ref[pl.ds(row0, pad), cols]
            da2 = dat_s[pl.ds(row0, pad), cols]
            dq = dk = dv = None
            for h in range(2):
                sel = first if h == 0 else jnp.logical_not(first)
                pb = p_ref[e, pair * 2 + h]
                p = pb.astype(F32)
                dah = jnp.where(sel, da2, zero)
                dp = nt(dah, v2)
                inner = jnp.sum(p * dp, axis=-1, keepdims=True)
                ds = (p * (dp - inner)).astype(BF16)
                dvh = tn(pb, dah)
                dqh = nn(ds, jnp.where(sel, k2, zero))
                dkh = tn(ds, jnp.where(sel, q2, zero))
                dq = dqh if dq is None else dq + dqh
                dk = dkh if dk is None else dk + dkh
                dv = dvh if dv is None else dv + dvh
            dq_s[pl.ds(row0, pad), cols] = (dq * 0.125).astype(BF16)
            dk_s[pl.ds(row0, pad), cols] = (dk * 0.125).astype(BF16)
            dv_s[pl.ds(row0, pad), cols] = dv.astype(BF16)
        return carry

    lax.fori_loop(0, ex, example, 0)
    z1 = z1_ref[...]
    dq, dk, dv = dq_s[...], dk_s[...], dv_s[...]
    width = z1.shape[1]
    for j, d in enumerate((dq, dk, dv)):
        if final:
            qkv_s[pl.ds(pl.multiple_of(j * width + gi * wide, wide), wide), :] = tn(d, z1).astype(BF16)
        else:
            qkv_s[j] = tn(d, z1).astype(BF16)
    acc[...] += nt(dq, wq_ref[...]) + nt(dk, wk_ref[...]) + nt(dv, wv_ref[...])
    bias_s[0, gi] = col_sum(dq.astype(F32))
    bias_s[1, gi] = col_sum(dv.astype(F32))

    if not final:
        return

    @pl.when(i == last)
    def _():
        nrm, r = ln_parts(h0_ref[...].astype(F32))
        dz = acc[...]
        g0 = g1_ref[...] + ln_back(dz, nrm, r, row_of(g_ref))
        n = width // 128
        vec_ref[5 * n :, :] = jnp.zeros_like(vec_ref[5 * n :, :])
        put_rows(vec_ref, n, col_sum(dz * nrm))
        put_rows(vec_ref, 2 * n, col_sum(dz))
        for j in range(2):
            for t in range(bias_s.shape[1]):
                put_rows(vec_ref, (3 + j) * n + t * (wide // 128), bias_s[j, t])
        gb = g0.astype(BF16)
        px = dtok_ref.shape[0] // ex
        pick_image = image_pick(px, pad, n_image, cols_real)
        tr = lax.broadcasted_iota(jnp.int32, (txt, pad), 0)
        tc = lax.broadcasted_iota(jnp.int32, (txt, pad), 1)
        pick_text = jnp.where(tc == tr + n_image, 1.0, 0.0).astype(BF16)
        tot = jnp.zeros((1, gb.shape[1]), F32)
        for e in range(ex):
            ge = gb[e * pad : (e + 1) * pad, :]
            text_ref[e] = nn(pick_text, ge).astype(BF16)
            dt = nn(pick_image, ge)
            dtok_ref[e * px : (e + 1) * px, :] = dt.astype(BF16)
            tot = tot + jnp.sum(dt, axis=0, keepdims=True)
        put_rows(vec_ref, 0, tot)
        if parted:
            core = place_ref[1]
            part_it(qkv_s, ak_ref, as_ref, core)
            proj_s[...] = tn(dtok_ref[...], stem_ref[...]).astype(BF16)
            part_it(proj_s, ak_ref, as_ref, core, at=(qkv_s.shape[0] + width) // (2 * ak_ref.shape[1]) * (width // 256))
            hi = ak_ref.shape[1]
            r = width // (2 * hi)
            at = qkv_s.shape[0] // (2 * hi) * (width // 256)
            for h in range(hi):
                mine = pl.ds(pl.multiple_of((2 * h + core) * r, 16), r)
                other = pl.ds(pl.multiple_of((2 * h + 1 - core) * r, 16), r)
                for blk in range(width // 128):
                    s, j = divmod(blk, width // 256)
                    t, lane = divmod(blk * 128, wide)
                    dst = slice(at + j * r, at + (j + 1) * r)
                    ak_ref[s, h, dst, :] = ow_s[t, mine, lane : lane + 128]
                    as_ref[s, h, dst, :] = ow_s[t, other, lane : lane + 128]


def image_pick(px, pad, n_image, cols_real):
    p = lax.broadcasted_iota(jnp.int32, (px, pad), 0)
    t = lax.broadcasted_iota(jnp.int32, (px, pad), 1)
    col = p & 15
    tok = (p >> 4) * cols_real + col
    return jnp.where((col < cols_real) & (tok == t) & (t < n_image), 1.0, 0.0).astype(BF16)


def attn_bwd(place, g1, out_w, attn, q, k, v, p, z1, h0, qkv_w, ln1_gain, ex, n_image, txt, img_rows, img_cols, pad, dp, parted,
             lo=0, hi=None, carry=(), stem=None, wide=256):
    rows, width = h0.shape
    groups = width // wide
    heads = width // HD
    hg = wide // HD
    px = img_rows * 16
    hi = groups if hi is None else hi
    final = hi == groups
    vec_rows = -(-5 * width // 128 // 8) * 8
    cols = lambda off: pl.BlockSpec((width, wide), lambda i: (0, i + lo + off * groups))
    part = pl.BlockSpec((rows, wide), lambda i: (0, i + lo))
    nat_o, nat_q = (groups, width, wide), (3 * width, width)
    sent = part_shape(4 * width, width, dp)
    if stem is not None:
        sent = sent[:2] + (sent[2] + part_shape(width, stem.shape[1], dp)[2], 128)
    scratch = [pltpu.VMEM((rows, width), BF16), pltpu.VMEM((width, rows), BF16)] + [pltpu.VMEM((rows, wide), BF16)] * 4
    args = [g1, out_w, attn, q, k, v, p, z1, qkv_w, qkv_w, qkv_w, *carry]
    in_specs = [SMEM, whole((rows, width)), pl.BlockSpec((wide, width), lambda i: (i + lo, 0)), part, part, part, part,
                pl.BlockSpec((ex, hg, pad, pad), lambda i: (0, i + lo, 0, 0)), whole((rows, width)), cols(0), cols(1), cols(2)]
    in_specs += [whole(c.shape) for c in carry]
    if final:
        outs = [(s, BF16) for s in ((sent, sent) if parted else (nat_o, nat_q))]
        outs += [((ex, txt, width), BF16), ((ex * px, width), BF16), ((vec_rows, 128), F32)]
        natural = [pltpu.VMEM(nat_o, BF16), pltpu.VMEM(nat_q, BF16), pltpu.VMEM((width, stem.shape[1]), BF16)] if parted else []
        scratch = natural + scratch + [pltpu.VMEM((rows, width), F32), pltpu.VMEM((2, groups, 1, wide), F32)]
        args += [h0, ln1_gain] + ([stem] if parted else [])
        in_specs += [whole((rows, width)), whole((width,))] + ([whole(stem.shape)] if parted else [])
    else:
        n = hi - lo
        outs = [((rows, width), F32), ((n, width, wide), BF16), ((3, n * wide, width), BF16), ((2, n, 1, wide), F32)]
    return pl.pallas_call(
        functools.partial(attn_bwd_kernel, ex, n_image, txt, img_cols, pad, parted, lo, final),
        grid=(hi - lo,),
        in_specs=in_specs,
        out_specs=[whole(s) for s, _ in outs],
        out_shape=[pltpu.HBM(s, d) for s, d in outs],
        scratch_shapes=scratch,
        compiler_params=pltpu.CompilerParams(dimension_semantics=("arbitrary",), vmem_limit_bytes=60 << 20),
        cost_estimate=pl.CostEstimate(flops=14 * (hi - lo) * 10**9, bytes_accessed=40 << 20, transcendentals=0),
        name="attention_backward",
    )(place, *[in_hbm(x) for x in args])

def stats_kernel(cols, x_ref, w_ref, parts_ref, xp):
    xp[...] = jnp.zeros_like(xp)
    shape = x_ref.shape
    xp[:, 0:cols, :] = x_ref[...].reshape(shape[0] * shape[1], cols, shape[3])
    a = nn(xp[...].reshape(shape[0] * shape[1] * 16, shape[3]), w_ref[...])
    put_stats(parts_ref, col_sum(a), col_sum(a * a))


def conv_fwd_kernel(count, ex, rows, cols, place_ref, parts_ref, own_ref, got_ref, win_ref, g_ref, s_ref, wmid_ref,
                    xs_ref, act1_ref, wide_ref, act2_ref, parts2_ref):
    s = place_ref[0]
    half = rows // 2
    px = rows * 16
    chan = xs_ref.shape[-1]
    xs_ref[...] = jnp.zeros_like(xs_ref)
    for e in range(ex):
        xs_ref[e, pl.ds(s * half, half), 0:cols, :] = own_ref[s * ex + e]
        xs_ref[e, pl.ds((1 - s) * half, half), 0:cols, :] = got_ref[e]
    a1 = nn(xs_ref[...].reshape(ex * px, chan), win_ref[...])
    act1_ref[...] = a1
    mid = a1.shape[1]
    mean, rstd = mean_rstd(parts_ref, mid, count)
    real = real_columns(ex * px, cols)
    act = gelu_of((a1 - mean) * rstd * row_of(g_ref) + row_of(s_ref))
    act = jnp.where(real, act, 0.0)
    for e in range(ex):
        part = act[e * px : (e + 1) * px]
        wide_ref[e, 0:16, :] = jnp.zeros((16, 3 * mid), BF16)
        wide_ref[e, px + 16 : px + 32, :] = jnp.zeros((16, 3 * mid), BF16)
        wide_ref[e, 16 : px + 16, 0:mid] = pltpu.roll(part, 1, 0).astype(BF16)
        wide_ref[e, 16 : px + 16, mid : 2 * mid] = part.astype(BF16)
        wide_ref[e, 16 : px + 16, 2 * mid : 3 * mid] = pltpu.roll(part, px - 1, 0).astype(BF16)
    one = real_columns(px, cols)
    t1 = jnp.zeros((1, mid), F32)
    t2 = jnp.zeros((1, mid), F32)
    for e in range(ex):
        a2 = nn(wide_ref[e, 0:px, :], wmid_ref[0])
        a2 = a2 + nn(wide_ref[e, 16 : px + 16, :], wmid_ref[1])
        a2 = a2 + nn(wide_ref[e, 32 : px + 32, :], wmid_ref[2])
        a2 = jnp.where(one, a2, 0.0)
        act2_ref[e * px : (e + 1) * px, :] = a2
        t1 = t1 + col_sum(a2)
        t2 = t2 + col_sum(a2 * a2)
    put_stats(parts2_ref, t1, t2)


def expand_kernel(count, cols, parts_ref, act2_ref, g_ref, s_ref, w_ref, relu2_ref, act3_ref, parts3_ref):
    a2 = act2_ref[...]
    mean, rstd = mean_rstd(parts_ref, a2.shape[1], count)
    act = gelu_of((a2 - mean) * rstd * row_of(g_ref) + row_of(s_ref))
    low = jnp.where(real_columns(a2.shape[0], cols), act, 0.0).astype(BF16)
    relu2_ref[...] = low
    a3 = nn(low, w_ref[...])
    act3_ref[...] = a3
    put_stats(parts3_ref, col_sum(a3), col_sum(a3 * a3))


def tokens_kernel(count, ex, cols, n_image, pad, parts_ref, act3_ref, xs_ref, g_ref, s_ref, w_ref, b_ref, text_ref,
                  stem_ref, h0_ref):
    a3 = act3_ref[...]
    mean, rstd = mean_rstd(parts_ref, a3.shape[1], count)
    pre = (a3 - mean) * rstd * row_of(g_ref) + row_of(s_ref) + xs_ref[...].reshape(a3.shape).astype(F32)
    stem = gelu_of(pre).astype(BF16)
    stem_ref[...] = stem
    tok = (nn(stem, w_ref[...]) + row_of(b_ref)).astype(BF16)
    px = a3.shape[0] // ex
    txt = text_ref.shape[1]
    t = lax.broadcasted_iota(jnp.int32, (pad, px), 0)
    p = lax.broadcasted_iota(jnp.int32, (pad, px), 1)
    col = p & 15
    pick = jnp.where((col < cols) & ((p >> 4) * cols + col == t), 1.0, 0.0).astype(BF16)
    tr = lax.broadcasted_iota(jnp.int32, (pad, txt), 0)
    tc = lax.broadcasted_iota(jnp.int32, (pad, txt), 1)
    pick_text = jnp.where(tr == tc + n_image, 1.0, 0.0).astype(BF16)
    for e in range(ex):
        both = nn(pick, tok[e * px : (e + 1) * px, :]) + nn(pick_text, text_ref[e])
        h0_ref[e * pad : (e + 1) * pad, :] = both.astype(BF16)


def dpre_kernel(count, ex, rows, place_ref, parts_ref, act3_ref, xs_ref, g_ref, s_ref, dtok_ref, w_ref, dpre_ref, send_ref, parts4_ref):
    a3 = act3_ref[...]
    mean, rstd = mean_rstd(parts_ref, a3.shape[1], count)
    nrm = (a3 - mean) * rstd
    pre = nrm * row_of(g_ref) + row_of(s_ref) + xs_ref[...].reshape(a3.shape).astype(F32)
    _, slope = gelu_and_slope(pre)
    d = nt(dtok_ref[...], w_ref[...]) * slope
    dpre_ref[...] = d.reshape(dpre_ref.shape)
    put_stats(parts4_ref, col_sum(d), col_sum(d * nrm))
    half = rows // 2
    other = 1 - place_ref[0]
    for e in range(ex):
        send_ref[e] = dpre_ref[e, pl.ds(other * half, half)].astype(BF16)


def back3_kernel(count, cols, parts4_ref, parts3_ref, parts2_ref, act3_ref, dpre_ref, g3_ref, w_ref, act2_ref, g2_ref, s2_ref, veca_ref, vecb_ref,
                 low3_ref, t2_ref, parts5_ref, gain_ref, shift_ref, small_s):
    a3 = act3_ref[...]
    chan = a3.shape[1]
    mean, rstd = mean_rstd(parts3_ref, chan, count)
    s1, s2 = get_stats(parts4_ref, chan)
    gain_ref[...] = s2.reshape(-1)
    shift_ref[...] = s1.reshape(-1)
    nrm = (a3 - mean) * rstd
    d = (row_of(g3_ref) * rstd) * (dpre_ref[...].reshape(a3.shape) - s1 * (1.0 / count) - nrm * (s2 * (1.0 / count)))
    low = jnp.where(real_columns(a3.shape[0], cols), d, 0.0).astype(BF16)
    low3_ref[...] = low
    a2 = act2_ref[...]
    mean2, rstd2 = mean_rstd(parts2_ref, a2.shape[1], count)
    nrm2 = (a2 - mean2) * rstd2
    _, slope = gelu_and_slope(nrm2 * row_of(g2_ref) + row_of(s2_ref))
    t2 = nt(low, w_ref[...]) * slope
    t2_ref[...] = t2
    parts5_ref[...] = jnp.zeros_like(parts5_ref)
    put_stats(parts5_ref, col_sum(t2), col_sum(t2 * nrm2))
    used = veca_ref.shape[0] + vecb_ref.shape[0]
    n = parts5_ref.shape[0]
    each = -(-used // n)
    small_s[0 : veca_ref.shape[0], :] = veca_ref[...]
    small_s[veca_ref.shape[0] : used, :] = vecb_ref[...]
    if used < small_s.shape[0]:
        small_s[used:, :] = jnp.zeros_like(small_s[used:, :])
    for d in range(n):
        parts5_ref[d, 4 : 4 + each, :] = small_s[d * each : (d + 1) * each, :]


def back2_kernel(count, ex, rows, cols, place_ref, parts5_ref, parts2_ref, parts1_ref, act2_ref, t2_ref, g2_ref, wmid_ref, act1_ref, g1_ref, s1_ref,
                 low2_ref, t1_ref, send_ref, parts6_ref, gain_ref, shift_ref, wide):
    a2 = act2_ref[...]
    mid = a2.shape[1]
    px = rows * 16
    mean, rstd = mean_rstd(parts2_ref, mid, count)
    s1, s2 = get_stats(parts5_ref, mid)
    gain_ref[...] = s2.reshape(-1)
    shift_ref[...] = s1.reshape(-1)
    nrm = (a2 - mean) * rstd
    d = (row_of(g2_ref) * rstd) * (t2_ref[...] - s1 * (1.0 / count) - nrm * (s2 * (1.0 / count)))
    d = jnp.where(real_columns(ex * px, cols), d, 0.0)
    low2_ref[...] = d.astype(BF16)
    for e in range(ex):
        part = d[e * px : (e + 1) * px]
        wide[e, 0:16, :] = jnp.zeros((16, 3 * mid), BF16)
        wide[e, px + 16 : px + 32, :] = jnp.zeros((16, 3 * mid), BF16)
        wide[e, 16 : px + 16, 0:mid] = pltpu.roll(part, px - 1, 0).astype(BF16)
        wide[e, 16 : px + 16, mid : 2 * mid] = part.astype(BF16)
        wide[e, 16 : px + 16, 2 * mid : 3 * mid] = pltpu.roll(part, 1, 0).astype(BF16)
    mean1, rstd1 = mean_rstd(parts1_ref, mid, count)
    one = real_columns(px, cols)
    q1 = jnp.zeros((1, mid), F32)
    q2 = jnp.zeros((1, mid), F32)
    for e in range(ex):
        t = None
        for r in range(3):
            for c in range(3):
                term = nt(wide[e, (2 - r) * 16 : (2 - r) * 16 + px, c * mid : (c + 1) * mid], wmid_ref[r, c * mid : (c + 1) * mid, :])
                t = term if t is None else t + term
        nrm1 = (act1_ref[e * px : (e + 1) * px, :] - mean1) * rstd1
        _, slope = gelu_and_slope(nrm1 * row_of(g1_ref) + row_of(s1_ref))
        t = jnp.where(one, t * slope, 0.0)
        t1_ref[e] = t.reshape(rows, 16, mid)
        q1 = q1 + col_sum(t)
        q2 = q2 + col_sum(t * nrm1)
    put_stats(parts6_ref, q1, q2)
    chunk = jnp.sum(parts5_ref[:, 4:8, :], axis=0)
    parts6_ref[:, 4:8, :] = jnp.broadcast_to(chunk[None], (parts6_ref.shape[0], 4, 128))
    half = rows // 2
    other = 1 - place_ref[0]
    for e in range(ex):
        send_ref[e] = t1_ref[e, pl.ds(other * half, half)].astype(BF16)


def conv_grads_kernel(ex, px, parted, place_ref, low2_ref, wide_ref, low3_ref, relu2_ref, *refs):
    mid = low2_ref.shape[1]
    nat_m, nat_o = (refs[2], refs[3]) if parted else (refs[0], refs[1])
    nat_o[...] = tn(low3_ref[...], relu2_ref[...]).astype(BF16)
    for r in range(3):
        tot = None
        for e in range(ex):
            term = tn(low2_ref[e * px : (e + 1) * px, :], wide_ref[e, r * 16 : r * 16 + px, :])
            tot = term if tot is None else tot + term
        for c in range(3):
            for h in range(2):
                at = (h * 9 + r * 3 + c) * (mid // 2)
                src = c * mid + h * (mid // 2)
                nat_m[:, at : at + mid // 2] = tot[:, src : src + mid // 2].astype(BF16)
    if parted:
        part_it(nat_m, refs[0], refs[1], place_ref[1])
        part_it(nat_o, refs[0], refs[1], place_ref[1], at=nat_m.shape[0] // (2 * refs[0].shape[1]) * (nat_m.shape[1] // 256))


def tn_kernel(parted, place_ref, a_ref, b_ref, *refs):
    natural = refs[2] if parted else refs[0]
    natural[...] = tn(a_ref[...], b_ref[...]).astype(BF16)
    if parted:
        part_it(natural, refs[0], refs[1], place_ref[1])


def image_kernel(count, ex, rows, cols, parted, each, places, place_ref, parts6_ref, parts1_ref, x_ref, win_ref, g_ref, t1_ref, gott_ref, dpre_ref, gotd_ref,
                 grad_ref, *refs):
    if parted:
        keep_ref, send_ref, win_grad_ref = refs[0], refs[1], refs[-1]
        refs = refs[2:-1]
    else:
        win_grad_ref, refs = refs[0], refs[1:]
    gain_ref, shift_ref, vec_refs, xp, small_s = refs[0], refs[1], refs[2:-2], refs[-2], refs[-1]
    s = place_ref[0]
    half = rows // 2
    chan = x_ref.shape[-1]
    mid = win_ref.shape[1]
    mean, rstd = mean_rstd(parts1_ref, mid, count)
    s1, s2 = get_stats(parts6_ref, mid)
    gain_ref[...] = s2.reshape(-1)
    shift_ref[...] = s1.reshape(-1)
    real = real_columns(ex * half * 16, cols)
    size = ex * half * 16
    xp[...] = jnp.zeros_like(xp)
    wg = None
    for own in (True, False):
        at = (s if own else 1 - s) * ex
        xp[:, 0:cols, :] = x_ref[pl.ds(at, ex)].reshape(ex * half, cols, chan)
        x = xp[...].reshape(size, chan)
        nrm = (nn(x, win_ref[...]) - mean) * rstd
        if own:
            t = t1_ref[:, pl.ds(s * half, half)].reshape(size, mid)
            dp = dpre_ref[:, pl.ds(s * half, half)].reshape(size, chan)
        else:
            t = gott_ref[...].reshape(size, mid).astype(F32)
            dp = gotd_ref[...].reshape(size, chan).astype(F32)
        d = (row_of(g_ref) * rstd) * (t - s1 * (1.0 / count) - nrm * (s2 * (1.0 / count)))
        low = jnp.where(real, d, 0.0).astype(BF16)
        grad = (nt(low, win_ref[...]) + dp).astype(BF16).reshape(ex, half, 16, chan)
        grad_ref[pl.ds(at, ex)] = grad[:, :, 0:cols, :]
        term = tn(low, x)
        wg = term if wg is None else wg + term
    win_grad_ref[...] = wg.astype(BF16)
    if parted:
        part_it(win_grad_ref, keep_ref, send_ref, place_ref[1])
    for d in range(parts6_ref.shape[0]):
        small_s[d * each : (d + 1) * each, :] = parts6_ref[d, 4 : 4 + each, :]
    for ref, at in zip(vec_refs, places):
        ref[...] = take_rows(small_s, at, ref.shape[0]).reshape(-1)


def in_hbm(x):
    return pltpu.with_memory_space_constraint(x, pltpu.HBM)


def call(kernel, outs, *args, moved=(), place=None, scratch=(), name=None, us=2, limit=40):
    nbytes = sum(a.size * a.dtype.itemsize for a in args)
    spec = lambda s: pl.BlockSpec(s, lambda i: (0,) * len(s))
    return pl.pallas_call(
        kernel,
        grid=(1,),
        out_shape=[pltpu.HBM(s, d) for s, d in outs],
        in_specs=([SMEM] if place is not None else []) + [spec(a.shape) for a in args],
        out_specs=[spec(s) for s, _ in outs],
        scratch_shapes=list(scratch),
        compiler_params=pltpu.CompilerParams(vmem_limit_bytes=limit << 20),
        cost_estimate=pl.CostEstimate(flops=us * 10**9, bytes_accessed=nbytes if us else 0, transcendentals=0),
        name=name,
    )(*([place] if place is not None else []), *[a if any(a is b for b in moved) else in_hbm(a) for a in args])


DP = ("far", "near", "core")
AXES = DP + ("space",)


def spread(parts):
    return lax.all_to_all(parts, AXES, split_axis=0, concat_axis=0, tiled=True)


def swap(x, axis="space"):
    return lax.ppermute(x, axis, [(0, 1), (1, 0)])


def tie(*values):
    return lax.optimization_barrier(values)


BITS = ("space", "f1", "f0", "near")


def bit_of(name):
    if name in ("f0", "f1"):
        return (lax.axis_index("far") // (1 if name == "f0" else 2)) % 2
    return lax.axis_index(name)


def sent(x, key):
    if key == ("core",):
        return swap(x, "core")
    flip = {n: int(n in key) for n in BITS}
    far, near, space = 2 * flip["f1"] + flip["f0"], flip["near"], flip["space"]
    if far and (near or space):
        raise ValueError
    if far:
        return lax.ppermute(x, "far", [(j, j ^ far) for j in range(4)])
    if near and space:
        return lax.ppermute(x, ("near", "space"), [(j, 3 - j) for j in range(4)])
    return swap(x, "near" if near else "space")


class Box:
    def __init__(self, value, moved=False):
        self.value, self.moved = value, moved


class Pack:
    def __init__(self, sources, left, size, at=0, rows=None):
        self.sources, self.left, self.size, self.at, self.rows = sources, left, size, at, size if rows is None else rows

    @classmethod
    def start(cls, keep, send):
        size = keep.shape[-2]
        got = sent(send, ("core",))
        return cls([(Box(keep.reshape(-1, 128)), 0), (Box(got.reshape(-1, 128), True), 0)], list(BITS), size)

    def thirds(self):
        r = self.size // 3
        return [Pack(self.sources, self.left, self.size, k * r, r) for k in range(3)]


def arrive(value, *packs):
    boxes = []
    for x in packs:
        boxes += [b for b, _ in x.sources if b.moved and b not in boxes]
    flat = tie(value, *[b.value for b in boxes])
    for b, v in zip(boxes, flat[1:]):
        b.value = v
    return flat[0]


def combine_kernel(plan, n_in, bits_ref, *refs):
    ins, outs = refs[:n_in], refs[n_in:]
    for sources, left, size, at, rows, names, dests in plan:
        rest = [d for d in left if d not in names]
        for rel, (out, to) in enumerate(dests):
            for c in range(2 ** len(rest)):
                place = 0
                for pos, d in enumerate(left):
                    stride = 2 ** (len(left) - 1 - pos)
                    if d in names:
                        bit = bits_ref[BITS.index(d)]
                        if (rel >> (len(names) - 1 - names.index(d))) & 1:
                            bit = 1 - bit
                    else:
                        bit = (c >> (len(rest) - 1 - rest.index(d))) & 1
                    place = place + bit * stride
                tot = None
                for idx, first in sources:
                    x = ins[idx][pl.ds(pl.multiple_of(first + place * size + at, 16), rows), :].astype(F32)
                    tot = x if tot is None else tot + x
                outs[out][to + c * rows : to + (c + 1) * rows, :] = tot.astype(BF16)


def step(bits, moves, tied):
    boxes, plan, keys, totals, after = [], [], [], {(): 0}, []
    for pack, names in moves:
        srcs = []
        for box, first in pack.sources:
            if box not in boxes:
                boxes.append(box)
            srcs.append((boxes.index(box), first))
        rest = [d for d in pack.left if d not in names]
        n = 2 ** len(rest) * pack.rows
        dests = []
        for rel in range(2 ** len(names)):
            key = tuple(d for j, d in enumerate(names) if (rel >> (len(names) - 1 - j)) & 1)
            key = tuple(sorted(key))
            if key not in totals:
                totals[key] = 0
            if key not in keys:
                keys.append(key)
            dests.append((key, totals[key]))
            totals[key] += n
        plan.append((srcs, list(pack.left), pack.size, pack.at, pack.rows, names, dests))
        after.append((rest, pack.rows, dests))
    plan = [(*p[:-1], [(keys.index(k), to) for k, to in p[-1]]) for p in plan]
    args = [b.value if b.moved else in_hbm(b.value) for b in boxes]
    one = lambda shape: pl.BlockSpec(shape, lambda t: (0, 0), pipeline_mode=pl.Buffered(1))
    res = pl.pallas_call(
        functools.partial(combine_kernel, plan, len(args)),
        grid=(1,),
        in_specs=[SMEM] + [one(x.shape) for x in args],
        out_specs=[one((totals[k], 128)) for k in keys],
        out_shape=[pltpu.HBM((totals[k], 128), BF16) for k in keys],
        compiler_params=pltpu.CompilerParams(vmem_limit_bytes=40 << 20),
        cost_estimate=pl.CostEstimate(flops=0, bytes_accessed=0, transcendentals=0),
        name="combine",
    )(bits, *args)
    flat = tie(tied, *res)
    arrays = {k: Box(flat[1 + j] if k == () else sent(flat[1 + j], k), k != ()) for j, k in enumerate(keys)}
    packs = [Pack([(arrays[k], to) for k, to in dests], rest, rows) for rest, rows, dests in after]
    return flat[0], packs


def finish_kernel(plan, n_in, *refs):
    ins, outs = refs[:n_in], refs[n_in:]
    for sources, pieces in plan:
        for first, r, blocks, out in pieces:
            for b in range(blocks):
                tot = None
                for idx, at in sources:
                    lo = at + first + b * r
                    if len(ins[idx].shape) == 3:
                        x = jnp.sum(ins[idx][:, lo : lo + r, :].astype(F32), axis=0)
                    else:
                        x = ins[idx][lo : lo + r, :].astype(F32)
                    tot = x if tot is None else tot + x
                if len(outs[out].shape) == 3:
                    outs[out][b] = tot
                else:
                    outs[out][:, b * 128 : (b + 1) * 128] = tot


def finish(groups, shapes, name):
    boxes, plan = [], []
    for sources, pieces in groups:
        srcs = []
        for box, first in sources:
            if box not in boxes:
                boxes.append(box)
            srcs.append((boxes.index(box), first))
        plan.append((srcs, pieces))
    args = [b.value for b in boxes]
    return call(functools.partial(finish_kernel, plan, len(args)), [(s, F32) for s in shapes], *args, moved=args, name=name)


def halve_dp(x, axis, bit):
    size = lax.axis_size(DP)
    mine = (lax.axis_index(DP) // bit) % 2
    keep = lax.dynamic_index_in_dim(x, mine, axis, keepdims=True)
    send = lax.dynamic_index_in_dim(x, 1 - mine, axis, keepdims=True)
    return keep + lax.ppermute(send, DP, [(j, j ^ bit) for j in range(size)])


def scattered(grad_t):
    size = lax.axis_size(DP)
    bits = size.bit_length() - 1
    cols, rows = grad_t.shape
    x = grad_t.reshape((2,) * bits + (cols // size, rows))
    for b in range(bits):
        x = halve_dp(x, bits - 1 - b, 1 << b)
    half = rows // 2
    mine = lax.axis_index("space")
    keep = lax.dynamic_slice_in_dim(x, mine * half, half, axis=x.ndim - 1)
    send = lax.dynamic_slice_in_dim(x, (1 - mine) * half, half, axis=x.ndim - 1)
    return (keep + swap(send)).reshape(cols // size, half).astype(F32).T


def shards(
    image_in, text_in, prefix, text_len, cotangent,
    conv_in_w, bn1_gain, bn1_shift, conv_mid_w, bn2_gain, bn2_shift, conv_out_w, bn3_gain, bn3_shift,
    proj_w, proj_b, ln1_gain, ln1_shift, qkv_w, query_bias, value_bias, out_w, out_b,
    ln2_gain, ln2_shift, up_w, up_b, down_w, down_b,
):
    n_dev, dp = lax.axis_size(AXES), lax.axis_size(DP)
    band_ex, band_rows, cols, chan = image_in.shape
    mid = conv_in_w.shape[1]
    width = proj_w.shape[1]
    ff = up_w.shape[1]
    ex, txt, _ = text_in.shape
    rows = band_rows * lax.axis_size("space")
    n_image = rows * cols
    seq = n_image + txt
    pad = -(-seq // 16) * 16
    px = rows * 16
    count = float(band_ex * band_rows * cols * n_dev)
    me = lax.axis_index("space").astype(jnp.int32)
    place = jnp.stack([me, lax.axis_index("core").astype(jnp.int32)])
    small, large = (n_dev, stat_rows(mid), 128), (n_dev, stat_rows(chan), 128)
    wmid = conv_mid_w.reshape(3, 3 * mid, mid)
    weights = [(mid, chan), (mid, 9 * mid), (chan, mid), (width, chan), (3 * width, width), (width, width), (ff, width), (width, ff)]
    parted = dp == 16 and mid == 256 and all(c % (16 * dp) == 0 and r % 256 == 0 for c, r in weights)
    hi = dp // 2

    def grad_outs(c, r):
        return [(part_shape(c, r, dp), BF16)] * 2 if parted else [((c, r), BF16)]

    def natural(c, r):
        return [pltpu.VMEM((c, r), BF16)] if parted else []

    got_x = swap(lax.dynamic_slice_in_dim(image_in, (1 - me) * ex, ex, axis=0))
    parts1, = call(functools.partial(stats_kernel, cols), [(small, F32)], image_in, conv_in_w,
                   scratch=[pltpu.VMEM((band_ex * band_rows, 16, chan), BF16)], name="stats_one")
    parts1 = spread(parts1)
    xs, act1, wide, act2, parts2 = call(
        functools.partial(conv_fwd_kernel, count, ex, rows, cols),
        [((ex, rows, 16, chan), BF16), ((ex * px, mid), F32), ((ex, px + 32, 3 * mid), BF16), ((ex * px, mid), F32), (small, F32)],
        parts1, image_in, got_x, conv_in_w, bn1_gain, bn1_shift, wmid, moved=(parts1, got_x), place=place, name="conv_three", us=4)
    parts2 = spread(parts2)
    relu2, act3, parts3 = call(
        functools.partial(expand_kernel, count, cols),
        [((ex * px, mid), BF16), ((ex * px, chan), F32), (large, F32)],
        parts2, act2, bn2_gain, bn2_shift, conv_out_w, moved=(parts2,), name="expand")
    parts3 = spread(parts3)
    stem, h0 = call(
        functools.partial(tokens_kernel, count, ex, cols, n_image, pad),
        [((ex * px, chan), BF16), ((ex * pad, width), BF16)],
        parts3, act3, xs, bn3_gain, bn3_shift, proj_w, proj_b, text_in, moved=(parts3,), name="tokens", us=5)
    z1, q, k, v, p, attn, h1, z2 = attn_fwd(h0, prefix, text_len, ln1_gain, ln1_shift, qkv_w, query_bias, value_bias,
                                            out_w, out_b, ln2_gain, ln2_shift, ex, n_image, pad)
    mlp_outs = mlp(place, z2, h1, cotangent, up_w, up_b, down_w, down_b, ln2_gain, pad, dp, parted)
    block_out, mlp_grads, (g1, veca) = mlp_outs[0], mlp_outs[1:-2], mlp_outs[-2:]
    if parted:
        bits = jnp.stack([bit_of(n) for n in BITS]).astype(jnp.int32)
        down, up = Pack.start(*mlp_grads[:2]), Pack.start(*mlp_grads[2:])
    back_args = (out_w, attn, q, k, v, p, z1, h0, qkv_w, ln1_gain, ex, n_image, txt, rows, cols, pad, dp, parted)
    if parted:
        carry = attn_bwd(place, g1, *back_args, hi=1)
        turns = [["space"], ["near"], ["f0"]]
        ffn = down.thirds() + up.thirds()
        g1, ffn = step(bits, list(zip(ffn, turns + turns)), tie(g1, *carry)[0])
        att_outs = attn_bwd(place, g1, *back_args, lo=1, carry=carry, stem=stem)
    else:
        att_outs = attn_bwd(place, g1, *back_args)
    att_grads, (text_grad, dtok, vecb) = att_outs[:-3], att_outs[-3:]
    if parted:
        later = turns[1:] + turns[:1]
        (dtok, att_send), ffn = step(bits, list(zip(ffn, later * 2)), (dtok, att_grads[1]))
        att = Pack.start(att_grads[0], att_send)
    dpre, dsend, parts4 = call(
        functools.partial(dpre_kernel, count, ex, rows),
        [((ex, rows, 16, chan), F32), ((ex, band_rows, 16, chan), BF16), (large, F32)],
        parts3, act3, xs, bn3_gain, bn3_shift, dtok, proj_w, moved=(parts3,), place=place, name="stem_back", us=7)
    got_d = swap(dsend)
    if parted:
        parts4 = arrive(parts4, *ffn, att)
    parts4 = spread(parts4)
    if parted:
        later = later[1:] + later[:1]
        dpre, moved = step(bits, list(zip(ffn, later * 2)) + list(zip(att.thirds(), later)), dpre)
        ffn, att = moved[:6], moved[6:]
    else:
        proj_g = call(functools.partial(tn_kernel, parted), grad_outs(width, chan), dtok, stem, place=place, name="proj_grad", us=0)
    low3, t2, parts5, bn3_gg, bn3_sg = call(
        functools.partial(back3_kernel, count, cols),
        [((ex * px, chan), BF16), ((ex * px, mid), F32), (small, F32), ((chan,), F32), ((chan,), F32)],
        parts4, parts3, parts2, act3, dpre, bn3_gain, conv_out_w, act2, bn2_gain, bn2_shift, veca, vecb, moved=(parts4, parts3, parts2),
        scratch=[pltpu.VMEM((n_dev * -(-(veca.shape[0] + vecb.shape[0]) // n_dev), 128), F32)], name="back_three", us=4)
    if parted:
        parts5 = arrive(parts5, *att)
    parts5 = spread(parts5)
    if parted:
        later = later[1:] + later[:1]
        t2, moved = step(bits, [(x, ["f1"]) for x in ffn] + list(zip(att, later)), t2)
        ffn, att = moved[:6], moved[6:]
    low2, t1, tsend, parts6, bn2_gg, bn2_sg = call(
        functools.partial(back2_kernel, count, ex, rows, cols),
        [((ex * px, mid), BF16), ((ex, rows, 16, mid), F32), ((ex, band_rows, 16, mid), BF16), (small, F32), ((mid,), F32), ((mid,), F32)],
        parts5, parts2, parts1, act2, t2, bn2_gain, wmid, act1, bn1_gain, bn1_shift,
        moved=(parts5, parts2, parts1), place=place, scratch=[pltpu.VMEM((ex, px + 32, 3 * mid), BF16)], name="back_two", us=4)
    got_t = swap(tsend)
    parts6 = spread(parts6)
    if parted:
        low2 = arrive(low2, *att)
    conv_g = call(
        functools.partial(conv_grads_kernel, ex, px, parted),
        [(part_shape(mid, 9 * mid, dp)[:2] + (part_shape(mid, 9 * mid, dp)[2] + part_shape(chan, mid, dp)[2], 128), BF16)] * 2
        if parted else [((mid, 9 * mid), BF16), ((chan, mid), BF16)],
        low2, wide, low3, relu2, place=place, scratch=natural(mid, 9 * mid) + natural(chan, mid), name="conv_grads", us=0)
    if parted:
        conv = Pack.start(*conv_g)
        later = later[1:] + later[:1]
        t1, moved = step(bits, list(zip(att, later)) + [(conv, ["near", "space"])], t1)
        att, conv = moved[:3], moved[3]
        t1 = arrive(t1, *ffn, *att, conv)
    each = -(-(veca.shape[0] + vecb.shape[0]) // n_dev)
    n, off = width // 128, veca.shape[0]
    places = [off, off + n, off + 2 * n, off + 3 * n, off + 4 * n, 3 * n, n, 2 * n, 4 * n, 0]
    sizes = [width] * 8 + [ff, width]
    last = call(
        functools.partial(image_kernel, count, ex, rows, cols, parted, each, places),
        [(image_in.shape, BF16)] + grad_outs(mid, chan) + [((mid,), F32)] * 2 + [((s,), F32) for s in sizes],
        parts6, parts1, image_in, conv_in_w, bn1_gain, t1, got_t, dpre, got_d,
        moved=(parts6, parts1, got_t, got_d), place=place, scratch=[pltpu.VMEM((ex * band_rows, 16, chan), BF16), pltpu.VMEM((n_dev * each, 128), F32)] + natural(mid, chan),
        name="image_back", us=5)
    image_grad, sums = last[0], last[3 if parted else 2 :]
    bn1_gg, bn1_sg, vecs = sums[0], sums[1], sums[2:]
    if parted:
        in_x = (last[1] + swap(last[2], "core")).reshape((2 * hi,) + last[1].shape[2:])
        in_x = lax.all_to_all(in_x, ("space", "far", "near"), split_axis=0, concat_axis=0, tiled=True)
        image_grad, moved = step(bits, [(x, ["f1"]) for x in att] + [(conv, ["f1", "f0"])], image_grad)
        att, conv = moved[:3], moved[3]
        r_mid, r_out3, r_q, r_w, r_f = mid // dp, chan // dp, 3 * width // dp, width // dp, ff // dp
        mids, half = r_mid * (9 * mid // 256), width // 256
        g_down, g_up = finish(
            [(ffn[0].sources, [(0, r_w, ff // 256, 0)]), (ffn[3].sources, [(0, r_f, half, 1)])],
            [(r_w, ff // 2), (r_f, width // 2)], "finish_early")
        g_qkv, g_out, g_proj, g_mid, g_out3, g_in = finish(
            [(att[0].sources, [(0, r_q, half, 0), (r_q * half, r_w, half, 1), ((r_q + r_w) * half, r_w, chan // 256, 2)]),
             (conv.sources, [(0, r_mid, 9 * mid // 256, 3), (mids, r_out3, mid // 256, 4)]),
             ([(Box(in_x), 0)], [(0, r_mid, chan // 256, 5)])],
            [(r_q, width // 2), (r_w, width // 2), (r_w, chan // 2), (9 * mid // 256, r_mid, 128), (r_out3, mid // 2), (r_mid, chan // 2)], "finish_late")
        g_down, g_up, g_qkv, g_out, g_proj, g_out3, g_in = [g.T for g in (g_down, g_up, g_qkv, g_out, g_proj, g_out3, g_in)]
        g_mid = g_mid.reshape(3, 3, r_mid, mid // 2).transpose(0, 1, 3, 2)
    else:
        out_n = att_outs[0].transpose(1, 0, 2).reshape(width, width)
        g_in, g_mid, g_out3, g_proj, g_qkv, g_out, g_up, g_down = [
            scattered(x) for x in (last[1], conv_g[0], conv_g[1], proj_g[0], att_outs[1], out_n, mlp_grads[1], mlp_grads[0])]
        g_mid = g_mid.reshape(3, 3, mid // 2, -1)
    return (
        block_out, image_grad, text_grad,
        g_in, bn1_gg, bn1_sg,
        g_mid, bn2_gg, bn2_sg,
        g_out3, bn3_gg, bn3_sg,
        g_proj, vecs[0], vecs[1], vecs[2],
        g_qkv, vecs[3], vecs[4],
        g_out, vecs[5], vecs[6], vecs[7],
        g_up, vecs[8],
        g_down, vecs[9],
    )


def solution(mesh):
    dp, space = mesh.devices.shape
    fine = Mesh(mesh.devices.reshape(dp // 4, 2, 2, space), AXES)
    return jax.shard_map(
        shards,
        mesh=fine,
        in_specs=(
            P(DP, "space", None, None),
            P(AXES, None, None),
            P(AXES),
            P(AXES),
            P(AXES, None, None),
            P(),
            P(),
            P(),
            P(),
            P(),
            P(),
            P(),
            P(),
            P(),
            P(),
            P(),
            P(),
            P(),
            P(),
            P(),
            P(),
            P(),
            P(),
            P(),
            P(),
            P(),
            P(),
            P(),
            P(),
        ),
        out_specs=(
            P(AXES, None, None),
            P(DP, "space", None, None),
            P(AXES, None, None),
            P("space", DP),
            P(),
            P(),
            P(None, None, "space", DP),
            P(),
            P(),
            P("space", DP),
            P(),
            P(),
            P("space", DP),
            P(),
            P(),
            P(),
            P("space", DP),
            P(),
            P(),
            P("space", DP),
            P(),
            P(),
            P(),
            P("space", DP),
            P(),
            P("space", DP),
            P(),
        ),
        check_vma=False,
    )
```

```python
import functools
import jax
import jax.numpy as jnp
from jax import lax
from jax.experimental import pallas as pl
from jax.experimental.pallas import tpu as pltpu
from jax.sharding import Mesh, PartitionSpec as P

HD = 64
F32 = jnp.float32
BF16 = jnp.bfloat16
eps_batch = 1e-05
eps_layer = 1e-06
masked_value = -1e30
GELU_C = 0.7978845608028654
GELU_A = 0.044715


def nn(a, b):
    return lax.dot_general(a, b, (((1,), (0,)), ((), ())), preferred_element_type=F32)


def nt(a, b):
    return lax.dot_general(a, b, (((1,), (1,)), ((), ())), preferred_element_type=F32)


def tn(a, b):
    return lax.dot_general(a, b, (((0,), (0,)), ((), ())), preferred_element_type=F32)


def gelu_of(x):
    t = jnp.tanh(GELU_C * (x + GELU_A * x * x * x))
    return 0.5 * x * (1.0 + t)


def gelu_and_slope(x):
    x2 = x * x
    t = jnp.tanh(x * (GELU_C + (GELU_C * GELU_A) * x2))
    half = 0.5 + 0.5 * t
    slope = half + (0.5 * x) * (1.0 - t * t) * (GELU_C + (3.0 * GELU_C * GELU_A) * x2)
    return x * half, slope


def ln_parts(x):
    mean = jnp.mean(x, axis=-1, keepdims=True)
    c = x - mean
    var = jnp.mean(c * c, axis=-1, keepdims=True)
    r = lax.rsqrt(var + eps_layer)
    return c * r, r


def ln_back(dz, nrm, r, gain):
    u = dz * gain
    return r * (u - jnp.mean(u, axis=-1, keepdims=True) - nrm * jnp.mean(u * nrm, axis=-1, keepdims=True))


def whole(shape):
    return pl.BlockSpec(shape, lambda *_: (0,) * len(shape), pipeline_mode=pl.Buffered(1))


SMEM = pl.BlockSpec(memory_space=pltpu.SMEM)
VMEM = pl.BlockSpec(memory_space=pltpu.VMEM)


def row_of(ref):
    return ref[...].reshape(1, -1)


def put_rows(ref, at, vector):
    for r in range(vector.shape[1] // 128):
        ref[at + r : at + r + 1, :] = vector[:, r * 128 : (r + 1) * 128]


def take_rows(ref, at, size):
    return jnp.concatenate([ref[at + r : at + r + 1, :] for r in range(size // 128)], axis=1)


def part_shape(cols, rows, dp):
    return (2, dp // 2, cols // dp * (rows // 2) // 128, 128)


def part_it(natural, keep_ref, send_ref, core, at=0, lead=None):
    rows, cols = natural.shape[-2:]
    _, hi = keep_ref.shape[:2]
    r, blocks = rows // (2 * hi), cols // 256
    for h in range(hi):
        mine = pl.ds(pl.multiple_of((2 * h + core) * r, 16), r)
        other = pl.ds(pl.multiple_of((2 * h + 1 - core) * r, 16), r)
        for s in range(2):
            for b in range(blocks):
                lanes = slice((s * blocks + b) * 128, (s * blocks + b + 1) * 128)
                keep_ref[s, h, at + b * r : at + (b + 1) * r, :] = natural[mine, lanes]
                send_ref[s, h, at + b * r : at + (b + 1) * r, :] = natural[other, lanes]


def mlp_kernel(ex, seq, pad, parted, place_ref, z2_ref, h1_ref, cot_ref, upw_ref, upb_ref, dnw_ref, dnb_ref, g_ref, *refs):
    if parted:
        out_ref, dk_ref, ds_ref, uk_ref, us_ref, g1_ref, vec_ref, g2_s, g2t_s, acc_o, acc_d, ub_s, bg_s = refs
    else:
        out_ref, dn_ref, up_ref, g1_ref, vec_ref, g2_s, g2t_s, acc_o, acc_d, ub_s, bg_s = refs
    i = pl.program_id(0)
    last = pl.num_programs(0) - 1
    tile = upw_ref.shape[1]

    @pl.when(i == 0)
    def _():
        g2_s[...] = jnp.zeros_like(g2_s)
        for e in range(ex):
            g2_s[e * pad : e * pad + seq, :] = cot_ref[e]
        g2t_s[...] = g2_s[...].T
        acc_o[...] = jnp.zeros_like(acc_o)
        acc_d[...] = jnp.zeros_like(acc_d)
        ub = row_of(upb_ref)
        for j in range(ub_s.shape[0]):
            ub_s[j] = ub[:, j * tile : (j + 1) * tile]

    z2 = z2_ref[...]
    g2 = g2_s[...]
    pre = nn(z2, upw_ref[...]) + ub_s[i]
    act, slope = gelu_and_slope(pre)
    low = act.astype(BF16)
    dg = (nt(g2, dnw_ref[...]) * slope).astype(BF16)
    acc_o[...] += nn(low, dnw_ref[...])
    acc_d[...] += nt(dg, upw_ref[...])
    dn = nn(g2t_s[...], low).astype(BF16)
    up = tn(dg, z2).astype(BF16)
    bg_s[i] = jnp.sum(dg.astype(F32), axis=0, keepdims=True)
    if parted:
        core = place_ref[1]
        even = core == 0
        hi = dk_ref.shape[1]
        r = dn.shape[0] // (2 * hi)
        for j in range(tile // 128):
            d4 = dn[:, j * 128 : (j + 1) * 128].reshape(hi, 2, r, 128)
            dk_ref[0, :, j * r : (j + 1) * r, :] = jnp.where(even, d4[:, 0], d4[:, 1])
            ds_ref[0, :, j * r : (j + 1) * r, :] = jnp.where(even, d4[:, 1], d4[:, 0])
        r, blocks = up.shape[0] // 4, up.shape[1] // 256
        for s in range(2):
            for j in range(blocks):
                lanes = slice((s * blocks + j) * 128, (s * blocks + j + 1) * 128)
                for t in range(2):
                    first, second = up[2 * t * r : (2 * t + 1) * r, lanes], up[(2 * t + 1) * r : (2 * t + 2) * r, lanes]
                    uk_ref[s, t, j * r : (j + 1) * r, :] = jnp.where(even, first, second)
                    us_ref[s, t, j * r : (j + 1) * r, :] = jnp.where(even, second, first)
    else:
        dn_ref[...] = dn
        up_ref[...] = up

    @pl.when(i == last)
    def _():
        h1 = h1_ref[...]
        out = (h1 + acc_o[...] + row_of(dnb_ref)).astype(BF16)
        for e in range(ex):
            out_ref[e] = out[e * pad : e * pad + seq, :]
        nrm, r = ln_parts(h1)
        dz = acc_d[...]
        gf = g2_s[...].astype(F32)
        g1 = gf + ln_back(dz, nrm, r, row_of(g_ref))
        g1_ref[...] = g1
        n = g1.shape[1] // 128
        for j, v in enumerate((col_sum(gf), col_sum(dz * nrm), col_sum(dz), col_sum(g1))):
            put_rows(vec_ref, j * n, v)
        for j in range(bg_s.shape[0]):
            put_rows(vec_ref, 4 * n + j * (tile // 128), bg_s[j])


def mlp(place, z2, h1, cot, up_w, up_b, down_w, down_b, gain, pad, dp, parted):
    ex, seq, width = cot.shape
    rows = z2.shape[0]
    ff = up_w.shape[1]
    tile = 4 * ff // dp if parted else 384
    steps = ff // tile
    vec_rows = 4 * width // 128 + ff // 128
    if parted:
        dn, up = part_shape(width, ff, dp), part_shape(ff, width, dp)
        per_half = steps // 2
        dn_spec = pl.BlockSpec((1, dn[1], dn[2] // per_half, 128), lambda i: (i // per_half, 0, i % per_half, 0))
        up_spec = pl.BlockSpec((2, 2, up[2], 128), lambda i: (0, i, 0, 0))
        grads = [(dn, dn_spec), (dn, dn_spec), (up, up_spec), (up, up_spec)]
    else:
        grads = [((width, ff), pl.BlockSpec((width, tile), lambda i: (0, i))),
                 ((ff, width), pl.BlockSpec((tile, width), lambda i: (i, 0)))]
    outs = [((ex, seq, width), whole((ex, seq, width)), BF16)] + [(s, b, BF16) for s, b in grads]
    outs += [((rows, width), whole((rows, width)), F32), ((vec_rows, 128), whole((vec_rows, 128)), F32)]
    return pl.pallas_call(
        functools.partial(mlp_kernel, ex, seq, pad, parted),
        grid=(steps,),
        in_specs=[
            SMEM, whole((rows, width)), whole((rows, width)), whole((ex, seq, width)),
            pl.BlockSpec((width, tile), lambda i: (0, i)), whole((ff,)),
            pl.BlockSpec((tile, width), lambda i: (i, 0)),
            whole((width,)), whole((width,)),
        ],
        out_specs=[b for _, b, _ in outs],
        out_shape=[pltpu.HBM(s, d) for s, _, d in outs],
        scratch_shapes=[
            pltpu.VMEM((rows, width), BF16), pltpu.VMEM((width, rows), BF16),
            pltpu.VMEM((rows, width), F32), pltpu.VMEM((rows, width), F32),
            pltpu.VMEM((steps, 1, tile), F32), pltpu.VMEM((steps, 1, tile), F32),
        ],
        compiler_params=pltpu.CompilerParams(dimension_semantics=("arbitrary",), vmem_limit_bytes=44 << 20),
        cost_estimate=pl.CostEstimate(flops=46 * 10**9, bytes_accessed=30 << 20, transcendentals=rows * ff),
        name="mlp_both_ways",
    )(place, *[in_hbm(x) for x in (z2, h1, cot, up_w, up_b, down_w, down_b, gain)])


def stat_rows(channels):
    return max(8, 2 * channels // 128)


def put_stats(ref, first, second):
    lanes = jnp.concatenate([first, second], axis=1)
    n = ref.shape[0]
    for r in range(lanes.shape[1] // 128):
        ref[:, r, :] = jnp.broadcast_to(lanes[:, r * 128 : (r + 1) * 128], (n, 128))


def get_stats(ref, channels):
    total = jnp.sum(ref[...], axis=0)
    rows = 2 * channels // 128
    half = rows // 2
    first = jnp.concatenate([total[r : r + 1, :] for r in range(half)], axis=1)
    second = jnp.concatenate([total[r : r + 1, :] for r in range(half, rows)], axis=1)
    return first, second


def mean_rstd(ref, channels, count):
    s1, s2 = get_stats(ref, channels)
    mean = s1 * (1.0 / count)
    return mean, lax.rsqrt(s2 * (1.0 / count) - mean * mean + eps_batch)


def real_columns(rows, cols):
    return (lax.broadcasted_iota(jnp.int32, (rows, 1), 0) & 15) < cols


def col_sum(x):
    return jnp.sum(x, axis=0, keepdims=True)


def row_blocks(rows):
    starts = list(range(0, rows - 63, 64))
    return [(a, b) for a, b in zip(starts, starts[1:] + [rows])]


def head_mask(rows, second):
    lane = lax.broadcasted_iota(jnp.int32, (rows, 2 * HD), 1)
    return (lane >= HD) if second else (lane < HD)


def attn_fwd_kernel(ex, n_image, pad, pre_ref, len_ref, h0_ref, g_ref, s_ref, wq_ref, wk_ref, wv_ref, qb_ref, vb_ref,
                    ow_ref, ob_ref, g2_ref, s2_ref,
                    z1_ref, q_ref, k_ref, v_ref, p_ref, attn_ref, h1_ref, z2_ref, acc, qb_s, vb_s):
    i = pl.program_id(0)
    last = pl.num_programs(0) - 1
    wide = wq_ref.shape[1]

    @pl.when(i == 0)
    def _():
        nrm, _r = ln_parts(h0_ref[...].astype(F32))
        z1_ref[...] = (nrm * row_of(g_ref) + row_of(s_ref)).astype(BF16)
        acc[...] = jnp.zeros_like(acc)
        qb, vb = row_of(qb_ref), row_of(vb_ref)
        for j in range(qb_s.shape[0]):
            qb_s[j] = qb[:, j * wide : (j + 1) * wide]
            vb_s[j] = vb[:, j * wide : (j + 1) * wide]

    z1 = z1_ref[...]
    q_ref[...] = (nn(z1, wq_ref[...]) + qb_s[i]).astype(BF16)
    k_ref[...] = nn(z1, wk_ref[...]).astype(BF16)
    v_ref[...] = (nn(z1, wv_ref[...]) + vb_s[i]).astype(BF16)
    zero = jnp.zeros((pad, 2 * HD), BF16)
    first = head_mask(pad, False)

    def example(e, carry):
        row0 = pl.multiple_of(e * pad, 16)
        key = lax.broadcasted_iota(jnp.int32, (pad, pad), 1)
        qry = lax.broadcasted_iota(jnp.int32, (pad, pad), 0)
        limit = jnp.maximum(qry + 1, n_image + pre_ref[e])
        limit = jnp.minimum(limit, n_image + len_ref[e])
        vis = key < limit
        for pair in range(wide // (2 * HD)):
            cols = slice(pair * 2 * HD, (pair + 1) * 2 * HD)
            q2 = q_ref[pl.ds(row0, pad), cols] * jnp.asarray(0.125, BF16)
            k2 = k_ref[pl.ds(row0, pad), cols]
            v2 = v_ref[pl.ds(row0, pad), cols]
            out = None
            for h in range(2):
                sel = first if h == 0 else jnp.logical_not(first)
                raw = nt(jnp.where(sel, q2, zero), k2)
                for lo, up in row_blocks(pad):
                    sc = jnp.where(vis[lo:up], raw[lo:up], masked_value)
                    top = jnp.max(sc, axis=-1, keepdims=True)
                    ex_ = jnp.exp(sc - top)
                    tot = jnp.sum(ex_, axis=-1, keepdims=True)
                    p_ref[e, pair * 2 + h, lo:up, :] = (ex_ * (1.0 / tot)).astype(BF16)
                o = nn(p_ref[e, pair * 2 + h], jnp.where(sel, v2, zero))
                out = o if out is None else out + o
            attn_ref[pl.ds(row0, pad), cols] = out.astype(BF16)
        return carry

    lax.fori_loop(0, ex, example, 0)
    acc[...] += nn(attn_ref[...], ow_ref[...])

    @pl.when(i == last)
    def _():
        h1 = h0_ref[...].astype(F32) + acc[...] + row_of(ob_ref)
        h1_ref[...] = h1
        nrm, _r = ln_parts(h1)
        z2_ref[...] = (nrm * row_of(g2_ref) + row_of(s2_ref)).astype(BF16)


def attn_fwd(h0, prefix, text_len, ln1_gain, ln1_shift, qkv_w, qb, vb, out_w, out_b, ln2_gain, ln2_shift, ex, n_image, pad, wide=256):
    rows, width = h0.shape
    groups = width // wide
    heads = width // HD
    hg = wide // HD
    cols = lambda off: pl.BlockSpec((width, wide), lambda i, *_: (0, i + off * groups))
    vec = whole((width,))
    part = pl.BlockSpec((rows, wide), lambda i, *_: (0, i))
    return pl.pallas_call(
        functools.partial(attn_fwd_kernel, ex, n_image, pad),
        grid_spec=pltpu.PrefetchScalarGridSpec(
            num_scalar_prefetch=2,
            grid=(groups,),
            in_specs=[whole((rows, width)), vec, vec, cols(0), cols(1), cols(2), vec, vec,
                      pl.BlockSpec((wide, width), lambda i, *_: (i, 0)), vec, vec, vec],
            out_specs=[whole((rows, width)), part, part, part,
                       pl.BlockSpec((ex, hg, pad, pad), lambda i, *_: (0, i, 0, 0)),
                       part, whole((rows, width)), whole((rows, width))],
            scratch_shapes=[pltpu.VMEM((rows, width), F32)] + [pltpu.VMEM((groups, 1, wide), F32)] * 2,
        ),
        out_shape=[pltpu.HBM((rows, width), BF16)] * 4 + [
            pltpu.HBM((ex, heads, pad, pad), BF16),
            pltpu.HBM((rows, width), BF16),
            pltpu.HBM((rows, width), F32),
            pltpu.HBM((rows, width), BF16)],
        compiler_params=pltpu.CompilerParams(dimension_semantics=("arbitrary",), vmem_limit_bytes=40 << 20),
        cost_estimate=pl.CostEstimate(flops=32 * 10**9, bytes_accessed=30 << 20, transcendentals=heads * rows * pad),
        name="attention_forward",
    )(prefix, text_len, *[in_hbm(x) for x in (h0, ln1_gain, ln1_shift, qkv_w, qkv_w, qkv_w, qb, vb, out_w, out_b, ln2_gain, ln2_shift)])


def attn_bwd_kernel(ex, n_image, txt, cols_real, pad, parted, lo, final, place_ref, g1_ref, ow_ref, attn_ref, q_ref, k_ref, v_ref, p_ref, z1_ref, wq_ref, wk_ref, wv_ref, *refs):
    if lo:
        acc_c, ow_c, qkv_c, bias_c = refs[:4]
        refs = refs[4:]
    if not final:
        acc, ow_s, qkv_s, bias_s = refs[:4]
        g1b_s, g1t_s, dat_s, dq_s, dk_s, dv_s = refs[4:]
    else:
        h0_ref, g_ref, refs = refs[0], refs[1], refs[2:]
        if parted:
            stem_ref, ak_ref, as_ref, text_ref, dtok_ref, vec_ref, ow_s, qkv_s, proj_s = refs[:9]
        else:
            ow_s, qkv_s, text_ref, dtok_ref, vec_ref = refs[:5]
        g1b_s, g1t_s, dat_s, dq_s, dk_s, dv_s, acc, bias_s = refs[-8:]
    i = pl.program_id(0)
    last = pl.num_programs(0) - 1
    wide = wq_ref.shape[1]

    @pl.when(i == 0)
    def _():
        g1b_s[...] = g1_ref[...].astype(BF16)
        g1t_s[...] = g1b_s[...].T
        if lo:
            acc[...] = acc_c[...]
            ow_s[0:lo] = ow_c[...]
            bias_s[:, 0:lo] = bias_c[...]
            for j in range(3):
                qkv_s[j * z1_ref.shape[1] : j * z1_ref.shape[1] + lo * wide, :] = qkv_c[j]
        else:
            acc[...] = jnp.zeros_like(acc)

    gi = i + lo
    ow_s[gi] = nn(g1t_s[...], attn_ref[...]).astype(BF16)
    dat_s[...] = nt(g1b_s[...], ow_ref[...]).astype(BF16)
    zero = jnp.zeros((pad, 2 * HD), BF16)
    first = head_mask(pad, False)

    def example(e, carry):
        row0 = pl.multiple_of(e * pad, 16)
        for pair in range(wide // (2 * HD)):
            cols = slice(pair * 2 * HD, (pair + 1) * 2 * HD)
            q2 = q_ref[pl.ds(row0, pad), cols]
            k2 = k_ref[pl.ds(row0, pad), cols]
            v2 = v_ref[pl.ds(row0, pad), cols]
            da2 = dat_s[pl.ds(row0, pad), cols]
            dq = dk = dv = None
            for h in range(2):
                sel = first if h == 0 else jnp.logical_not(first)
                pb = p_ref[e, pair * 2 + h]
                dah = jnp.where(sel, da2, zero)
                whole_dp = nt(dah, v2)
                parts = []
                for first_row, end_row in row_blocks(pad):
                    p = pb[first_row:end_row].astype(F32)
                    dp = whole_dp[first_row:end_row]
                    inner = jnp.sum(p * dp, axis=-1, keepdims=True)
                    parts.append((p * (dp - inner)).astype(BF16))
                ds = jnp.concatenate(parts, axis=0)
                dvh = tn(pb, dah)
                dqh = nn(ds, jnp.where(sel, k2, zero))
                dkh = tn(ds, jnp.where(sel, q2, zero))
                dq = dqh if dq is None else dq + dqh
                dk = dkh if dk is None else dk + dkh
                dv = dvh if dv is None else dv + dvh
            dq_s[pl.ds(row0, pad), cols] = (dq * 0.125).astype(BF16)
            dk_s[pl.ds(row0, pad), cols] = (dk * 0.125).astype(BF16)
            dv_s[pl.ds(row0, pad), cols] = dv.astype(BF16)
        return carry

    lax.fori_loop(0, ex, example, 0)
    z1 = z1_ref[...]
    dq, dk, dv = dq_s[...], dk_s[...], dv_s[...]
    width = z1.shape[1]
    for j, d in enumerate((dq, dk, dv)):
        if final:
            qkv_s[pl.ds(pl.multiple_of(j * width + gi * wide, wide), wide), :] = tn(d, z1).astype(BF16)
        else:
            qkv_s[j] = tn(d, z1).astype(BF16)
    acc[...] += nt(dq, wq_ref[...]) + nt(dk, wk_ref[...]) + nt(dv, wv_ref[...])
    bias_s[0, gi] = col_sum(dq.astype(F32))
    bias_s[1, gi] = col_sum(dv.astype(F32))

    if not final:
        return

    @pl.when(i == last)
    def _():
        nrm, r = ln_parts(h0_ref[...].astype(F32))
        dz = acc[...]
        g0 = g1_ref[...] + ln_back(dz, nrm, r, row_of(g_ref))
        n = width // 128
        vec_ref[5 * n :, :] = jnp.zeros_like(vec_ref[5 * n :, :])
        put_rows(vec_ref, n, col_sum(dz * nrm))
        put_rows(vec_ref, 2 * n, col_sum(dz))
        for j in range(2):
            for t in range(bias_s.shape[1]):
                put_rows(vec_ref, (3 + j) * n + t * (wide // 128), bias_s[j, t])
        gb = g0.astype(BF16)
        px = dtok_ref.shape[0] // ex
        pick_image = image_pick(px, pad, n_image, cols_real)
        tr = lax.broadcasted_iota(jnp.int32, (txt, pad), 0)
        tc = lax.broadcasted_iota(jnp.int32, (txt, pad), 1)
        pick_text = jnp.where(tc == tr + n_image, 1.0, 0.0).astype(BF16)
        tot = jnp.zeros((1, gb.shape[1]), F32)
        for e in range(ex):
            ge = gb[e * pad : (e + 1) * pad, :]
            text_ref[e] = nn(pick_text, ge).astype(BF16)
            dt = nn(pick_image, ge)
            dtok_ref[e * px : (e + 1) * px, :] = dt.astype(BF16)
            tot = tot + jnp.sum(dt, axis=0, keepdims=True)
        put_rows(vec_ref, 0, tot)
        if parted:
            core = place_ref[1]
            part_it(qkv_s, ak_ref, as_ref, core)
            proj_s[...] = tn(dtok_ref[...], stem_ref[...]).astype(BF16)
            part_it(proj_s, ak_ref, as_ref, core, at=(qkv_s.shape[0] + width) // (2 * ak_ref.shape[1]) * (width // 256))
            hi = ak_ref.shape[1]
            r = width // (2 * hi)
            at = qkv_s.shape[0] // (2 * hi) * (width // 256)
            for h in range(hi):
                mine = pl.ds(pl.multiple_of((2 * h + core) * r, 16), r)
                other = pl.ds(pl.multiple_of((2 * h + 1 - core) * r, 16), r)
                for blk in range(width // 128):
                    s, j = divmod(blk, width // 256)
                    t, lane = divmod(blk * 128, wide)
                    dst = slice(at + j * r, at + (j + 1) * r)
                    ak_ref[s, h, dst, :] = ow_s[t, mine, lane : lane + 128]
                    as_ref[s, h, dst, :] = ow_s[t, other, lane : lane + 128]


def image_pick(px, pad, n_image, cols_real):
    p = lax.broadcasted_iota(jnp.int32, (px, pad), 0)
    t = lax.broadcasted_iota(jnp.int32, (px, pad), 1)
    col = p & 15
    tok = (p >> 4) * cols_real + col
    return jnp.where((col < cols_real) & (tok == t) & (t < n_image), 1.0, 0.0).astype(BF16)


def attn_bwd(place, g1, out_w, attn, q, k, v, p, z1, h0, qkv_w, ln1_gain, ex, n_image, txt, img_rows, img_cols, pad, dp, parted,
             lo=0, hi=None, carry=(), stem=None, wide=256):
    rows, width = h0.shape
    groups = width // wide
    heads = width // HD
    hg = wide // HD
    px = img_rows * 16
    hi = groups if hi is None else hi
    final = hi == groups
    vec_rows = -(-5 * width // 128 // 8) * 8
    cols = lambda off: pl.BlockSpec((width, wide), lambda i: (0, i + lo + off * groups))
    part = pl.BlockSpec((rows, wide), lambda i: (0, i + lo))
    nat_o, nat_q = (groups, width, wide), (3 * width, width)
    sent = part_shape(4 * width, width, dp)
    if stem is not None:
        sent = sent[:2] + (sent[2] + part_shape(width, stem.shape[1], dp)[2], 128)
    scratch = [pltpu.VMEM((rows, width), BF16), pltpu.VMEM((width, rows), BF16)] + [pltpu.VMEM((rows, wide), BF16)] * 4
    args = [g1, out_w, attn, q, k, v, p, z1, qkv_w, qkv_w, qkv_w, *carry]
    in_specs = [SMEM, whole((rows, width)), pl.BlockSpec((wide, width), lambda i: (i + lo, 0)), part, part, part, part,
                pl.BlockSpec((ex, hg, pad, pad), lambda i: (0, i + lo, 0, 0)), whole((rows, width)), cols(0), cols(1), cols(2)]
    in_specs += [whole(c.shape) for c in carry]
    if final:
        outs = [(s, BF16) for s in ((sent, sent) if parted else (nat_o, nat_q))]
        outs += [((ex, txt, width), BF16), ((ex * px, width), BF16), ((vec_rows, 128), F32)]
        natural = [pltpu.VMEM(nat_o, BF16), pltpu.VMEM(nat_q, BF16), pltpu.VMEM((width, stem.shape[1]), BF16)] if parted else []
        scratch = natural + scratch + [pltpu.VMEM((rows, width), F32), pltpu.VMEM((2, groups, 1, wide), F32)]
        args += [h0, ln1_gain] + ([stem] if parted else [])
        in_specs += [whole((rows, width)), whole((width,))] + ([whole(stem.shape)] if parted else [])
    else:
        n = hi - lo
        outs = [((rows, width), F32), ((n, width, wide), BF16), ((3, n * wide, width), BF16), ((2, n, 1, wide), F32)]
    return pl.pallas_call(
        functools.partial(attn_bwd_kernel, ex, n_image, txt, img_cols, pad, parted, lo, final),
        grid=(hi - lo,),
        in_specs=in_specs,
        out_specs=[whole(s) for s, _ in outs],
        out_shape=[pltpu.HBM(s, d) for s, d in outs],
        scratch_shapes=scratch,
        compiler_params=pltpu.CompilerParams(dimension_semantics=("arbitrary",), vmem_limit_bytes=60 << 20),
        cost_estimate=pl.CostEstimate(flops=14 * (hi - lo) * 10**9, bytes_accessed=40 << 20, transcendentals=0),
        name="attention_backward",
    )(place, *[in_hbm(x) for x in args])

def over_pixels(shape, body, init=0):
    ex, rows = shape[:2]
    per = rows // 2

    def one(j, carry):
        return body(j // per, j % per * 2, pl.ds(pl.multiple_of(j * 32, 32), 32), carry)

    return lax.fori_loop(0, ex * per, one, init)


def stats_kernel(cols, x_ref, w_ref, parts_ref, xp):
    xp[...] = jnp.zeros_like(xp)
    shape = x_ref.shape
    xp[:, 0:cols, :] = x_ref[...].reshape(shape[0] * shape[1], cols, shape[3])
    a = nn(xp[...].reshape(shape[0] * shape[1] * 16, shape[3]), w_ref[...])
    put_stats(parts_ref, col_sum(a), col_sum(a * a))


def conv_fwd_kernel(count, ex, rows, cols, place_ref, parts_ref, own_ref, got_ref, win_ref, g_ref, s_ref, wmid_ref,
                    xs_ref, act1_ref, wide_ref, act2_ref, parts2_ref):
    s = place_ref[0]
    half = rows // 2
    px = rows * 16
    chan = xs_ref.shape[-1]
    xs_ref[...] = jnp.zeros_like(xs_ref)
    for e in range(ex):
        xs_ref[e, pl.ds(s * half, half), 0:cols, :] = own_ref[s * ex + e]
        xs_ref[e, pl.ds((1 - s) * half, half), 0:cols, :] = got_ref[e]
    a1 = nn(xs_ref[...].reshape(ex * px, chan), win_ref[...])
    act1_ref[...] = a1
    mid = a1.shape[1]
    mean, rstd = mean_rstd(parts_ref, mid, count)
    real = real_columns(ex * px, cols)
    act = gelu_of((a1 - mean) * rstd * row_of(g_ref) + row_of(s_ref))
    act = jnp.where(real, act, 0.0)
    for e in range(ex):
        part = act[e * px : (e + 1) * px]
        wide_ref[e, 0:16, :] = jnp.zeros((16, 3 * mid), BF16)
        wide_ref[e, px + 16 : px + 32, :] = jnp.zeros((16, 3 * mid), BF16)
        wide_ref[e, 16 : px + 16, 0:mid] = pltpu.roll(part, 1, 0).astype(BF16)
        wide_ref[e, 16 : px + 16, mid : 2 * mid] = part.astype(BF16)
        wide_ref[e, 16 : px + 16, 2 * mid : 3 * mid] = pltpu.roll(part, px - 1, 0).astype(BF16)
    one = real_columns(px, cols)
    t1 = jnp.zeros((1, mid), F32)
    t2 = jnp.zeros((1, mid), F32)
    for e in range(ex):
        a2 = nn(wide_ref[e, 0:px, :], wmid_ref[0])
        a2 = a2 + nn(wide_ref[e, 16 : px + 16, :], wmid_ref[1])
        a2 = a2 + nn(wide_ref[e, 32 : px + 32, :], wmid_ref[2])
        a2 = jnp.where(one, a2, 0.0)
        act2_ref[e * px : (e + 1) * px, :] = a2
        t1 = t1 + col_sum(a2)
        t2 = t2 + col_sum(a2 * a2)
    put_stats(parts2_ref, t1, t2)


def expand_kernel(count, cols, parts_ref, act2_ref, g_ref, s_ref, w_ref, relu2_ref, act3_ref, parts3_ref):
    a2 = act2_ref[...]
    mean, rstd = mean_rstd(parts_ref, a2.shape[1], count)
    act = gelu_of((a2 - mean) * rstd * row_of(g_ref) + row_of(s_ref))
    low = jnp.where(real_columns(a2.shape[0], cols), act, 0.0).astype(BF16)
    relu2_ref[...] = low
    a3 = nn(low, w_ref[...])
    act3_ref[...] = a3
    put_stats(parts3_ref, col_sum(a3), col_sum(a3 * a3))


def tokens_kernel(count, ex, cols, n_image, pad, parts_ref, act3_ref, xs_ref, g_ref, s_ref, w_ref, b_ref, text_ref,
                  stem_ref, h0_ref):
    mean, rstd = mean_rstd(parts_ref, act3_ref.shape[1], count)
    scale = rstd * row_of(g_ref)
    offset = row_of(s_ref) - mean * scale

    def body(e, r, rs, carry):
        pre = act3_ref[rs, :] * scale + offset + xs_ref[e, pl.ds(r, 2)].reshape(32, -1).astype(F32)
        stem_ref[rs, :] = gelu_of(pre).astype(BF16)
        return carry

    over_pixels(xs_ref.shape, body)
    tok = (nn(stem_ref[...], w_ref[...]) + row_of(b_ref)).astype(BF16)
    px = act3_ref.shape[0] // ex
    txt = text_ref.shape[1]
    t = lax.broadcasted_iota(jnp.int32, (pad, px), 0)
    p = lax.broadcasted_iota(jnp.int32, (pad, px), 1)
    col = p & 15
    pick = jnp.where((col < cols) & ((p >> 4) * cols + col == t), 1.0, 0.0).astype(BF16)
    tr = lax.broadcasted_iota(jnp.int32, (pad, txt), 0)
    tc = lax.broadcasted_iota(jnp.int32, (pad, txt), 1)
    pick_text = jnp.where(tr == tc + n_image, 1.0, 0.0).astype(BF16)
    for e in range(ex):
        both = nn(pick, tok[e * px : (e + 1) * px, :]) + nn(pick_text, text_ref[e])
        h0_ref[e * pad : (e + 1) * pad, :] = both.astype(BF16)


def dpre_kernel(count, ex, rows, place_ref, parts_ref, act3_ref, xs_ref, g_ref, s_ref, dtok_ref, w_ref, dpre_ref, send_ref, parts4_ref):
    chan = act3_ref.shape[1]
    mean, rstd = mean_rstd(parts_ref, chan, count)
    gain, shift = row_of(g_ref), row_of(s_ref)
    dpre_ref[...] = nt(dtok_ref[...], w_ref[...]).reshape(dpre_ref.shape)

    def body(e, r, rs, carry):
        nrm = (act3_ref[rs, :] - mean) * rstd
        _, slope = gelu_and_slope(nrm * gain + shift + xs_ref[e, pl.ds(r, 2)].reshape(32, chan).astype(F32))
        d = dpre_ref[e, pl.ds(r, 2)].reshape(32, chan) * slope
        dpre_ref[e, pl.ds(r, 2)] = d.reshape(2, 16, chan)
        return carry[0] + jnp.sum(d.reshape(4, 8, chan), axis=0), carry[1] + jnp.sum((d * nrm).reshape(4, 8, chan), axis=0)

    zero = jnp.zeros((8, chan), F32)
    a, b = over_pixels(xs_ref.shape, body, (zero, zero))
    put_stats(parts4_ref, col_sum(a), col_sum(b))
    half = rows // 2
    other = 1 - place_ref[0]
    for e in range(ex):
        send_ref[e] = dpre_ref[e, pl.ds(other * half, half)].astype(BF16)


def back3_kernel(count, cols, parts4_ref, parts3_ref, parts2_ref, act3_ref, dpre_ref, g3_ref, w_ref, act2_ref, g2_ref, s2_ref, veca_ref, vecb_ref,
                 low3_ref, t2_ref, parts5_ref, gain_ref, shift_ref, small_s):
    chan = act3_ref.shape[1]
    mean, rstd = mean_rstd(parts3_ref, chan, count)
    s1, s2 = get_stats(parts4_ref, chan)
    gain_ref[...] = s2.reshape(-1)
    shift_ref[...] = s1.reshape(-1)
    scale = row_of(g3_ref) * rstd
    c1, c2 = s1 * (1.0 / count), s2 * (1.0 / count)
    real = real_columns(32, cols)

    def body(e, r, rs, carry):
        nrm = (act3_ref[rs, :] - mean) * rstd
        d = scale * (dpre_ref[e, pl.ds(r, 2)].reshape(32, chan) - c1 - nrm * c2)
        low3_ref[rs, :] = jnp.where(real, d, 0.0).astype(BF16)
        return carry

    over_pixels(dpre_ref.shape, body)
    a2 = act2_ref[...]
    mean2, rstd2 = mean_rstd(parts2_ref, a2.shape[1], count)
    nrm2 = (a2 - mean2) * rstd2
    _, slope = gelu_and_slope(nrm2 * row_of(g2_ref) + row_of(s2_ref))
    t2 = nt(low3_ref[...], w_ref[...]) * slope
    t2_ref[...] = t2
    parts5_ref[...] = jnp.zeros_like(parts5_ref)
    put_stats(parts5_ref, col_sum(t2), col_sum(t2 * nrm2))
    used = veca_ref.shape[0] + vecb_ref.shape[0]
    n = parts5_ref.shape[0]
    each = -(-used // n)
    small_s[0 : veca_ref.shape[0], :] = veca_ref[...]
    small_s[veca_ref.shape[0] : used, :] = vecb_ref[...]
    if used < small_s.shape[0]:
        small_s[used:, :] = jnp.zeros_like(small_s[used:, :])
    for d in range(n):
        parts5_ref[d, 4 : 4 + each, :] = small_s[d * each : (d + 1) * each, :]


def back2_kernel(count, ex, rows, cols, place_ref, parts5_ref, parts2_ref, parts1_ref, act2_ref, t2_ref, g2_ref, wmid_ref, act1_ref, g1_ref, s1_ref,
                 low2_ref, t1_ref, send_ref, parts6_ref, gain_ref, shift_ref, wide):
    a2 = act2_ref[...]
    mid = a2.shape[1]
    px = rows * 16
    mean, rstd = mean_rstd(parts2_ref, mid, count)
    s1, s2 = get_stats(parts5_ref, mid)
    gain_ref[...] = s2.reshape(-1)
    shift_ref[...] = s1.reshape(-1)
    nrm = (a2 - mean) * rstd
    d = (row_of(g2_ref) * rstd) * (t2_ref[...] - s1 * (1.0 / count) - nrm * (s2 * (1.0 / count)))
    d = jnp.where(real_columns(ex * px, cols), d, 0.0)
    low2_ref[...] = d.astype(BF16)
    for e in range(ex):
        part = d[e * px : (e + 1) * px]
        wide[e, 0:16, :] = jnp.zeros((16, 3 * mid), BF16)
        wide[e, px + 16 : px + 32, :] = jnp.zeros((16, 3 * mid), BF16)
        wide[e, 16 : px + 16, 0:mid] = pltpu.roll(part, px - 1, 0).astype(BF16)
        wide[e, 16 : px + 16, mid : 2 * mid] = part.astype(BF16)
        wide[e, 16 : px + 16, 2 * mid : 3 * mid] = pltpu.roll(part, 1, 0).astype(BF16)
    mean1, rstd1 = mean_rstd(parts1_ref, mid, count)
    one = real_columns(px, cols)
    q1 = jnp.zeros((1, mid), F32)
    q2 = jnp.zeros((1, mid), F32)
    for e in range(ex):
        t = None
        for r in range(3):
            for c in range(3):
                term = nt(wide[e, (2 - r) * 16 : (2 - r) * 16 + px, c * mid : (c + 1) * mid], wmid_ref[r, c * mid : (c + 1) * mid, :])
                t = term if t is None else t + term
        nrm1 = (act1_ref[e * px : (e + 1) * px, :] - mean1) * rstd1
        _, slope = gelu_and_slope(nrm1 * row_of(g1_ref) + row_of(s1_ref))
        t = jnp.where(one, t * slope, 0.0)
        t1_ref[e] = t.reshape(rows, 16, mid)
        q1 = q1 + col_sum(t)
        q2 = q2 + col_sum(t * nrm1)
    put_stats(parts6_ref, q1, q2)
    chunk = jnp.sum(parts5_ref[:, 4:8, :], axis=0)
    parts6_ref[:, 4:8, :] = jnp.broadcast_to(chunk[None], (parts6_ref.shape[0], 4, 128))
    half = rows // 2
    other = 1 - place_ref[0]
    for e in range(ex):
        send_ref[e] = t1_ref[e, pl.ds(other * half, half)].astype(BF16)


def conv_grads_kernel(ex, px, parted, place_ref, low2_ref, wide_ref, low3_ref, relu2_ref, *refs):
    mid = low2_ref.shape[1]
    nat_m, nat_o = (refs[2], refs[3]) if parted else (refs[0], refs[1])
    nat_o[...] = tn(low3_ref[...], relu2_ref[...]).astype(BF16)
    for r in range(3):
        tot = None
        for e in range(ex):
            term = tn(low2_ref[e * px : (e + 1) * px, :], wide_ref[e, r * 16 : r * 16 + px, :])
            tot = term if tot is None else tot + term
        for c in range(3):
            for h in range(2):
                at = (h * 9 + r * 3 + c) * (mid // 2)
                src = c * mid + h * (mid // 2)
                nat_m[:, at : at + mid // 2] = tot[:, src : src + mid // 2].astype(BF16)
    if parted:
        part_it(nat_m, refs[0], refs[1], place_ref[1])
        part_it(nat_o, refs[0], refs[1], place_ref[1], at=nat_m.shape[0] // (2 * refs[0].shape[1]) * (nat_m.shape[1] // 256))


def tn_kernel(parted, place_ref, a_ref, b_ref, *refs):
    natural = refs[2] if parted else refs[0]
    natural[...] = tn(a_ref[...], b_ref[...]).astype(BF16)
    if parted:
        part_it(natural, refs[0], refs[1], place_ref[1])


def first_back_kernel(count, ex, rows, cols, parted, each, places, place_ref, parts6_ref, parts1_ref, x_ref, win_ref, g_ref, t1_ref, gott_ref,
                      low_ref, *refs):
    if parted:
        keep_ref, send_ref, win_grad_ref = refs[0], refs[1], refs[-1]
        refs = refs[2:-1]
    else:
        win_grad_ref, refs = refs[0], refs[1:]
    gain_ref, shift_ref, vec_refs, xp, small_s = refs[0], refs[1], refs[2:-2], refs[-2], refs[-1]
    s = place_ref[0]
    half = rows // 2
    chan = x_ref.shape[-1]
    mid = win_ref.shape[1]
    mean, rstd = mean_rstd(parts1_ref, mid, count)
    s1, s2 = get_stats(parts6_ref, mid)
    gain_ref[...] = s2.reshape(-1)
    shift_ref[...] = s1.reshape(-1)
    real = real_columns(ex * half * 16, cols)
    size = ex * half * 16
    xp[...] = jnp.zeros_like(xp)
    wg = None
    for own in (True, False):
        at = (s if own else 1 - s) * ex
        xp[:, 0:cols, :] = x_ref[pl.ds(at, ex)].reshape(ex * half, cols, chan)
        x = xp[...].reshape(size, chan)
        nrm = (nn(x, win_ref[...]) - mean) * rstd
        if own:
            t = t1_ref[:, pl.ds(s * half, half)].reshape(size, mid)
        else:
            t = gott_ref[...].reshape(size, mid).astype(F32)
        d = (row_of(g_ref) * rstd) * (t - s1 * (1.0 / count) - nrm * (s2 * (1.0 / count)))
        low = jnp.where(real, d, 0.0).astype(BF16)
        low_ref[0 if own else 1] = low
        term = tn(low, x)
        wg = term if wg is None else wg + term
    win_grad_ref[...] = wg.astype(BF16)
    if parted:
        part_it(win_grad_ref, keep_ref, send_ref, place_ref[1])
    for d in range(parts6_ref.shape[0]):
        small_s[d * each : (d + 1) * each, :] = parts6_ref[d, 4 : 4 + each, :]
    for ref, at in zip(vec_refs, places):
        ref[...] = take_rows(small_s, at, ref.shape[0]).reshape(-1)


def image_kernel(ex, rows, cols, place_ref, low_ref, win_ref, dpre_ref, gotd_ref, grad_ref):
    s = place_ref[0]
    half = rows // 2
    chan = win_ref.shape[0]
    size = ex * half * 16
    for own in (True, False):
        at = (s if own else 1 - s) * ex
        dp = dpre_ref[:, pl.ds(s * half, half)] if own else gotd_ref[...]
        grad = nt(low_ref[0 if own else 1], win_ref[...]) + dp.reshape(size, chan).astype(F32)
        grad_ref[pl.ds(at, ex)] = grad.astype(BF16).reshape(ex, half, 16, chan)[:, :, 0:cols, :]


def in_hbm(x):
    return pltpu.with_memory_space_constraint(x, pltpu.HBM)


def call(kernel, outs, *args, moved=(), place=None, scratch=(), name=None, us=2, limit=40):
    nbytes = sum(a.size * a.dtype.itemsize for a in args)
    spec = lambda s: pl.BlockSpec(s, lambda i: (0,) * len(s))
    return pl.pallas_call(
        kernel,
        grid=(1,),
        out_shape=[pltpu.HBM(s, d) for s, d in outs],
        in_specs=([SMEM] if place is not None else []) + [spec(a.shape) for a in args],
        out_specs=[spec(s) for s, _ in outs],
        scratch_shapes=list(scratch),
        compiler_params=pltpu.CompilerParams(vmem_limit_bytes=limit << 20),
        cost_estimate=pl.CostEstimate(flops=us * 10**9, bytes_accessed=nbytes if us else 0, transcendentals=0),
        name=name,
    )(*([place] if place is not None else []), *[a if any(a is b for b in moved) else in_hbm(a) for a in args])


DP = ("far", "near", "core")
AXES = DP + ("space",)


def spread(parts):
    return lax.all_to_all(parts, AXES, split_axis=0, concat_axis=0, tiled=True)


def swap(x, axis="space"):
    return lax.ppermute(x, axis, [(0, 1), (1, 0)])


def tie(*values):
    return lax.optimization_barrier(values)


BITS = ("space", "f1", "f0", "near")


def bit_of(name):
    if name in ("f0", "f1"):
        return (lax.axis_index("far") // (1 if name == "f0" else 2)) % 2
    return lax.axis_index(name)


def sent(x, key):
    if key == ("core",):
        return swap(x, "core")
    flip = {n: int(n in key) for n in BITS}
    far, near, space = 2 * flip["f1"] + flip["f0"], flip["near"], flip["space"]
    if far and (near or space):
        raise ValueError
    if far:
        return lax.ppermute(x, "far", [(j, j ^ far) for j in range(4)])
    if near and space:
        return lax.ppermute(x, ("near", "space"), [(j, 3 - j) for j in range(4)])
    return swap(x, "near" if near else "space")


class Box:
    def __init__(self, value, moved=False):
        self.value, self.moved = value, moved


class Pack:
    def __init__(self, sources, left, size, at=0, rows=None):
        self.sources, self.left, self.size, self.at, self.rows = sources, left, size, at, size if rows is None else rows

    @classmethod
    def start(cls, keep, send):
        size = keep.shape[-2]
        got = sent(send, ("core",))
        return cls([(Box(keep.reshape(-1, 128)), 0), (Box(got.reshape(-1, 128), True), 0)], list(BITS), size)

    def thirds(self):
        r = self.size // 3
        return [Pack(self.sources, self.left, self.size, k * r, r) for k in range(3)]


def arrive(value, *packs):
    boxes = []
    for x in packs:
        boxes += [b for b, _ in x.sources if b.moved and b not in boxes]
    flat = tie(value, *[b.value for b in boxes])
    for b, v in zip(boxes, flat[1:], strict=True):
        b.value = v
    return flat[0]


def combine_kernel(plan, n_in, bits_ref, *refs):
    ins, outs = refs[:n_in], refs[n_in:]
    for sources, left, size, at, rows, names, dests in plan:
        rest = [d for d in left if d not in names]
        for rel, (out, to) in enumerate(dests):
            for c in range(2 ** len(rest)):
                place = 0
                for pos, d in enumerate(left):
                    stride = 2 ** (len(left) - 1 - pos)
                    if d in names:
                        bit = bits_ref[BITS.index(d)]
                        if (rel >> (len(names) - 1 - names.index(d))) & 1:
                            bit = 1 - bit
                    else:
                        bit = (c >> (len(rest) - 1 - rest.index(d))) & 1
                    place = place + bit * stride
                tot = None
                for idx, first in sources:
                    x = ins[idx][pl.ds(pl.multiple_of(first + place * size + at, 16), rows), :].astype(F32)
                    tot = x if tot is None else tot + x
                outs[out][to + c * rows : to + (c + 1) * rows, :] = tot.astype(BF16)


def step(bits, moves, tied):
    boxes, plan, keys, totals, after = [], [], [], {(): 0}, []
    for pack, names in moves:
        srcs = []
        for box, first in pack.sources:
            if box not in boxes:
                boxes.append(box)
            srcs.append((boxes.index(box), first))
        rest = [d for d in pack.left if d not in names]
        n = 2 ** len(rest) * pack.rows
        dests = []
        for rel in range(2 ** len(names)):
            key = tuple(d for j, d in enumerate(names) if (rel >> (len(names) - 1 - j)) & 1)
            key = tuple(sorted(key))
            if key not in totals:
                totals[key] = 0
            if key not in keys:
                keys.append(key)
            dests.append((key, totals[key]))
            totals[key] += n
        plan.append((srcs, list(pack.left), pack.size, pack.at, pack.rows, names, dests))
        after.append((rest, pack.rows, dests))
    plan = [(*p[:-1], [(keys.index(k), to) for k, to in p[-1]]) for p in plan]
    args = [b.value if b.moved else in_hbm(b.value) for b in boxes]
    one = lambda shape: pl.BlockSpec(shape, lambda t: (0, 0), pipeline_mode=pl.Buffered(1))
    res = pl.pallas_call(
        functools.partial(combine_kernel, plan, len(args)),
        grid=(1,),
        in_specs=[SMEM] + [one(x.shape) for x in args],
        out_specs=[one((totals[k], 128)) for k in keys],
        out_shape=[pltpu.HBM((totals[k], 128), BF16) for k in keys],
        compiler_params=pltpu.CompilerParams(vmem_limit_bytes=40 << 20),
        cost_estimate=pl.CostEstimate(flops=0, bytes_accessed=0, transcendentals=0),
        name="combine",
    )(bits, *args)
    flat = tie(tied, *res)
    arrays = {k: Box(flat[1 + j] if k == () else sent(flat[1 + j], k), k != ()) for j, k in enumerate(keys)}
    packs = [Pack([(arrays[k], to) for k, to in dests], rest, rows) for rest, rows, dests in after]
    return flat[0], packs


def finish_kernel(plan, n_in, *refs):
    ins, outs = refs[:n_in], refs[n_in:]
    for sources, pieces in plan:
        for first, r, blocks, out in pieces:
            for b in range(blocks):
                tot = None
                for idx, at in sources:
                    lo = at + first + b * r
                    if len(ins[idx].shape) == 3:
                        x = jnp.sum(ins[idx][:, lo : lo + r, :].astype(F32), axis=0)
                    else:
                        x = ins[idx][lo : lo + r, :].astype(F32)
                    tot = x if tot is None else tot + x
                if len(outs[out].shape) == 3:
                    outs[out][b] = tot
                else:
                    outs[out][:, b * 128 : (b + 1) * 128] = tot


def finish(groups, shapes, name):
    boxes, plan = [], []
    for sources, pieces in groups:
        srcs = []
        for box, first in sources:
            if box not in boxes:
                boxes.append(box)
            srcs.append((boxes.index(box), first))
        plan.append((srcs, pieces))
    args = [b.value for b in boxes]
    return call(functools.partial(finish_kernel, plan, len(args)), [(s, F32) for s in shapes], *args, moved=args, name=name)


def halve_dp(x, axis, bit):
    size = lax.axis_size(DP)
    mine = (lax.axis_index(DP) // bit) % 2
    keep = lax.dynamic_index_in_dim(x, mine, axis, keepdims=True)
    send = lax.dynamic_index_in_dim(x, 1 - mine, axis, keepdims=True)
    return keep + lax.ppermute(send, DP, [(j, j ^ bit) for j in range(size)])


def scattered(grad_t):
    size = lax.axis_size(DP)
    bits = size.bit_length() - 1
    cols, rows = grad_t.shape
    x = grad_t.reshape((2,) * bits + (cols // size, rows))
    for b in range(bits):
        x = halve_dp(x, bits - 1 - b, 1 << b)
    half = rows // 2
    mine = lax.axis_index("space")
    keep = lax.dynamic_slice_in_dim(x, mine * half, half, axis=x.ndim - 1)
    send = lax.dynamic_slice_in_dim(x, (1 - mine) * half, half, axis=x.ndim - 1)
    return (keep + swap(send)).reshape(cols // size, half).astype(F32).T


def shards(
    image_in, text_in, prefix, text_len, cotangent,
    conv_in_w, bn1_gain, bn1_shift, conv_mid_w, bn2_gain, bn2_shift, conv_out_w, bn3_gain, bn3_shift,
    proj_w, proj_b, ln1_gain, ln1_shift, qkv_w, query_bias, value_bias, out_w, out_b,
    ln2_gain, ln2_shift, up_w, up_b, down_w, down_b,
):
    n_dev, dp = lax.axis_size(AXES), lax.axis_size(DP)
    band_ex, band_rows, cols, chan = image_in.shape
    mid = conv_in_w.shape[1]
    width = proj_w.shape[1]
    ff = up_w.shape[1]
    ex, txt, _ = text_in.shape
    rows = band_rows * lax.axis_size("space")
    n_image = rows * cols
    seq = n_image + txt
    pad = -(-seq // 16) * 16
    px = rows * 16
    count = float(band_ex * band_rows * cols * n_dev)
    me = lax.axis_index("space").astype(jnp.int32)
    place = jnp.stack([me, lax.axis_index("core").astype(jnp.int32)])
    small, large = (n_dev, stat_rows(mid), 128), (n_dev, stat_rows(chan), 128)
    wmid = conv_mid_w.reshape(3, 3 * mid, mid)
    weights = [(mid, chan), (mid, 9 * mid), (chan, mid), (width, chan), (3 * width, width), (width, width), (ff, width), (width, ff)]
    parted = dp == 16 and mid == 256 and all(c % (16 * dp) == 0 and r % 256 == 0 for c, r in weights)
    hi = dp // 2

    def grad_outs(c, r):
        return [(part_shape(c, r, dp), BF16)] * 2 if parted else [((c, r), BF16)]

    def natural(c, r):
        return [pltpu.VMEM((c, r), BF16)] if parted else []

    got_x = swap(lax.dynamic_slice_in_dim(image_in, (1 - me) * ex, ex, axis=0))
    parts1, = call(functools.partial(stats_kernel, cols), [(small, F32)], image_in, conv_in_w,
                   scratch=[pltpu.VMEM((band_ex * band_rows, 16, chan), BF16)], name="stats_one")
    parts1 = spread(parts1)
    xs, act1, wide, act2, parts2 = call(
        functools.partial(conv_fwd_kernel, count, ex, rows, cols),
        [((ex, rows, 16, chan), BF16), ((ex * px, mid), F32), ((ex, px + 32, 3 * mid), BF16), ((ex * px, mid), F32), (small, F32)],
        parts1, image_in, got_x, conv_in_w, bn1_gain, bn1_shift, wmid, moved=(parts1, got_x), place=place, name="conv_three", us=4)
    parts2 = spread(parts2)
    relu2, act3, parts3 = call(
        functools.partial(expand_kernel, count, cols),
        [((ex * px, mid), BF16), ((ex * px, chan), F32), (large, F32)],
        parts2, act2, bn2_gain, bn2_shift, conv_out_w, moved=(parts2,), name="expand")
    parts3 = spread(parts3)
    stem, h0 = call(
        functools.partial(tokens_kernel, count, ex, cols, n_image, pad),
        [((ex * px, chan), BF16), ((ex * pad, width), BF16)],
        parts3, act3, xs, bn3_gain, bn3_shift, proj_w, proj_b, text_in, moved=(parts3,), name="tokens", us=5)
    z1, q, k, v, p, attn, h1, z2 = attn_fwd(h0, prefix, text_len, ln1_gain, ln1_shift, qkv_w, query_bias, value_bias,
                                            out_w, out_b, ln2_gain, ln2_shift, ex, n_image, pad)
    mlp_outs = mlp(place, z2, h1, cotangent, up_w, up_b, down_w, down_b, ln2_gain, pad, dp, parted)
    block_out, mlp_grads, (g1, veca) = mlp_outs[0], mlp_outs[1:-2], mlp_outs[-2:]
    if parted:
        bits = jnp.stack([bit_of(n) for n in BITS]).astype(jnp.int32)
        down, up = Pack.start(*mlp_grads[:2]), Pack.start(*mlp_grads[2:])
    back_args = (out_w, attn, q, k, v, p, z1, h0, qkv_w, ln1_gain, ex, n_image, txt, rows, cols, pad, dp, parted)
    if parted:
        carry = attn_bwd(place, g1, *back_args, hi=1)
        turns = [["space"], ["near"], ["f0"]]
        ffn = down.thirds() + up.thirds()
        g1, ffn = step(bits, list(zip(ffn, turns + turns)), tie(g1, *carry)[0])
        att_outs = attn_bwd(place, g1, *back_args, lo=1, carry=carry, stem=stem)
    else:
        att_outs = attn_bwd(place, g1, *back_args)
    att_grads, (text_grad, dtok, vecb) = att_outs[:-3], att_outs[-3:]
    if parted:
        later = turns[1:] + turns[:1]
        (dtok, att_send), ffn = step(bits, list(zip(ffn, later * 2)), (dtok, att_grads[1]))
        att = Pack.start(att_grads[0], att_send)
    dpre, dsend, parts4 = call(
        functools.partial(dpre_kernel, count, ex, rows),
        [((ex, rows, 16, chan), F32), ((ex, band_rows, 16, chan), BF16), (large, F32)],
        parts3, act3, xs, bn3_gain, bn3_shift, dtok, proj_w, moved=(parts3,), place=place, name="stem_back", us=7)
    got_d = swap(dsend)
    if parted:
        parts4 = arrive(parts4, *ffn, att)
    parts4 = spread(parts4)
    if parted:
        later = later[1:] + later[:1]
        dpre, moved = step(bits, list(zip(ffn, later * 2)) + list(zip(att.thirds(), later)), dpre)
        ffn, att = moved[:6], moved[6:]
    else:
        proj_g = call(functools.partial(tn_kernel, parted), grad_outs(width, chan), dtok, stem, place=place, name="proj_grad", us=0)
    low3, t2, parts5, bn3_gg, bn3_sg = call(
        functools.partial(back3_kernel, count, cols),
        [((ex * px, chan), BF16), ((ex * px, mid), F32), (small, F32), ((chan,), F32), ((chan,), F32)],
        parts4, parts3, parts2, act3, dpre, bn3_gain, conv_out_w, act2, bn2_gain, bn2_shift, veca, vecb, moved=(parts4, parts3, parts2),
        scratch=[pltpu.VMEM((n_dev * -(-(veca.shape[0] + vecb.shape[0]) // n_dev), 128), F32)], name="back_three", us=4)
    if parted:
        t2 = arrive(t2, *att)
    parts5 = spread(parts5)
    if parted:
        later = later[1:] + later[:1]
        t2, moved = step(bits, [(x, ["f1"]) for x in ffn] + list(zip(att, later)), t2)
        ffn, att = moved[:6], moved[6:]
    low2, t1, tsend, parts6, bn2_gg, bn2_sg = call(
        functools.partial(back2_kernel, count, ex, rows, cols),
        [((ex * px, mid), BF16), ((ex, rows, 16, mid), F32), ((ex, band_rows, 16, mid), BF16), (small, F32), ((mid,), F32), ((mid,), F32)],
        parts5, parts2, parts1, act2, t2, bn2_gain, wmid, act1, bn1_gain, bn1_shift,
        moved=(parts5, parts2, parts1), place=place, scratch=[pltpu.VMEM((ex, px + 32, 3 * mid), BF16)], name="back_two", us=4)
    got_t = swap(tsend)
    parts6 = spread(parts6)
    if parted:
        low2, got_t = arrive(tie(low2, got_t), *att)
    conv_g = call(
        functools.partial(conv_grads_kernel, ex, px, parted),
        [(part_shape(mid, 9 * mid, dp)[:2] + (part_shape(mid, 9 * mid, dp)[2] + part_shape(chan, mid, dp)[2], 128), BF16)] * 2
        if parted else [((mid, 9 * mid), BF16), ((chan, mid), BF16)],
        low2, wide, low3, relu2, place=place, scratch=natural(mid, 9 * mid) + natural(chan, mid), name="conv_grads", us=4)
    if parted:
        parts6, conv_send = arrive(tie(parts6, conv_g[1]), *ffn, *att)
        conv = Pack.start(conv_g[0], conv_send)
    each = -(-(veca.shape[0] + vecb.shape[0]) // n_dev)
    n, off = width // 128, veca.shape[0]
    places = [off, off + n, off + 2 * n, off + 3 * n, off + 4 * n, 3 * n, n, 2 * n, 4 * n, 0]
    sizes = [width] * 8 + [ff, width]
    last = call(
        functools.partial(first_back_kernel, count, ex, rows, cols, parted, each, places),
        [((2, ex * band_rows * 16, mid), BF16)] + grad_outs(mid, chan) + [((mid,), F32)] * 2 + [((s,), F32) for s in sizes],
        parts6, parts1, image_in, conv_in_w, bn1_gain, t1, got_t,
        moved=(parts6, parts1, got_t), place=place, scratch=[pltpu.VMEM((ex * band_rows, 16, chan), BF16), pltpu.VMEM((n_dev * each, 128), F32)] + natural(mid, chan),
        name="first_back", us=3)
    low1, sums = last[0], last[3 if parted else 2 :]
    bn1_gg, bn1_sg, vecs = sums[0], sums[1], sums[2:]
    if parted:
        later = later[1:] + later[:1]
        (low1, keep_x), moved = step(bits, list(zip(att, later)) + [(conv, ["near", "space"])], (low1, last[1]))
        att, conv = moved[:3], moved[3]
    image_grad, = call(functools.partial(image_kernel, ex, rows, cols), [(image_in.shape, BF16)], low1, conv_in_w, dpre, got_d,
                       moved=(got_d,), place=place, name="image_back", us=4)
    if parted:
        in_x = (keep_x + swap(last[2], "core")).reshape((2 * hi,) + keep_x.shape[2:])
        in_x = lax.all_to_all(in_x, ("space", "far", "near"), split_axis=0, concat_axis=0, tiled=True)
        image_grad, moved = step(bits, [(x, ["f1"]) for x in att] + [(conv, ["f1", "f0"])], image_grad)
        att, conv = moved[:3], moved[3]
        r_mid, r_out3, r_q, r_w, r_f = mid // dp, chan // dp, 3 * width // dp, width // dp, ff // dp
        mids, half = r_mid * (9 * mid // 256), width // 256
        g_down, g_up = finish(
            [(ffn[0].sources, [(0, r_w, ff // 256, 0)]), (ffn[3].sources, [(0, r_f, half, 1)])],
            [(r_w, ff // 2), (r_f, width // 2)], "finish_early")
        g_qkv, g_out, g_proj, g_mid, g_out3, g_in = finish(
            [(att[0].sources, [(0, r_q, half, 0), (r_q * half, r_w, half, 1), ((r_q + r_w) * half, r_w, chan // 256, 2)]),
             (conv.sources, [(0, r_mid, 9 * mid // 256, 3), (mids, r_out3, mid // 256, 4)]),
             ([(Box(in_x), 0)], [(0, r_mid, chan // 256, 5)])],
            [(r_q, width // 2), (r_w, width // 2), (r_w, chan // 2), (9 * mid // 256, r_mid, 128), (r_out3, mid // 2), (r_mid, chan // 2)], "finish_late")
        g_down, g_up, g_qkv, g_out, g_proj, g_out3, g_in = [g.T for g in (g_down, g_up, g_qkv, g_out, g_proj, g_out3, g_in)]
        g_mid = g_mid.reshape(3, 3, r_mid, mid // 2).transpose(0, 1, 3, 2)
    else:
        out_n = att_outs[0].transpose(1, 0, 2).reshape(width, width)
        g_in, g_mid, g_out3, g_proj, g_qkv, g_out, g_up, g_down = [
            scattered(x) for x in (last[1], conv_g[0], conv_g[1], proj_g[0], att_outs[1], out_n, mlp_grads[1], mlp_grads[0])]
        g_mid = g_mid.reshape(3, 3, mid // 2, -1)
    return (
        block_out, image_grad, text_grad,
        g_in, bn1_gg, bn1_sg,
        g_mid, bn2_gg, bn2_sg,
        g_out3, bn3_gg, bn3_sg,
        g_proj, vecs[0], vecs[1], vecs[2],
        g_qkv, vecs[3], vecs[4],
        g_out, vecs[5], vecs[6], vecs[7],
        g_up, vecs[8],
        g_down, vecs[9],
    )


def solution(mesh):
    dp, space = mesh.devices.shape
    fine = Mesh(mesh.devices.reshape(dp // 4, 2, 2, space), AXES)
    return jax.shard_map(
        shards,
        mesh=fine,
        in_specs=(
            P(DP, "space", None, None),
            P(AXES, None, None),
            P(AXES),
            P(AXES),
            P(AXES, None, None),
            P(),
            P(),
            P(),
            P(),
            P(),
            P(),
            P(),
            P(),
            P(),
            P(),
            P(),
            P(),
            P(),
            P(),
            P(),
            P(),
            P(),
            P(),
            P(),
            P(),
            P(),
            P(),
            P(),
            P(),
        ),
        out_specs=(
            P(AXES, None, None),
            P(DP, "space", None, None),
            P(AXES, None, None),
            P("space", DP),
            P(),
            P(),
            P(None, None, "space", DP),
            P(),
            P(),
            P("space", DP),
            P(),
            P(),
            P("space", DP),
            P(),
            P(),
            P(),
            P("space", DP),
            P(),
            P(),
            P("space", DP),
            P(),
            P(),
            P(),
            P("space", DP),
            P(),
            P("space", DP),
            P(),
        ),
        check_vma=False,
    )
```

```python
import functools
import jax
import jax.numpy as jnp
from jax import lax
from jax.experimental import pallas as pl
from jax.experimental.pallas import tpu as pltpu
from jax.sharding import Mesh, PartitionSpec as P

HD = 64
F32 = jnp.float32
BF16 = jnp.bfloat16
eps_batch = 1e-05
eps_layer = 1e-06
masked_value = -1e30
GELU_C = 0.7978845608028654
GELU_A = 0.044715


def nn(a, b):
    return lax.dot_general(a, b, (((1,), (0,)), ((), ())), preferred_element_type=F32)


def nt(a, b):
    return lax.dot_general(a, b, (((1,), (1,)), ((), ())), preferred_element_type=F32)


def tn(a, b):
    return lax.dot_general(a, b, (((0,), (0,)), ((), ())), preferred_element_type=F32)


def gelu_of(x):
    t = jnp.tanh(GELU_C * (x + GELU_A * x * x * x))
    return 0.5 * x * (1.0 + t)


def gelu_and_slope(x):
    x2 = x * x
    t = jnp.tanh(x * (GELU_C + (GELU_C * GELU_A) * x2))
    half = 0.5 + 0.5 * t
    slope = half + (0.5 * x) * (1.0 - t * t) * (GELU_C + (3.0 * GELU_C * GELU_A) * x2)
    return x * half, slope


def ln_parts(x):
    mean = jnp.mean(x, axis=-1, keepdims=True)
    c = x - mean
    var = jnp.mean(c * c, axis=-1, keepdims=True)
    r = lax.rsqrt(var + eps_layer)
    return c * r, r


def ln_back(dz, nrm, r, gain):
    u = dz * gain
    return r * (u - jnp.mean(u, axis=-1, keepdims=True) - nrm * jnp.mean(u * nrm, axis=-1, keepdims=True))


def whole(shape):
    return pl.BlockSpec(shape, lambda *_: (0,) * len(shape), pipeline_mode=pl.Buffered(1))


SMEM = pl.BlockSpec(memory_space=pltpu.SMEM)
VMEM = pl.BlockSpec(memory_space=pltpu.VMEM)


def row_of(ref):
    return ref[...].reshape(1, -1)


def put_rows(ref, at, vector):
    for r in range(vector.shape[1] // 128):
        ref[at + r : at + r + 1, :] = vector[:, r * 128 : (r + 1) * 128]


def take_rows(ref, at, size):
    return jnp.concatenate([ref[at + r : at + r + 1, :] for r in range(size // 128)], axis=1)


def part_shape(cols, rows, dp):
    return (2, dp // 2, cols // dp * (rows // 2) // 128, 128)


def part_it(natural, keep_ref, send_ref, core, at=0):
    rows, cols = natural.shape[-2:]
    hi = keep_ref.shape[1]
    r, blocks = rows // (2 * hi), cols // 256

    def one(h, carry):
        mine = pl.ds(pl.multiple_of((2 * h + core) * r, 16), r)
        other = pl.ds(pl.multiple_of((2 * h + 1 - core) * r, 16), r)
        for s in range(2):
            for b in range(blocks):
                lanes = slice((s * blocks + b) * 128, (s * blocks + b + 1) * 128)
                keep_ref[s, h, at + b * r : at + (b + 1) * r, :] = natural[mine, lanes]
                send_ref[s, h, at + b * r : at + (b + 1) * r, :] = natural[other, lanes]
        return carry

    lax.fori_loop(0, hi, one, 0)


def mlp_kernel(ex, seq, pad, parted, place_ref, z2_ref, h1_ref, cot_ref, upw_ref, upb_ref, dnw_ref, dnb_ref, g_ref, *refs):
    if parted:
        out_ref, dk_ref, ds_ref, uk_ref, us_ref, g1_ref, vec_ref, g2_s, g2t_s, acc_o, acc_d, ub_s, bg_s = refs
    else:
        out_ref, dn_ref, up_ref, g1_ref, vec_ref, g2_s, g2t_s, acc_o, acc_d, ub_s, bg_s = refs
    i = pl.program_id(0)
    last = pl.num_programs(0) - 1
    tile = upw_ref.shape[1]

    @pl.when(i == 0)
    def _():
        g2_s[...] = jnp.zeros_like(g2_s)
        for e in range(ex):
            g2_s[e * pad : e * pad + seq, :] = cot_ref[e]
        g2t_s[...] = g2_s[...].T
        acc_o[...] = jnp.zeros_like(acc_o)
        acc_d[...] = jnp.zeros_like(acc_d)
        ub = row_of(upb_ref)
        for j in range(ub_s.shape[0]):
            ub_s[j] = ub[:, j * tile : (j + 1) * tile]

    z2 = z2_ref[...]
    g2 = g2_s[...]
    pre = nn(z2, upw_ref[...]) + ub_s[i]
    act, slope = gelu_and_slope(pre)
    low = act.astype(BF16)
    dg = (nt(g2, dnw_ref[...]) * slope).astype(BF16)
    acc_o[...] += nn(low, dnw_ref[...])
    acc_d[...] += nt(dg, upw_ref[...])
    dn = nn(g2t_s[...], low).astype(BF16)
    up = tn(dg, z2).astype(BF16)
    bg_s[i] = jnp.sum(dg.astype(F32), axis=0, keepdims=True)
    if parted:
        core = place_ref[1]
        even = core == 0
        hi = dk_ref.shape[1]
        r = dn.shape[0] // (2 * hi)
        for j in range(tile // 128):
            d4 = dn[:, j * 128 : (j + 1) * 128].reshape(hi, 2, r, 128)
            dk_ref[0, :, j * r : (j + 1) * r, :] = jnp.where(even, d4[:, 0], d4[:, 1])
            ds_ref[0, :, j * r : (j + 1) * r, :] = jnp.where(even, d4[:, 1], d4[:, 0])
        r, blocks = up.shape[0] // 4, up.shape[1] // 256
        for s in range(2):
            for j in range(blocks):
                lanes = slice((s * blocks + j) * 128, (s * blocks + j + 1) * 128)
                for t in range(2):
                    first, second = up[2 * t * r : (2 * t + 1) * r, lanes], up[(2 * t + 1) * r : (2 * t + 2) * r, lanes]
                    uk_ref[s, t, j * r : (j + 1) * r, :] = jnp.where(even, first, second)
                    us_ref[s, t, j * r : (j + 1) * r, :] = jnp.where(even, second, first)
    else:
        dn_ref[...] = dn
        up_ref[...] = up

    @pl.when(i == last)
    def _():
        h1 = h1_ref[...]
        out = (h1 + acc_o[...] + row_of(dnb_ref)).astype(BF16)
        for e in range(ex):
            out_ref[e] = out[e * pad : e * pad + seq, :]
        nrm, r = ln_parts(h1)
        dz = acc_d[...]
        gf = g2_s[...].astype(F32)
        g1 = gf + ln_back(dz, nrm, r, row_of(g_ref))
        g1_ref[...] = g1
        n = g1.shape[1] // 128
        for j, v in enumerate((col_sum(gf), col_sum(dz * nrm), col_sum(dz), col_sum(g1))):
            put_rows(vec_ref, j * n, v)
        for j in range(bg_s.shape[0]):
            put_rows(vec_ref, 4 * n + j * (tile // 128), bg_s[j])


def mlp(place, z2, h1, cot, up_w, up_b, down_w, down_b, gain, pad, dp, parted):
    ex, seq, width = cot.shape
    rows = z2.shape[0]
    ff = up_w.shape[1]
    tile = 4 * ff // dp if parted else 384
    steps = ff // tile
    vec_rows = 4 * width // 128 + ff // 128
    if parted:
        dn, up = part_shape(width, ff, dp), part_shape(ff, width, dp)
        per_half = steps // 2
        dn_spec = pl.BlockSpec((1, dn[1], dn[2] // per_half, 128), lambda i: (i // per_half, 0, i % per_half, 0))
        up_spec = pl.BlockSpec((2, 2, up[2], 128), lambda i: (0, i, 0, 0))
        grads = [(dn, dn_spec), (dn, dn_spec), (up, up_spec), (up, up_spec)]
    else:
        grads = [((width, ff), pl.BlockSpec((width, tile), lambda i: (0, i))),
                 ((ff, width), pl.BlockSpec((tile, width), lambda i: (i, 0)))]
    outs = [((ex, seq, width), whole((ex, seq, width)), BF16)] + [(s, b, BF16) for s, b in grads]
    outs += [((rows, width), whole((rows, width)), F32), ((vec_rows, 128), whole((vec_rows, 128)), F32)]
    return pl.pallas_call(
        functools.partial(mlp_kernel, ex, seq, pad, parted),
        grid=(steps,),
        in_specs=[
            SMEM, whole((rows, width)), whole((rows, width)), whole((ex, seq, width)),
            pl.BlockSpec((width, tile), lambda i: (0, i)), whole((ff,)),
            pl.BlockSpec((tile, width), lambda i: (i, 0)),
            whole((width,)), whole((width,)),
        ],
        out_specs=[b for _, b, _ in outs],
        out_shape=[pltpu.HBM(s, d) for s, _, d in outs],
        scratch_shapes=[
            pltpu.VMEM((rows, width), BF16), pltpu.VMEM((width, rows), BF16),
            pltpu.VMEM((rows, width), F32), pltpu.VMEM((rows, width), F32),
            pltpu.VMEM((steps, 1, tile), F32), pltpu.VMEM((steps, 1, tile), F32),
        ],
        compiler_params=pltpu.CompilerParams(dimension_semantics=("arbitrary",), vmem_limit_bytes=44 << 20),
        cost_estimate=pl.CostEstimate(flops=46 * 10**9, bytes_accessed=30 << 20, transcendentals=rows * ff),
        name="mlp_both_ways",
    )(place, *[in_hbm(x) for x in (z2, h1, cot, up_w, up_b, down_w, down_b, gain)])


def stat_rows(channels):
    return max(8, 2 * channels // 128)


def put_stats(ref, first, second):
    lanes = jnp.concatenate([first, second], axis=1)
    n = ref.shape[0]
    for r in range(lanes.shape[1] // 128):
        ref[:, r, :] = jnp.broadcast_to(lanes[:, r * 128 : (r + 1) * 128], (n, 128))


def get_stats(ref, channels):
    total = jnp.sum(ref[...], axis=0)
    rows = 2 * channels // 128
    half = rows // 2
    first = jnp.concatenate([total[r : r + 1, :] for r in range(half)], axis=1)
    second = jnp.concatenate([total[r : r + 1, :] for r in range(half, rows)], axis=1)
    return first, second


def mean_rstd(ref, channels, count):
    s1, s2 = get_stats(ref, channels)
    mean = s1 * (1.0 / count)
    return mean, lax.rsqrt(s2 * (1.0 / count) - mean * mean + eps_batch)


def real_columns(rows, cols):
    return (lax.broadcasted_iota(jnp.int32, (rows, 1), 0) & 15) < cols


def col_sum(x):
    return jnp.sum(x, axis=0, keepdims=True)


def row_blocks(rows):
    starts = list(range(0, rows - 63, 64))
    return [(a, b) for a, b in zip(starts, starts[1:] + [rows])]


def head_mask(rows, second):
    lane = lax.broadcasted_iota(jnp.int32, (rows, 2 * HD), 1)
    return (lane >= HD) if second else (lane < HD)


def attn_fwd_kernel(ex, n_image, pad, pre_ref, len_ref, h0_ref, g_ref, s_ref, wq_ref, wk_ref, wv_ref, qb_ref, vb_ref,
                    ow_ref, ob_ref, g2_ref, s2_ref,
                    z1_ref, q_ref, k_ref, v_ref, p_ref, attn_ref, h1_ref, z2_ref, acc, qb_s, vb_s):
    i = pl.program_id(0)
    last = pl.num_programs(0) - 1
    wide = wq_ref.shape[1]

    @pl.when(i == 0)
    def _():
        nrm, _r = ln_parts(h0_ref[...].astype(F32))
        z1_ref[...] = (nrm * row_of(g_ref) + row_of(s_ref)).astype(BF16)
        acc[...] = jnp.zeros_like(acc)
        qb, vb = row_of(qb_ref), row_of(vb_ref)
        for j in range(qb_s.shape[0]):
            qb_s[j] = qb[:, j * wide : (j + 1) * wide]
            vb_s[j] = vb[:, j * wide : (j + 1) * wide]

    z1 = z1_ref[...]
    q_ref[...] = (nn(z1, wq_ref[...]) + qb_s[i]).astype(BF16)
    k_ref[...] = nn(z1, wk_ref[...]).astype(BF16)
    v_ref[...] = (nn(z1, wv_ref[...]) + vb_s[i]).astype(BF16)
    zero = jnp.zeros((pad, 2 * HD), BF16)
    first = head_mask(pad, False)

    def example(e, carry):
        row0 = pl.multiple_of(e * pad, 16)
        key = lax.broadcasted_iota(jnp.int32, (pad, pad), 1)
        qry = lax.broadcasted_iota(jnp.int32, (pad, pad), 0)
        limit = jnp.maximum(qry + 1, n_image + pre_ref[e])
        limit = jnp.minimum(limit, n_image + len_ref[e])
        vis = key < limit
        for pair in range(wide // (2 * HD)):
            cols = slice(pair * 2 * HD, (pair + 1) * 2 * HD)
            q2 = q_ref[pl.ds(row0, pad), cols] * jnp.asarray(0.125, BF16)
            k2 = k_ref[pl.ds(row0, pad), cols]
            v2 = v_ref[pl.ds(row0, pad), cols]
            out = None
            for h in range(2):
                sel = first if h == 0 else jnp.logical_not(first)
                raw = nt(jnp.where(sel, q2, zero), k2)
                for lo, up in row_blocks(pad):
                    sc = jnp.where(vis[lo:up], raw[lo:up], masked_value)
                    top = jnp.max(sc, axis=-1, keepdims=True)
                    ex_ = jnp.exp(sc - top)
                    tot = jnp.sum(ex_, axis=-1, keepdims=True)
                    p_ref[e, pair * 2 + h, lo:up, :] = (ex_ * (1.0 / tot)).astype(BF16)
                o = nn(p_ref[e, pair * 2 + h], jnp.where(sel, v2, zero))
                out = o if out is None else out + o
            attn_ref[pl.ds(row0, pad), cols] = out.astype(BF16)
        return carry

    lax.fori_loop(0, ex, example, 0)
    acc[...] += nn(attn_ref[...], ow_ref[...])

    @pl.when(i == last)
    def _():
        h1 = h0_ref[...].astype(F32) + acc[...] + row_of(ob_ref)
        h1_ref[...] = h1
        nrm, _r = ln_parts(h1)
        z2_ref[...] = (nrm * row_of(g2_ref) + row_of(s2_ref)).astype(BF16)


def attn_fwd(h0, prefix, text_len, ln1_gain, ln1_shift, qkv_w, qb, vb, out_w, out_b, ln2_gain, ln2_shift, ex, n_image, pad, wide=256):
    rows, width = h0.shape
    groups = width // wide
    heads = width // HD
    hg = wide // HD
    cols = lambda off: pl.BlockSpec((width, wide), lambda i, *_: (0, i + off * groups))
    vec = whole((width,))
    part = pl.BlockSpec((rows, wide), lambda i, *_: (0, i))
    return pl.pallas_call(
        functools.partial(attn_fwd_kernel, ex, n_image, pad),
        grid_spec=pltpu.PrefetchScalarGridSpec(
            num_scalar_prefetch=2,
            grid=(groups,),
            in_specs=[whole((rows, width)), vec, vec, cols(0), cols(1), cols(2), vec, vec,
                      pl.BlockSpec((wide, width), lambda i, *_: (i, 0)), vec, vec, vec],
            out_specs=[whole((rows, width)), part, part, part,
                       pl.BlockSpec((ex, hg, pad, pad), lambda i, *_: (0, i, 0, 0)),
                       part, whole((rows, width)), whole((rows, width))],
            scratch_shapes=[pltpu.VMEM((rows, width), F32)] + [pltpu.VMEM((groups, 1, wide), F32)] * 2,
        ),
        out_shape=[pltpu.HBM((rows, width), BF16)] * 4 + [
            pltpu.HBM((ex, heads, pad, pad), BF16),
            pltpu.HBM((rows, width), BF16),
            pltpu.HBM((rows, width), F32),
            pltpu.HBM((rows, width), BF16)],
        compiler_params=pltpu.CompilerParams(dimension_semantics=("arbitrary",), vmem_limit_bytes=40 << 20),
        cost_estimate=pl.CostEstimate(flops=32 * 10**9, bytes_accessed=30 << 20, transcendentals=heads * rows * pad),
        name="attention_forward",
    )(prefix, text_len, *[in_hbm(x) for x in (h0, ln1_gain, ln1_shift, qkv_w, qkv_w, qkv_w, qb, vb, out_w, out_b, ln2_gain, ln2_shift)])


def attn_bwd_kernel(ex, n_image, txt, cols_real, pad, parted, lo, final, place_ref, g1_ref, ow_ref, attn_ref, q_ref, k_ref, v_ref, p_ref, z1_ref, wq_ref, wk_ref, wv_ref, *refs):
    if lo:
        acc_c, ow_c, qkv_c, bias_c = refs[:4]
        refs = refs[4:]
    if not final:
        acc, ow_s, qkv_s, bias_s = refs[:4]
        g1b_s, g1t_s, dat_s, dq_s, dk_s, dv_s = refs[4:]
    else:
        h0_ref, g_ref, refs = refs[0], refs[1], refs[2:]
        if parted:
            stem_ref, ak_ref, as_ref, text_ref, dtok_ref, vec_ref, ow_s, qkv_s, proj_s = refs[:9]
        else:
            ow_s, qkv_s, text_ref, dtok_ref, vec_ref = refs[:5]
        g1b_s, g1t_s, dat_s, dq_s, dk_s, dv_s, acc, bias_s = refs[-8:]
    i = pl.program_id(0)
    last = pl.num_programs(0) - 1
    wide = wq_ref.shape[1]

    @pl.when(i == 0)
    def _():
        g1b_s[...] = g1_ref[...].astype(BF16)
        g1t_s[...] = g1b_s[...].T
        if lo:
            acc[...] = acc_c[...]
            ow_s[0:lo] = ow_c[...]
            bias_s[:, 0:lo] = bias_c[...]
            for j in range(3):
                qkv_s[j * z1_ref.shape[1] : j * z1_ref.shape[1] + lo * wide, :] = qkv_c[j]
        else:
            acc[...] = jnp.zeros_like(acc)

    gi = i + lo
    ow_s[gi] = nn(g1t_s[...], attn_ref[...]).astype(BF16)
    dat_s[...] = nt(g1b_s[...], ow_ref[...]).astype(BF16)
    zero = jnp.zeros((pad, 2 * HD), BF16)
    first = head_mask(pad, False)

    def example(e, carry):
        row0 = pl.multiple_of(e * pad, 16)
        for pair in range(wide // (2 * HD)):
            cols = slice(pair * 2 * HD, (pair + 1) * 2 * HD)
            q2 = q_ref[pl.ds(row0, pad), cols]
            k2 = k_ref[pl.ds(row0, pad), cols]
            v2 = v_ref[pl.ds(row0, pad), cols]
            da2 = dat_s[pl.ds(row0, pad), cols]
            dq = dk = dv = None
            for h in range(2):
                sel = first if h == 0 else jnp.logical_not(first)
                pb = p_ref[e, pair * 2 + h]
                dah = jnp.where(sel, da2, zero)
                whole_dp = nt(dah, v2)
                parts = []
                for first_row, end_row in row_blocks(pad):
                    p = pb[first_row:end_row].astype(F32)
                    dp = whole_dp[first_row:end_row]
                    inner = jnp.sum(p * dp, axis=-1, keepdims=True)
                    parts.append((p * (dp - inner)).astype(BF16))
                ds = jnp.concatenate(parts, axis=0)
                dvh = tn(pb, dah)
                dqh = nn(ds, jnp.where(sel, k2, zero))
                dkh = tn(ds, jnp.where(sel, q2, zero))
                dq = dqh if dq is None else dq + dqh
                dk = dkh if dk is None else dk + dkh
                dv = dvh if dv is None else dv + dvh
            dq_s[pl.ds(row0, pad), cols] = (dq * 0.125).astype(BF16)
            dk_s[pl.ds(row0, pad), cols] = (dk * 0.125).astype(BF16)
            dv_s[pl.ds(row0, pad), cols] = dv.astype(BF16)
        return carry

    lax.fori_loop(0, ex, example, 0)
    z1 = z1_ref[...]
    dq, dk, dv = dq_s[...], dk_s[...], dv_s[...]
    width = z1.shape[1]
    for j, d in enumerate((dq, dk, dv)):
        if final:
            qkv_s[pl.ds(pl.multiple_of(j * width + gi * wide, wide), wide), :] = tn(d, z1).astype(BF16)
        else:
            qkv_s[j] = tn(d, z1).astype(BF16)
    acc[...] += nt(dq, wq_ref[...]) + nt(dk, wk_ref[...]) + nt(dv, wv_ref[...])
    bias_s[0, gi] = col_sum(dq.astype(F32))
    bias_s[1, gi] = col_sum(dv.astype(F32))

    if not final:
        return

    @pl.when(i == last)
    def _():
        nrm, r = ln_parts(h0_ref[...].astype(F32))
        dz = acc[...]
        g0 = g1_ref[...] + ln_back(dz, nrm, r, row_of(g_ref))
        n = width // 128
        vec_ref[5 * n :, :] = jnp.zeros_like(vec_ref[5 * n :, :])
        put_rows(vec_ref, n, col_sum(dz * nrm))
        put_rows(vec_ref, 2 * n, col_sum(dz))
        for j in range(2):
            for t in range(bias_s.shape[1]):
                put_rows(vec_ref, (3 + j) * n + t * (wide // 128), bias_s[j, t])
        gb = g0.astype(BF16)
        px = dtok_ref.shape[0] // ex
        pick_image = image_pick(px, pad, n_image, cols_real)
        tr = lax.broadcasted_iota(jnp.int32, (txt, pad), 0)
        tc = lax.broadcasted_iota(jnp.int32, (txt, pad), 1)
        pick_text = jnp.where(tc == tr + n_image, 1.0, 0.0).astype(BF16)
        tot = jnp.zeros((1, gb.shape[1]), F32)
        for e in range(ex):
            ge = gb[e * pad : (e + 1) * pad, :]
            text_ref[e] = nn(pick_text, ge).astype(BF16)
            dt = nn(pick_image, ge)
            dtok_ref[e * px : (e + 1) * px, :] = dt.astype(BF16)
            tot = tot + jnp.sum(dt, axis=0, keepdims=True)
        put_rows(vec_ref, 0, tot)
        if parted:
            core = place_ref[1]
            part_it(qkv_s, ak_ref, as_ref, core)
            proj_s[...] = tn(dtok_ref[...], stem_ref[...]).astype(BF16)
            part_it(proj_s, ak_ref, as_ref, core, at=(qkv_s.shape[0] + width) // (2 * ak_ref.shape[1]) * (width // 256))
            hi = ak_ref.shape[1]
            r = width // (2 * hi)
            at = qkv_s.shape[0] // (2 * hi) * (width // 256)

            def one(h, carry):
                mine = pl.ds(pl.multiple_of((2 * h + core) * r, 16), r)
                other = pl.ds(pl.multiple_of((2 * h + 1 - core) * r, 16), r)
                for blk in range(width // 128):
                    s, j = divmod(blk, width // 256)
                    t, lane = divmod(blk * 128, wide)
                    dst = slice(at + j * r, at + (j + 1) * r)
                    ak_ref[s, h, dst, :] = ow_s[t, mine, lane : lane + 128]
                    as_ref[s, h, dst, :] = ow_s[t, other, lane : lane + 128]
                return carry

            lax.fori_loop(0, hi, one, 0)


def image_pick(px, pad, n_image, cols_real):
    p = lax.broadcasted_iota(jnp.int32, (px, pad), 0)
    t = lax.broadcasted_iota(jnp.int32, (px, pad), 1)
    col = p & 15
    tok = (p >> 4) * cols_real + col
    return jnp.where((col < cols_real) & (tok == t) & (t < n_image), 1.0, 0.0).astype(BF16)


def attn_bwd(place, g1, out_w, attn, q, k, v, p, z1, h0, qkv_w, ln1_gain, ex, n_image, txt, img_rows, img_cols, pad, dp, parted,
             lo=0, hi=None, carry=(), stem=None, wide=256):
    rows, width = h0.shape
    groups = width // wide
    heads = width // HD
    hg = wide // HD
    px = img_rows * 16
    hi = groups if hi is None else hi
    final = hi == groups
    vec_rows = -(-5 * width // 128 // 8) * 8
    cols = lambda off: pl.BlockSpec((width, wide), lambda i: (0, i + lo + off * groups))
    part = pl.BlockSpec((rows, wide), lambda i: (0, i + lo))
    nat_o, nat_q = (groups, width, wide), (3 * width, width)
    sent = part_shape(4 * width, width, dp)
    if stem is not None:
        sent = sent[:2] + (sent[2] + part_shape(width, stem.shape[1], dp)[2], 128)
    scratch = [pltpu.VMEM((rows, width), BF16), pltpu.VMEM((width, rows), BF16)] + [pltpu.VMEM((rows, wide), BF16)] * 4
    args = [g1, out_w, attn, q, k, v, p, z1, qkv_w, qkv_w, qkv_w, *carry]
    in_specs = [SMEM, whole((rows, width)), pl.BlockSpec((wide, width), lambda i: (i + lo, 0)), part, part, part, part,
                pl.BlockSpec((ex, hg, pad, pad), lambda i: (0, i + lo, 0, 0)), whole((rows, width)), cols(0), cols(1), cols(2)]
    in_specs += [whole(c.shape) for c in carry]
    if final:
        outs = [(s, BF16) for s in ((sent, sent) if parted else (nat_o, nat_q))]
        outs += [((ex, txt, width), BF16), ((ex * px, width), BF16), ((vec_rows, 128), F32)]
        natural = [pltpu.VMEM(nat_o, BF16), pltpu.VMEM(nat_q, BF16), pltpu.VMEM((width, stem.shape[1]), BF16)] if parted else []
        scratch = natural + scratch + [pltpu.VMEM((rows, width), F32), pltpu.VMEM((2, groups, 1, wide), F32)]
        args += [h0, ln1_gain] + ([stem] if parted else [])
        in_specs += [whole((rows, width)), whole((width,))] + ([whole(stem.shape)] if parted else [])
    else:
        n = hi - lo
        outs = [((rows, width), F32), ((n, width, wide), BF16), ((3, n * wide, width), BF16), ((2, n, 1, wide), F32)]
    return pl.pallas_call(
        functools.partial(attn_bwd_kernel, ex, n_image, txt, img_cols, pad, parted, lo, final),
        grid=(hi - lo,),
        in_specs=in_specs,
        out_specs=[whole(s) for s, _ in outs],
        out_shape=[pltpu.HBM(s, d) for s, d in outs],
        scratch_shapes=scratch,
        compiler_params=pltpu.CompilerParams(dimension_semantics=("arbitrary",), vmem_limit_bytes=60 << 20),
        cost_estimate=pl.CostEstimate(flops=14 * (hi - lo) * 10**9, bytes_accessed=40 << 20, transcendentals=0),
        name="attention_backward",
    )(place, *[in_hbm(x) for x in args])

def over_pixels(shape, body, init=0):
    ex, rows = shape[:2]
    per = rows // 2

    def one(j, carry):
        return body(j // per, j % per * 2, pl.ds(pl.multiple_of(j * 32, 32), 32), carry)

    return lax.fori_loop(0, ex * per, one, init)


def stats_kernel(cols, x_ref, w_ref, parts_ref, xp):
    xp[...] = jnp.zeros_like(xp)
    shape = x_ref.shape
    xp[:, 0:cols, :] = x_ref[...].reshape(shape[0] * shape[1], cols, shape[3])
    a = nn(xp[...].reshape(shape[0] * shape[1] * 16, shape[3]), w_ref[...])
    put_stats(parts_ref, col_sum(a), col_sum(a * a))


def conv_fwd_kernel(count, ex, rows, cols, place_ref, parts_ref, own_ref, got_ref, win_ref, g_ref, s_ref, wmid_ref,
                    xs_ref, act1_ref, wide_ref, act2_ref, parts2_ref):
    s = place_ref[0]
    half = rows // 2
    px = rows * 16
    chan = xs_ref.shape[-1]
    xs_ref[...] = jnp.zeros_like(xs_ref)
    for e in range(ex):
        xs_ref[e, pl.ds(s * half, half), 0:cols, :] = own_ref[s * ex + e]
        xs_ref[e, pl.ds((1 - s) * half, half), 0:cols, :] = got_ref[e]
    a1 = nn(xs_ref[...].reshape(ex * px, chan), win_ref[...])
    act1_ref[...] = a1
    mid = a1.shape[1]
    mean, rstd = mean_rstd(parts_ref, mid, count)
    real = real_columns(ex * px, cols)
    act = gelu_of((a1 - mean) * rstd * row_of(g_ref) + row_of(s_ref))
    act = jnp.where(real, act, 0.0)
    for e in range(ex):
        part = act[e * px : (e + 1) * px]
        wide_ref[e, 0:16, :] = jnp.zeros((16, 3 * mid), BF16)
        wide_ref[e, px + 16 : px + 32, :] = jnp.zeros((16, 3 * mid), BF16)
        wide_ref[e, 16 : px + 16, 0:mid] = pltpu.roll(part, 1, 0).astype(BF16)
        wide_ref[e, 16 : px + 16, mid : 2 * mid] = part.astype(BF16)
        wide_ref[e, 16 : px + 16, 2 * mid : 3 * mid] = pltpu.roll(part, px - 1, 0).astype(BF16)
    one = real_columns(px, cols)
    t1 = jnp.zeros((1, mid), F32)
    t2 = jnp.zeros((1, mid), F32)
    for e in range(ex):
        a2 = nn(wide_ref[e, 0:px, :], wmid_ref[0])
        a2 = a2 + nn(wide_ref[e, 16 : px + 16, :], wmid_ref[1])
        a2 = a2 + nn(wide_ref[e, 32 : px + 32, :], wmid_ref[2])
        a2 = jnp.where(one, a2, 0.0)
        act2_ref[e * px : (e + 1) * px, :] = a2
        t1 = t1 + col_sum(a2)
        t2 = t2 + col_sum(a2 * a2)
    put_stats(parts2_ref, t1, t2)


def expand_kernel(count, cols, parts_ref, act2_ref, g_ref, s_ref, w_ref, relu2_ref, act3_ref, parts3_ref):
    a2 = act2_ref[...]
    mean, rstd = mean_rstd(parts_ref, a2.shape[1], count)
    act = gelu_of((a2 - mean) * rstd * row_of(g_ref) + row_of(s_ref))
    low = jnp.where(real_columns(a2.shape[0], cols), act, 0.0).astype(BF16)
    relu2_ref[...] = low
    a3 = nn(low, w_ref[...])
    act3_ref[...] = a3
    put_stats(parts3_ref, col_sum(a3), col_sum(a3 * a3))


def tokens_kernel(count, ex, cols, n_image, pad, parts_ref, act3_ref, xs_ref, g_ref, s_ref, w_ref, b_ref, text_ref,
                  stem_ref, h0_ref):
    mean, rstd = mean_rstd(parts_ref, act3_ref.shape[1], count)
    scale = rstd * row_of(g_ref)
    offset = row_of(s_ref) - mean * scale

    def body(e, r, rs, carry):
        pre = act3_ref[rs, :] * scale + offset + xs_ref[e, pl.ds(r, 2)].reshape(32, -1).astype(F32)
        stem_ref[rs, :] = gelu_of(pre).astype(BF16)
        return carry

    over_pixels(xs_ref.shape, body)
    tok = (nn(stem_ref[...], w_ref[...]) + row_of(b_ref)).astype(BF16)
    px = act3_ref.shape[0] // ex
    txt = text_ref.shape[1]
    t = lax.broadcasted_iota(jnp.int32, (pad, px), 0)
    p = lax.broadcasted_iota(jnp.int32, (pad, px), 1)
    col = p & 15
    pick = jnp.where((col < cols) & ((p >> 4) * cols + col == t), 1.0, 0.0).astype(BF16)
    tr = lax.broadcasted_iota(jnp.int32, (pad, txt), 0)
    tc = lax.broadcasted_iota(jnp.int32, (pad, txt), 1)
    pick_text = jnp.where(tr == tc + n_image, 1.0, 0.0).astype(BF16)
    for e in range(ex):
        both = nn(pick, tok[e * px : (e + 1) * px, :]) + nn(pick_text, text_ref[e])
        h0_ref[e * pad : (e + 1) * pad, :] = both.astype(BF16)


def dpre_kernel(count, ex, rows, place_ref, parts_ref, act3_ref, xs_ref, g_ref, s_ref, dtok_ref, w_ref, dpre_ref, send_ref, parts4_ref):
    chan = act3_ref.shape[1]
    mean, rstd = mean_rstd(parts_ref, chan, count)
    gain, shift = row_of(g_ref), row_of(s_ref)
    dpre_ref[...] = nt(dtok_ref[...], w_ref[...]).reshape(dpre_ref.shape)

    def body(e, r, rs, carry):
        nrm = (act3_ref[rs, :] - mean) * rstd
        _, slope = gelu_and_slope(nrm * gain + shift + xs_ref[e, pl.ds(r, 2)].reshape(32, chan).astype(F32))
        d = dpre_ref[e, pl.ds(r, 2)].reshape(32, chan) * slope
        dpre_ref[e, pl.ds(r, 2)] = d.reshape(2, 16, chan)
        return carry[0] + jnp.sum(d.reshape(4, 8, chan), axis=0), carry[1] + jnp.sum((d * nrm).reshape(4, 8, chan), axis=0)

    zero = jnp.zeros((8, chan), F32)
    a, b = over_pixels(xs_ref.shape, body, (zero, zero))
    put_stats(parts4_ref, col_sum(a), col_sum(b))
    half = rows // 2
    other = 1 - place_ref[0]
    for e in range(ex):
        send_ref[e] = dpre_ref[e, pl.ds(other * half, half)].astype(BF16)


def back3_kernel(count, cols, parts4_ref, parts3_ref, parts2_ref, act3_ref, dpre_ref, g3_ref, w_ref, act2_ref, g2_ref, s2_ref, veca_ref, vecb_ref,
                 low3_ref, t2_ref, parts5_ref, gain_ref, shift_ref, small_s):
    chan = act3_ref.shape[1]
    mean, rstd = mean_rstd(parts3_ref, chan, count)
    s1, s2 = get_stats(parts4_ref, chan)
    gain_ref[...] = s2.reshape(-1)
    shift_ref[...] = s1.reshape(-1)
    scale = row_of(g3_ref) * rstd
    c1, c2 = s1 * (1.0 / count), s2 * (1.0 / count)
    real = real_columns(32, cols)

    def body(e, r, rs, carry):
        nrm = (act3_ref[rs, :] - mean) * rstd
        d = scale * (dpre_ref[e, pl.ds(r, 2)].reshape(32, chan) - c1 - nrm * c2)
        low3_ref[rs, :] = jnp.where(real, d, 0.0).astype(BF16)
        return carry

    over_pixels(dpre_ref.shape, body)
    a2 = act2_ref[...]
    mean2, rstd2 = mean_rstd(parts2_ref, a2.shape[1], count)
    nrm2 = (a2 - mean2) * rstd2
    _, slope = gelu_and_slope(nrm2 * row_of(g2_ref) + row_of(s2_ref))
    t2 = nt(low3_ref[...], w_ref[...]) * slope
    t2_ref[...] = t2
    parts5_ref[...] = jnp.zeros_like(parts5_ref)
    put_stats(parts5_ref, col_sum(t2), col_sum(t2 * nrm2))
    used = veca_ref.shape[0] + vecb_ref.shape[0]
    n = parts5_ref.shape[0]
    each = -(-used // n)
    small_s[0 : veca_ref.shape[0], :] = veca_ref[...]
    small_s[veca_ref.shape[0] : used, :] = vecb_ref[...]
    if used < small_s.shape[0]:
        small_s[used:, :] = jnp.zeros_like(small_s[used:, :])
    for d in range(n):
        parts5_ref[d, 4 : 4 + each, :] = small_s[d * each : (d + 1) * each, :]


def back2_kernel(count, ex, rows, cols, place_ref, parts5_ref, parts2_ref, parts1_ref, act2_ref, t2_ref, g2_ref, wmid_ref, act1_ref, g1_ref, s1_ref,
                 low2_ref, t1_ref, send_ref, parts6_ref, gain_ref, shift_ref, wide):
    a2 = act2_ref[...]
    mid = a2.shape[1]
    px = rows * 16
    mean, rstd = mean_rstd(parts2_ref, mid, count)
    s1, s2 = get_stats(parts5_ref, mid)
    gain_ref[...] = s2.reshape(-1)
    shift_ref[...] = s1.reshape(-1)
    nrm = (a2 - mean) * rstd
    d = (row_of(g2_ref) * rstd) * (t2_ref[...] - s1 * (1.0 / count) - nrm * (s2 * (1.0 / count)))
    d = jnp.where(real_columns(ex * px, cols), d, 0.0)
    low2_ref[...] = d.astype(BF16)
    for e in range(ex):
        part = d[e * px : (e + 1) * px]
        wide[e, 0:16, :] = jnp.zeros((16, 3 * mid), BF16)
        wide[e, px + 16 : px + 32, :] = jnp.zeros((16, 3 * mid), BF16)
        wide[e, 16 : px + 16, 0:mid] = pltpu.roll(part, px - 1, 0).astype(BF16)
        wide[e, 16 : px + 16, mid : 2 * mid] = part.astype(BF16)
        wide[e, 16 : px + 16, 2 * mid : 3 * mid] = pltpu.roll(part, 1, 0).astype(BF16)
    mean1, rstd1 = mean_rstd(parts1_ref, mid, count)
    one = real_columns(px, cols)
    q1 = jnp.zeros((1, mid), F32)
    q2 = jnp.zeros((1, mid), F32)
    for e in range(ex):
        t = None
        for r in range(3):
            for c in range(3):
                term = nt(wide[e, (2 - r) * 16 : (2 - r) * 16 + px, c * mid : (c + 1) * mid], wmid_ref[r, c * mid : (c + 1) * mid, :])
                t = term if t is None else t + term
        nrm1 = (act1_ref[e * px : (e + 1) * px, :] - mean1) * rstd1
        _, slope = gelu_and_slope(nrm1 * row_of(g1_ref) + row_of(s1_ref))
        t = jnp.where(one, t * slope, 0.0)
        t1_ref[e] = t.reshape(rows, 16, mid)
        q1 = q1 + col_sum(t)
        q2 = q2 + col_sum(t * nrm1)
    put_stats(parts6_ref, q1, q2)
    chunk = jnp.sum(parts5_ref[:, 4:8, :], axis=0)
    parts6_ref[:, 4:8, :] = jnp.broadcast_to(chunk[None], (parts6_ref.shape[0], 4, 128))
    half = rows // 2
    other = 1 - place_ref[0]
    for e in range(ex):
        send_ref[e] = t1_ref[e, pl.ds(other * half, half)].astype(BF16)


def conv_grads_kernel(ex, px, parted, place_ref, low2_ref, wide_ref, low3_ref, relu2_ref, *refs):
    mid = low2_ref.shape[1]
    nat_m, nat_o = (refs[2], refs[3]) if parted else (refs[0], refs[1])
    nat_o[...] = tn(low3_ref[...], relu2_ref[...]).astype(BF16)
    for r in range(3):
        tot = None
        for e in range(ex):
            term = tn(low2_ref[e * px : (e + 1) * px, :], wide_ref[e, r * 16 : r * 16 + px, :])
            tot = term if tot is None else tot + term
        for c in range(3):
            for h in range(2):
                at = (h * 9 + r * 3 + c) * (mid // 2)
                src = c * mid + h * (mid // 2)
                nat_m[:, at : at + mid // 2] = tot[:, src : src + mid // 2].astype(BF16)
    if parted:
        part_it(nat_m, refs[0], refs[1], place_ref[1])
        part_it(nat_o, refs[0], refs[1], place_ref[1], at=nat_m.shape[0] // (2 * refs[0].shape[1]) * (nat_m.shape[1] // 256))


def tn_kernel(parted, place_ref, a_ref, b_ref, *refs):
    natural = refs[2] if parted else refs[0]
    natural[...] = tn(a_ref[...], b_ref[...]).astype(BF16)
    if parted:
        part_it(natural, refs[0], refs[1], place_ref[1])


def first_back_kernel(count, ex, rows, cols, parted, each, places, place_ref, parts6_ref, parts1_ref, x_ref, win_ref, g_ref, t1_ref, gott_ref,
                      low_ref, *refs):
    if parted:
        keep_ref, send_ref, win_grad_ref = refs[0], refs[1], refs[-1]
        refs = refs[2:-1]
    else:
        win_grad_ref, refs = refs[0], refs[1:]
    gain_ref, shift_ref, vec_refs, xp, small_s = refs[0], refs[1], refs[2:-2], refs[-2], refs[-1]
    s = place_ref[0]
    half = rows // 2
    chan = x_ref.shape[-1]
    mid = win_ref.shape[1]
    mean, rstd = mean_rstd(parts1_ref, mid, count)
    s1, s2 = get_stats(parts6_ref, mid)
    gain_ref[...] = s2.reshape(-1)
    shift_ref[...] = s1.reshape(-1)
    real = real_columns(ex * half * 16, cols)
    size = ex * half * 16
    xp[...] = jnp.zeros_like(xp)
    wg = None
    for own in (True, False):
        at = (s if own else 1 - s) * ex
        xp[:, 0:cols, :] = x_ref[pl.ds(at, ex)].reshape(ex * half, cols, chan)
        x = xp[...].reshape(size, chan)
        nrm = (nn(x, win_ref[...]) - mean) * rstd
        if own:
            t = t1_ref[:, pl.ds(s * half, half)].reshape(size, mid)
        else:
            t = gott_ref[...].reshape(size, mid).astype(F32)
        d = (row_of(g_ref) * rstd) * (t - s1 * (1.0 / count) - nrm * (s2 * (1.0 / count)))
        low = jnp.where(real, d, 0.0).astype(BF16)
        low_ref[0 if own else 1] = low
        term = tn(low, x)
        wg = term if wg is None else wg + term
    win_grad_ref[...] = wg.astype(BF16)
    if parted:
        part_it(win_grad_ref, keep_ref, send_ref, place_ref[1])
    for d in range(parts6_ref.shape[0]):
        small_s[d * each : (d + 1) * each, :] = parts6_ref[d, 4 : 4 + each, :]
    for ref, at in zip(vec_refs, places):
        ref[...] = take_rows(small_s, at, ref.shape[0]).reshape(-1)


def image_kernel(ex, rows, cols, place_ref, low_ref, win_ref, dpre_ref, gotd_ref, grad_ref):
    s = place_ref[0]
    half = rows // 2
    chan = win_ref.shape[0]
    size = ex * half * 16
    for own in (True, False):
        at = (s if own else 1 - s) * ex
        dp = dpre_ref[:, pl.ds(s * half, half)] if own else gotd_ref[...]
        grad = nt(low_ref[0 if own else 1], win_ref[...]) + dp.reshape(size, chan).astype(F32)
        grad_ref[pl.ds(at, ex)] = grad.astype(BF16).reshape(ex, half, 16, chan)[:, :, 0:cols, :]


def in_hbm(x):
    return pltpu.with_memory_space_constraint(x, pltpu.HBM)


def call(kernel, outs, *args, moved=(), place=None, scratch=(), name=None, us=2, limit=40):
    nbytes = sum(a.size * a.dtype.itemsize for a in args)
    spec = lambda s: pl.BlockSpec(s, lambda i: (0,) * len(s))
    return pl.pallas_call(
        kernel,
        grid=(1,),
        out_shape=[pltpu.HBM(s, d) for s, d in outs],
        in_specs=([SMEM] if place is not None else []) + [spec(a.shape) for a in args],
        out_specs=[spec(s) for s, _ in outs],
        scratch_shapes=list(scratch),
        compiler_params=pltpu.CompilerParams(vmem_limit_bytes=limit << 20),
        cost_estimate=pl.CostEstimate(flops=us * 10**9, bytes_accessed=nbytes if us else 0, transcendentals=0),
        name=name,
    )(*([place] if place is not None else []), *[a if any(a is b for b in moved) else in_hbm(a) for a in args])


DP = ("far", "near", "core")
AXES = DP + ("space",)


def spread(parts):
    return lax.all_to_all(parts, AXES, split_axis=0, concat_axis=0, tiled=True)


def swap(x, axis="space"):
    return lax.ppermute(x, axis, [(0, 1), (1, 0)])


def tie(*values):
    return lax.optimization_barrier(values)


BITS = ("space", "f1", "f0", "near")


def bit_of(name):
    if name in ("f0", "f1"):
        return (lax.axis_index("far") // (1 if name == "f0" else 2)) % 2
    return lax.axis_index(name)


def sent(x, key):
    if key == ("core",):
        return swap(x, "core")
    flip = {n: int(n in key) for n in BITS}
    far, near, space = 2 * flip["f1"] + flip["f0"], flip["near"], flip["space"]
    if far and (near or space):
        raise ValueError
    if far:
        return lax.ppermute(x, "far", [(j, j ^ far) for j in range(4)])
    if near and space:
        return lax.ppermute(x, ("near", "space"), [(j, 3 - j) for j in range(4)])
    return swap(x, "near" if near else "space")


class Box:
    def __init__(self, value, moved=False):
        self.value, self.moved = value, moved


class Pack:
    def __init__(self, sources, left, size, at=0, rows=None):
        self.sources, self.left, self.size, self.at, self.rows = sources, left, size, at, size if rows is None else rows

    @classmethod
    def start(cls, keep, send):
        size = keep.shape[-2]
        got = sent(send, ("core",))
        return cls([(Box(keep.reshape(-1, 128)), 0), (Box(got.reshape(-1, 128), True), 0)], list(BITS), size)

    def thirds(self):
        r = self.size // 3
        return [Pack(self.sources, self.left, self.size, k * r, r) for k in range(3)]


def arrive(value, *packs):
    boxes = []
    for x in packs:
        boxes += [b for b, _ in x.sources if b.moved and b not in boxes]
    flat = tie(value, *[b.value for b in boxes])
    for b, v in zip(boxes, flat[1:], strict=True):
        b.value = v
    return flat[0]


def combine_kernel(plan, n_in, bits_ref, *refs):
    ins, outs = refs[:n_in], refs[n_in:]
    for sources, left, size, at, rows, names, dests in plan:
        rest = [d for d in left if d not in names]
        for rel, (out, to) in enumerate(dests):
            for c in range(2 ** len(rest)):
                place = 0
                for pos, d in enumerate(left):
                    stride = 2 ** (len(left) - 1 - pos)
                    if d in names:
                        bit = bits_ref[BITS.index(d)]
                        if (rel >> (len(names) - 1 - names.index(d))) & 1:
                            bit = 1 - bit
                    else:
                        bit = (c >> (len(rest) - 1 - rest.index(d))) & 1
                    place = place + bit * stride
                tot = None
                for idx, first in sources:
                    x = ins[idx][pl.ds(pl.multiple_of(first + place * size + at, 16), rows), :].astype(F32)
                    tot = x if tot is None else tot + x
                outs[out][to + c * rows : to + (c + 1) * rows, :] = tot.astype(BF16)


def step(bits, moves, tied):
    boxes, plan, keys, totals, after = [], [], [], {(): 0}, []
    for pack, names in moves:
        srcs = []
        for box, first in pack.sources:
            if box not in boxes:
                boxes.append(box)
            srcs.append((boxes.index(box), first))
        rest = [d for d in pack.left if d not in names]
        n = 2 ** len(rest) * pack.rows
        dests = []
        for rel in range(2 ** len(names)):
            key = tuple(d for j, d in enumerate(names) if (rel >> (len(names) - 1 - j)) & 1)
            key = tuple(sorted(key))
            if key not in totals:
                totals[key] = 0
            if key not in keys:
                keys.append(key)
            dests.append((key, totals[key]))
            totals[key] += n
        plan.append((srcs, list(pack.left), pack.size, pack.at, pack.rows, names, dests))
        after.append((rest, pack.rows, dests))
    plan = [(*p[:-1], [(keys.index(k), to) for k, to in p[-1]]) for p in plan]
    args = [b.value if b.moved else in_hbm(b.value) for b in boxes]
    one = lambda shape: pl.BlockSpec(shape, lambda t: (0, 0), pipeline_mode=pl.Buffered(1))
    res = pl.pallas_call(
        functools.partial(combine_kernel, plan, len(args)),
        grid=(1,),
        in_specs=[SMEM] + [one(x.shape) for x in args],
        out_specs=[one((totals[k], 128)) for k in keys],
        out_shape=[pltpu.HBM((totals[k], 128), BF16) for k in keys],
        compiler_params=pltpu.CompilerParams(vmem_limit_bytes=40 << 20),
        cost_estimate=pl.CostEstimate(flops=0, bytes_accessed=0, transcendentals=0),
        name="combine",
    )(bits, *args)
    flat = tie(tied, *res)
    arrays = {k: Box(flat[1 + j] if k == () else sent(flat[1 + j], k), k != ()) for j, k in enumerate(keys)}
    packs = [Pack([(arrays[k], to) for k, to in dests], rest, rows) for rest, rows, dests in after]
    return flat[0], packs


def finish_kernel(plan, n_in, *refs):
    ins, outs = refs[:n_in], refs[n_in:]
    for sources, pieces in plan:
        for first, r, blocks, out in pieces:
            for b in range(blocks):
                tot = None
                for idx, at in sources:
                    lo = at + first + b * r
                    if len(ins[idx].shape) == 3:
                        x = jnp.sum(ins[idx][:, lo : lo + r, :].astype(F32), axis=0)
                    else:
                        x = ins[idx][lo : lo + r, :].astype(F32)
                    tot = x if tot is None else tot + x
                if len(outs[out].shape) == 3:
                    outs[out][b] = tot
                else:
                    outs[out][:, b * 128 : (b + 1) * 128] = tot


def finish(groups, shapes, name):
    boxes, plan = [], []
    for sources, pieces in groups:
        srcs = []
        for box, first in sources:
            if box not in boxes:
                boxes.append(box)
            srcs.append((boxes.index(box), first))
        plan.append((srcs, pieces))
    args = [b.value for b in boxes]
    return call(functools.partial(finish_kernel, plan, len(args)), [(s, F32) for s in shapes], *args, moved=args, name=name)


def halve_dp(x, axis, bit):
    size = lax.axis_size(DP)
    mine = (lax.axis_index(DP) // bit) % 2
    keep = lax.dynamic_index_in_dim(x, mine, axis, keepdims=True)
    send = lax.dynamic_index_in_dim(x, 1 - mine, axis, keepdims=True)
    return keep + lax.ppermute(send, DP, [(j, j ^ bit) for j in range(size)])


def scattered(grad_t):
    size = lax.axis_size(DP)
    bits = size.bit_length() - 1
    cols, rows = grad_t.shape
    x = grad_t.reshape((2,) * bits + (cols // size, rows))
    for b in range(bits):
        x = halve_dp(x, bits - 1 - b, 1 << b)
    half = rows // 2
    mine = lax.axis_index("space")
    keep = lax.dynamic_slice_in_dim(x, mine * half, half, axis=x.ndim - 1)
    send = lax.dynamic_slice_in_dim(x, (1 - mine) * half, half, axis=x.ndim - 1)
    return (keep + swap(send)).reshape(cols // size, half).astype(F32).T


def shards(
    image_in, text_in, prefix, text_len, cotangent,
    conv_in_w, bn1_gain, bn1_shift, conv_mid_w, bn2_gain, bn2_shift, conv_out_w, bn3_gain, bn3_shift,
    proj_w, proj_b, ln1_gain, ln1_shift, qkv_w, query_bias, value_bias, out_w, out_b,
    ln2_gain, ln2_shift, up_w, up_b, down_w, down_b,
):
    n_dev, dp = lax.axis_size(AXES), lax.axis_size(DP)
    band_ex, band_rows, cols, chan = image_in.shape
    mid = conv_in_w.shape[1]
    width = proj_w.shape[1]
    ff = up_w.shape[1]
    ex, txt, _ = text_in.shape
    rows = band_rows * lax.axis_size("space")
    n_image = rows * cols
    seq = n_image + txt
    pad = -(-seq // 16) * 16
    px = rows * 16
    count = float(band_ex * band_rows * cols * n_dev)
    me = lax.axis_index("space").astype(jnp.int32)
    place = jnp.stack([me, lax.axis_index("core").astype(jnp.int32)])
    small, large, tiny = (n_dev, stat_rows(mid), 128), (n_dev, stat_rows(chan), 128), (n_dev, 2 * mid // 128, 128)
    wmid = conv_mid_w.reshape(3, 3 * mid, mid)
    weights = [(mid, chan), (mid, 9 * mid), (chan, mid), (width, chan), (3 * width, width), (width, width), (ff, width), (width, ff)]
    parted = dp == 16 and mid == 256 and all(c % (16 * dp) == 0 and r % 256 == 0 for c, r in weights)
    hi = dp // 2

    def grad_outs(c, r):
        return [(part_shape(c, r, dp), BF16)] * 2 if parted else [((c, r), BF16)]

    def natural(c, r):
        return [pltpu.VMEM((c, r), BF16)] if parted else []

    got_x = swap(lax.dynamic_slice_in_dim(image_in, (1 - me) * ex, ex, axis=0))
    parts1, = call(functools.partial(stats_kernel, cols), [(tiny, F32)], image_in, conv_in_w,
                   scratch=[pltpu.VMEM((band_ex * band_rows, 16, chan), BF16)], name="stats_one")
    parts1 = spread(parts1)
    xs, act1, wide, act2, parts2 = call(
        functools.partial(conv_fwd_kernel, count, ex, rows, cols),
        [((ex, rows, 16, chan), BF16), ((ex * px, mid), F32), ((ex, px + 32, 3 * mid), BF16), ((ex * px, mid), F32), (tiny, F32)],
        parts1, image_in, got_x, conv_in_w, bn1_gain, bn1_shift, wmid, moved=(parts1, got_x), place=place, name="conv_three", us=4)
    parts2 = spread(parts2)
    relu2, act3, parts3 = call(
        functools.partial(expand_kernel, count, cols),
        [((ex * px, mid), BF16), ((ex * px, chan), F32), (large, F32)],
        parts2, act2, bn2_gain, bn2_shift, conv_out_w, moved=(parts2,), name="expand")
    parts3 = spread(parts3)
    stem, h0 = call(
        functools.partial(tokens_kernel, count, ex, cols, n_image, pad),
        [((ex * px, chan), BF16), ((ex * pad, width), BF16)],
        parts3, act3, xs, bn3_gain, bn3_shift, proj_w, proj_b, text_in, moved=(parts3,), name="tokens", us=5)
    z1, q, k, v, p, attn, h1, z2 = attn_fwd(h0, prefix, text_len, ln1_gain, ln1_shift, qkv_w, query_bias, value_bias,
                                            out_w, out_b, ln2_gain, ln2_shift, ex, n_image, pad)
    mlp_outs = mlp(place, z2, h1, cotangent, up_w, up_b, down_w, down_b, ln2_gain, pad, dp, parted)
    block_out, mlp_grads, (g1, veca) = mlp_outs[0], mlp_outs[1:-2], mlp_outs[-2:]
    if parted:
        bits = jnp.stack([bit_of(n) for n in BITS]).astype(jnp.int32)
        down, up = Pack.start(*mlp_grads[:2]), Pack.start(*mlp_grads[2:])
    back_args = (out_w, attn, q, k, v, p, z1, h0, qkv_w, ln1_gain, ex, n_image, txt, rows, cols, pad, dp, parted)
    if parted:
        carry = attn_bwd(place, g1, *back_args, hi=1)
        turns = [["space"], ["near"], ["f0"]]
        ffn = down.thirds() + up.thirds()
        g1, ffn = step(bits, list(zip(ffn, turns + turns)), tie(g1, *carry)[0])
        att_outs = attn_bwd(place, g1, *back_args, lo=1, carry=carry, stem=stem)
    else:
        att_outs = attn_bwd(place, g1, *back_args)
    att_grads, (text_grad, dtok, vecb) = att_outs[:-3], att_outs[-3:]
    if parted:
        later = turns[1:] + turns[:1]
        (dtok, att_send), ffn = step(bits, list(zip(ffn, later * 2)), (dtok, att_grads[1]))
        att = Pack.start(att_grads[0], att_send)
    dpre, dsend, parts4 = call(
        functools.partial(dpre_kernel, count, ex, rows),
        [((ex, rows, 16, chan), F32), ((ex, band_rows, 16, chan), BF16), (large, F32)],
        parts3, act3, xs, bn3_gain, bn3_shift, dtok, proj_w, moved=(parts3,), place=place, name="stem_back", us=7)
    got_d = swap(dsend)
    if parted:
        parts4 = arrive(parts4, *ffn, att)
    parts4 = spread(parts4)
    if parted:
        later = later[1:] + later[:1]
        dpre, moved = step(bits, list(zip(ffn, later * 2)) + list(zip(att.thirds(), later)), dpre)
        ffn, att = moved[:6], moved[6:]
    else:
        proj_g = call(functools.partial(tn_kernel, parted), grad_outs(width, chan), dtok, stem, place=place, name="proj_grad", us=0)
    low3, t2, parts5, bn3_gg, bn3_sg = call(
        functools.partial(back3_kernel, count, cols),
        [((ex * px, chan), BF16), ((ex * px, mid), F32), (small, F32), ((chan,), F32), ((chan,), F32)],
        parts4, parts3, parts2, act3, dpre, bn3_gain, conv_out_w, act2, bn2_gain, bn2_shift, veca, vecb, moved=(parts4, parts3, parts2),
        scratch=[pltpu.VMEM((n_dev * -(-(veca.shape[0] + vecb.shape[0]) // n_dev), 128), F32)], name="back_three", us=4)
    if parted:
        t2 = arrive(t2, *att)
    parts5 = spread(parts5)
    if parted:
        later = later[1:] + later[:1]
        t2, moved = step(bits, [(x, ["f1"]) for x in ffn] + list(zip(att, later)), t2)
        ffn, att = moved[:6], moved[6:]
    low2, t1, tsend, parts6, bn2_gg, bn2_sg = call(
        functools.partial(back2_kernel, count, ex, rows, cols),
        [((ex * px, mid), BF16), ((ex, rows, 16, mid), F32), ((ex, band_rows, 16, mid), BF16), (small, F32), ((mid,), F32), ((mid,), F32)],
        parts5, parts2, parts1, act2, t2, bn2_gain, wmid, act1, bn1_gain, bn1_shift,
        moved=(parts5, parts2, parts1), place=place, scratch=[pltpu.VMEM((ex, px + 32, 3 * mid), BF16)], name="back_two", us=4)
    got_t = swap(tsend)
    parts6 = spread(parts6)
    if parted:
        low2, got_t = arrive(tie(low2, got_t), *att)
    conv_g = call(
        functools.partial(conv_grads_kernel, ex, px, parted),
        [(part_shape(mid, 9 * mid, dp)[:2] + (part_shape(mid, 9 * mid, dp)[2] + part_shape(chan, mid, dp)[2], 128), BF16)] * 2
        if parted else [((mid, 9 * mid), BF16), ((chan, mid), BF16)],
        low2, wide, low3, relu2, place=place, scratch=natural(mid, 9 * mid) + natural(chan, mid), name="conv_grads", us=4)
    if parted:
        parts6, conv_send = arrive(tie(parts6, conv_g[1]), *ffn, *att)
        conv = Pack.start(conv_g[0], conv_send)
    each = -(-(veca.shape[0] + vecb.shape[0]) // n_dev)
    n, off = width // 128, veca.shape[0]
    places = [off, off + n, off + 2 * n, off + 3 * n, off + 4 * n, 3 * n, n, 2 * n, 4 * n, 0]
    sizes = [width] * 8 + [ff, width]
    last = call(
        functools.partial(first_back_kernel, count, ex, rows, cols, parted, each, places),
        [((2, ex * band_rows * 16, mid), BF16)] + grad_outs(mid, chan) + [((mid,), F32)] * 2 + [((s,), F32) for s in sizes],
        parts6, parts1, image_in, conv_in_w, bn1_gain, t1, got_t,
        moved=(parts6, parts1, got_t), place=place, scratch=[pltpu.VMEM((ex * band_rows, 16, chan), BF16), pltpu.VMEM((n_dev * each, 128), F32)] + natural(mid, chan),
        name="first_back", us=3)
    low1, sums = last[0], last[3 if parted else 2 :]
    bn1_gg, bn1_sg, vecs = sums[0], sums[1], sums[2:]
    if parted:
        later = later[1:] + later[:1]
        (low1, keep_x), moved = step(bits, list(zip(att, later)) + [(conv, ["near", "space"])], (low1, last[1]))
        att, conv = moved[:3], moved[3]
    image_grad, = call(functools.partial(image_kernel, ex, rows, cols), [(image_in.shape, BF16)], low1, conv_in_w, dpre, got_d,
                       moved=(got_d,), place=place, name="image_back", us=4)
    if parted:
        in_x = (keep_x + swap(last[2], "core")).reshape((2 * hi,) + keep_x.shape[2:])
        in_x = lax.all_to_all(in_x, ("space", "far", "near"), split_axis=0, concat_axis=0, tiled=True)
        image_grad, moved = step(bits, [(x, ["f1"]) for x in att] + [(conv, ["f1", "f0"])], image_grad)
        att, conv = moved[:3], moved[3]
        r_mid, r_out3, r_q, r_w, r_f = mid // dp, chan // dp, 3 * width // dp, width // dp, ff // dp
        mids, half = r_mid * (9 * mid // 256), width // 256
        g_down, g_up = finish(
            [(ffn[0].sources, [(0, r_w, ff // 256, 0)]), (ffn[3].sources, [(0, r_f, half, 1)])],
            [(r_w, ff // 2), (r_f, width // 2)], "finish_early")
        g_qkv, g_out, g_proj, g_mid, g_out3, g_in = finish(
            [(att[0].sources, [(0, r_q, half, 0), (r_q * half, r_w, half, 1), ((r_q + r_w) * half, r_w, chan // 256, 2)]),
             (conv.sources, [(0, r_mid, 9 * mid // 256, 3), (mids, r_out3, mid // 256, 4)]),
             ([(Box(in_x), 0)], [(0, r_mid, chan // 256, 5)])],
            [(r_q, width // 2), (r_w, width // 2), (r_w, chan // 2), (9 * mid // 256, r_mid, 128), (r_out3, mid // 2), (r_mid, chan // 2)], "finish_late")
        g_down, g_up, g_qkv, g_out, g_proj, g_out3, g_in = [g.T for g in (g_down, g_up, g_qkv, g_out, g_proj, g_out3, g_in)]
        g_mid = g_mid.reshape(3, 3, r_mid, mid // 2).transpose(0, 1, 3, 2)
    else:
        out_n = att_outs[0].transpose(1, 0, 2).reshape(width, width)
        g_in, g_mid, g_out3, g_proj, g_qkv, g_out, g_up, g_down = [
            scattered(x) for x in (last[1], conv_g[0], conv_g[1], proj_g[0], att_outs[1], out_n, mlp_grads[1], mlp_grads[0])]
        g_mid = g_mid.reshape(3, 3, mid // 2, -1)
    return (
        block_out, image_grad, text_grad,
        g_in, bn1_gg, bn1_sg,
        g_mid, bn2_gg, bn2_sg,
        g_out3, bn3_gg, bn3_sg,
        g_proj, vecs[0], vecs[1], vecs[2],
        g_qkv, vecs[3], vecs[4],
        g_out, vecs[5], vecs[6], vecs[7],
        g_up, vecs[8],
        g_down, vecs[9],
    )


def solution(mesh):
    dp, space = mesh.devices.shape
    fine = Mesh(mesh.devices.reshape(dp // 4, 2, 2, space), AXES)
    return jax.shard_map(
        shards,
        mesh=fine,
        in_specs=(
            P(DP, "space", None, None),
            P(AXES, None, None),
            P(AXES),
            P(AXES),
            P(AXES, None, None),
            P(),
            P(),
            P(),
            P(),
            P(),
            P(),
            P(),
            P(),
            P(),
            P(),
            P(),
            P(),
            P(),
            P(),
            P(),
            P(),
            P(),
            P(),
            P(),
            P(),
            P(),
            P(),
            P(),
            P(),
        ),
        out_specs=(
            P(AXES, None, None),
            P(DP, "space", None, None),
            P(AXES, None, None),
            P("space", DP),
            P(),
            P(),
            P(None, None, "space", DP),
            P(),
            P(),
            P("space", DP),
            P(),
            P(),
            P("space", DP),
            P(),
            P(),
            P(),
            P("space", DP),
            P(),
            P(),
            P("space", DP),
            P(),
            P(),
            P(),
            P("space", DP),
            P(),
            P("space", DP),
            P(),
        ),
        check_vma=False,
    )
```

```python
import functools
import jax
import jax.numpy as jnp
from jax import lax
from jax.experimental import pallas as pl
from jax.experimental.pallas import tpu as pltpu
from jax.sharding import Mesh, PartitionSpec as P

HD = 64
F32 = jnp.float32
BF16 = jnp.bfloat16
eps_batch = 1e-05
eps_layer = 1e-06
masked_value = -1e30
GELU_C = 0.7978845608028654
GELU_A = 0.044715


def nn(a, b):
    return lax.dot_general(a, b, (((1,), (0,)), ((), ())), preferred_element_type=F32)


def nt(a, b):
    return lax.dot_general(a, b, (((1,), (1,)), ((), ())), preferred_element_type=F32)


def tn(a, b):
    return lax.dot_general(a, b, (((0,), (0,)), ((), ())), preferred_element_type=F32)


def gelu_of(x):
    t = jnp.tanh(GELU_C * (x + GELU_A * x * x * x))
    return 0.5 * x * (1.0 + t)


def gelu_and_slope(x):
    x2 = x * x
    t = jnp.tanh(x * (GELU_C + (GELU_C * GELU_A) * x2))
    half = 0.5 + 0.5 * t
    slope = half + (0.5 * x) * (1.0 - t * t) * (GELU_C + (3.0 * GELU_C * GELU_A) * x2)
    return x * half, slope


def ln_parts(x):
    mean = jnp.mean(x, axis=-1, keepdims=True)
    c = x - mean
    var = jnp.mean(c * c, axis=-1, keepdims=True)
    r = lax.rsqrt(var + eps_layer)
    return c * r, r


def ln_back(dz, nrm, r, gain):
    u = dz * gain
    return r * (u - jnp.mean(u, axis=-1, keepdims=True) - nrm * jnp.mean(u * nrm, axis=-1, keepdims=True))


def whole(shape):
    return pl.BlockSpec(shape, lambda *_: (0,) * len(shape), pipeline_mode=pl.Buffered(1))


SMEM = pl.BlockSpec(memory_space=pltpu.SMEM)
VMEM = pl.BlockSpec(memory_space=pltpu.VMEM)


def row_of(ref):
    return ref[...].reshape(1, -1)


def put_rows(ref, at, vector):
    for r in range(vector.shape[1] // 128):
        ref[at + r : at + r + 1, :] = vector[:, r * 128 : (r + 1) * 128]


def take_rows(ref, at, size):
    return jnp.concatenate([ref[at + r : at + r + 1, :] for r in range(size // 128)], axis=1)


def part_shape(cols, rows, dp):
    return (2, dp // 2, cols // dp * (rows // 2) // 128, 128)


def part_it(natural, keep_ref, send_ref, core, at=0):
    rows, cols = natural.shape[-2:]
    hi = keep_ref.shape[1]
    r, blocks = rows // (2 * hi), cols // 256

    def one(h, carry):
        mine = pl.ds(pl.multiple_of((2 * h + core) * r, 16), r)
        other = pl.ds(pl.multiple_of((2 * h + 1 - core) * r, 16), r)
        for s in range(2):
            for b in range(blocks):
                lanes = slice((s * blocks + b) * 128, (s * blocks + b + 1) * 128)
                keep_ref[s, h, at + b * r : at + (b + 1) * r, :] = natural[mine, lanes]
                send_ref[s, h, at + b * r : at + (b + 1) * r, :] = natural[other, lanes]
        return carry

    lax.fori_loop(0, hi, one, 0)


def mlp_kernel(ex, seq, pad, parted, place_ref, z2_ref, h1_ref, cot_ref, upw_ref, upb_ref, dnw_ref, dnb_ref, g_ref, *refs):
    if parted:
        out_ref, dk_ref, ds_ref, uk_ref, us_ref, g1_ref, vec_ref, g2_s, g2t_s, acc_o, acc_d, ub_s, bg_s = refs
    else:
        out_ref, dn_ref, up_ref, g1_ref, vec_ref, g2_s, g2t_s, acc_o, acc_d, ub_s, bg_s = refs
    i = pl.program_id(0)
    last = pl.num_programs(0) - 1
    tile = upw_ref.shape[1]

    @pl.when(i == 0)
    def _():
        g2_s[...] = jnp.zeros_like(g2_s)
        for e in range(ex):
            g2_s[e * pad : e * pad + seq, :] = cot_ref[e]
        g2t_s[...] = g2_s[...].T
        acc_o[...] = jnp.zeros_like(acc_o)
        acc_d[...] = jnp.zeros_like(acc_d)
        ub = row_of(upb_ref)
        for j in range(ub_s.shape[0]):
            ub_s[j] = ub[:, j * tile : (j + 1) * tile]

    z2 = z2_ref[...]
    g2 = g2_s[...]
    pre = nn(z2, upw_ref[...]) + ub_s[i]
    act, slope = gelu_and_slope(pre)
    low = act.astype(BF16)
    dg = (nt(g2, dnw_ref[...]) * slope).astype(BF16)
    acc_o[...] += nn(low, dnw_ref[...])
    acc_d[...] += nt(dg, upw_ref[...])
    dn = nn(g2t_s[...], low).astype(BF16)
    up = tn(dg, z2).astype(BF16)
    bg_s[i] = jnp.sum(dg.astype(F32), axis=0, keepdims=True)
    if parted:
        core = place_ref[1]
        even = core == 0
        hi = dk_ref.shape[1]
        r = dn.shape[0] // (2 * hi)
        for j in range(tile // 128):
            d4 = dn[:, j * 128 : (j + 1) * 128].reshape(hi, 2, r, 128)
            dk_ref[0, :, j * r : (j + 1) * r, :] = jnp.where(even, d4[:, 0], d4[:, 1])
            ds_ref[0, :, j * r : (j + 1) * r, :] = jnp.where(even, d4[:, 1], d4[:, 0])
        r, blocks = up.shape[0] // 4, up.shape[1] // 256
        for s in range(2):
            for j in range(blocks):
                lanes = slice((s * blocks + j) * 128, (s * blocks + j + 1) * 128)
                for t in range(2):
                    first, second = up[2 * t * r : (2 * t + 1) * r, lanes], up[(2 * t + 1) * r : (2 * t + 2) * r, lanes]
                    uk_ref[s, t, j * r : (j + 1) * r, :] = jnp.where(even, first, second)
                    us_ref[s, t, j * r : (j + 1) * r, :] = jnp.where(even, second, first)
    else:
        dn_ref[...] = dn
        up_ref[...] = up

    @pl.when(i == last)
    def _():
        h1 = h1_ref[...]
        out = (h1 + acc_o[...] + row_of(dnb_ref)).astype(BF16)
        for e in range(ex):
            out_ref[e] = out[e * pad : e * pad + seq, :]
        nrm, r = ln_parts(h1)
        dz = acc_d[...]
        gf = g2_s[...].astype(F32)
        g1 = gf + ln_back(dz, nrm, r, row_of(g_ref))
        g1_ref[...] = g1
        n = g1.shape[1] // 128
        for j, v in enumerate((col_sum(gf), col_sum(dz * nrm), col_sum(dz), col_sum(g1))):
            put_rows(vec_ref, j * n, v)
        for j in range(bg_s.shape[0]):
            put_rows(vec_ref, 4 * n + j * (tile // 128), bg_s[j])


def mlp(place, z2, h1, cot, up_w, up_b, down_w, down_b, gain, pad, dp, parted):
    ex, seq, width = cot.shape
    rows = z2.shape[0]
    ff = up_w.shape[1]
    tile = 4 * ff // dp if parted else 384
    steps = ff // tile
    vec_rows = 4 * width // 128 + ff // 128
    if parted:
        dn, up = part_shape(width, ff, dp), part_shape(ff, width, dp)
        per_half = steps // 2
        dn_spec = pl.BlockSpec((1, dn[1], dn[2] // per_half, 128), lambda i: (i // per_half, 0, i % per_half, 0))
        up_spec = pl.BlockSpec((2, 2, up[2], 128), lambda i: (0, i, 0, 0))
        grads = [(dn, dn_spec), (dn, dn_spec), (up, up_spec), (up, up_spec)]
    else:
        grads = [((width, ff), pl.BlockSpec((width, tile), lambda i: (0, i))),
                 ((ff, width), pl.BlockSpec((tile, width), lambda i: (i, 0)))]
    outs = [((ex, seq, width), whole((ex, seq, width)), BF16)] + [(s, b, BF16) for s, b in grads]
    outs += [((rows, width), whole((rows, width)), F32), ((vec_rows, 128), whole((vec_rows, 128)), F32)]
    return pl.pallas_call(
        functools.partial(mlp_kernel, ex, seq, pad, parted),
        grid=(steps,),
        in_specs=[
            SMEM, whole((rows, width)), whole((rows, width)), whole((ex, seq, width)),
            pl.BlockSpec((width, tile), lambda i: (0, i)), whole((ff,)),
            pl.BlockSpec((tile, width), lambda i: (i, 0)),
            whole((width,)), whole((width,)),
        ],
        out_specs=[b for _, b, _ in outs],
        out_shape=[pltpu.HBM(s, d) for s, _, d in outs],
        scratch_shapes=[
            pltpu.VMEM((rows, width), BF16), pltpu.VMEM((width, rows), BF16),
            pltpu.VMEM((rows, width), F32), pltpu.VMEM((rows, width), F32),
            pltpu.VMEM((steps, 1, tile), F32), pltpu.VMEM((steps, 1, tile), F32),
        ],
        compiler_params=pltpu.CompilerParams(dimension_semantics=("arbitrary",), vmem_limit_bytes=44 << 20),
        cost_estimate=pl.CostEstimate(flops=46 * 10**9, bytes_accessed=30 << 20, transcendentals=rows * ff),
        name="mlp_both_ways",
    )(place, *[in_hbm(x) for x in (z2, h1, cot, up_w, up_b, down_w, down_b, gain)])


def stat_rows(channels):
    return max(8, 2 * channels // 128)


def put_stats(ref, first, second):
    lanes = jnp.concatenate([first, second], axis=1)
    n = ref.shape[0]
    for r in range(lanes.shape[1] // 128):
        ref[:, r, :] = jnp.broadcast_to(lanes[:, r * 128 : (r + 1) * 128], (n, 128))


def get_stats(ref, channels):
    total = jnp.sum(ref[...], axis=0)
    rows = 2 * channels // 128
    half = rows // 2
    first = jnp.concatenate([total[r : r + 1, :] for r in range(half)], axis=1)
    second = jnp.concatenate([total[r : r + 1, :] for r in range(half, rows)], axis=1)
    return first, second


def mean_rstd(ref, channels, count):
    s1, s2 = get_stats(ref, channels)
    mean = s1 * (1.0 / count)
    return mean, lax.rsqrt(s2 * (1.0 / count) - mean * mean + eps_batch)


def real_columns(rows, cols):
    return (lax.broadcasted_iota(jnp.int32, (rows, 1), 0) & 15) < cols


def col_sum(x):
    return jnp.sum(x, axis=0, keepdims=True)


def row_blocks(rows):
    starts = list(range(0, rows - 63, 64))
    return [(a, b) for a, b in zip(starts, starts[1:] + [rows])]


def head_mask(rows, second):
    lane = lax.broadcasted_iota(jnp.int32, (rows, 2 * HD), 1)
    return (lane >= HD) if second else (lane < HD)


def attn_fwd_kernel(ex, n_image, pad, pre_ref, len_ref, h0_ref, g_ref, s_ref, wq_ref, wk_ref, wv_ref, qb_ref, vb_ref,
                    ow_ref, ob_ref, g2_ref, s2_ref,
                    z1_ref, q_ref, k_ref, v_ref, p_ref, attn_ref, h1_ref, z2_ref, acc, qb_s, vb_s):
    i = pl.program_id(0)
    last = pl.num_programs(0) - 1
    wide = wq_ref.shape[1]

    @pl.when(i == 0)
    def _():
        nrm, _r = ln_parts(h0_ref[...].astype(F32))
        z1_ref[...] = (nrm * row_of(g_ref) + row_of(s_ref)).astype(BF16)
        acc[...] = jnp.zeros_like(acc)
        qb, vb = row_of(qb_ref), row_of(vb_ref)
        for j in range(qb_s.shape[0]):
            qb_s[j] = qb[:, j * wide : (j + 1) * wide]
            vb_s[j] = vb[:, j * wide : (j + 1) * wide]

    z1 = z1_ref[...]
    q_ref[...] = (nn(z1, wq_ref[...]) + qb_s[i]).astype(BF16)
    k_ref[...] = nn(z1, wk_ref[...]).astype(BF16)
    v_ref[...] = (nn(z1, wv_ref[...]) + vb_s[i]).astype(BF16)
    zero = jnp.zeros((pad, 2 * HD), BF16)
    first = head_mask(pad, False)

    def example(e, carry):
        row0 = pl.multiple_of(e * pad, 16)
        key = lax.broadcasted_iota(jnp.int32, (pad, pad), 1)
        qry = lax.broadcasted_iota(jnp.int32, (pad, pad), 0)
        limit = jnp.maximum(qry + 1, n_image + pre_ref[e])
        limit = jnp.minimum(limit, n_image + len_ref[e])
        vis = key < limit
        for pair in range(wide // (2 * HD)):
            cols = slice(pair * 2 * HD, (pair + 1) * 2 * HD)
            q2 = q_ref[pl.ds(row0, pad), cols] * jnp.asarray(0.125, BF16)
            k2 = k_ref[pl.ds(row0, pad), cols]
            v2 = v_ref[pl.ds(row0, pad), cols]
            out = None
            for h in range(2):
                sel = first if h == 0 else jnp.logical_not(first)
                raw = nt(jnp.where(sel, q2, zero), k2)
                for lo, up in row_blocks(pad):
                    sc = jnp.where(vis[lo:up], raw[lo:up], masked_value)
                    top = jnp.max(sc, axis=-1, keepdims=True)
                    ex_ = jnp.exp(sc - top)
                    tot = jnp.sum(ex_, axis=-1, keepdims=True)
                    p_ref[e, pair * 2 + h, lo:up, :] = (ex_ * (1.0 / tot)).astype(BF16)
                o = nn(p_ref[e, pair * 2 + h], jnp.where(sel, v2, zero))
                out = o if out is None else out + o
            attn_ref[pl.ds(row0, pad), cols] = out.astype(BF16)
        return carry

    lax.fori_loop(0, ex, example, 0)
    acc[...] += nn(attn_ref[...], ow_ref[...])

    @pl.when(i == last)
    def _():
        h1 = h0_ref[...].astype(F32) + acc[...] + row_of(ob_ref)
        h1_ref[...] = h1
        nrm, _r = ln_parts(h1)
        z2_ref[...] = (nrm * row_of(g2_ref) + row_of(s2_ref)).astype(BF16)


def attn_fwd(h0, prefix, text_len, ln1_gain, ln1_shift, qkv_w, qb, vb, out_w, out_b, ln2_gain, ln2_shift, ex, n_image, pad, wide=256):
    rows, width = h0.shape
    groups = width // wide
    heads = width // HD
    hg = wide // HD
    cols = lambda off: pl.BlockSpec((width, wide), lambda i, *_: (0, i + off * groups))
    vec = whole((width,))
    part = pl.BlockSpec((rows, wide), lambda i, *_: (0, i))
    return pl.pallas_call(
        functools.partial(attn_fwd_kernel, ex, n_image, pad),
        grid_spec=pltpu.PrefetchScalarGridSpec(
            num_scalar_prefetch=2,
            grid=(groups,),
            in_specs=[whole((rows, width)), vec, vec, cols(0), cols(1), cols(2), vec, vec,
                      pl.BlockSpec((wide, width), lambda i, *_: (i, 0)), vec, vec, vec],
            out_specs=[whole((rows, width)), part, part, part,
                       pl.BlockSpec((ex, hg, pad, pad), lambda i, *_: (0, i, 0, 0)),
                       part, whole((rows, width)), whole((rows, width))],
            scratch_shapes=[pltpu.VMEM((rows, width), F32)] + [pltpu.VMEM((groups, 1, wide), F32)] * 2,
        ),
        out_shape=[pltpu.HBM((rows, width), BF16)] * 4 + [
            pltpu.HBM((ex, heads, pad, pad), BF16),
            pltpu.HBM((rows, width), BF16),
            pltpu.HBM((rows, width), F32),
            pltpu.HBM((rows, width), BF16)],
        compiler_params=pltpu.CompilerParams(dimension_semantics=("arbitrary",), vmem_limit_bytes=40 << 20),
        cost_estimate=pl.CostEstimate(flops=32 * 10**9, bytes_accessed=30 << 20, transcendentals=heads * rows * pad),
        name="attention_forward",
    )(prefix, text_len, *[in_hbm(x) for x in (h0, ln1_gain, ln1_shift, qkv_w, qkv_w, qkv_w, qb, vb, out_w, out_b, ln2_gain, ln2_shift)])


def attn_bwd_kernel(ex, n_image, txt, cols_real, pad, parted, lo, final, place_ref, g1_ref, ow_ref, attn_ref, q_ref, k_ref, v_ref, p_ref, z1_ref, wq_ref, wk_ref, wv_ref, *refs):
    if lo:
        acc_c, ow_c, qkv_c, bias_c = refs[:4]
        refs = refs[4:]
    if not final:
        acc, ow_s, qkv_s, bias_s = refs[:4]
        g1b_s, g1t_s, dat_s, dq_s, dk_s, dv_s = refs[4:]
    else:
        h0_ref, g_ref, refs = refs[0], refs[1], refs[2:]
        if parted:
            stem_ref, ak_ref, as_ref, text_ref, dtok_ref, vec_ref, ow_s, qkv_s, proj_s = refs[:9]
        else:
            ow_s, qkv_s, text_ref, dtok_ref, vec_ref = refs[:5]
        g1b_s, g1t_s, dat_s, dq_s, dk_s, dv_s, acc, bias_s = refs[-8:]
    i = pl.program_id(0)
    last = pl.num_programs(0) - 1
    wide = wq_ref.shape[1]

    @pl.when(i == 0)
    def _():
        g1b_s[...] = g1_ref[...].astype(BF16)
        g1t_s[...] = g1b_s[...].T
        if lo:
            acc[...] = acc_c[...]
            ow_s[0:lo] = ow_c[...]
            bias_s[:, 0:lo] = bias_c[...]
            for j in range(3):
                qkv_s[j * z1_ref.shape[1] : j * z1_ref.shape[1] + lo * wide, :] = qkv_c[j]
        else:
            acc[...] = jnp.zeros_like(acc)

    gi = i + lo
    ow_s[gi] = nn(g1t_s[...], attn_ref[...]).astype(BF16)
    dat_s[...] = nt(g1b_s[...], ow_ref[...]).astype(BF16)
    zero = jnp.zeros((pad, 2 * HD), BF16)
    first = head_mask(pad, False)

    def example(e, carry):
        row0 = pl.multiple_of(e * pad, 16)
        for pair in range(wide // (2 * HD)):
            cols = slice(pair * 2 * HD, (pair + 1) * 2 * HD)
            q2 = q_ref[pl.ds(row0, pad), cols]
            k2 = k_ref[pl.ds(row0, pad), cols]
            v2 = v_ref[pl.ds(row0, pad), cols]
            da2 = dat_s[pl.ds(row0, pad), cols]
            dq = dk = dv = None
            for h in range(2):
                sel = first if h == 0 else jnp.logical_not(first)
                pb = p_ref[e, pair * 2 + h]
                dah = jnp.where(sel, da2, zero)
                whole_dp = nt(dah, v2)
                parts = []
                for first_row, end_row in row_blocks(pad):
                    p = pb[first_row:end_row].astype(F32)
                    dp = whole_dp[first_row:end_row]
                    inner = jnp.sum(p * dp, axis=-1, keepdims=True)
                    parts.append((p * (dp - inner)).astype(BF16))
                ds = jnp.concatenate(parts, axis=0)
                dvh = tn(pb, dah)
                dqh = nn(ds, jnp.where(sel, k2, zero))
                dkh = tn(ds, jnp.where(sel, q2, zero))
                dq = dqh if dq is None else dq + dqh
                dk = dkh if dk is None else dk + dkh
                dv = dvh if dv is None else dv + dvh
            dq_s[pl.ds(row0, pad), cols] = (dq * 0.125).astype(BF16)
            dk_s[pl.ds(row0, pad), cols] = (dk * 0.125).astype(BF16)
            dv_s[pl.ds(row0, pad), cols] = dv.astype(BF16)
        return carry

    lax.fori_loop(0, ex, example, 0)
    z1 = z1_ref[...]
    dq, dk, dv = dq_s[...], dk_s[...], dv_s[...]
    width = z1.shape[1]
    for j, d in enumerate((dq, dk, dv)):
        if final:
            qkv_s[pl.ds(pl.multiple_of(j * width + gi * wide, wide), wide), :] = tn(d, z1).astype(BF16)
        else:
            qkv_s[j] = tn(d, z1).astype(BF16)
    acc[...] += nt(dq, wq_ref[...]) + nt(dk, wk_ref[...]) + nt(dv, wv_ref[...])
    bias_s[0, gi] = col_sum(dq.astype(F32))
    bias_s[1, gi] = col_sum(dv.astype(F32))

    if not final:
        return

    @pl.when(i == last)
    def _():
        nrm, r = ln_parts(h0_ref[...].astype(F32))
        dz = acc[...]
        g0 = g1_ref[...] + ln_back(dz, nrm, r, row_of(g_ref))
        n = width // 128
        vec_ref[5 * n :, :] = jnp.zeros_like(vec_ref[5 * n :, :])
        put_rows(vec_ref, n, col_sum(dz * nrm))
        put_rows(vec_ref, 2 * n, col_sum(dz))
        for j in range(2):
            for t in range(bias_s.shape[1]):
                put_rows(vec_ref, (3 + j) * n + t * (wide // 128), bias_s[j, t])
        gb = g0.astype(BF16)
        px = dtok_ref.shape[0] // ex
        pick_image = image_pick(px, pad, n_image, cols_real)
        tr = lax.broadcasted_iota(jnp.int32, (txt, pad), 0)
        tc = lax.broadcasted_iota(jnp.int32, (txt, pad), 1)
        pick_text = jnp.where(tc == tr + n_image, 1.0, 0.0).astype(BF16)
        tot = jnp.zeros((1, gb.shape[1]), F32)
        for e in range(ex):
            ge = gb[e * pad : (e + 1) * pad, :]
            text_ref[e] = nn(pick_text, ge).astype(BF16)
            dt = nn(pick_image, ge)
            dtok_ref[e * px : (e + 1) * px, :] = dt.astype(BF16)
            tot = tot + jnp.sum(dt, axis=0, keepdims=True)
        put_rows(vec_ref, 0, tot)
        if parted:
            core = place_ref[1]
            part_it(qkv_s, ak_ref, as_ref, core)
            proj_s[...] = tn(dtok_ref[...], stem_ref[...]).astype(BF16)
            part_it(proj_s, ak_ref, as_ref, core, at=(qkv_s.shape[0] + width) // (2 * ak_ref.shape[1]) * (width // 256))
            hi = ak_ref.shape[1]
            r = width // (2 * hi)
            at = qkv_s.shape[0] // (2 * hi) * (width // 256)

            def one(h, carry):
                mine = pl.ds(pl.multiple_of((2 * h + core) * r, 16), r)
                other = pl.ds(pl.multiple_of((2 * h + 1 - core) * r, 16), r)
                for blk in range(width // 128):
                    s, j = divmod(blk, width // 256)
                    t, lane = divmod(blk * 128, wide)
                    dst = slice(at + j * r, at + (j + 1) * r)
                    ak_ref[s, h, dst, :] = ow_s[t, mine, lane : lane + 128]
                    as_ref[s, h, dst, :] = ow_s[t, other, lane : lane + 128]
                return carry

            lax.fori_loop(0, hi, one, 0)


def image_pick(px, pad, n_image, cols_real):
    p = lax.broadcasted_iota(jnp.int32, (px, pad), 0)
    t = lax.broadcasted_iota(jnp.int32, (px, pad), 1)
    col = p & 15
    tok = (p >> 4) * cols_real + col
    return jnp.where((col < cols_real) & (tok == t) & (t < n_image), 1.0, 0.0).astype(BF16)


def attn_bwd(place, g1, out_w, attn, q, k, v, p, z1, h0, qkv_w, ln1_gain, ex, n_image, txt, img_rows, img_cols, pad, dp, parted,
             lo=0, hi=None, carry=(), stem=None, wide=256):
    rows, width = h0.shape
    groups = width // wide
    heads = width // HD
    hg = wide // HD
    px = img_rows * 16
    hi = groups if hi is None else hi
    final = hi == groups
    vec_rows = -(-5 * width // 128 // 8) * 8
    cols = lambda off: pl.BlockSpec((width, wide), lambda i: (0, i + lo + off * groups))
    part = pl.BlockSpec((rows, wide), lambda i: (0, i + lo))
    nat_o, nat_q = (groups, width, wide), (3 * width, width)
    sent = part_shape(4 * width, width, dp)
    if stem is not None:
        sent = sent[:2] + (sent[2] + part_shape(width, stem.shape[1], dp)[2], 128)
    scratch = [pltpu.VMEM((rows, width), BF16), pltpu.VMEM((width, rows), BF16)] + [pltpu.VMEM((rows, wide), BF16)] * 4
    args = [g1, out_w, attn, q, k, v, p, z1, qkv_w, qkv_w, qkv_w, *carry]
    in_specs = [SMEM, whole((rows, width)), pl.BlockSpec((wide, width), lambda i: (i + lo, 0)), part, part, part, part,
                pl.BlockSpec((ex, hg, pad, pad), lambda i: (0, i + lo, 0, 0)), whole((rows, width)), cols(0), cols(1), cols(2)]
    in_specs += [whole(c.shape) for c in carry]
    if final:
        outs = [(s, BF16) for s in ((sent, sent) if parted else (nat_o, nat_q))]
        outs += [((ex, txt, width), BF16), ((ex * px, width), BF16), ((vec_rows, 128), F32)]
        natural = [pltpu.VMEM(nat_o, BF16), pltpu.VMEM(nat_q, BF16), pltpu.VMEM((width, stem.shape[1]), BF16)] if parted else []
        scratch = natural + scratch + [pltpu.VMEM((rows, width), F32), pltpu.VMEM((2, groups, 1, wide), F32)]
        args += [h0, ln1_gain] + ([stem] if parted else [])
        in_specs += [whole((rows, width)), whole((width,))] + ([whole(stem.shape)] if parted else [])
    else:
        n = hi - lo
        outs = [((rows, width), F32), ((n, width, wide), BF16), ((3, n * wide, width), BF16), ((2, n, 1, wide), F32)]
    return pl.pallas_call(
        functools.partial(attn_bwd_kernel, ex, n_image, txt, img_cols, pad, parted, lo, final),
        grid=(hi - lo,),
        in_specs=in_specs,
        out_specs=[whole(s) for s, _ in outs],
        out_shape=[pltpu.HBM(s, d) for s, d in outs],
        scratch_shapes=scratch,
        compiler_params=pltpu.CompilerParams(dimension_semantics=("arbitrary",), vmem_limit_bytes=60 << 20),
        cost_estimate=pl.CostEstimate(flops=14 * (hi - lo) * 10**9, bytes_accessed=40 << 20, transcendentals=0),
        name="attention_backward",
    )(place, *[in_hbm(x) for x in args])

def over_pixels(shape, body, init=0):
    ex, rows = shape[:2]
    per = rows // 2

    def one(j, carry):
        return body(j // per, j % per * 2, pl.ds(pl.multiple_of(j * 32, 32), 32), carry)

    return lax.fori_loop(0, ex * per, one, init)


def stats_kernel(cols, x_ref, w_ref, parts_ref, xp):
    xp[...] = jnp.zeros_like(xp)
    shape = x_ref.shape
    xp[:, 0:cols, :] = x_ref[...].reshape(shape[0] * shape[1], cols, shape[3])
    a = nn(xp[...].reshape(shape[0] * shape[1] * 16, shape[3]), w_ref[...])
    put_stats(parts_ref, col_sum(a), col_sum(a * a))


def conv_fwd_kernel(count, ex, rows, cols, place_ref, parts_ref, own_ref, got_ref, win_ref, g_ref, s_ref, wmid_ref,
                    xs_ref, act1_ref, wide_ref, act2_ref, parts2_ref):
    s = place_ref[0]
    half = rows // 2
    px = rows * 16
    chan = xs_ref.shape[-1]
    xs_ref[...] = jnp.zeros_like(xs_ref)
    for e in range(ex):
        xs_ref[e, pl.ds(s * half, half), 0:cols, :] = own_ref[s * ex + e]
        xs_ref[e, pl.ds((1 - s) * half, half), 0:cols, :] = got_ref[e]
    a1 = nn(xs_ref[...].reshape(ex * px, chan), win_ref[...])
    act1_ref[...] = a1
    mid = a1.shape[1]
    mean, rstd = mean_rstd(parts_ref, mid, count)
    real = real_columns(ex * px, cols)
    act = gelu_of((a1 - mean) * rstd * row_of(g_ref) + row_of(s_ref))
    act = jnp.where(real, act, 0.0)
    for e in range(ex):
        part = act[e * px : (e + 1) * px]
        wide_ref[e, 0:16, :] = jnp.zeros((16, 3 * mid), BF16)
        wide_ref[e, px + 16 : px + 32, :] = jnp.zeros((16, 3 * mid), BF16)
        wide_ref[e, 16 : px + 16, 0:mid] = pltpu.roll(part, 1, 0).astype(BF16)
        wide_ref[e, 16 : px + 16, mid : 2 * mid] = part.astype(BF16)
        wide_ref[e, 16 : px + 16, 2 * mid : 3 * mid] = pltpu.roll(part, px - 1, 0).astype(BF16)
    one = real_columns(px, cols)
    t1 = jnp.zeros((1, mid), F32)
    t2 = jnp.zeros((1, mid), F32)
    for e in range(ex):
        a2 = nn(wide_ref[e, 0:px, :], wmid_ref[0])
        a2 = a2 + nn(wide_ref[e, 16 : px + 16, :], wmid_ref[1])
        a2 = a2 + nn(wide_ref[e, 32 : px + 32, :], wmid_ref[2])
        a2 = jnp.where(one, a2, 0.0)
        act2_ref[e * px : (e + 1) * px, :] = a2
        t1 = t1 + col_sum(a2)
        t2 = t2 + col_sum(a2 * a2)
    put_stats(parts2_ref, t1, t2)


def expand_kernel(count, cols, parts_ref, act2_ref, g_ref, s_ref, w_ref, relu2_ref, act3_ref, parts3_ref):
    a2 = act2_ref[...]
    mean, rstd = mean_rstd(parts_ref, a2.shape[1], count)
    act = gelu_of((a2 - mean) * rstd * row_of(g_ref) + row_of(s_ref))
    low = jnp.where(real_columns(a2.shape[0], cols), act, 0.0).astype(BF16)
    relu2_ref[...] = low
    a3 = nn(low, w_ref[...])
    act3_ref[...] = a3
    put_stats(parts3_ref, col_sum(a3), col_sum(a3 * a3))


def tokens_kernel(count, ex, cols, n_image, pad, parts_ref, act3_ref, xs_ref, g_ref, s_ref, w_ref, b_ref, text_ref,
                  stem_ref, h0_ref):
    mean, rstd = mean_rstd(parts_ref, act3_ref.shape[1], count)
    scale = rstd * row_of(g_ref)
    offset = row_of(s_ref) - mean * scale

    def body(e, r, rs, carry):
        pre = act3_ref[rs, :] * scale + offset + xs_ref[e, pl.ds(r, 2)].reshape(32, -1).astype(F32)
        stem_ref[rs, :] = gelu_of(pre).astype(BF16)
        return carry

    over_pixels(xs_ref.shape, body)
    tok = (nn(stem_ref[...], w_ref[...]) + row_of(b_ref)).astype(BF16)
    px = act3_ref.shape[0] // ex
    txt = text_ref.shape[1]
    t = lax.broadcasted_iota(jnp.int32, (pad, px), 0)
    p = lax.broadcasted_iota(jnp.int32, (pad, px), 1)
    col = p & 15
    pick = jnp.where((col < cols) & ((p >> 4) * cols + col == t), 1.0, 0.0).astype(BF16)
    tr = lax.broadcasted_iota(jnp.int32, (pad, txt), 0)
    tc = lax.broadcasted_iota(jnp.int32, (pad, txt), 1)
    pick_text = jnp.where(tr == tc + n_image, 1.0, 0.0).astype(BF16)
    for e in range(ex):
        both = nn(pick, tok[e * px : (e + 1) * px, :]) + nn(pick_text, text_ref[e])
        h0_ref[e * pad : (e + 1) * pad, :] = both.astype(BF16)


def dpre_kernel(count, ex, rows, place_ref, parts_ref, act3_ref, xs_ref, g_ref, s_ref, dtok_ref, w_ref, dpre_ref, send_ref, parts4_ref, raw_s):
    chan = act3_ref.shape[1]
    mean, rstd = mean_rstd(parts_ref, chan, count)
    gain, shift = row_of(g_ref), row_of(s_ref)
    raw_s[...] = nt(dtok_ref[...], w_ref[...])

    def body(e, r, rs, carry):
        nrm = (act3_ref[rs, :] - mean) * rstd
        _, slope = gelu_and_slope(nrm * gain + shift + xs_ref[e, pl.ds(r, 2)].reshape(32, chan).astype(F32))
        d = raw_s[rs, :] * slope
        dpre_ref[e, pl.ds(r, 2)] = d.astype(BF16).reshape(2, 16, chan)
        return carry[0] + jnp.sum(d.reshape(4, 8, chan), axis=0), carry[1] + jnp.sum((d * nrm).reshape(4, 8, chan), axis=0)

    zero = jnp.zeros((8, chan), F32)
    a, b = over_pixels(xs_ref.shape, body, (zero, zero))
    put_stats(parts4_ref, col_sum(a), col_sum(b))
    half = rows // 2
    other = 1 - place_ref[0]
    for e in range(ex):
        send_ref[e] = dpre_ref[e, pl.ds(other * half, half)]


def back3_kernel(count, cols, parts4_ref, parts3_ref, parts2_ref, act3_ref, dpre_ref, g3_ref, w_ref, act2_ref, g2_ref, s2_ref, veca_ref, vecb_ref,
                 low3_ref, t2_ref, parts5_ref, gain_ref, shift_ref, small_s):
    chan = act3_ref.shape[1]
    mean, rstd = mean_rstd(parts3_ref, chan, count)
    s1, s2 = get_stats(parts4_ref, chan)
    gain_ref[...] = s2.reshape(-1)
    shift_ref[...] = s1.reshape(-1)
    scale = row_of(g3_ref) * rstd
    c1, c2 = s1 * (1.0 / count), s2 * (1.0 / count)
    real = real_columns(32, cols)

    def body(e, r, rs, carry):
        nrm = (act3_ref[rs, :] - mean) * rstd
        d = scale * (dpre_ref[e, pl.ds(r, 2)].reshape(32, chan).astype(F32) - c1 - nrm * c2)
        low3_ref[rs, :] = jnp.where(real, d, 0.0).astype(BF16)
        return carry

    over_pixels(dpre_ref.shape, body)
    a2 = act2_ref[...]
    mean2, rstd2 = mean_rstd(parts2_ref, a2.shape[1], count)
    nrm2 = (a2 - mean2) * rstd2
    _, slope = gelu_and_slope(nrm2 * row_of(g2_ref) + row_of(s2_ref))
    t2 = nt(low3_ref[...], w_ref[...]) * slope
    t2_ref[...] = t2
    parts5_ref[...] = jnp.zeros_like(parts5_ref)
    put_stats(parts5_ref, col_sum(t2), col_sum(t2 * nrm2))
    used = veca_ref.shape[0] + vecb_ref.shape[0]
    n = parts5_ref.shape[0]
    each = -(-used // n)
    small_s[0 : veca_ref.shape[0], :] = veca_ref[...]
    small_s[veca_ref.shape[0] : used, :] = vecb_ref[...]
    if used < small_s.shape[0]:
        small_s[used:, :] = jnp.zeros_like(small_s[used:, :])
    for d in range(n):
        parts5_ref[d, 4 : 4 + each, :] = small_s[d * each : (d + 1) * each, :]


def back2_kernel(count, ex, rows, cols, place_ref, parts5_ref, parts2_ref, parts1_ref, act2_ref, t2_ref, g2_ref, wmid_ref, act1_ref, g1_ref, s1_ref,
                 low2_ref, t1_ref, send_ref, parts6_ref, gain_ref, shift_ref, wide):
    a2 = act2_ref[...]
    mid = a2.shape[1]
    px = rows * 16
    mean, rstd = mean_rstd(parts2_ref, mid, count)
    s1, s2 = get_stats(parts5_ref, mid)
    gain_ref[...] = s2.reshape(-1)
    shift_ref[...] = s1.reshape(-1)
    nrm = (a2 - mean) * rstd
    d = (row_of(g2_ref) * rstd) * (t2_ref[...] - s1 * (1.0 / count) - nrm * (s2 * (1.0 / count)))
    d = jnp.where(real_columns(ex * px, cols), d, 0.0)
    low2_ref[...] = d.astype(BF16)
    for e in range(ex):
        part = d[e * px : (e + 1) * px]
        wide[e, 0:16, :] = jnp.zeros((16, 3 * mid), BF16)
        wide[e, px + 16 : px + 32, :] = jnp.zeros((16, 3 * mid), BF16)
        wide[e, 16 : px + 16, 0:mid] = pltpu.roll(part, px - 1, 0).astype(BF16)
        wide[e, 16 : px + 16, mid : 2 * mid] = part.astype(BF16)
        wide[e, 16 : px + 16, 2 * mid : 3 * mid] = pltpu.roll(part, 1, 0).astype(BF16)
    mean1, rstd1 = mean_rstd(parts1_ref, mid, count)
    one = real_columns(px, cols)
    q1 = jnp.zeros((1, mid), F32)
    q2 = jnp.zeros((1, mid), F32)
    for e in range(ex):
        t = None
        for r in range(3):
            for c in range(3):
                term = nt(wide[e, (2 - r) * 16 : (2 - r) * 16 + px, c * mid : (c + 1) * mid], wmid_ref[r, c * mid : (c + 1) * mid, :])
                t = term if t is None else t + term
        nrm1 = (act1_ref[e * px : (e + 1) * px, :] - mean1) * rstd1
        _, slope = gelu_and_slope(nrm1 * row_of(g1_ref) + row_of(s1_ref))
        t = jnp.where(one, t * slope, 0.0)
        t1_ref[e] = t.reshape(rows, 16, mid)
        q1 = q1 + col_sum(t)
        q2 = q2 + col_sum(t * nrm1)
    put_stats(parts6_ref, q1, q2)
    chunk = jnp.sum(parts5_ref[:, 4:8, :], axis=0)
    parts6_ref[:, 4:8, :] = jnp.broadcast_to(chunk[None], (parts6_ref.shape[0], 4, 128))
    half = rows // 2
    other = 1 - place_ref[0]
    for e in range(ex):
        send_ref[e] = t1_ref[e, pl.ds(other * half, half)].astype(BF16)


def conv_grads_kernel(ex, px, parted, place_ref, low2_ref, wide_ref, low3_ref, relu2_ref, *refs):
    mid = low2_ref.shape[1]
    nat_m, nat_o = (refs[2], refs[3]) if parted else (refs[0], refs[1])
    nat_o[...] = tn(low3_ref[...], relu2_ref[...]).astype(BF16)
    for r in range(3):
        tot = None
        for e in range(ex):
            term = tn(low2_ref[e * px : (e + 1) * px, :], wide_ref[e, r * 16 : r * 16 + px, :])
            tot = term if tot is None else tot + term
        for c in range(3):
            for h in range(2):
                at = (h * 9 + r * 3 + c) * (mid // 2)
                src = c * mid + h * (mid // 2)
                nat_m[:, at : at + mid // 2] = tot[:, src : src + mid // 2].astype(BF16)
    if parted:
        part_it(nat_m, refs[0], refs[1], place_ref[1])
        part_it(nat_o, refs[0], refs[1], place_ref[1], at=nat_m.shape[0] // (2 * refs[0].shape[1]) * (nat_m.shape[1] // 256))


def tn_kernel(parted, place_ref, a_ref, b_ref, *refs):
    natural = refs[2] if parted else refs[0]
    natural[...] = tn(a_ref[...], b_ref[...]).astype(BF16)
    if parted:
        part_it(natural, refs[0], refs[1], place_ref[1])


def first_back_kernel(count, ex, rows, cols, parted, each, places, place_ref, parts6_ref, parts1_ref, x_ref, win_ref, g_ref, t1_ref, gott_ref,
                      low_ref, *refs):
    if parted:
        keep_ref, send_ref, win_grad_ref = refs[0], refs[1], refs[-1]
        refs = refs[2:-1]
    else:
        win_grad_ref, refs = refs[0], refs[1:]
    gain_ref, shift_ref, vec_refs, xp, small_s = refs[0], refs[1], refs[2:-2], refs[-2], refs[-1]
    s = place_ref[0]
    half = rows // 2
    chan = x_ref.shape[-1]
    mid = win_ref.shape[1]
    mean, rstd = mean_rstd(parts1_ref, mid, count)
    s1, s2 = get_stats(parts6_ref, mid)
    gain_ref[...] = s2.reshape(-1)
    shift_ref[...] = s1.reshape(-1)
    real = real_columns(ex * half * 16, cols)
    size = ex * half * 16
    xp[...] = jnp.zeros_like(xp)
    wg = None
    for own in (True, False):
        at = (s if own else 1 - s) * ex
        xp[:, 0:cols, :] = x_ref[pl.ds(at, ex)].reshape(ex * half, cols, chan)
        x = xp[...].reshape(size, chan)
        nrm = (nn(x, win_ref[...]) - mean) * rstd
        if own:
            t = t1_ref[:, pl.ds(s * half, half)].reshape(size, mid)
        else:
            t = gott_ref[...].reshape(size, mid).astype(F32)
        d = (row_of(g_ref) * rstd) * (t - s1 * (1.0 / count) - nrm * (s2 * (1.0 / count)))
        low = jnp.where(real, d, 0.0).astype(BF16)
        low_ref[0 if own else 1] = low
        term = tn(low, x)
        wg = term if wg is None else wg + term
    win_grad_ref[...] = wg.astype(BF16)
    if parted:
        part_it(win_grad_ref, keep_ref, send_ref, place_ref[1])
    for d in range(parts6_ref.shape[0]):
        small_s[d * each : (d + 1) * each, :] = parts6_ref[d, 4 : 4 + each, :]
    for ref, at in zip(vec_refs, places):
        ref[...] = take_rows(small_s, at, ref.shape[0]).reshape(-1)


def image_kernel(ex, rows, cols, place_ref, low_ref, win_ref, dpre_ref, gotd_ref, grad_ref):
    s = place_ref[0]
    half = rows // 2
    chan = win_ref.shape[0]
    size = ex * half * 16
    for own in (True, False):
        at = (s if own else 1 - s) * ex
        dp = dpre_ref[:, pl.ds(s * half, half)] if own else gotd_ref[...]
        grad = nt(low_ref[0 if own else 1], win_ref[...]) + dp.reshape(size, chan).astype(F32)
        grad_ref[pl.ds(at, ex)] = grad.astype(BF16).reshape(ex, half, 16, chan)[:, :, 0:cols, :]


def in_hbm(x):
    return pltpu.with_memory_space_constraint(x, pltpu.HBM)


def call(kernel, outs, *args, moved=(), place=None, scratch=(), name=None, us=2, limit=40):
    nbytes = sum(a.size * a.dtype.itemsize for a in args)
    spec = lambda s: pl.BlockSpec(s, lambda i: (0,) * len(s))
    return pl.pallas_call(
        kernel,
        grid=(1,),
        out_shape=[pltpu.HBM(s, d) for s, d in outs],
        in_specs=([SMEM] if place is not None else []) + [spec(a.shape) for a in args],
        out_specs=[spec(s) for s, _ in outs],
        scratch_shapes=list(scratch),
        compiler_params=pltpu.CompilerParams(vmem_limit_bytes=limit << 20),
        cost_estimate=pl.CostEstimate(flops=us * 10**9, bytes_accessed=nbytes if us else 0, transcendentals=0),
        name=name,
    )(*([place] if place is not None else []), *[a if any(a is b for b in moved) else in_hbm(a) for a in args])


DP = ("far", "near", "core")
AXES = DP + ("space",)


def spread(parts):
    return lax.all_to_all(parts, AXES, split_axis=0, concat_axis=0, tiled=True)


def swap(x, axis="space"):
    return lax.ppermute(x, axis, [(0, 1), (1, 0)])


def tie(*values):
    return lax.optimization_barrier(values)


BITS = ("space", "f1", "f0", "near")


def bit_of(name):
    if name in ("f0", "f1"):
        return (lax.axis_index("far") // (1 if name == "f0" else 2)) % 2
    return lax.axis_index(name)


def sent(x, key):
    if key == ("core",):
        return swap(x, "core")
    flip = {n: int(n in key) for n in BITS}
    far, near, space = 2 * flip["f1"] + flip["f0"], flip["near"], flip["space"]
    if far and (near or space):
        raise ValueError
    if far:
        return lax.ppermute(x, "far", [(j, j ^ far) for j in range(4)])
    if near and space:
        return lax.ppermute(x, ("near", "space"), [(j, 3 - j) for j in range(4)])
    return swap(x, "near" if near else "space")


class Box:
    def __init__(self, value, moved=False):
        self.value, self.moved = value, moved


class Pack:
    def __init__(self, sources, left, size, at=0, rows=None):
        self.sources, self.left, self.size, self.at, self.rows = sources, left, size, at, size if rows is None else rows

    @classmethod
    def start(cls, keep, send):
        size = keep.shape[-2]
        got = sent(send, ("core",))
        return cls([(Box(keep.reshape(-1, 128)), 0), (Box(got.reshape(-1, 128), True), 0)], list(BITS), size)

    def thirds(self):
        r = self.size // 3
        return [Pack(self.sources, self.left, self.size, k * r, r) for k in range(3)]


def arrive(value, *packs):
    boxes = []
    for x in packs:
        boxes += [b for b, _ in x.sources if b.moved and b not in boxes]
    flat = tie(value, *[b.value for b in boxes])
    for b, v in zip(boxes, flat[1:], strict=True):
        b.value = v
    return flat[0]


def combine_kernel(plan, n_in, bits_ref, *refs):
    ins, outs = refs[:n_in], refs[n_in:]
    for sources, left, size, at, rows, names, dests in plan:
        rest = [d for d in left if d not in names]
        for rel, (out, to) in enumerate(dests):
            for c in range(2 ** len(rest)):
                place = 0
                for pos, d in enumerate(left):
                    stride = 2 ** (len(left) - 1 - pos)
                    if d in names:
                        bit = bits_ref[BITS.index(d)]
                        if (rel >> (len(names) - 1 - names.index(d))) & 1:
                            bit = 1 - bit
                    else:
                        bit = (c >> (len(rest) - 1 - rest.index(d))) & 1
                    place = place + bit * stride
                tot = None
                for idx, first in sources:
                    x = ins[idx][pl.ds(pl.multiple_of(first + place * size + at, 16), rows), :].astype(F32)
                    tot = x if tot is None else tot + x
                outs[out][to + c * rows : to + (c + 1) * rows, :] = tot.astype(BF16)


def step(bits, moves, tied):
    boxes, plan, keys, totals, after = [], [], [], {(): 0}, []
    for pack, names in moves:
        srcs = []
        for box, first in pack.sources:
            if box not in boxes:
                boxes.append(box)
            srcs.append((boxes.index(box), first))
        rest = [d for d in pack.left if d not in names]
        n = 2 ** len(rest) * pack.rows
        dests = []
        for rel in range(2 ** len(names)):
            key = tuple(d for j, d in enumerate(names) if (rel >> (len(names) - 1 - j)) & 1)
            key = tuple(sorted(key))
            if key not in totals:
                totals[key] = 0
            if key not in keys:
                keys.append(key)
            dests.append((key, totals[key]))
            totals[key] += n
        plan.append((srcs, list(pack.left), pack.size, pack.at, pack.rows, names, dests))
        after.append((rest, pack.rows, dests))
    plan = [(*p[:-1], [(keys.index(k), to) for k, to in p[-1]]) for p in plan]
    args = [b.value if b.moved else in_hbm(b.value) for b in boxes]
    one = lambda shape: pl.BlockSpec(shape, lambda t: (0, 0), pipeline_mode=pl.Buffered(1))
    res = pl.pallas_call(
        functools.partial(combine_kernel, plan, len(args)),
        grid=(1,),
        in_specs=[SMEM] + [one(x.shape) for x in args],
        out_specs=[one((totals[k], 128)) for k in keys],
        out_shape=[pltpu.HBM((totals[k], 128), BF16) for k in keys],
        compiler_params=pltpu.CompilerParams(vmem_limit_bytes=40 << 20),
        cost_estimate=pl.CostEstimate(flops=0, bytes_accessed=0, transcendentals=0),
        name="combine",
    )(bits, *args)
    flat = tie(tied, *res)
    arrays = {k: Box(flat[1 + j] if k == () else sent(flat[1 + j], k), k != ()) for j, k in enumerate(keys)}
    packs = [Pack([(arrays[k], to) for k, to in dests], rest, rows) for rest, rows, dests in after]
    return flat[0], packs


def finish_kernel(plan, n_in, *refs):
    ins, outs = refs[:n_in], refs[n_in:]
    for sources, pieces in plan:
        for first, r, blocks, out in pieces:
            for b in range(blocks):
                tot = None
                for idx, at in sources:
                    lo = at + first + b * r
                    if len(ins[idx].shape) == 3:
                        x = jnp.sum(ins[idx][:, lo : lo + r, :].astype(F32), axis=0)
                    else:
                        x = ins[idx][lo : lo + r, :].astype(F32)
                    tot = x if tot is None else tot + x
                if len(outs[out].shape) == 3:
                    outs[out][b] = tot
                else:
                    outs[out][:, b * 128 : (b + 1) * 128] = tot


def finish(groups, shapes, name):
    boxes, plan = [], []
    for sources, pieces in groups:
        srcs = []
        for box, first in sources:
            if box not in boxes:
                boxes.append(box)
            srcs.append((boxes.index(box), first))
        plan.append((srcs, pieces))
    args = [b.value for b in boxes]
    return call(functools.partial(finish_kernel, plan, len(args)), [(s, F32) for s in shapes], *args, moved=args, name=name)


def halve_dp(x, axis, bit):
    size = lax.axis_size(DP)
    mine = (lax.axis_index(DP) // bit) % 2
    keep = lax.dynamic_index_in_dim(x, mine, axis, keepdims=True)
    send = lax.dynamic_index_in_dim(x, 1 - mine, axis, keepdims=True)
    return keep + lax.ppermute(send, DP, [(j, j ^ bit) for j in range(size)])


def scattered(grad_t):
    size = lax.axis_size(DP)
    bits = size.bit_length() - 1
    cols, rows = grad_t.shape
    x = grad_t.reshape((2,) * bits + (cols // size, rows))
    for b in range(bits):
        x = halve_dp(x, bits - 1 - b, 1 << b)
    half = rows // 2
    mine = lax.axis_index("space")
    keep = lax.dynamic_slice_in_dim(x, mine * half, half, axis=x.ndim - 1)
    send = lax.dynamic_slice_in_dim(x, (1 - mine) * half, half, axis=x.ndim - 1)
    return (keep + swap(send)).reshape(cols // size, half).astype(F32).T


def shards(
    image_in, text_in, prefix, text_len, cotangent,
    conv_in_w, bn1_gain, bn1_shift, conv_mid_w, bn2_gain, bn2_shift, conv_out_w, bn3_gain, bn3_shift,
    proj_w, proj_b, ln1_gain, ln1_shift, qkv_w, query_bias, value_bias, out_w, out_b,
    ln2_gain, ln2_shift, up_w, up_b, down_w, down_b,
):
    n_dev, dp = lax.axis_size(AXES), lax.axis_size(DP)
    band_ex, band_rows, cols, chan = image_in.shape
    mid = conv_in_w.shape[1]
    width = proj_w.shape[1]
    ff = up_w.shape[1]
    ex, txt, _ = text_in.shape
    rows = band_rows * lax.axis_size("space")
    n_image = rows * cols
    seq = n_image + txt
    pad = -(-seq // 16) * 16
    px = rows * 16
    count = float(band_ex * band_rows * cols * n_dev)
    me = lax.axis_index("space").astype(jnp.int32)
    place = jnp.stack([me, lax.axis_index("core").astype(jnp.int32)])
    small, large, tiny = (n_dev, stat_rows(mid), 128), (n_dev, stat_rows(chan), 128), (n_dev, 2 * mid // 128, 128)
    wmid = conv_mid_w.reshape(3, 3 * mid, mid)
    weights = [(mid, chan), (mid, 9 * mid), (chan, mid), (width, chan), (3 * width, width), (width, width), (ff, width), (width, ff)]
    parted = dp == 16 and mid == 256 and all(c % (16 * dp) == 0 and r % 256 == 0 for c, r in weights)
    hi = dp // 2

    def grad_outs(c, r):
        return [(part_shape(c, r, dp), BF16)] * 2 if parted else [((c, r), BF16)]

    def natural(c, r):
        return [pltpu.VMEM((c, r), BF16)] if parted else []

    got_x = swap(lax.dynamic_slice_in_dim(image_in, (1 - me) * ex, ex, axis=0))
    parts1, = call(functools.partial(stats_kernel, cols), [(tiny, F32)], image_in, conv_in_w,
                   scratch=[pltpu.VMEM((band_ex * band_rows, 16, chan), BF16)], name="stats_one")
    parts1 = spread(parts1)
    xs, act1, wide, act2, parts2 = call(
        functools.partial(conv_fwd_kernel, count, ex, rows, cols),
        [((ex, rows, 16, chan), BF16), ((ex * px, mid), F32), ((ex, px + 32, 3 * mid), BF16), ((ex * px, mid), F32), (tiny, F32)],
        parts1, image_in, got_x, conv_in_w, bn1_gain, bn1_shift, wmid, moved=(parts1, got_x), place=place, name="conv_three", us=4)
    parts2 = spread(parts2)
    relu2, act3, parts3 = call(
        functools.partial(expand_kernel, count, cols),
        [((ex * px, mid), BF16), ((ex * px, chan), F32), (large, F32)],
        parts2, act2, bn2_gain, bn2_shift, conv_out_w, moved=(parts2,), name="expand")
    parts3 = spread(parts3)
    stem, h0 = call(
        functools.partial(tokens_kernel, count, ex, cols, n_image, pad),
        [((ex * px, chan), BF16), ((ex * pad, width), BF16)],
        parts3, act3, xs, bn3_gain, bn3_shift, proj_w, proj_b, text_in, moved=(parts3,), name="tokens", us=5)
    z1, q, k, v, p, attn, h1, z2 = attn_fwd(h0, prefix, text_len, ln1_gain, ln1_shift, qkv_w, query_bias, value_bias,
                                            out_w, out_b, ln2_gain, ln2_shift, ex, n_image, pad)
    mlp_outs = mlp(place, z2, h1, cotangent, up_w, up_b, down_w, down_b, ln2_gain, pad, dp, parted)
    block_out, mlp_grads, (g1, veca) = mlp_outs[0], mlp_outs[1:-2], mlp_outs[-2:]
    if parted:
        bits = jnp.stack([bit_of(n) for n in BITS]).astype(jnp.int32)
        down, up = Pack.start(*mlp_grads[:2]), Pack.start(*mlp_grads[2:])
    back_args = (out_w, attn, q, k, v, p, z1, h0, qkv_w, ln1_gain, ex, n_image, txt, rows, cols, pad, dp, parted)
    if parted:
        carry = attn_bwd(place, g1, *back_args, hi=1)
        turns = [["space"], ["near"], ["f0"]]
        ffn = down.thirds() + up.thirds()
        g1, ffn = step(bits, list(zip(ffn, turns + turns)), tie(g1, *carry)[0])
        att_outs = attn_bwd(place, g1, *back_args, lo=1, carry=carry, stem=stem)
    else:
        att_outs = attn_bwd(place, g1, *back_args)
    att_grads, (text_grad, dtok, vecb) = att_outs[:-3], att_outs[-3:]
    if parted:
        later = turns[1:] + turns[:1]
        (dtok, att_send), ffn = step(bits, list(zip(ffn, later * 2)), (dtok, att_grads[1]))
        att = Pack.start(att_grads[0], att_send)
    dpre, dsend, parts4 = call(
        functools.partial(dpre_kernel, count, ex, rows),
        [((ex, rows, 16, chan), BF16), ((ex, band_rows, 16, chan), BF16), (large, F32)],
        parts3, act3, xs, bn3_gain, bn3_shift, dtok, proj_w, moved=(parts3,), place=place, scratch=[pltpu.VMEM((ex * px, chan), F32)], name="stem_back", us=7)
    got_d = swap(dsend)
    if parted:
        parts4 = arrive(parts4, *ffn, att)
    parts4 = spread(parts4)
    if parted:
        later = later[1:] + later[:1]
        dpre, moved = step(bits, list(zip(ffn, later * 2)) + list(zip(att.thirds(), later)), dpre)
        ffn, att = moved[:6], moved[6:]
    else:
        proj_g = call(functools.partial(tn_kernel, parted), grad_outs(width, chan), dtok, stem, place=place, name="proj_grad", us=0)
    low3, t2, parts5, bn3_gg, bn3_sg = call(
        functools.partial(back3_kernel, count, cols),
        [((ex * px, chan), BF16), ((ex * px, mid), F32), (small, F32), ((chan,), F32), ((chan,), F32)],
        parts4, parts3, parts2, act3, dpre, bn3_gain, conv_out_w, act2, bn2_gain, bn2_shift, veca, vecb, moved=(parts4, parts3, parts2),
        scratch=[pltpu.VMEM((n_dev * -(-(veca.shape[0] + vecb.shape[0]) // n_dev), 128), F32)], name="back_three", us=4)
    if parted:
        t2 = arrive(t2, *att)
    parts5 = spread(parts5)
    if parted:
        later = later[1:] + later[:1]
        t2, moved = step(bits, [(x, ["f1"]) for x in ffn] + list(zip(att, later)), t2)
        ffn, att = moved[:6], moved[6:]
    low2, t1, tsend, parts6, bn2_gg, bn2_sg = call(
        functools.partial(back2_kernel, count, ex, rows, cols),
        [((ex * px, mid), BF16), ((ex, rows, 16, mid), F32), ((ex, band_rows, 16, mid), BF16), (small, F32), ((mid,), F32), ((mid,), F32)],
        parts5, parts2, parts1, act2, t2, bn2_gain, wmid, act1, bn1_gain, bn1_shift,
        moved=(parts5, parts2, parts1), place=place, scratch=[pltpu.VMEM((ex, px + 32, 3 * mid), BF16)], name="back_two", us=4)
    got_t = swap(tsend)
    parts6 = spread(parts6)
    if parted:
        low2, got_t = arrive(tie(low2, got_t), *att)
    conv_g = call(
        functools.partial(conv_grads_kernel, ex, px, parted),
        [(part_shape(mid, 9 * mid, dp)[:2] + (part_shape(mid, 9 * mid, dp)[2] + part_shape(chan, mid, dp)[2], 128), BF16)] * 2
        if parted else [((mid, 9 * mid), BF16), ((chan, mid), BF16)],
        low2, wide, low3, relu2, place=place, scratch=natural(mid, 9 * mid) + natural(chan, mid), name="conv_grads", us=4)
    if parted:
        parts6, conv_send = arrive(tie(parts6, conv_g[1]), *ffn, *att)
        conv = Pack.start(conv_g[0], conv_send)
    each = -(-(veca.shape[0] + vecb.shape[0]) // n_dev)
    n, off = width // 128, veca.shape[0]
    places = [off, off + n, off + 2 * n, off + 3 * n, off + 4 * n, 3 * n, n, 2 * n, 4 * n, 0]
    sizes = [width] * 8 + [ff, width]
    last = call(
        functools.partial(first_back_kernel, count, ex, rows, cols, parted, each, places),
        [((2, ex * band_rows * 16, mid), BF16)] + grad_outs(mid, chan) + [((mid,), F32)] * 2 + [((s,), F32) for s in sizes],
        parts6, parts1, image_in, conv_in_w, bn1_gain, t1, got_t,
        moved=(parts6, parts1, got_t), place=place, scratch=[pltpu.VMEM((ex * band_rows, 16, chan), BF16), pltpu.VMEM((n_dev * each, 128), F32)] + natural(mid, chan),
        name="first_back", us=3)
    low1, sums = last[0], last[3 if parted else 2 :]
    bn1_gg, bn1_sg, vecs = sums[0], sums[1], sums[2:]
    if parted:
        later = later[1:] + later[:1]
        (low1, keep_x), moved = step(bits, list(zip(att, later)) + [(conv, ["near", "space"])], (low1, last[1]))
        att, conv = moved[:3], moved[3]
    image_grad, = call(functools.partial(image_kernel, ex, rows, cols), [(image_in.shape, BF16)], low1, conv_in_w, dpre, got_d,
                       moved=(got_d,), place=place, name="image_back", us=4)
    if parted:
        in_x = (keep_x + swap(last[2], "core")).reshape((2 * hi,) + keep_x.shape[2:])
        in_x = lax.all_to_all(in_x, ("space", "far", "near"), split_axis=0, concat_axis=0, tiled=True)
        image_grad, moved = step(bits, [(x, ["f1"]) for x in att] + [(conv, ["f1", "f0"])], image_grad)
        att, conv = moved[:3], moved[3]
        r_mid, r_out3, r_q, r_w, r_f = mid // dp, chan // dp, 3 * width // dp, width // dp, ff // dp
        mids, half = r_mid * (9 * mid // 256), width // 256
        g_down, g_up = finish(
            [(ffn[0].sources, [(0, r_w, ff // 256, 0)]), (ffn[3].sources, [(0, r_f, half, 1)])],
            [(r_w, ff // 2), (r_f, width // 2)], "finish_early")
        g_qkv, g_out, g_proj, g_mid, g_out3, g_in = finish(
            [(att[0].sources, [(0, r_q, half, 0), (r_q * half, r_w, half, 1), ((r_q + r_w) * half, r_w, chan // 256, 2)]),
             (conv.sources, [(0, r_mid, 9 * mid // 256, 3), (mids, r_out3, mid // 256, 4)]),
             ([(Box(in_x), 0)], [(0, r_mid, chan // 256, 5)])],
            [(r_q, width // 2), (r_w, width // 2), (r_w, chan // 2), (9 * mid // 256, r_mid, 128), (r_out3, mid // 2), (r_mid, chan // 2)], "finish_late")
        g_down, g_up, g_qkv, g_out, g_proj, g_out3, g_in = [g.T for g in (g_down, g_up, g_qkv, g_out, g_proj, g_out3, g_in)]
        g_mid = g_mid.reshape(3, 3, r_mid, mid // 2).transpose(0, 1, 3, 2)
    else:
        out_n = att_outs[0].transpose(1, 0, 2).reshape(width, width)
        g_in, g_mid, g_out3, g_proj, g_qkv, g_out, g_up, g_down = [
            scattered(x) for x in (last[1], conv_g[0], conv_g[1], proj_g[0], att_outs[1], out_n, mlp_grads[1], mlp_grads[0])]
        g_mid = g_mid.reshape(3, 3, mid // 2, -1)
    return (
        block_out, image_grad, text_grad,
        g_in, bn1_gg, bn1_sg,
        g_mid, bn2_gg, bn2_sg,
        g_out3, bn3_gg, bn3_sg,
        g_proj, vecs[0], vecs[1], vecs[2],
        g_qkv, vecs[3], vecs[4],
        g_out, vecs[5], vecs[6], vecs[7],
        g_up, vecs[8],
        g_down, vecs[9],
    )


def solution(mesh):
    dp, space = mesh.devices.shape
    fine = Mesh(mesh.devices.reshape(dp // 4, 2, 2, space), AXES)
    return jax.shard_map(
        shards,
        mesh=fine,
        in_specs=(
            P(DP, "space", None, None),
            P(AXES, None, None),
            P(AXES),
            P(AXES),
            P(AXES, None, None),
            P(),
            P(),
            P(),
            P(),
            P(),
            P(),
            P(),
            P(),
            P(),
            P(),
            P(),
            P(),
            P(),
            P(),
            P(),
            P(),
            P(),
            P(),
            P(),
            P(),
            P(),
            P(),
            P(),
            P(),
        ),
        out_specs=(
            P(AXES, None, None),
            P(DP, "space", None, None),
            P(AXES, None, None),
            P("space", DP),
            P(),
            P(),
            P(None, None, "space", DP),
            P(),
            P(),
            P("space", DP),
            P(),
            P(),
            P("space", DP),
            P(),
            P(),
            P(),
            P("space", DP),
            P(),
            P(),
            P("space", DP),
            P(),
            P(),
            P(),
            P("space", DP),
            P(),
            P("space", DP),
            P(),
        ),
        check_vma=False,
    )
```

```python
import functools
import jax
import jax.numpy as jnp
from jax import lax
from jax.experimental import pallas as pl
from jax.experimental.pallas import tpu as pltpu
from jax.sharding import Mesh, PartitionSpec as P

HD = 64
F32 = jnp.float32
BF16 = jnp.bfloat16
eps_batch = 1e-05
eps_layer = 1e-06
masked_value = -1e30
GELU_C = 0.7978845608028654
GELU_A = 0.044715


def nn(a, b):
    return lax.dot_general(a, b, (((1,), (0,)), ((), ())), preferred_element_type=F32)


def nt(a, b):
    return lax.dot_general(a, b, (((1,), (1,)), ((), ())), preferred_element_type=F32)


def tn(a, b):
    return lax.dot_general(a, b, (((0,), (0,)), ((), ())), preferred_element_type=F32)


def gelu_of(x):
    t = jnp.tanh(GELU_C * (x + GELU_A * x * x * x))
    return 0.5 * x * (1.0 + t)


def gelu_and_slope(x):
    x2 = x * x
    t = jnp.tanh(x * (GELU_C + (GELU_C * GELU_A) * x2))
    half = 0.5 + 0.5 * t
    slope = half + (0.5 * x) * (1.0 - t * t) * (GELU_C + (3.0 * GELU_C * GELU_A) * x2)
    return x * half, slope


def ln_parts(x):
    mean = jnp.mean(x, axis=-1, keepdims=True)
    c = x - mean
    var = jnp.mean(c * c, axis=-1, keepdims=True)
    r = lax.rsqrt(var + eps_layer)
    return c * r, r


def ln_back(dz, nrm, r, gain):
    u = dz * gain
    return r * (u - jnp.mean(u, axis=-1, keepdims=True) - nrm * jnp.mean(u * nrm, axis=-1, keepdims=True))


def whole(shape):
    return pl.BlockSpec(shape, lambda *_: (0,) * len(shape), pipeline_mode=pl.Buffered(1))


SMEM = pl.BlockSpec(memory_space=pltpu.SMEM)
VMEM = pl.BlockSpec(memory_space=pltpu.VMEM)


def row_of(ref):
    return ref[...].reshape(1, -1)


def put_rows(ref, at, vector):
    for r in range(vector.shape[1] // 128):
        ref[at + r : at + r + 1, :] = vector[:, r * 128 : (r + 1) * 128]


def take_rows(ref, at, size):
    return jnp.concatenate([ref[at + r : at + r + 1, :] for r in range(size // 128)], axis=1)


def part_shape(cols, rows, dp):
    return (2, dp // 2, cols // dp * (rows // 2) // 128, 128)


def part_it(natural, keep_ref, send_ref, core, at=0):
    rows, cols = natural.shape[-2:]
    hi = keep_ref.shape[1]
    r, blocks = rows // (2 * hi), cols // 256

    def one(h, carry):
        mine = pl.ds(pl.multiple_of((2 * h + core) * r, 16), r)
        other = pl.ds(pl.multiple_of((2 * h + 1 - core) * r, 16), r)
        for s in range(2):
            for b in range(blocks):
                lanes = slice((s * blocks + b) * 128, (s * blocks + b + 1) * 128)
                keep_ref[s, h, at + b * r : at + (b + 1) * r, :] = natural[mine, lanes]
                send_ref[s, h, at + b * r : at + (b + 1) * r, :] = natural[other, lanes]
        return carry

    lax.fori_loop(0, hi, one, 0)


def mlp_kernel(ex, seq, pad, parted, place_ref, z2_ref, h1_ref, cot_ref, upw_ref, upb_ref, dnw_ref, dnb_ref, g_ref, *refs):
    if parted:
        out_ref, dk_ref, ds_ref, uk_ref, us_ref, g1_ref, vec_ref, g2_s, g2t_s, acc_o, acc_d, ub_s, bg_s = refs
    else:
        out_ref, dn_ref, up_ref, g1_ref, vec_ref, g2_s, g2t_s, acc_o, acc_d, ub_s, bg_s = refs
    i = pl.program_id(0)
    last = pl.num_programs(0) - 1
    tile = upw_ref.shape[1]

    @pl.when(i == 0)
    def _():
        g2_s[...] = jnp.zeros_like(g2_s)
        for e in range(ex):
            g2_s[e * pad : e * pad + seq, :] = cot_ref[e]
        g2t_s[...] = g2_s[...].T
        acc_o[...] = jnp.zeros_like(acc_o)
        acc_d[...] = jnp.zeros_like(acc_d)
        ub = row_of(upb_ref)
        for j in range(ub_s.shape[0]):
            ub_s[j] = ub[:, j * tile : (j + 1) * tile]

    z2 = z2_ref[...]
    g2 = g2_s[...]
    pre = nn(z2, upw_ref[...]) + ub_s[i]
    act, slope = gelu_and_slope(pre)
    low = act.astype(BF16)
    dg = (nt(g2, dnw_ref[...]) * slope).astype(BF16)
    acc_o[...] += nn(low, dnw_ref[...])
    acc_d[...] += nt(dg, upw_ref[...])
    dn = nn(g2t_s[...], low).astype(BF16)
    up = tn(dg, z2).astype(BF16)
    bg_s[i] = jnp.sum(dg.astype(F32), axis=0, keepdims=True)
    if parted:
        core = place_ref[1]
        even = core == 0
        hi = dk_ref.shape[1]
        r = dn.shape[0] // (2 * hi)
        for j in range(tile // 128):
            d4 = dn[:, j * 128 : (j + 1) * 128].reshape(hi, 2, r, 128)
            dk_ref[0, :, j * r : (j + 1) * r, :] = jnp.where(even, d4[:, 0], d4[:, 1])
            ds_ref[0, :, j * r : (j + 1) * r, :] = jnp.where(even, d4[:, 1], d4[:, 0])
        r, blocks = up.shape[0] // 4, up.shape[1] // 256
        for s in range(2):
            for j in range(blocks):
                lanes = slice((s * blocks + j) * 128, (s * blocks + j + 1) * 128)
                for t in range(2):
                    first, second = up[2 * t * r : (2 * t + 1) * r, lanes], up[(2 * t + 1) * r : (2 * t + 2) * r, lanes]
                    uk_ref[s, t, j * r : (j + 1) * r, :] = jnp.where(even, first, second)
                    us_ref[s, t, j * r : (j + 1) * r, :] = jnp.where(even, second, first)
    else:
        dn_ref[...] = dn
        up_ref[...] = up

    @pl.when(i == last)
    def _():
        h1 = h1_ref[...]
        out = (h1 + acc_o[...] + row_of(dnb_ref)).astype(BF16)
        for e in range(ex):
            out_ref[e] = out[e * pad : e * pad + seq, :]
        nrm, r = ln_parts(h1)
        dz = acc_d[...]
        gf = g2_s[...].astype(F32)
        g1 = gf + ln_back(dz, nrm, r, row_of(g_ref))
        g1_ref[...] = g1
        n = g1.shape[1] // 128
        for j, v in enumerate((col_sum(gf), col_sum(dz * nrm), col_sum(dz), col_sum(g1))):
            put_rows(vec_ref, j * n, v)
        for j in range(bg_s.shape[0]):
            put_rows(vec_ref, 4 * n + j * (tile // 128), bg_s[j])


def mlp(place, z2, h1, cot, up_w, up_b, down_w, down_b, gain, pad, dp, parted):
    ex, seq, width = cot.shape
    rows = z2.shape[0]
    ff = up_w.shape[1]
    tile = 4 * ff // dp if parted else 384
    steps = ff // tile
    vec_rows = 4 * width // 128 + ff // 128
    if parted:
        dn, up = part_shape(width, ff, dp), part_shape(ff, width, dp)
        per_half = steps // 2
        dn_spec = pl.BlockSpec((1, dn[1], dn[2] // per_half, 128), lambda i: (i // per_half, 0, i % per_half, 0))
        up_spec = pl.BlockSpec((2, 2, up[2], 128), lambda i: (0, i, 0, 0))
        grads = [(dn, dn_spec), (dn, dn_spec), (up, up_spec), (up, up_spec)]
    else:
        grads = [((width, ff), pl.BlockSpec((width, tile), lambda i: (0, i))),
                 ((ff, width), pl.BlockSpec((tile, width), lambda i: (i, 0)))]
    outs = [((ex, seq, width), whole((ex, seq, width)), BF16)] + [(s, b, BF16) for s, b in grads]
    outs += [((rows, width), whole((rows, width)), F32), ((vec_rows, 128), whole((vec_rows, 128)), F32)]
    return pl.pallas_call(
        functools.partial(mlp_kernel, ex, seq, pad, parted),
        grid=(steps,),
        in_specs=[
            SMEM, whole((rows, width)), whole((rows, width)), whole((ex, seq, width)),
            pl.BlockSpec((width, tile), lambda i: (0, i)), whole((ff,)),
            pl.BlockSpec((tile, width), lambda i: (i, 0)),
            whole((width,)), whole((width,)),
        ],
        out_specs=[b for _, b, _ in outs],
        out_shape=[pltpu.HBM(s, d) for s, _, d in outs],
        scratch_shapes=[
            pltpu.VMEM((rows, width), BF16), pltpu.VMEM((width, rows), BF16),
            pltpu.VMEM((rows, width), F32), pltpu.VMEM((rows, width), F32),
            pltpu.VMEM((steps, 1, tile), F32), pltpu.VMEM((steps, 1, tile), F32),
        ],
        compiler_params=pltpu.CompilerParams(dimension_semantics=("arbitrary",), vmem_limit_bytes=44 << 20),
        cost_estimate=pl.CostEstimate(flops=46 * 10**9, bytes_accessed=30 << 20, transcendentals=rows * ff),
        name="mlp_both_ways",
    )(place, *[in_hbm(x) for x in (z2, h1, cot, up_w, up_b, down_w, down_b, gain)])


def stat_rows(channels):
    return max(8, 2 * channels // 128)


def put_stats(ref, first, second):
    lanes = jnp.concatenate([first, second], axis=1)
    n = ref.shape[0]
    for r in range(lanes.shape[1] // 128):
        ref[:, r, :] = jnp.broadcast_to(lanes[:, r * 128 : (r + 1) * 128], (n, 128))


def get_stats(ref, channels):
    total = jnp.sum(ref[...], axis=0)
    rows = 2 * channels // 128
    half = rows // 2
    first = jnp.concatenate([total[r : r + 1, :] for r in range(half)], axis=1)
    second = jnp.concatenate([total[r : r + 1, :] for r in range(half, rows)], axis=1)
    return first, second


def mean_rstd(ref, channels, count):
    s1, s2 = get_stats(ref, channels)
    mean = s1 * (1.0 / count)
    return mean, lax.rsqrt(s2 * (1.0 / count) - mean * mean + eps_batch)


def real_columns(rows, cols):
    return (lax.broadcasted_iota(jnp.int32, (rows, 1), 0) & 15) < cols


def col_sum(x):
    return jnp.sum(x, axis=0, keepdims=True)


def row_blocks(rows):
    starts = list(range(0, rows - 63, 64))
    return [(a, b) for a, b in zip(starts, starts[1:] + [rows])]


def head_mask(rows, second):
    lane = lax.broadcasted_iota(jnp.int32, (rows, 2 * HD), 1)
    return (lane >= HD) if second else (lane < HD)


def attn_fwd_kernel(ex, n_image, pad, pre_ref, len_ref, h0_ref, g_ref, s_ref, wq_ref, wk_ref, wv_ref, qb_ref, vb_ref,
                    ow_ref, ob_ref, g2_ref, s2_ref,
                    z1_ref, q_ref, k_ref, v_ref, p_ref, attn_ref, h1_ref, z2_ref, acc, qb_s, vb_s):
    i = pl.program_id(0)
    last = pl.num_programs(0) - 1
    wide = wq_ref.shape[1]

    @pl.when(i == 0)
    def _():
        nrm, _r = ln_parts(h0_ref[...].astype(F32))
        z1_ref[...] = (nrm * row_of(g_ref) + row_of(s_ref)).astype(BF16)
        acc[...] = jnp.zeros_like(acc)
        qb, vb = row_of(qb_ref), row_of(vb_ref)
        for j in range(qb_s.shape[0]):
            qb_s[j] = qb[:, j * wide : (j + 1) * wide]
            vb_s[j] = vb[:, j * wide : (j + 1) * wide]

    z1 = z1_ref[...]
    q_ref[...] = (nn(z1, wq_ref[...]) + qb_s[i]).astype(BF16)
    k_ref[...] = nn(z1, wk_ref[...]).astype(BF16)
    v_ref[...] = (nn(z1, wv_ref[...]) + vb_s[i]).astype(BF16)
    zero = jnp.zeros((pad, 2 * HD), BF16)
    first = head_mask(pad, False)

    def example(e, carry):
        row0 = pl.multiple_of(e * pad, 16)
        key = lax.broadcasted_iota(jnp.int32, (pad, pad), 1)
        qry = lax.broadcasted_iota(jnp.int32, (pad, pad), 0)
        limit = jnp.maximum(qry + 1, n_image + pre_ref[e])
        limit = jnp.minimum(limit, n_image + len_ref[e])
        vis = key < limit
        for pair in range(wide // (2 * HD)):
            cols = slice(pair * 2 * HD, (pair + 1) * 2 * HD)
            q2 = q_ref[pl.ds(row0, pad), cols] * jnp.asarray(0.125, BF16)
            k2 = k_ref[pl.ds(row0, pad), cols]
            v2 = v_ref[pl.ds(row0, pad), cols]
            out = None
            for h in range(2):
                sel = first if h == 0 else jnp.logical_not(first)
                raw = nt(jnp.where(sel, q2, zero), k2)
                for lo, up in row_blocks(pad):
                    sc = jnp.where(vis[lo:up], raw[lo:up], masked_value)
                    top = jnp.max(sc, axis=-1, keepdims=True)
                    ex_ = jnp.exp(sc - top)
                    tot = jnp.sum(ex_, axis=-1, keepdims=True)
                    p_ref[e, pair * 2 + h, lo:up, :] = (ex_ * (1.0 / tot)).astype(BF16)
                o = nn(p_ref[e, pair * 2 + h], jnp.where(sel, v2, zero))
                out = o if out is None else out + o
            attn_ref[pl.ds(row0, pad), cols] = out.astype(BF16)
        return carry

    lax.fori_loop(0, ex, example, 0)
    acc[...] += nn(attn_ref[...], ow_ref[...])

    @pl.when(i == last)
    def _():
        h1 = h0_ref[...].astype(F32) + acc[...] + row_of(ob_ref)
        h1_ref[...] = h1
        nrm, _r = ln_parts(h1)
        z2_ref[...] = (nrm * row_of(g2_ref) + row_of(s2_ref)).astype(BF16)


def attn_fwd(h0, prefix, text_len, ln1_gain, ln1_shift, qkv_w, qb, vb, out_w, out_b, ln2_gain, ln2_shift, ex, n_image, pad, wide=256):
    rows, width = h0.shape
    groups = width // wide
    heads = width // HD
    hg = wide // HD
    cols = lambda off: pl.BlockSpec((width, wide), lambda i, *_: (0, i + off * groups))
    vec = whole((width,))
    part = pl.BlockSpec((rows, wide), lambda i, *_: (0, i))
    return pl.pallas_call(
        functools.partial(attn_fwd_kernel, ex, n_image, pad),
        grid_spec=pltpu.PrefetchScalarGridSpec(
            num_scalar_prefetch=2,
            grid=(groups,),
            in_specs=[whole((rows, width)), vec, vec, cols(0), cols(1), cols(2), vec, vec,
                      pl.BlockSpec((wide, width), lambda i, *_: (i, 0)), vec, vec, vec],
            out_specs=[whole((rows, width)), part, part, part,
                       pl.BlockSpec((ex, hg, pad, pad), lambda i, *_: (0, i, 0, 0)),
                       part, whole((rows, width)), whole((rows, width))],
            scratch_shapes=[pltpu.VMEM((rows, width), F32)] + [pltpu.VMEM((groups, 1, wide), F32)] * 2,
        ),
        out_shape=[pltpu.HBM((rows, width), BF16)] * 4 + [
            pltpu.HBM((ex, heads, pad, pad), BF16),
            pltpu.HBM((rows, width), BF16),
            pltpu.HBM((rows, width), F32),
            pltpu.HBM((rows, width), BF16)],
        compiler_params=pltpu.CompilerParams(dimension_semantics=("arbitrary",), vmem_limit_bytes=40 << 20),
        cost_estimate=pl.CostEstimate(flops=32 * 10**9, bytes_accessed=30 << 20, transcendentals=heads * rows * pad),
        name="attention_forward",
    )(prefix, text_len, *[in_hbm(x) for x in (h0, ln1_gain, ln1_shift, qkv_w, qkv_w, qkv_w, qb, vb, out_w, out_b, ln2_gain, ln2_shift)])


def attn_bwd_kernel(ex, n_image, txt, cols_real, pad, parted, lo, final, place_ref, g1_ref, ow_ref, attn_ref, q_ref, k_ref, v_ref, p_ref, z1_ref, wq_ref, wk_ref, wv_ref, *refs):
    if lo:
        acc_c, ow_c, qkv_c, bias_c = refs[:4]
        refs = refs[4:]
    if not final:
        acc, ow_s, qkv_s, bias_s = refs[:4]
        g1b_s, g1t_s, dat_s, dq_s, dk_s, dv_s = refs[4:]
    else:
        h0_ref, g_ref, refs = refs[0], refs[1], refs[2:]
        if parted:
            stem_ref, ak_ref, as_ref, text_ref, dtok_ref, vec_ref, ow_s, qkv_s, proj_s = refs[:9]
        else:
            ow_s, qkv_s, text_ref, dtok_ref, vec_ref = refs[:5]
        g1b_s, g1t_s, dat_s, dq_s, dk_s, dv_s, acc, bias_s = refs[-8:]
    i = pl.program_id(0)
    last = pl.num_programs(0) - 1
    wide = wq_ref.shape[1]

    @pl.when(i == 0)
    def _():
        g1b_s[...] = g1_ref[...].astype(BF16)
        g1t_s[...] = g1b_s[...].T
        if lo:
            acc[...] = acc_c[...]
            ow_s[0:lo] = ow_c[...]
            bias_s[:, 0:lo] = bias_c[...]
            for j in range(3):
                qkv_s[j * z1_ref.shape[1] : j * z1_ref.shape[1] + lo * wide, :] = qkv_c[j]
        else:
            acc[...] = jnp.zeros_like(acc)

    gi = i + lo
    ow_s[gi] = nn(g1t_s[...], attn_ref[...]).astype(BF16)
    dat_s[...] = nt(g1b_s[...], ow_ref[...]).astype(BF16)
    zero = jnp.zeros((pad, 2 * HD), BF16)
    first = head_mask(pad, False)

    def example(e, carry):
        row0 = pl.multiple_of(e * pad, 16)
        for pair in range(wide // (2 * HD)):
            cols = slice(pair * 2 * HD, (pair + 1) * 2 * HD)
            q2 = q_ref[pl.ds(row0, pad), cols]
            k2 = k_ref[pl.ds(row0, pad), cols]
            v2 = v_ref[pl.ds(row0, pad), cols]
            da2 = dat_s[pl.ds(row0, pad), cols]
            dq = dk = dv = None
            for h in range(2):
                sel = first if h == 0 else jnp.logical_not(first)
                pb = p_ref[e, pair * 2 + h]
                dah = jnp.where(sel, da2, zero)
                whole_dp = nt(dah, v2)
                parts = []
                for first_row, end_row in row_blocks(pad):
                    p = pb[first_row:end_row].astype(F32)
                    dp = whole_dp[first_row:end_row]
                    inner = jnp.sum(p * dp, axis=-1, keepdims=True)
                    parts.append((p * (dp - inner)).astype(BF16))
                ds = jnp.concatenate(parts, axis=0)
                dvh = tn(pb, dah)
                dqh = nn(ds, jnp.where(sel, k2, zero))
                dkh = tn(ds, jnp.where(sel, q2, zero))
                dq = dqh if dq is None else dq + dqh
                dk = dkh if dk is None else dk + dkh
                dv = dvh if dv is None else dv + dvh
            dq_s[pl.ds(row0, pad), cols] = (dq * 0.125).astype(BF16)
            dk_s[pl.ds(row0, pad), cols] = (dk * 0.125).astype(BF16)
            dv_s[pl.ds(row0, pad), cols] = dv.astype(BF16)
        return carry

    lax.fori_loop(0, ex, example, 0)
    z1 = z1_ref[...]
    dq, dk, dv = dq_s[...], dk_s[...], dv_s[...]
    width = z1.shape[1]
    for j, d in enumerate((dq, dk, dv)):
        if final:
            qkv_s[pl.ds(pl.multiple_of(j * width + gi * wide, wide), wide), :] = tn(d, z1).astype(BF16)
        else:
            qkv_s[j] = tn(d, z1).astype(BF16)
    acc[...] += nt(dq, wq_ref[...]) + nt(dk, wk_ref[...]) + nt(dv, wv_ref[...])
    bias_s[0, gi] = col_sum(dq.astype(F32))
    bias_s[1, gi] = col_sum(dv.astype(F32))

    if not final:
        return

    @pl.when(i == last)
    def _():
        nrm, r = ln_parts(h0_ref[...].astype(F32))
        dz = acc[...]
        g0 = g1_ref[...] + ln_back(dz, nrm, r, row_of(g_ref))
        n = width // 128
        vec_ref[5 * n :, :] = jnp.zeros_like(vec_ref[5 * n :, :])
        put_rows(vec_ref, n, col_sum(dz * nrm))
        put_rows(vec_ref, 2 * n, col_sum(dz))
        for j in range(2):
            for t in range(bias_s.shape[1]):
                put_rows(vec_ref, (3 + j) * n + t * (wide // 128), bias_s[j, t])
        gb = g0.astype(BF16)
        px = dtok_ref.shape[0] // ex
        pick_image = image_pick(px, pad, n_image, cols_real)
        tr = lax.broadcasted_iota(jnp.int32, (txt, pad), 0)
        tc = lax.broadcasted_iota(jnp.int32, (txt, pad), 1)
        pick_text = jnp.where(tc == tr + n_image, 1.0, 0.0).astype(BF16)
        tot = jnp.zeros((1, gb.shape[1]), F32)
        for e in range(ex):
            ge = gb[e * pad : (e + 1) * pad, :]
            text_ref[e] = nn(pick_text, ge).astype(BF16)
            dt = nn(pick_image, ge)
            dtok_ref[e * px : (e + 1) * px, :] = dt.astype(BF16)
            tot = tot + jnp.sum(dt, axis=0, keepdims=True)
        put_rows(vec_ref, 0, tot)
        if parted:
            core = place_ref[1]
            part_it(qkv_s, ak_ref, as_ref, core)
            proj_s[...] = tn(dtok_ref[...], stem_ref[...]).astype(BF16)
            part_it(proj_s, ak_ref, as_ref, core, at=(qkv_s.shape[0] + width) // (2 * ak_ref.shape[1]) * (width // 256))
            hi = ak_ref.shape[1]
            r = width // (2 * hi)
            at = qkv_s.shape[0] // (2 * hi) * (width // 256)

            def one(h, carry):
                mine = pl.ds(pl.multiple_of((2 * h + core) * r, 16), r)
                other = pl.ds(pl.multiple_of((2 * h + 1 - core) * r, 16), r)
                for blk in range(width // 128):
                    s, j = divmod(blk, width // 256)
                    t, lane = divmod(blk * 128, wide)
                    dst = slice(at + j * r, at + (j + 1) * r)
                    ak_ref[s, h, dst, :] = ow_s[t, mine, lane : lane + 128]
                    as_ref[s, h, dst, :] = ow_s[t, other, lane : lane + 128]
                return carry

            lax.fori_loop(0, hi, one, 0)


def image_pick(px, pad, n_image, cols_real):
    p = lax.broadcasted_iota(jnp.int32, (px, pad), 0)
    t = lax.broadcasted_iota(jnp.int32, (px, pad), 1)
    col = p & 15
    tok = (p >> 4) * cols_real + col
    return jnp.where((col < cols_real) & (tok == t) & (t < n_image), 1.0, 0.0).astype(BF16)


def attn_bwd(place, g1, out_w, attn, q, k, v, p, z1, h0, qkv_w, ln1_gain, ex, n_image, txt, img_rows, img_cols, pad, dp, parted,
             lo=0, hi=None, carry=(), stem=None, wide=256):
    rows, width = h0.shape
    groups = width // wide
    heads = width // HD
    hg = wide // HD
    px = img_rows * 16
    hi = groups if hi is None else hi
    final = hi == groups
    vec_rows = -(-5 * width // 128 // 8) * 8
    cols = lambda off: pl.BlockSpec((width, wide), lambda i: (0, i + lo + off * groups))
    part = pl.BlockSpec((rows, wide), lambda i: (0, i + lo))
    nat_o, nat_q = (groups, width, wide), (3 * width, width)
    sent = part_shape(4 * width, width, dp)
    if stem is not None:
        sent = sent[:2] + (sent[2] + part_shape(width, stem.shape[1], dp)[2], 128)
    scratch = [pltpu.VMEM((rows, width), BF16), pltpu.VMEM((width, rows), BF16)] + [pltpu.VMEM((rows, wide), BF16)] * 4
    args = [g1, out_w, attn, q, k, v, p, z1, qkv_w, qkv_w, qkv_w, *carry]
    in_specs = [SMEM, whole((rows, width)), pl.BlockSpec((wide, width), lambda i: (i + lo, 0)), part, part, part, part,
                pl.BlockSpec((ex, hg, pad, pad), lambda i: (0, i + lo, 0, 0)), whole((rows, width)), cols(0), cols(1), cols(2)]
    in_specs += [whole(c.shape) for c in carry]
    if final:
        outs = [(s, BF16) for s in ((sent, sent) if parted else (nat_o, nat_q))]
        outs += [((ex, txt, width), BF16), ((ex * px, width), BF16), ((vec_rows, 128), F32)]
        natural = [pltpu.VMEM(nat_o, BF16), pltpu.VMEM(nat_q, BF16), pltpu.VMEM((width, stem.shape[1]), BF16)] if parted else []
        scratch = natural + scratch + [pltpu.VMEM((rows, width), F32), pltpu.VMEM((2, groups, 1, wide), F32)]
        args += [h0, ln1_gain] + ([stem] if parted else [])
        in_specs += [whole((rows, width)), whole((width,))] + ([whole(stem.shape)] if parted else [])
    else:
        n = hi - lo
        outs = [((rows, width), F32), ((n, width, wide), BF16), ((3, n * wide, width), BF16), ((2, n, 1, wide), F32)]
    return pl.pallas_call(
        functools.partial(attn_bwd_kernel, ex, n_image, txt, img_cols, pad, parted, lo, final),
        grid=(hi - lo,),
        in_specs=in_specs,
        out_specs=[whole(s) for s, _ in outs],
        out_shape=[pltpu.HBM(s, d) for s, d in outs],
        scratch_shapes=scratch,
        compiler_params=pltpu.CompilerParams(dimension_semantics=("arbitrary",), vmem_limit_bytes=60 << 20),
        cost_estimate=pl.CostEstimate(flops=14 * (hi - lo) * 10**9, bytes_accessed=40 << 20, transcendentals=0),
        name="attention_backward",
    )(place, *[in_hbm(x) for x in args])

def over_pixels(shape, body, init=0):
    ex, rows = shape[:2]
    per = rows // 2

    def one(j, carry):
        return body(j // per, j % per * 2, pl.ds(pl.multiple_of(j * 32, 32), 32), carry)

    return lax.fori_loop(0, ex * per, one, init, unroll=3)


def stats_kernel(cols, x_ref, w_ref, parts_ref, xp):
    xp[...] = jnp.zeros_like(xp)
    shape = x_ref.shape
    xp[:, 0:cols, :] = x_ref[...].reshape(shape[0] * shape[1], cols, shape[3])
    a = nn(xp[...].reshape(shape[0] * shape[1] * 16, shape[3]), w_ref[...])
    put_stats(parts_ref, col_sum(a), col_sum(a * a))


def conv_fwd_kernel(count, ex, rows, cols, place_ref, parts_ref, own_ref, got_ref, win_ref, g_ref, s_ref, wmid_ref,
                    xs_ref, act1_ref, wide_ref, act2_ref, parts2_ref):
    s = place_ref[0]
    half = rows // 2
    px = rows * 16
    chan = xs_ref.shape[-1]
    xs_ref[...] = jnp.zeros_like(xs_ref)
    for e in range(ex):
        xs_ref[e, pl.ds(s * half, half), 0:cols, :] = own_ref[s * ex + e]
        xs_ref[e, pl.ds((1 - s) * half, half), 0:cols, :] = got_ref[e]
    a1 = nn(xs_ref[...].reshape(ex * px, chan), win_ref[...])
    act1_ref[...] = a1
    mid = a1.shape[1]
    mean, rstd = mean_rstd(parts_ref, mid, count)
    real = real_columns(ex * px, cols)
    act = gelu_of((a1 - mean) * rstd * row_of(g_ref) + row_of(s_ref))
    act = jnp.where(real, act, 0.0)
    for e in range(ex):
        part = act[e * px : (e + 1) * px]
        wide_ref[e, 0:16, :] = jnp.zeros((16, 3 * mid), BF16)
        wide_ref[e, px + 16 : px + 32, :] = jnp.zeros((16, 3 * mid), BF16)
        wide_ref[e, 16 : px + 16, 0:mid] = pltpu.roll(part, 1, 0).astype(BF16)
        wide_ref[e, 16 : px + 16, mid : 2 * mid] = part.astype(BF16)
        wide_ref[e, 16 : px + 16, 2 * mid : 3 * mid] = pltpu.roll(part, px - 1, 0).astype(BF16)
    one = real_columns(px, cols)
    t1 = jnp.zeros((1, mid), F32)
    t2 = jnp.zeros((1, mid), F32)
    for e in range(ex):
        a2 = nn(wide_ref[e, 0:px, :], wmid_ref[0])
        a2 = a2 + nn(wide_ref[e, 16 : px + 16, :], wmid_ref[1])
        a2 = a2 + nn(wide_ref[e, 32 : px + 32, :], wmid_ref[2])
        a2 = jnp.where(one, a2, 0.0)
        act2_ref[e * px : (e + 1) * px, :] = a2
        t1 = t1 + col_sum(a2)
        t2 = t2 + col_sum(a2 * a2)
    put_stats(parts2_ref, t1, t2)


def expand_kernel(count, cols, parts_ref, act2_ref, g_ref, s_ref, w_ref, relu2_ref, act3_ref, parts3_ref):
    a2 = act2_ref[...]
    mean, rstd = mean_rstd(parts_ref, a2.shape[1], count)
    act = gelu_of((a2 - mean) * rstd * row_of(g_ref) + row_of(s_ref))
    low = jnp.where(real_columns(a2.shape[0], cols), act, 0.0).astype(BF16)
    relu2_ref[...] = low
    a3 = nn(low, w_ref[...])
    act3_ref[...] = a3
    put_stats(parts3_ref, col_sum(a3), col_sum(a3 * a3))


def tokens_kernel(count, ex, cols, n_image, pad, parts_ref, act3_ref, xs_ref, g_ref, s_ref, w_ref, b_ref, text_ref,
                  stem_ref, h0_ref):
    mean, rstd = mean_rstd(parts_ref, act3_ref.shape[1], count)
    scale = rstd * row_of(g_ref)
    offset = row_of(s_ref) - mean * scale

    def body(e, r, rs, carry):
        pre = act3_ref[rs, :] * scale + offset + xs_ref[e, pl.ds(r, 2)].reshape(32, -1).astype(F32)
        stem_ref[rs, :] = gelu_of(pre).astype(BF16)
        return carry

    over_pixels(xs_ref.shape, body)
    tok = (nn(stem_ref[...], w_ref[...]) + row_of(b_ref)).astype(BF16)
    px = act3_ref.shape[0] // ex
    txt = text_ref.shape[1]
    t = lax.broadcasted_iota(jnp.int32, (pad, px), 0)
    p = lax.broadcasted_iota(jnp.int32, (pad, px), 1)
    col = p & 15
    pick = jnp.where((col < cols) & ((p >> 4) * cols + col == t), 1.0, 0.0).astype(BF16)
    tr = lax.broadcasted_iota(jnp.int32, (pad, txt), 0)
    tc = lax.broadcasted_iota(jnp.int32, (pad, txt), 1)
    pick_text = jnp.where(tr == tc + n_image, 1.0, 0.0).astype(BF16)
    for e in range(ex):
        both = nn(pick, tok[e * px : (e + 1) * px, :]) + nn(pick_text, text_ref[e])
        h0_ref[e * pad : (e + 1) * pad, :] = both.astype(BF16)


def dpre_kernel(count, ex, rows, place_ref, parts_ref, act3_ref, xs_ref, g_ref, s_ref, dtok_ref, w_ref, dpre_ref, send_ref, parts4_ref, raw_s):
    chan = act3_ref.shape[1]
    mean, rstd = mean_rstd(parts_ref, chan, count)
    gain, shift = row_of(g_ref), row_of(s_ref)
    raw_s[...] = nt(dtok_ref[...], w_ref[...])

    def body(e, r, rs, carry):
        nrm = (act3_ref[rs, :] - mean) * rstd
        _, slope = gelu_and_slope(nrm * gain + shift + xs_ref[e, pl.ds(r, 2)].reshape(32, chan).astype(F32))
        d = raw_s[rs, :] * slope
        dpre_ref[e, pl.ds(r, 2)] = d.astype(BF16).reshape(2, 16, chan)
        return carry[0] + jnp.sum(d.reshape(4, 8, chan), axis=0), carry[1] + jnp.sum((d * nrm).reshape(4, 8, chan), axis=0)

    zero = jnp.zeros((8, chan), F32)
    a, b = over_pixels(xs_ref.shape, body, (zero, zero))
    put_stats(parts4_ref, col_sum(a), col_sum(b))
    half = rows // 2
    other = 1 - place_ref[0]
    for e in range(ex):
        send_ref[e] = dpre_ref[e, pl.ds(other * half, half)]


def back3_kernel(count, cols, parts4_ref, parts3_ref, parts2_ref, act3_ref, dpre_ref, g3_ref, w_ref, act2_ref, g2_ref, s2_ref, veca_ref, vecb_ref,
                 low3_ref, t2_ref, parts5_ref, gain_ref, shift_ref, small_s):
    chan = act3_ref.shape[1]
    mean, rstd = mean_rstd(parts3_ref, chan, count)
    s1, s2 = get_stats(parts4_ref, chan)
    gain_ref[...] = s2.reshape(-1)
    shift_ref[...] = s1.reshape(-1)
    scale = row_of(g3_ref) * rstd
    c1, c2 = s1 * (1.0 / count), s2 * (1.0 / count)
    real = real_columns(32, cols)

    def body(e, r, rs, carry):
        nrm = (act3_ref[rs, :] - mean) * rstd
        d = scale * (dpre_ref[e, pl.ds(r, 2)].reshape(32, chan).astype(F32) - c1 - nrm * c2)
        low3_ref[rs, :] = jnp.where(real, d, 0.0).astype(BF16)
        return carry

    over_pixels(dpre_ref.shape, body)
    a2 = act2_ref[...]
    mean2, rstd2 = mean_rstd(parts2_ref, a2.shape[1], count)
    nrm2 = (a2 - mean2) * rstd2
    _, slope = gelu_and_slope(nrm2 * row_of(g2_ref) + row_of(s2_ref))
    t2 = nt(low3_ref[...], w_ref[...]) * slope
    t2_ref[...] = t2
    parts5_ref[...] = jnp.zeros_like(parts5_ref)
    put_stats(parts5_ref, col_sum(t2), col_sum(t2 * nrm2))
    used = veca_ref.shape[0] + vecb_ref.shape[0]
    n = parts5_ref.shape[0]
    each = -(-used // n)
    small_s[0 : veca_ref.shape[0], :] = veca_ref[...]
    small_s[veca_ref.shape[0] : used, :] = vecb_ref[...]
    if used < small_s.shape[0]:
        small_s[used:, :] = jnp.zeros_like(small_s[used:, :])
    for d in range(n):
        parts5_ref[d, 4 : 4 + each, :] = small_s[d * each : (d + 1) * each, :]


def back2_kernel(count, ex, rows, cols, place_ref, parts5_ref, parts2_ref, parts1_ref, act2_ref, t2_ref, g2_ref, wmid_ref, act1_ref, g1_ref, s1_ref,
                 low2_ref, t1_ref, send_ref, parts6_ref, gain_ref, shift_ref, wide):
    a2 = act2_ref[...]
    mid = a2.shape[1]
    px = rows * 16
    mean, rstd = mean_rstd(parts2_ref, mid, count)
    s1, s2 = get_stats(parts5_ref, mid)
    gain_ref[...] = s2.reshape(-1)
    shift_ref[...] = s1.reshape(-1)
    nrm = (a2 - mean) * rstd
    d = (row_of(g2_ref) * rstd) * (t2_ref[...] - s1 * (1.0 / count) - nrm * (s2 * (1.0 / count)))
    d = jnp.where(real_columns(ex * px, cols), d, 0.0)
    low2_ref[...] = d.astype(BF16)
    for e in range(ex):
        part = d[e * px : (e + 1) * px]
        wide[e, 0:16, :] = jnp.zeros((16, 3 * mid), BF16)
        wide[e, px + 16 : px + 32, :] = jnp.zeros((16, 3 * mid), BF16)
        wide[e, 16 : px + 16, 0:mid] = pltpu.roll(part, px - 1, 0).astype(BF16)
        wide[e, 16 : px + 16, mid : 2 * mid] = part.astype(BF16)
        wide[e, 16 : px + 16, 2 * mid : 3 * mid] = pltpu.roll(part, 1, 0).astype(BF16)
    mean1, rstd1 = mean_rstd(parts1_ref, mid, count)
    one = real_columns(px, cols)
    q1 = jnp.zeros((1, mid), F32)
    q2 = jnp.zeros((1, mid), F32)
    for e in range(ex):
        t = None
        for r in range(3):
            for c in range(3):
                term = nt(wide[e, (2 - r) * 16 : (2 - r) * 16 + px, c * mid : (c + 1) * mid], wmid_ref[r, c * mid : (c + 1) * mid, :])
                t = term if t is None else t + term
        nrm1 = (act1_ref[e * px : (e + 1) * px, :] - mean1) * rstd1
        _, slope = gelu_and_slope(nrm1 * row_of(g1_ref) + row_of(s1_ref))
        t = jnp.where(one, t * slope, 0.0)
        t1_ref[e] = t.reshape(rows, 16, mid)
        q1 = q1 + col_sum(t)
        q2 = q2 + col_sum(t * nrm1)
    put_stats(parts6_ref, q1, q2)
    chunk = jnp.sum(parts5_ref[:, 4:8, :], axis=0)
    parts6_ref[:, 4:8, :] = jnp.broadcast_to(chunk[None], (parts6_ref.shape[0], 4, 128))
    half = rows // 2
    other = 1 - place_ref[0]
    for e in range(ex):
        send_ref[e] = t1_ref[e, pl.ds(other * half, half)].astype(BF16)


def conv_grads_kernel(ex, px, parted, place_ref, low2_ref, wide_ref, low3_ref, relu2_ref, *refs):
    mid = low2_ref.shape[1]
    nat_m, nat_o = (refs[2], refs[3]) if parted else (refs[0], refs[1])
    nat_o[...] = tn(low3_ref[...], relu2_ref[...]).astype(BF16)
    for r in range(3):
        tot = None
        for e in range(ex):
            term = tn(low2_ref[e * px : (e + 1) * px, :], wide_ref[e, r * 16 : r * 16 + px, :])
            tot = term if tot is None else tot + term
        for c in range(3):
            for h in range(2):
                at = (h * 9 + r * 3 + c) * (mid // 2)
                src = c * mid + h * (mid // 2)
                nat_m[:, at : at + mid // 2] = tot[:, src : src + mid // 2].astype(BF16)
    if parted:
        part_it(nat_m, refs[0], refs[1], place_ref[1])
        part_it(nat_o, refs[0], refs[1], place_ref[1], at=nat_m.shape[0] // (2 * refs[0].shape[1]) * (nat_m.shape[1] // 256))


def tn_kernel(parted, place_ref, a_ref, b_ref, *refs):
    natural = refs[2] if parted else refs[0]
    natural[...] = tn(a_ref[...], b_ref[...]).astype(BF16)
    if parted:
        part_it(natural, refs[0], refs[1], place_ref[1])


def first_back_kernel(count, ex, rows, cols, parted, each, places, place_ref, parts6_ref, parts1_ref, x_ref, win_ref, g_ref, t1_ref, gott_ref,
                      low_ref, *refs):
    if parted:
        keep_ref, send_ref, win_grad_ref = refs[0], refs[1], refs[-1]
        refs = refs[2:-1]
    else:
        win_grad_ref, refs = refs[0], refs[1:]
    gain_ref, shift_ref, vec_refs, xp, small_s = refs[0], refs[1], refs[2:-2], refs[-2], refs[-1]
    s = place_ref[0]
    half = rows // 2
    chan = x_ref.shape[-1]
    mid = win_ref.shape[1]
    mean, rstd = mean_rstd(parts1_ref, mid, count)
    s1, s2 = get_stats(parts6_ref, mid)
    gain_ref[...] = s2.reshape(-1)
    shift_ref[...] = s1.reshape(-1)
    real = real_columns(ex * half * 16, cols)
    size = ex * half * 16
    xp[...] = jnp.zeros_like(xp)
    wg = None
    for own in (True, False):
        at = (s if own else 1 - s) * ex
        xp[:, 0:cols, :] = x_ref[pl.ds(at, ex)].reshape(ex * half, cols, chan)
        x = xp[...].reshape(size, chan)
        nrm = (nn(x, win_ref[...]) - mean) * rstd
        if own:
            t = t1_ref[:, pl.ds(s * half, half)].reshape(size, mid)
        else:
            t = gott_ref[...].reshape(size, mid).astype(F32)
        d = (row_of(g_ref) * rstd) * (t - s1 * (1.0 / count) - nrm * (s2 * (1.0 / count)))
        low = jnp.where(real, d, 0.0).astype(BF16)
        low_ref[0 if own else 1] = low
        term = tn(low, x)
        wg = term if wg is None else wg + term
    win_grad_ref[...] = wg.astype(BF16)
    if parted:
        part_it(win_grad_ref, keep_ref, send_ref, place_ref[1])
    for d in range(parts6_ref.shape[0]):
        small_s[d * each : (d + 1) * each, :] = parts6_ref[d, 4 : 4 + each, :]
    for ref, at in zip(vec_refs, places):
        ref[...] = take_rows(small_s, at, ref.shape[0]).reshape(-1)


def image_kernel(ex, rows, cols, place_ref, low_ref, win_ref, dpre_ref, gotd_ref, grad_ref):
    s = place_ref[0]
    half = rows // 2
    chan = win_ref.shape[0]
    size = ex * half * 16
    for own in (True, False):
        at = (s if own else 1 - s) * ex
        dp = dpre_ref[:, pl.ds(s * half, half)] if own else gotd_ref[...]
        grad = nt(low_ref[0 if own else 1], win_ref[...]) + dp.reshape(size, chan).astype(F32)
        grad_ref[pl.ds(at, ex)] = grad.astype(BF16).reshape(ex, half, 16, chan)[:, :, 0:cols, :]


def in_hbm(x):
    return pltpu.with_memory_space_constraint(x, pltpu.HBM)


def call(kernel, outs, *args, moved=(), place=None, scratch=(), name=None, us=2, limit=40):
    nbytes = sum(a.size * a.dtype.itemsize for a in args)
    spec = lambda s: pl.BlockSpec(s, lambda i: (0,) * len(s))
    return pl.pallas_call(
        kernel,
        grid=(1,),
        out_shape=[pltpu.HBM(s, d) for s, d in outs],
        in_specs=([SMEM] if place is not None else []) + [spec(a.shape) for a in args],
        out_specs=[spec(s) for s, _ in outs],
        scratch_shapes=list(scratch),
        compiler_params=pltpu.CompilerParams(vmem_limit_bytes=limit << 20),
        cost_estimate=pl.CostEstimate(flops=us * 10**9, bytes_accessed=nbytes if us else 0, transcendentals=0),
        name=name,
    )(*([place] if place is not None else []), *[a if any(a is b for b in moved) else in_hbm(a) for a in args])


DP = ("far", "near", "core")
AXES = DP + ("space",)


def spread(parts):
    return lax.all_to_all(parts, AXES, split_axis=0, concat_axis=0, tiled=True)


def swap(x, axis="space"):
    return lax.ppermute(x, axis, [(0, 1), (1, 0)])


def tie(*values):
    return lax.optimization_barrier(values)


BITS = ("space", "f1", "f0", "near")


def bit_of(name):
    if name in ("f0", "f1"):
        return (lax.axis_index("far") // (1 if name == "f0" else 2)) % 2
    return lax.axis_index(name)


def sent(x, key):
    if key == ("core",):
        return swap(x, "core")
    flip = {n: int(n in key) for n in BITS}
    far, near, space = 2 * flip["f1"] + flip["f0"], flip["near"], flip["space"]
    if far and (near or space):
        raise ValueError
    if far:
        return lax.ppermute(x, "far", [(j, j ^ far) for j in range(4)])
    if near and space:
        return lax.ppermute(x, ("near", "space"), [(j, 3 - j) for j in range(4)])
    return swap(x, "near" if near else "space")


class Box:
    def __init__(self, value, moved=False):
        self.value, self.moved = value, moved


class Pack:
    def __init__(self, sources, left, size, at=0, rows=None):
        self.sources, self.left, self.size, self.at, self.rows = sources, left, size, at, size if rows is None else rows

    @classmethod
    def start(cls, keep, send):
        size = keep.shape[-2]
        got = sent(send, ("core",))
        return cls([(Box(keep.reshape(-1, 128)), 0), (Box(got.reshape(-1, 128), True), 0)], list(BITS), size)

    def thirds(self):
        r = self.size // 3
        return [Pack(self.sources, self.left, self.size, k * r, r) for k in range(3)]


def arrive(value, *packs):
    boxes = []
    for x in packs:
        boxes += [b for b, _ in x.sources if b.moved and b not in boxes]
    flat = tie(value, *[b.value for b in boxes])
    for b, v in zip(boxes, flat[1:], strict=True):
        b.value = v
    return flat[0]


def combine_kernel(plan, n_in, bits_ref, *refs):
    ins, outs = refs[:n_in], refs[n_in:]
    for sources, left, size, at, rows, names, dests in plan:
        rest = [d for d in left if d not in names]
        for rel, (out, to) in enumerate(dests):
            for c in range(2 ** len(rest)):
                place = 0
                for pos, d in enumerate(left):
                    stride = 2 ** (len(left) - 1 - pos)
                    if d in names:
                        bit = bits_ref[BITS.index(d)]
                        if (rel >> (len(names) - 1 - names.index(d))) & 1:
                            bit = 1 - bit
                    else:
                        bit = (c >> (len(rest) - 1 - rest.index(d))) & 1
                    place = place + bit * stride
                tot = None
                for idx, first in sources:
                    x = ins[idx][pl.ds(pl.multiple_of(first + place * size + at, 16), rows), :].astype(F32)
                    tot = x if tot is None else tot + x
                outs[out][to + c * rows : to + (c + 1) * rows, :] = tot.astype(BF16)


def step(bits, moves, tied):
    boxes, plan, keys, totals, after = [], [], [], {(): 0}, []
    for pack, names in moves:
        srcs = []
        for box, first in pack.sources:
            if box not in boxes:
                boxes.append(box)
            srcs.append((boxes.index(box), first))
        rest = [d for d in pack.left if d not in names]
        n = 2 ** len(rest) * pack.rows
        dests = []
        for rel in range(2 ** len(names)):
            key = tuple(d for j, d in enumerate(names) if (rel >> (len(names) - 1 - j)) & 1)
            key = tuple(sorted(key))
            if key not in totals:
                totals[key] = 0
            if key not in keys:
                keys.append(key)
            dests.append((key, totals[key]))
            totals[key] += n
        plan.append((srcs, list(pack.left), pack.size, pack.at, pack.rows, names, dests))
        after.append((rest, pack.rows, dests))
    plan = [(*p[:-1], [(keys.index(k), to) for k, to in p[-1]]) for p in plan]
    args = [b.value if b.moved else in_hbm(b.value) for b in boxes]
    one = lambda shape: pl.BlockSpec(shape, lambda t: (0, 0), pipeline_mode=pl.Buffered(1))
    res = pl.pallas_call(
        functools.partial(combine_kernel, plan, len(args)),
        grid=(1,),
        in_specs=[SMEM] + [one(x.shape) for x in args],
        out_specs=[one((totals[k], 128)) for k in keys],
        out_shape=[pltpu.HBM((totals[k], 128), BF16) for k in keys],
        compiler_params=pltpu.CompilerParams(vmem_limit_bytes=40 << 20),
        cost_estimate=pl.CostEstimate(flops=0, bytes_accessed=0, transcendentals=0),
        name="combine",
    )(bits, *args)
    flat = tie(tied, *res)
    arrays = {k: Box(flat[1 + j] if k == () else sent(flat[1 + j], k), k != ()) for j, k in enumerate(keys)}
    packs = [Pack([(arrays[k], to) for k, to in dests], rest, rows) for rest, rows, dests in after]
    return flat[0], packs


def finish_kernel(plan, n_in, *refs):
    ins, outs = refs[:n_in], refs[n_in:]
    for sources, pieces in plan:
        for first, r, blocks, out in pieces:
            for b in range(blocks):
                tot = None
                for idx, at in sources:
                    lo = at + first + b * r
                    if len(ins[idx].shape) == 3:
                        x = jnp.sum(ins[idx][:, lo : lo + r, :].astype(F32), axis=0)
                    else:
                        x = ins[idx][lo : lo + r, :].astype(F32)
                    tot = x if tot is None else tot + x
                if len(outs[out].shape) == 3:
                    outs[out][b] = tot
                else:
                    outs[out][:, b * 128 : (b + 1) * 128] = tot


def finish(groups, shapes, name):
    boxes, plan = [], []
    for sources, pieces in groups:
        srcs = []
        for box, first in sources:
            if box not in boxes:
                boxes.append(box)
            srcs.append((boxes.index(box), first))
        plan.append((srcs, pieces))
    args = [b.value for b in boxes]
    return call(functools.partial(finish_kernel, plan, len(args)), [(s, F32) for s in shapes], *args, moved=args, name=name)


def halve_dp(x, axis, bit):
    size = lax.axis_size(DP)
    mine = (lax.axis_index(DP) // bit) % 2
    keep = lax.dynamic_index_in_dim(x, mine, axis, keepdims=True)
    send = lax.dynamic_index_in_dim(x, 1 - mine, axis, keepdims=True)
    return keep + lax.ppermute(send, DP, [(j, j ^ bit) for j in range(size)])


def scattered(grad_t):
    size = lax.axis_size(DP)
    bits = size.bit_length() - 1
    cols, rows = grad_t.shape
    x = grad_t.reshape((2,) * bits + (cols // size, rows))
    for b in range(bits):
        x = halve_dp(x, bits - 1 - b, 1 << b)
    half = rows // 2
    mine = lax.axis_index("space")
    keep = lax.dynamic_slice_in_dim(x, mine * half, half, axis=x.ndim - 1)
    send = lax.dynamic_slice_in_dim(x, (1 - mine) * half, half, axis=x.ndim - 1)
    return (keep + swap(send)).reshape(cols // size, half).astype(F32).T


def shards(
    image_in, text_in, prefix, text_len, cotangent,
    conv_in_w, bn1_gain, bn1_shift, conv_mid_w, bn2_gain, bn2_shift, conv_out_w, bn3_gain, bn3_shift,
    proj_w, proj_b, ln1_gain, ln1_shift, qkv_w, query_bias, value_bias, out_w, out_b,
    ln2_gain, ln2_shift, up_w, up_b, down_w, down_b,
):
    n_dev, dp = lax.axis_size(AXES), lax.axis_size(DP)
    band_ex, band_rows, cols, chan = image_in.shape
    mid = conv_in_w.shape[1]
    width = proj_w.shape[1]
    ff = up_w.shape[1]
    ex, txt, _ = text_in.shape
    rows = band_rows * lax.axis_size("space")
    n_image = rows * cols
    seq = n_image + txt
    pad = -(-seq // 16) * 16
    px = rows * 16
    count = float(band_ex * band_rows * cols * n_dev)
    me = lax.axis_index("space").astype(jnp.int32)
    place = jnp.stack([me, lax.axis_index("core").astype(jnp.int32)])
    small, large, tiny = (n_dev, stat_rows(mid), 128), (n_dev, stat_rows(chan), 128), (n_dev, 2 * mid // 128, 128)
    wmid = conv_mid_w.reshape(3, 3 * mid, mid)
    weights = [(mid, chan), (mid, 9 * mid), (chan, mid), (width, chan), (3 * width, width), (width, width), (ff, width), (width, ff)]
    parted = dp == 16 and mid == 256 and all(c % (16 * dp) == 0 and r % 256 == 0 for c, r in weights)
    hi = dp // 2

    def grad_outs(c, r):
        return [(part_shape(c, r, dp), BF16)] * 2 if parted else [((c, r), BF16)]

    def natural(c, r):
        return [pltpu.VMEM((c, r), BF16)] if parted else []

    got_x = swap(lax.dynamic_slice_in_dim(image_in, (1 - me) * ex, ex, axis=0))
    parts1, = call(functools.partial(stats_kernel, cols), [(tiny, F32)], image_in, conv_in_w,
                   scratch=[pltpu.VMEM((band_ex * band_rows, 16, chan), BF16)], name="stats_one")
    parts1 = spread(parts1)
    xs, act1, wide, act2, parts2 = call(
        functools.partial(conv_fwd_kernel, count, ex, rows, cols),
        [((ex, rows, 16, chan), BF16), ((ex * px, mid), F32), ((ex, px + 32, 3 * mid), BF16), ((ex * px, mid), F32), (tiny, F32)],
        parts1, image_in, got_x, conv_in_w, bn1_gain, bn1_shift, wmid, moved=(parts1, got_x), place=place, name="conv_three", us=4)
    parts2 = spread(parts2)
    relu2, act3, parts3 = call(
        functools.partial(expand_kernel, count, cols),
        [((ex * px, mid), BF16), ((ex * px, chan), F32), (large, F32)],
        parts2, act2, bn2_gain, bn2_shift, conv_out_w, moved=(parts2,), name="expand")
    parts3 = spread(parts3)
    stem, h0 = call(
        functools.partial(tokens_kernel, count, ex, cols, n_image, pad),
        [((ex * px, chan), BF16), ((ex * pad, width), BF16)],
        parts3, act3, xs, bn3_gain, bn3_shift, proj_w, proj_b, text_in, moved=(parts3,), name="tokens", us=5)
    z1, q, k, v, p, attn, h1, z2 = attn_fwd(h0, prefix, text_len, ln1_gain, ln1_shift, qkv_w, query_bias, value_bias,
                                            out_w, out_b, ln2_gain, ln2_shift, ex, n_image, pad)
    mlp_outs = mlp(place, z2, h1, cotangent, up_w, up_b, down_w, down_b, ln2_gain, pad, dp, parted)
    block_out, mlp_grads, (g1, veca) = mlp_outs[0], mlp_outs[1:-2], mlp_outs[-2:]
    if parted:
        bits = jnp.stack([bit_of(n) for n in BITS]).astype(jnp.int32)
        down, up = Pack.start(*mlp_grads[:2]), Pack.start(*mlp_grads[2:])
    back_args = (out_w, attn, q, k, v, p, z1, h0, qkv_w, ln1_gain, ex, n_image, txt, rows, cols, pad, dp, parted)
    if parted:
        carry = attn_bwd(place, g1, *back_args, hi=1)
        turns = [["space"], ["near"], ["f0"]]
        ffn = down.thirds() + up.thirds()
        g1, ffn = step(bits, list(zip(ffn, turns + turns)), tie(g1, *carry)[0])
        att_outs = attn_bwd(place, g1, *back_args, lo=1, carry=carry, stem=stem)
    else:
        att_outs = attn_bwd(place, g1, *back_args)
    att_grads, (text_grad, dtok, vecb) = att_outs[:-3], att_outs[-3:]
    if parted:
        later = turns[1:] + turns[:1]
        (dtok, att_send), ffn = step(bits, list(zip(ffn, later * 2)), (dtok, att_grads[1]))
        att = Pack.start(att_grads[0], att_send)
    dpre, dsend, parts4 = call(
        functools.partial(dpre_kernel, count, ex, rows),
        [((ex, rows, 16, chan), BF16), ((ex, band_rows, 16, chan), BF16), (large, F32)],
        parts3, act3, xs, bn3_gain, bn3_shift, dtok, proj_w, moved=(parts3,), place=place, scratch=[pltpu.VMEM((ex * px, chan), F32)], name="stem_back", us=7)
    got_d = swap(dsend)
    if parted:
        parts4 = arrive(parts4, *ffn, att)
    parts4 = spread(parts4)
    if parted:
        later = later[1:] + later[:1]
        dpre, moved = step(bits, list(zip(ffn, later * 2)) + list(zip(att.thirds(), later)), dpre)
        ffn, att = moved[:6], moved[6:]
    else:
        proj_g = call(functools.partial(tn_kernel, parted), grad_outs(width, chan), dtok, stem, place=place, name="proj_grad", us=0)
    low3, t2, parts5, bn3_gg, bn3_sg = call(
        functools.partial(back3_kernel, count, cols),
        [((ex * px, chan), BF16), ((ex * px, mid), F32), (small, F32), ((chan,), F32), ((chan,), F32)],
        parts4, parts3, parts2, act3, dpre, bn3_gain, conv_out_w, act2, bn2_gain, bn2_shift, veca, vecb, moved=(parts4, parts3, parts2),
        scratch=[pltpu.VMEM((n_dev * -(-(veca.shape[0] + vecb.shape[0]) // n_dev), 128), F32)], name="back_three", us=4)
    if parted:
        t2 = arrive(t2, *att)
    parts5 = spread(parts5)
    if parted:
        later = later[1:] + later[:1]
        t2, moved = step(bits, [(x, ["f1"]) for x in ffn] + list(zip(att, later)), t2)
        ffn, att = moved[:6], moved[6:]
    low2, t1, tsend, parts6, bn2_gg, bn2_sg = call(
        functools.partial(back2_kernel, count, ex, rows, cols),
        [((ex * px, mid), BF16), ((ex, rows, 16, mid), F32), ((ex, band_rows, 16, mid), BF16), (small, F32), ((mid,), F32), ((mid,), F32)],
        parts5, parts2, parts1, act2, t2, bn2_gain, wmid, act1, bn1_gain, bn1_shift,
        moved=(parts5, parts2, parts1), place=place, scratch=[pltpu.VMEM((ex, px + 32, 3 * mid), BF16)], name="back_two", us=4)
    got_t = swap(tsend)
    parts6 = spread(parts6)
    if parted:
        low2, got_t = arrive(tie(low2, got_t), *att)
    conv_g = call(
        functools.partial(conv_grads_kernel, ex, px, parted),
        [(part_shape(mid, 9 * mid, dp)[:2] + (part_shape(mid, 9 * mid, dp)[2] + part_shape(chan, mid, dp)[2], 128), BF16)] * 2
        if parted else [((mid, 9 * mid), BF16), ((chan, mid), BF16)],
        low2, wide, low3, relu2, place=place, scratch=natural(mid, 9 * mid) + natural(chan, mid), name="conv_grads", us=4)
    if parted:
        parts6, conv_send = arrive(tie(parts6, conv_g[1]), *ffn, *att)
        conv = Pack.start(conv_g[0], conv_send)
    each = -(-(veca.shape[0] + vecb.shape[0]) // n_dev)
    n, off = width // 128, veca.shape[0]
    places = [off, off + n, off + 2 * n, off + 3 * n, off + 4 * n, 3 * n, n, 2 * n, 4 * n, 0]
    sizes = [width] * 8 + [ff, width]
    last = call(
        functools.partial(first_back_kernel, count, ex, rows, cols, parted, each, places),
        [((2, ex * band_rows * 16, mid), BF16)] + grad_outs(mid, chan) + [((mid,), F32)] * 2 + [((s,), F32) for s in sizes],
        parts6, parts1, image_in, conv_in_w, bn1_gain, t1, got_t,
        moved=(parts6, parts1, got_t), place=place, scratch=[pltpu.VMEM((ex * band_rows, 16, chan), BF16), pltpu.VMEM((n_dev * each, 128), F32)] + natural(mid, chan),
        name="first_back", us=3)
    low1, sums = last[0], last[3 if parted else 2 :]
    bn1_gg, bn1_sg, vecs = sums[0], sums[1], sums[2:]
    if parted:
        later = later[1:] + later[:1]
        (low1, keep_x), moved = step(bits, list(zip(att, later)) + [(conv, ["near", "space"])], (low1, last[1]))
        att, conv = moved[:3], moved[3]
    image_grad, = call(functools.partial(image_kernel, ex, rows, cols), [(image_in.shape, BF16)], low1, conv_in_w, dpre, got_d,
                       moved=(got_d,), place=place, name="image_back", us=4)
    if parted:
        in_x = (keep_x + swap(last[2], "core")).reshape((2 * hi,) + keep_x.shape[2:])
        in_x = lax.all_to_all(in_x, ("space", "far", "near"), split_axis=0, concat_axis=0, tiled=True)
        image_grad, moved = step(bits, [(x, ["f1"]) for x in att] + [(conv, ["f1", "f0"])], image_grad)
        att, conv = moved[:3], moved[3]
        r_mid, r_out3, r_q, r_w, r_f = mid // dp, chan // dp, 3 * width // dp, width // dp, ff // dp
        mids, half = r_mid * (9 * mid // 256), width // 256
        g_down, g_up = finish(
            [(ffn[0].sources, [(0, r_w, ff // 256, 0)]), (ffn[3].sources, [(0, r_f, half, 1)])],
            [(r_w, ff // 2), (r_f, width // 2)], "finish_early")
        g_qkv, g_out, g_proj, g_mid, g_out3, g_in = finish(
            [(att[0].sources, [(0, r_q, half, 0), (r_q * half, r_w, half, 1), ((r_q + r_w) * half, r_w, chan // 256, 2)]),
             (conv.sources, [(0, r_mid, 9 * mid // 256, 3), (mids, r_out3, mid // 256, 4)]),
             ([(Box(in_x), 0)], [(0, r_mid, chan // 256, 5)])],
            [(r_q, width // 2), (r_w, width // 2), (r_w, chan // 2), (9 * mid // 256, r_mid, 128), (r_out3, mid // 2), (r_mid, chan // 2)], "finish_late")
        g_down, g_up, g_qkv, g_out, g_proj, g_out3, g_in = [g.T for g in (g_down, g_up, g_qkv, g_out, g_proj, g_out3, g_in)]
        g_mid = g_mid.reshape(3, 3, r_mid, mid // 2).transpose(0, 1, 3, 2)
    else:
        out_n = att_outs[0].transpose(1, 0, 2).reshape(width, width)
        g_in, g_mid, g_out3, g_proj, g_qkv, g_out, g_up, g_down = [
            scattered(x) for x in (last[1], conv_g[0], conv_g[1], proj_g[0], att_outs[1], out_n, mlp_grads[1], mlp_grads[0])]
        g_mid = g_mid.reshape(3, 3, mid // 2, -1)
    return (
        block_out, image_grad, text_grad,
        g_in, bn1_gg, bn1_sg,
        g_mid, bn2_gg, bn2_sg,
        g_out3, bn3_gg, bn3_sg,
        g_proj, vecs[0], vecs[1], vecs[2],
        g_qkv, vecs[3], vecs[4],
        g_out, vecs[5], vecs[6], vecs[7],
        g_up, vecs[8],
        g_down, vecs[9],
    )


def solution(mesh):
    dp, space = mesh.devices.shape
    fine = Mesh(mesh.devices.reshape(dp // 4, 2, 2, space), AXES)
    return jax.shard_map(
        shards,
        mesh=fine,
        in_specs=(
            P(DP, "space", None, None),
            P(AXES, None, None),
            P(AXES),
            P(AXES),
            P(AXES, None, None),
            P(),
            P(),
            P(),
            P(),
            P(),
            P(),
            P(),
            P(),
            P(),
            P(),
            P(),
            P(),
            P(),
            P(),
            P(),
            P(),
            P(),
            P(),
            P(),
            P(),
            P(),
            P(),
            P(),
            P(),
        ),
        out_specs=(
            P(AXES, None, None),
            P(DP, "space", None, None),
            P(AXES, None, None),
            P("space", DP),
            P(),
            P(),
            P(None, None, "space", DP),
            P(),
            P(),
            P("space", DP),
            P(),
            P(),
            P("space", DP),
            P(),
            P(),
            P(),
            P("space", DP),
            P(),
            P(),
            P("space", DP),
            P(),
            P(),
            P(),
            P("space", DP),
            P(),
            P("space", DP),
            P(),
        ),
        check_vma=False,
    )
```
